32 devices in a mesh: rep: 4 (over z), grp: 8 (over y, x, core).
Axes of the slice: x: 2, y: 2, z: 4, core: 2. Of those that a mesh axis runs over, the one named last changes fastest.
Arguments:
- tokens: bfloat16 [8192, 2048], P(('rep', 'grp')), may hold values from -6 to 6
- response_sensitivity: bfloat16 [8192, 2048], P(('rep', 'grp')), may hold values from -6 to 6
- seq_lengths: int32 [8], replicated, may hold values from 1024 to 1024, as said below
- prefix_lengths: int32 [8], replicated, may hold values from 204 to 512, as said below
- adapter_ids: int32 [8], replicated, may hold values from 0 to 7, as said below
- attn_gain: float32 [2048], replicated, may hold values from 0.1 to 1.9
- mlp_gain: float32 [2048], replicated, may hold values from 0.1 to 1.9
- qkv_weight: bfloat16 [2048, 2560], P(None, 'grp'), may hold values from -0.125 to 0.125
- out_weight: bfloat16 [2048, 2048], P(None, 'grp'), may hold values from -2 to 2
- gate_up_weight: bfloat16 [2048, 11264], P(None, 'grp'), may hold values from -0.125 to 0.125
- down_weight: bfloat16 [5632, 2048], P(None, 'grp'), may hold values from -0.078125 to 0.078125
- query_in: bfloat16 [2048, 128], replicated, may hold values from -0.125 to 0.125
- asking_right_pieces: bfloat16 [128, 2048], replicated, may hold values from -0.75 to 0.75
- key_in: bfloat16 [2048, 128], replicated, may hold values from -0.125 to 0.125
- lookup_right_pieces: bfloat16 [128, 256], replicated, may hold values from -0.75 to 0.75
- value_in: bfloat16 [2048, 128], replicated, may hold values from -0.125 to 0.125
- content_right_pieces: bfloat16 [128, 256], replicated, may hold values from -0.75 to 0.75
- output_in: bfloat16 [2048, 128], replicated, may hold values from -2 to 2
- final_right_pieces: bfloat16 [128, 2048], replicated, may hold values from -0.75 to 0.75
- gate_in: bfloat16 [2048, 128], replicated, may hold values from -0.125 to 0.125
- switch_right_pieces: bfloat16 [128, 5632], replicated, may hold values from -0.75 to 0.75
- up_in: bfloat16 [2048, 128], replicated, may hold values from -0.125 to 0.125
- lift_right_pieces: bfloat16 [128, 5632], replicated, may hold values from -0.75 to 0.75
- down_in: bfloat16 [5632, 128], replicated, may hold values from -0.078125 to 0.078125
- lower_right_pieces: bfloat16 [128, 2048], replicated, may hold values from -0.75 to 0.75
Outputs:
- level_response: bfloat16 [8192, 2048], P(('rep', 'grp'))
- input_grad: bfloat16 [8192, 2048], P(('rep', 'grp'))
- query_in_grad: float32 [2048, 128], P('grp')
- asking_right_sens: float32 [128, 2048], P(None, 'grp')
- key_in_grad: float32 [2048, 128], P('grp')
- lookup_right_sens: float32 [128, 256], P(None, 'grp')
- value_in_grad: float32 [2048, 128], P('grp')
- content_right_sens: float32 [128, 256], P(None, 'grp')
- output_in_grad: float32 [2048, 128], P('grp')
- final_right_sens: float32 [128, 2048], P(None, 'grp')
- gate_in_grad: float32 [2048, 128], P('grp')
- switch_right_sens: float32 [128, 5632], P(None, 'grp')
- up_in_grad: float32 [2048, 128], P('grp')
- lift_right_sens: float32 [128, 5632], P(None, 'grp')
- down_in_grad: float32 [5632, 128], P('grp')
- lower_right_sens: float32 [128, 2048], P(None, 'grp')
The draws below stay inside these ranges and needn't reach their ends.
Inputs may be any that keep to these rules, and one draw needn't show every extreme that they name: `seq_lengths`: entries 2r and 2r + 1 are the lengths of the two sequences of rep group r, in order; they sum to 2048. `prefix_lengths`: entry s is the prefix length of sequence s; it never exceeds half of that sequence's length. `adapter_ids`: each adapter serves exactly 1 sequence.
All inputs are finite; a program needn't handle non-finite values.
Results may differ from the reference program's by a relative error of at most 0.02.
The reference program's roundings to bfloat16 on the way count: a program that leaves them out, or rounds other values in their place, can miss the bound.
Values may be sent and summed in bfloat16 or wider, within the bound.
No kernel may reach another device: no remote copies, remote signals or barrier semaphores. Data moves between devices by JAX's collectives and lax.ppermute only.
A program may use at most 320 MiB of HBM per device.

```python
import jax
import jax.numpy as jnp
from jax import lax

D = 2048
HEADS = 32
KV_HEADS = 4
HEAD_DIM = 64
FF = 5632
RANK = 16
ADAPTERS = 8
LMIN = 1024
TOKG = 2048
TOKENS = 8192
SEQS = 8
KVD = 256
QKV = 2560
ADAPTER_COLS = 128
PMIN = 204
PMAX = 512
N_REP = 4


def sequence_split(key):
    first = jax.random.randint(jax.random.fold_in(key, 11), (N_REP,), LMIN, TOKG - LMIN + 1)
    first = jnp.where(jnp.arange(N_REP) == 0, TOKG - LMIN, first)
    return jnp.stack([first, TOKG - first], axis=1).reshape(SEQS).astype(jnp.int32)


def draw_seq_lengths(key, part):
    return sequence_split(key)


def draw_prefix_lengths(key, part):
    lengths = sequence_split(key)
    bounds = lengths // 2
    fresh = jax.random.randint(jax.random.fold_in(key, 23), (SEQS,), 0, 1 << 20)
    values = PMIN + fresh % (bounds - PMIN + 1)
    index = jnp.arange(SEQS)
    values = jnp.where(index == 0, PMAX, values)
    values = jnp.where(index == 1, PMIN, values)
    return values.astype(jnp.int32)


def draw_adapter_ids(key, part):
    order = jax.random.permutation(jax.random.fold_in(key, 37), SEQS)
    return (order % ADAPTERS).astype(jnp.int32)


def block_levels(own_key, shape, cuts, low, largest):
    def one(axis_at, parts):
        draws = jax.random.uniform(jax.random.fold_in(jax.random.fold_in(own_key, 6), axis_at), (parts,), jnp.float32, low / len(cuts), largest / len(cuts))
        return jnp.repeat(jnp.exp(draws), shape[axis_at] // parts).reshape((-1,) + (1,) * (len(shape) - axis_at - 1))

    factor_of = one(*cuts[0])
    for cut in cuts[1:]:
        factor_of = factor_of * one(*cut)
    return factor_of


def scatter_about(rng, dims, width, bound, pieces=(), dtype=jnp.bfloat16):
    entries = width * jax.random.normal(rng, dims, jnp.float32)
    if pieces:
        entries = entries * block_levels(rng, dims, pieces, -0.22, 0.18)
    return jnp.clip(entries, -bound, bound).astype(dtype)


def setup_inputs(seed: int = 0) -> dict:
    keys = jax.random.split(jax.random.key(seed), 26)
    return {
        "tokens": scatter_about(keys[0], (TOKENS, D), 1.0, 6.0, ((0, 32),)),
        "response_sensitivity": scatter_about(keys[1], (TOKENS, D), 1.0, 6.0, ((0, 32),)),
        "seq_lengths": draw_seq_lengths(jax.random.fold_in(keys[25], 71), 0),
        "prefix_lengths": draw_prefix_lengths(jax.random.fold_in(keys[25], 71), 0),
        "adapter_ids": draw_adapter_ids(jax.random.fold_in(keys[25], 71), 0),
        "attn_gain": jnp.clip(1.0 + 0.18 * jax.random.normal(keys[5], (D,), jnp.float32), 0.1, 1.9),
        "mlp_gain": jnp.clip(1.0 + 0.18 * jax.random.normal(keys[6], (D,), jnp.float32), 0.1, 1.9),
        "qkv_weight": scatter_about(keys[7], (D, QKV), D ** -0.5, 0.125, ((1, 8),)),
        "out_weight": scatter_about(keys[8], (D, D), (D * 4 // LMIN) ** -0.5, 2.0, ((1, 8),)),
        "gate_up_weight": scatter_about(keys[9], (D, 2 * FF), D ** -0.5, 0.125, ((1, 8),)),
        "down_weight": scatter_about(keys[10], (FF, D), FF ** -0.5, 0.078125, ((1, 8),)),
        "query_in": scatter_about(keys[11], (D, ADAPTER_COLS), D ** -0.5, 0.125),
        "asking_right_pieces": scatter_about(keys[12], (ADAPTER_COLS, D), (4 * RANK) ** -0.5, 0.75),
        "key_in": scatter_about(keys[13], (D, ADAPTER_COLS), D ** -0.5, 0.125),
        "lookup_right_pieces": scatter_about(keys[14], (ADAPTER_COLS, KVD), (4 * RANK) ** -0.5, 0.75),
        "value_in": scatter_about(keys[15], (D, ADAPTER_COLS), D ** -0.5, 0.125),
        "content_right_pieces": scatter_about(keys[16], (ADAPTER_COLS, KVD), (4 * RANK) ** -0.5, 0.75),
        "output_in": scatter_about(keys[17], (D, ADAPTER_COLS), (D * 4 // LMIN) ** -0.5, 2.0),
        "final_right_pieces": scatter_about(keys[18], (ADAPTER_COLS, D), (4 * RANK) ** -0.5, 0.75),
        "gate_in": scatter_about(keys[19], (D, ADAPTER_COLS), D ** -0.5, 0.125),
        "switch_right_pieces": scatter_about(keys[20], (ADAPTER_COLS, FF), (4 * RANK) ** -0.5, 0.75),
        "up_in": scatter_about(keys[21], (D, ADAPTER_COLS), D ** -0.5, 0.125),
        "lift_right_pieces": scatter_about(keys[22], (ADAPTER_COLS, FF), (4 * RANK) ** -0.5, 0.75),
        "down_in": scatter_about(keys[23], (FF, ADAPTER_COLS), FF ** -0.5, 0.078125),
        "lower_right_pieces": scatter_about(keys[24], (ADAPTER_COLS, D), (4 * RANK) ** -0.5, 0.75),
    }


@jax.custom_vjp
def low(v):
    return lax.optimization_barrier(v.astype(jnp.bfloat16)).astype(jnp.float32)

@jax.custom_vjp
def low_back(v):
    return v

def low_keep(v):
    return (low(v), None)

def low_pass(kept, grad):
    return (grad,)

def back_keep(v):
    return (v, None)

def back_low(kept, grad):
    return (low(grad),)
low.defvjp(low_keep, low_pass)
low_back.defvjp(back_keep, back_low)
EPS = 1e-05
LOWRANK_FACTOR = 2.0
MASKED = -1e+30
HIGH = lax.Precision.HIGHEST

def composed_entries(left, right):
    return jnp.dot(left, right, precision=HIGH, preferred_element_type=jnp.float32)

def rms_norm(value, gain):
    return value * lax.rsqrt(lax.optimization_barrier(jnp.mean(value * value, axis=-1, keepdims=True)) + EPS) * gain

def rotary_tables(positions, head_dim):
    half = head_dim // 2
    freqs = 10000.0 ** (-2.0 * jnp.arange(half).astype(jnp.float32) / head_dim)
    angles = positions.astype(jnp.float32)[:, None] * freqs[None, :]
    angles = jnp.concatenate([angles, angles], axis=1)
    return (jnp.cos(angles), jnp.sin(angles))

def rotate(value, cosines, sines):
    half = value.shape[-1] // 2
    turned = jnp.concatenate([-value[..., half:], value[..., :half]], axis=-1)
    return value * cosines[:, None, :] + turned * sines[:, None, :]

def adapter(value, weight_in, final_coefficients, visibility_table):
    narrow_code = low_back(low(composed_entries(value, weight_in) * visibility_table))
    return LOWRANK_FACTOR * composed_entries(narrow_code, final_coefficients)

def group_layer(state, items):
    frozen, adapters = state
    incoming_tokens, lengths, prefixes, chosen_ids = items
    gain_one, gain_two, w_qkv, w_out, w_gate_up, w_down = frozen
    q_in, q_out, k_in, k_out, v_in, v_out, o_in, o_out, g_in, g_out, u_in, u_out, d_in, d_out = adapters
    count = incoming_tokens.shape[0]
    index = jnp.arange(count).astype(jnp.int32)
    second = (index >= lengths[0]).astype(jnp.int32)
    position = index - second * lengths[0]
    prefix = jnp.where(second == 0, prefixes[0], prefixes[1])
    chosen = jnp.where(second == 0, chosen_ids[0], chosen_ids[1])
    columns = jnp.arange(ADAPTER_COLS).astype(jnp.int32) // RANK
    visibility_table = (chosen[:, None] == columns[None, :]).astype(jnp.float32)
    kv_width = KV_HEADS * HEAD_DIM
    share = HEADS // KV_HEADS
    scale = HEAD_DIM ** (-0.5)
    norm1 = low(rms_norm(incoming_tokens, gain_one))
    adapted = jnp.concatenate([adapter(norm1, q_in, q_out, visibility_table), adapter(norm1, k_in, k_out, visibility_table), adapter(norm1, v_in, v_out, visibility_table)], axis=1)
    qkv = low_back(composed_entries(norm1, w_qkv) + adapted)
    cosines, sines = rotary_tables(position, HEAD_DIM)
    query = low(rotate(qkv[:, :D].reshape(count, HEADS, HEAD_DIM), cosines, sines))
    query = query.reshape(count, KV_HEADS, share, HEAD_DIM)
    key = low(rotate(qkv[:, D:D + kv_width].reshape(count, KV_HEADS, HEAD_DIM), cosines, sines))
    value = low(qkv[:, D + kv_width:].reshape(count, KV_HEADS, HEAD_DIM))
    block = min(512, count)

    def attend(start):
        rows_q = lax.dynamic_slice_in_dim(query, start, block, 0)
        pos_q = lax.dynamic_slice_in_dim(position, start, block, 0)
        seq_q = lax.dynamic_slice_in_dim(second, start, block, 0)
        pre_q = lax.dynamic_slice_in_dim(prefix, start, block, 0)
        scores = low_back(jnp.einsum('qhgd,khd->hgqk', rows_q, key, precision=HIGH) * scale)
        allowed = (seq_q[:, None] == second[None, :]) & ((position[None, :] <= pos_q[:, None]) | (position[None, :] < pre_q[:, None]))
        scores = jnp.where(allowed[None, None], scores, MASKED)
        peak = lax.optimization_barrier(jnp.max(scores, axis=-1, keepdims=True))
        weights = jnp.exp(scores - peak)
        probs = weights / lax.optimization_barrier(jnp.sum(weights, axis=-1, keepdims=True))
        mixed = jnp.einsum('hgqk,khd->qhgd', low(probs), value, precision=HIGH)
        return mixed.reshape(block, D)
    starts = jnp.arange(count // block).astype(jnp.int32) * block
    attended = lax.map(jax.checkpoint(attend), starts).reshape(count, D)
    attended = low_back(low(attended))
    branch = low_back(composed_entries(attended, w_out) + adapter(attended, o_in, o_out, visibility_table))
    residual_stream = incoming_tokens + branch
    norm2 = low(rms_norm(residual_stream, gain_two))
    gate_up = low_back(composed_entries(norm2, w_gate_up) + jnp.concatenate([adapter(norm2, g_in, g_out, visibility_table), adapter(norm2, u_in, u_out, visibility_table)], axis=1))
    gate = gate_up[:, :FF]
    up = gate_up[:, FF:]
    act = low(gate * jax.nn.sigmoid(gate) * up)
    return residual_stream + composed_entries(act, w_down) + adapter(act, d_in, d_out, visibility_table)

def reference(tokens, response_sensitivity, seq_lengths, prefix_lengths, adapter_ids, attn_gain, mlp_gain, qkv_weight, out_weight, gate_up_weight, down_weight, query_in, asking_right_pieces, key_in, lookup_right_pieces, value_in, content_right_pieces, output_in, final_right_pieces, gate_in, switch_right_pieces, up_in, lift_right_pieces, down_in, lower_right_pieces):
    frozen = tuple((w.astype(jnp.float32) for w in (attn_gain, mlp_gain, qkv_weight, out_weight, gate_up_weight, down_weight)))
    adapters = tuple((w.astype(jnp.float32) for w in (query_in, asking_right_pieces, key_in, lookup_right_pieces, value_in, content_right_pieces, output_in, final_right_pieces, gate_in, switch_right_pieces, up_in, lift_right_pieces, down_in, lower_right_pieces)))
    stacked_ints = (seq_lengths.reshape(N_REP, 2), prefix_lengths.reshape(N_REP, 2), adapter_ids.reshape(N_REP, 2))
    layer = jax.checkpoint(group_layer)

    def whole(incoming_tokens, weights):

        def step(state, items):
            return (state, layer(state, items))
        items = (incoming_tokens.reshape(N_REP, TOKG, D),) + stacked_ints
        state, outputs = lax.scan(step, (frozen, weights), items)
        return outputs.reshape(TOKENS, D)
    output, pullback = jax.vjp(whole, tokens.astype(jnp.float32), adapters)
    input_grad, grads = pullback(response_sensitivity.astype(jnp.float32))
    return (output.astype(jnp.bfloat16), input_grad.astype(jnp.bfloat16), grads[0], grads[1], grads[2], grads[3], grads[4], grads[5], grads[6], grads[7], grads[8], grads[9], grads[10], grads[11], grads[12], grads[13])
```

```python
import functools

import jax
import jax.numpy as jnp
from jax import lax
from jax.experimental import pallas as pl
from jax.experimental.pallas import tpu as pltpu
from jax.sharding import PartitionSpec as P

HEADS = 32
KV_HEADS = 4
HEAD_DIM = 64
RANK = 16
LANES = 128
KEY_BLOCK = 512

EPS = 1e-05
LOWRANK_FACTOR = 2.0
MASKED = -1e30
F32 = jnp.float32
BF16 = jnp.bfloat16


def mm(left, right):
    return jnp.dot(left, right, preferred_element_type=F32)


def mm_nt(left, right):
    return lax.dot_general(left, right, (((1,), (1,)), ((), ())), preferred_element_type=F32)


def mm_tn(left, right):
    return lax.dot_general(left, right, (((0,), (0,)), ((), ())), preferred_element_type=F32)


def inverse_rms(value):
    return lax.rsqrt(jnp.mean(value * value, axis=-1, keepdims=True) + EPS)


def norm_backward(value, scale, gain, grad):
    scaled = gain * grad
    return scale * scaled - value * (scale * scale * scale) * jnp.mean(
        scaled * value, axis=-1, keepdims=True
    )


def half_turn(value):
    half = HEAD_DIM // 2
    lane = lax.broadcasted_iota(jnp.int32, value.shape, 1) % HEAD_DIM
    return jnp.where(
        lane < half, -jnp.roll(value, -half, axis=1), jnp.roll(value, half, axis=1)
    )


def rotate(value, cosines, sines):
    return value * cosines + half_turn(value) * sines


def unrotate(grad, cosines, sines):
    return grad * cosines - half_turn(grad * sines)


def attention_forward_kernel(span, q_ref, k_ref, v_ref, bias_ref, out_ref, lse_ref):
    tokens = q_ref.shape[0]
    query = q_ref[...]

    def step(index, carry):
        start = pl.multiple_of(index * KEY_BLOCK, KEY_BLOCK)
        bias = bias_ref[pl.ds(start, KEY_BLOCK), :]
        mixed = carry[4]
        new, parts, decays = [], [], []
        for side in range(2):
            peak, total = carry[2 * side], carry[2 * side + 1]
            scores = mm_nt(k_ref[0, side, pl.ds(start, KEY_BLOCK), :], query) + bias
            top = jnp.maximum(peak, jnp.max(scores, axis=0, keepdims=True))
            decay = jnp.exp(peak - top)
            probs = jnp.exp(scores - top)
            total = total * decay + jnp.sum(probs, axis=0, keepdims=True)
            new += [top, total]
            decays.append(jnp.broadcast_to(decay, (HEAD_DIM, tokens)))
            parts.append(mm_tn(v_ref[0, side, pl.ds(start, KEY_BLOCK), :], probs.astype(BF16)))
        mixed = mixed * jnp.concatenate(decays, axis=0) + (parts[0] + parts[1])
        return (*new, mixed)

    low = jnp.full((1, tokens), MASKED, F32)
    none = jnp.zeros((1, tokens), F32)
    peak0, total0, peak1, total1, mixed = lax.fori_loop(
        span[0], span[1], step, (low, none, low, none, jnp.zeros((LANES, tokens), F32))
    )
    weight = jnp.concatenate(
        [
            jnp.broadcast_to(1.0 / total0, (HEAD_DIM, tokens)),
            jnp.broadcast_to(1.0 / total1, (HEAD_DIM, tokens)),
        ],
        axis=0,
    )
    out_ref[...] = (mixed * weight).T.astype(BF16)
    lse_ref[0] = jnp.concatenate([peak0 + jnp.log(total0), peak1 + jnp.log(total1)], axis=0)


def attention_forward(span, query, key_pairs, value_pairs, bias):
    tokens, width = query.shape
    keys = bias.shape[0]
    pairs = width // LANES
    per_kv = pairs // KV_HEADS
    pair_spec = pl.BlockSpec((tokens, LANES), lambda j, s: (0, j))
    kv_spec = pl.BlockSpec((1, 2, keys, LANES), lambda j, s: (j // per_kv, 0, 0, 0))
    return pl.pallas_call(
        attention_forward_kernel,
        out_shape=(
            jax.ShapeDtypeStruct((tokens, width), BF16),
            jax.ShapeDtypeStruct((pairs, 2, tokens), F32),
        ),
        grid_spec=pltpu.PrefetchScalarGridSpec(
            num_scalar_prefetch=1,
            grid=(pairs,),
            in_specs=[
                pair_spec,
                kv_spec,
                kv_spec,
                pl.BlockSpec((keys, tokens), lambda j, s: (0, 0)),
            ],
            out_specs=(pair_spec, pl.BlockSpec((1, 2, tokens), lambda j, s: (j, 0, 0))),
        ),
        compiler_params=pltpu.CompilerParams(
            dimension_semantics=("arbitrary",), vmem_limit_bytes=40 << 20
        ),
        cost_estimate=pl.CostEstimate(
            flops=4 * tokens * keys * width,
            transcendentals=tokens * keys * HEADS // 2,
            bytes_accessed=4 * tokens * width + 16 * keys * LANES * KV_HEADS,
        ),
        name="attention_forward",
    )(span, query, key_pairs, value_pairs, bias)


def attention_backward_kernel(
    span, q_ref, do_ref, o_ref, lse_ref, k_ref, v_ref, bias_ref, dq_ref, dk_ref, dv_ref
):
    tokens = q_ref.shape[0]
    per_kv = pl.num_programs(0) // KV_HEADS
    member = lax.rem(pl.program_id(0), per_kv)

    @pl.when(member == 0)
    def _():
        dk_ref[...] = jnp.zeros_like(dk_ref)
        dv_ref[...] = jnp.zeros_like(dv_ref)

    query = q_ref[...]
    grad = do_ref[...]
    lane = lax.broadcasted_iota(jnp.int32, (tokens, LANES), 1)
    none = jnp.zeros_like(query)
    query_stack = jnp.concatenate(
        [jnp.where(lane < HEAD_DIM, query, none), jnp.where(lane < HEAD_DIM, none, query)], axis=0
    )
    grad_stack = jnp.concatenate(
        [jnp.where(lane < HEAD_DIM, grad, none), jnp.where(lane < HEAD_DIM, none, grad)], axis=0
    )
    product = grad.astype(F32) * o_ref[...].astype(F32)
    row = lax.broadcasted_iota(jnp.int32, (8, LANES), 0)
    column = lax.broadcasted_iota(jnp.int32, (8, LANES), 1)
    chooser = jnp.where(row == column // HEAD_DIM, 1.0, 0.0).astype(F32)
    deltas = lax.dot_general(
        chooser,
        product,
        (((1,), (1,)), ((), ())),
        precision=lax.Precision.HIGHEST,
        preferred_element_type=F32,
    )

    def step(index, dquery):
        start = pl.multiple_of(index * KEY_BLOCK, KEY_BLOCK)
        rows = pl.ds(start, KEY_BLOCK)
        bias = bias_ref[rows, :]
        all_probs, all_dscores = [], []
        for side in range(2):
            scores = mm_nt(k_ref[0, side, rows, :], query) + bias
            probs = jnp.exp(scores - lse_ref[0, side : side + 1, :])
            dprobs = mm_nt(v_ref[0, side, rows, :], grad)
            dscores = (probs * (dprobs - deltas[side : side + 1, :])).astype(BF16)
            all_probs.append(probs.astype(BF16))
            all_dscores.append(dscores)
            dquery = dquery + mm_tn(k_ref[0, side, rows, :], dscores)
        dk_ref[0, rows, :] += mm(jnp.concatenate(all_dscores, axis=1), query_stack)
        dv_ref[0, rows, :] += mm(jnp.concatenate(all_probs, axis=1), grad_stack)
        return dquery

    dquery = lax.fori_loop(span[0], span[1], step, jnp.zeros((LANES, tokens), F32))
    dq_ref[...] = dquery.T * (HEAD_DIM**-0.5)


def attention_backward(span, query, grad, attended, lse, key_pairs, value_pairs, bias):
    tokens, width = query.shape
    keys = bias.shape[0]
    pairs = width // LANES
    per_kv = pairs // KV_HEADS
    pair_spec = pl.BlockSpec((tokens, LANES), lambda j, s: (0, j))
    kv_spec = pl.BlockSpec((1, 2, keys, LANES), lambda j, s: (j // per_kv, 0, 0, 0))
    dkv_spec = pl.BlockSpec((1, keys, LANES), lambda j, s: (j // per_kv, 0, 0))
    return pl.pallas_call(
        attention_backward_kernel,
        out_shape=(
            jax.ShapeDtypeStruct((tokens, width), F32),
            jax.ShapeDtypeStruct((KV_HEADS, keys, LANES), F32),
            jax.ShapeDtypeStruct((KV_HEADS, keys, LANES), F32),
        ),
        grid_spec=pltpu.PrefetchScalarGridSpec(
            num_scalar_prefetch=1,
            grid=(pairs,),
            in_specs=[
                pair_spec,
                pair_spec,
                pair_spec,
                pl.BlockSpec((1, 2, tokens), lambda j, s: (j, 0, 0)),
                kv_spec,
                kv_spec,
                pl.BlockSpec((keys, tokens), lambda j, s: (0, 0)),
            ],
            out_specs=(pair_spec, dkv_spec, dkv_spec),
        ),
        compiler_params=pltpu.CompilerParams(
            dimension_semantics=("arbitrary",), vmem_limit_bytes=48 << 20
        ),
        cost_estimate=pl.CostEstimate(
            flops=10 * tokens * keys * width,
            transcendentals=tokens * keys * HEADS // 2,
            bytes_accessed=10 * tokens * width + 24 * keys * LANES * KV_HEADS,
        ),
        name="attention_backward",
    )(span, query, grad, attended, lse, key_pairs, value_pairs, bias)


def side_pairs(array):
    keys = array.shape[0]
    heads = array.reshape(keys, KV_HEADS, HEAD_DIM).transpose(1, 0, 2)
    none = jnp.zeros_like(heads)
    return jnp.stack(
        [jnp.concatenate([heads, none], axis=2), jnp.concatenate([none, heads], axis=2)], axis=1
    )


def join_sides(array):
    summed = array[:, :, :HEAD_DIM] + array[:, :, HEAD_DIM:]
    return summed.transpose(1, 0, 2).reshape(array.shape[1], KV_HEADS * HEAD_DIM)


def exchange_sum(parts):
    received = lax.all_to_all(parts.astype(BF16), "grp", 0, 0, tiled=True)
    return jnp.sum(received.astype(F32), axis=0)


def shards(
    tokens,
    response_sensitivity,
    seq_lengths,
    prefix_lengths,
    adapter_ids,
    attn_gain,
    mlp_gain,
    qkv_weight,
    out_weight,
    gate_up_weight,
    down_weight,
    query_in,
    asking_right_pieces,
    key_in,
    lookup_right_pieces,
    value_in,
    content_right_pieces,
    output_in,
    final_right_pieces,
    gate_in,
    switch_right_pieces,
    up_in,
    lift_right_pieces,
    down_in,
    lower_right_pieces,
):
    count, width = tokens.shape
    members = lax.axis_size("grp")
    groups = lax.axis_size("rep")
    kv_width = lookup_right_pieces.shape[1]
    narrow = query_in.shape[1]
    hidden_width = down_weight.shape[0]
    group = lax.axis_index("rep")
    member = lax.axis_index("grp")
    lengths = lax.dynamic_slice_in_dim(seq_lengths, 2 * group, 2)
    prefixes = lax.dynamic_slice_in_dim(prefix_lengths, 2 * group, 2)
    chosen_ids = lax.dynamic_slice_in_dim(adapter_ids, 2 * group, 2)
    key_count = count * members

    qkv_full = lax.all_gather(qkv_weight, "grp", axis=1, tiled=True)
    out_full = lax.all_gather(out_weight, "grp", axis=1, tiled=True)
    down_full = lax.all_gather(down_weight, "grp", axis=1, tiled=True)
    gate_up_full = lax.all_gather(gate_up_weight, "grp", axis=1, tiled=True)

    key_index = jnp.arange(key_count, dtype=jnp.int32)
    key_second = (key_index >= lengths[0]).astype(jnp.int32)
    key_position = key_index - key_second * lengths[0]
    own_index = member * count + jnp.arange(count, dtype=jnp.int32)
    own_second = (own_index >= lengths[0]).astype(jnp.int32)
    position = own_index - own_second * lengths[0]
    prefix = jnp.where(own_second == 0, prefixes[0], prefixes[1])
    chosen = jnp.where(own_second == 0, chosen_ids[0], chosen_ids[1])
    allowed = (key_second[:, None] == own_second[None, :]) & (
        (key_position[:, None] <= position[None, :]) | (key_position[:, None] < prefix[None, :])
    )
    bias = jnp.where(allowed, 0.0, MASKED).astype(F32)
    first_key = own_second[0] * lengths[0]
    last_key = jnp.max(own_second * lengths[0] + jnp.maximum(position, prefix - 1))
    span = jnp.stack([first_key // KEY_BLOCK, last_key // KEY_BLOCK + 1]).astype(jnp.int32)

    columns = jnp.arange(narrow, dtype=jnp.int32)
    visible = (chosen[:, None] == columns[None, :] // RANK).astype(F32)
    mask_two = jnp.concatenate([visible, visible], axis=1)
    mask_three = jnp.concatenate([visible, visible, visible], axis=1)
    slots = 2 * RANK
    slot = jnp.arange(slots, dtype=jnp.int32)
    slot_column = chosen_ids[slot // RANK] * RANK + slot % RANK
    pick = (columns[:, None] == slot_column[None, :]).astype(BF16)
    slot_visible = (own_second[:, None] == slot[None, :] // RANK).astype(F32)

    def compact(latent):
        return (mm(latent, pick) * slot_visible).astype(BF16)

    incoming = tokens.astype(F32)
    scale_one = inverse_rms(incoming)
    norm1 = (incoming * scale_one * attn_gain).astype(BF16)
    qkv_in = jnp.concatenate([query_in, key_in, value_in], axis=1)
    latent_qkv = (mm(norm1, qkv_in) * mask_three).astype(BF16)
    latent_q, latent_k, latent_v = (
        latent_qkv[:, :narrow],
        latent_qkv[:, narrow : 2 * narrow],
        latent_qkv[:, 2 * narrow :],
    )
    adapted = LOWRANK_FACTOR * jnp.concatenate(
        [
            mm(latent_q, asking_right_pieces),
            mm(latent_k, lookup_right_pieces),
            mm(latent_v, content_right_pieces),
        ],
        axis=1,
    )
    half = HEAD_DIM // 2
    freqs = 10000.0 ** (-2.0 * jnp.arange(half).astype(F32) / HEAD_DIM)
    angles = position.astype(F32)[:, None] * jnp.concatenate([freqs, freqs])[None, :]
    cosines = jnp.cos(angles)
    sines = jnp.sin(angles)
    wide_cos, wide_sin = jnp.tile(cosines, (1, HEADS)), jnp.tile(sines, (1, HEADS))
    kv_cos, kv_sin = jnp.tile(cosines, (1, KV_HEADS)), jnp.tile(sines, (1, KV_HEADS))

    qkv = mm(norm1, qkv_full) + adapted
    scale = HEAD_DIM**-0.5
    query = (rotate(qkv[:, :width], wide_cos, wide_sin)).astype(BF16) * jnp.asarray(scale, BF16)
    key_own = rotate(qkv[:, width : width + kv_width], kv_cos, kv_sin).astype(BF16)
    value_own = qkv[:, width + kv_width :].astype(BF16)
    key_value = lax.all_gather(
        jnp.concatenate([key_own, value_own], axis=1), "grp", axis=0, tiled=True
    )
    key_pairs = side_pairs(key_value[:, :kv_width])
    value_pairs = side_pairs(key_value[:, kv_width:])
    attended_low, lse = attention_forward(span, query, key_pairs, value_pairs, bias)

    latent_o = (mm(attended_low, output_in) * visible).astype(BF16)
    stream = incoming + (
        mm(attended_low, out_full) + LOWRANK_FACTOR * mm(latent_o, final_right_pieces)
    )
    scale_two = inverse_rms(stream)
    norm2 = (stream * scale_two * mlp_gain).astype(BF16)
    ffn_in = jnp.concatenate([gate_in, up_in], axis=1)
    latent_gu = (mm(norm2, ffn_in) * mask_two).astype(BF16)
    latent_g, latent_u = latent_gu[:, :narrow], latent_gu[:, narrow:]
    gate_up = mm(norm2, gate_up_full) + LOWRANK_FACTOR * jnp.concatenate(
        [mm(latent_g, switch_right_pieces), mm(latent_u, lift_right_pieces)], axis=1
    )
    gate = gate_up[:, :hidden_width]
    up = gate_up[:, hidden_width:]
    sigma = jax.nn.sigmoid(gate)
    act = (gate * sigma * up).astype(BF16)
    latent_d = (mm(act, down_in) * visible).astype(BF16)
    level_response = (
        stream + mm(act, down_full) + LOWRANK_FACTOR * mm(latent_d, lower_right_pieces)
    ).astype(BF16)

    sens = response_sensitivity
    dlat_d = (LOWRANK_FACTOR * mm_nt(sens, lower_right_pieces) * visible).astype(BF16)
    dact = mm_nt(sens, down_full) + mm_nt(dlat_d, down_in)
    dgate = (dact * up * (sigma * (1.0 + gate * (1.0 - sigma)))).astype(BF16)
    dup = (dact * gate * sigma).astype(BF16)
    dlat_gu = (
        LOWRANK_FACTOR
        * jnp.concatenate(
            [mm_nt(dgate, switch_right_pieces), mm_nt(dup, lift_right_pieces)], axis=1
        )
        * mask_two
    ).astype(BF16)
    dnorm2 = (
        mm_nt(dgate, gate_up_full[:, :hidden_width])
        + mm_nt(dup, gate_up_full[:, hidden_width:])
        + mm_nt(dlat_gu, ffn_in)
    )
    dhidden = sens.astype(F32) + norm_backward(stream, scale_two, mlp_gain, dnorm2)
    dbranch = dhidden.astype(BF16)
    dlat_o = (LOWRANK_FACTOR * mm_nt(dbranch, final_right_pieces) * visible).astype(BF16)
    dattended = (mm_nt(dbranch, out_full) + mm_nt(dlat_o, output_in)).astype(BF16)

    def blocks(array):
        return array.reshape(members, array.shape[0] // members, array.shape[1])

    wide = jnp.concatenate(
        [
            LOWRANK_FACTOR * mm_tn(sens, compact(latent_d)),
            mm_tn(norm2, jnp.concatenate([compact(dlat_gu[:, :narrow]), compact(dlat_gu[:, narrow:])], axis=1)),
            mm_tn(attended_low, compact(dlat_o)),
        ],
        axis=1,
    ).astype(BF16)
    final_part = (LOWRANK_FACTOR * mm_tn(dbranch, compact(latent_o))).astype(BF16)
    deep = jnp.concatenate(
        [
            mm_tn(act, compact(dlat_d)),
            LOWRANK_FACTOR * mm_tn(dgate, compact(latent_g)),
            LOWRANK_FACTOR * mm_tn(dup, compact(latent_u)),
        ],
        axis=1,
    ).astype(BF16)
    wide_rows, deep_rows = width // members, hidden_width // members
    final_blocks = jnp.pad(blocks(final_part), ((0, 0), (0, deep_rows - wide_rows), (0, 0)))
    early = jnp.concatenate(
        [blocks(wide), jnp.concatenate([blocks(deep), final_blocks], axis=2)], axis=1
    )
    early_sum = lax.psum_scatter(early, "grp", scatter_dimension=0, tiled=True)
    early_sum = early_sum.reshape(wide_rows + deep_rows, 4 * slots)
    early_all = lax.all_gather(early_sum, "rep", axis=0)

    dquery, dkeys, dvalues = attention_backward(
        span, query, dattended, attended_low, lse, key_pairs, value_pairs, bias
    )
    dkv = jnp.concatenate([join_sides(dkeys), join_sides(dvalues)], axis=1)
    dkv_own = exchange_sum(dkv.reshape(members, count, 2 * kv_width))
    dq = unrotate(dquery, wide_cos, wide_sin).astype(BF16)
    dk = unrotate(dkv_own[:, :kv_width], kv_cos, kv_sin).astype(BF16)
    dv = dkv_own[:, kv_width:].astype(BF16)
    dlat_qkv = (
        LOWRANK_FACTOR
        * jnp.concatenate(
            [
                mm_nt(dq, asking_right_pieces),
                mm_nt(dk, lookup_right_pieces),
                mm_nt(dv, content_right_pieces),
            ],
            axis=1,
        )
        * mask_three
    ).astype(BF16)
    dqkv = jnp.concatenate([dq, dk, dv], axis=1)
    late_wide = jnp.concatenate(
        [
            mm_tn(
                norm1,
                jnp.concatenate(
                    [compact(dlat_qkv[:, i * narrow : (i + 1) * narrow]) for i in range(3)], axis=1
                ),
            ),
            LOWRANK_FACTOR * mm_tn(dq, compact(latent_q)),
        ],
        axis=1,
    ).astype(BF16)
    late_thin = jnp.concatenate(
        [
            LOWRANK_FACTOR * mm_tn(dk, compact(latent_k)),
            LOWRANK_FACTOR * mm_tn(dv, compact(latent_v)),
        ],
        axis=1,
    ).astype(BF16)
    thin_rows = kv_width // members
    late = jnp.concatenate(
        [blocks(late_wide), jnp.pad(blocks(late_thin), ((0, 0), (0, 0), (0, 2 * slots)))], axis=1
    )
    late_sum = exchange_sum(late).astype(BF16)
    late_all = lax.all_gather(late_sum, "rep", axis=0)
    dnorm1 = mm_nt(dqkv, qkv_full) + mm_nt(dlat_qkv, qkv_in)
    input_grad = (dhidden + norm_backward(incoming, scale_one, attn_gain, dnorm1)).astype(BF16)

    all_slot = jnp.arange(groups * slots, dtype=jnp.int32)
    all_column = adapter_ids[all_slot // RANK] * RANK + all_slot % RANK
    place = (all_column[:, None] == columns[None, :]).astype(BF16)

    def gathered(array, start, rows, index):
        piece = lax.slice_in_dim(array, start, start + rows, axis=1)
        piece = piece[:, :, index * slots : (index + 1) * slots]
        return piece.transpose(1, 0, 2).reshape(rows, groups * slots)

    def as_rows(array, start, rows, index):
        return mm(gathered(array, start, rows, index), place)

    def as_columns(array, start, rows, index):
        return lax.dot_general(
            place,
            gathered(array, start, rows, index),
            (((0,), (1,)), ((), ())),
            preferred_element_type=F32,
        )

    return (
        level_response,
        input_grad,
        as_rows(late_all, 0, wide_rows, 0),
        as_columns(late_all, 0, wide_rows, 3),
        as_rows(late_all, 0, wide_rows, 1),
        as_columns(late_all, wide_rows, thin_rows, 0),
        as_rows(late_all, 0, wide_rows, 2),
        as_columns(late_all, wide_rows, thin_rows, 1),
        as_rows(early_all, 0, wide_rows, 3),
        as_columns(early_all, wide_rows, wide_rows, 3),
        as_rows(early_all, 0, wide_rows, 1),
        as_columns(early_all, wide_rows, deep_rows, 1),
        as_rows(early_all, 0, wide_rows, 2),
        as_columns(early_all, wide_rows, deep_rows, 2),
        as_rows(early_all, wide_rows, deep_rows, 0),
        as_columns(early_all, 0, wide_rows, 0),
    )


def solution(mesh):
    rows = P(("rep", "grp"), None)
    split = P(None, "grp")
    in_specs = (rows, rows, *[P()] * 5, *[split] * 4, *[P()] * 14)
    out_specs = (rows, rows, *[P("grp", None), P(None, "grp")] * 7)
    return jax.shard_map(shards, mesh=mesh, in_specs=in_specs, out_specs=out_specs, check_vma=False)
```

```python
import functools

import jax
import jax.numpy as jnp
from jax import lax
from jax.experimental import pallas as pl
from jax.experimental.pallas import tpu as pltpu
from jax.sharding import PartitionSpec as P

HEADS = 32
KV_HEADS = 4
HEAD_DIM = 64
RANK = 16
LANES = 128
KEY_BLOCK = 512

EPS = 1e-05
LOWRANK_FACTOR = 2.0
MASKED = -1e30
F32 = jnp.float32
BF16 = jnp.bfloat16


def mm(left, right):
    return jnp.dot(left, right, preferred_element_type=F32)


def mm_nt(left, right):
    return lax.dot_general(left, right, (((1,), (1,)), ((), ())), preferred_element_type=F32)


def mm_tn(left, right):
    return lax.dot_general(left, right, (((0,), (0,)), ((), ())), preferred_element_type=F32)


def inverse_rms(value):
    return lax.rsqrt(jnp.mean(value * value, axis=-1, keepdims=True) + EPS)


def norm_backward(value, scale, gain, grad):
    scaled = gain * grad
    return scale * scaled - value * (scale * scale * scale) * jnp.mean(
        scaled * value, axis=-1, keepdims=True
    )


def half_turn(value):
    half = HEAD_DIM // 2
    lane = lax.broadcasted_iota(jnp.int32, value.shape, 1) % HEAD_DIM
    return jnp.where(
        lane < half, -jnp.roll(value, -half, axis=1), jnp.roll(value, half, axis=1)
    )


def rotate(value, cosines, sines):
    return value * cosines + half_turn(value) * sines


def unrotate(grad, cosines, sines):
    return grad * cosines - half_turn(grad * sines)


def attention_forward_kernel(span, q_ref, k_ref, v_ref, bias_ref, out_ref, lse_ref):
    tokens = q_ref.shape[0]
    query = q_ref[...]

    def step(index, carry):
        start = pl.multiple_of(index * KEY_BLOCK, KEY_BLOCK)
        bias = bias_ref[pl.ds(start, KEY_BLOCK), :]
        mixed = carry[4]
        new, parts, decays = [], [], []
        for side in range(2):
            peak, total = carry[2 * side], carry[2 * side + 1]
            scores = mm_nt(k_ref[0, side, pl.ds(start, KEY_BLOCK), :], query) + bias
            top = jnp.maximum(peak, jnp.max(scores, axis=0, keepdims=True))
            decay = jnp.exp(peak - top)
            probs = jnp.exp(scores - top)
            total = total * decay + jnp.sum(probs, axis=0, keepdims=True)
            new += [top, total]
            decays.append(jnp.broadcast_to(decay, (HEAD_DIM, tokens)))
            parts.append(mm_tn(v_ref[0, side, pl.ds(start, KEY_BLOCK), :], probs.astype(BF16)))
        mixed = mixed * jnp.concatenate(decays, axis=0) + (parts[0] + parts[1])
        return (*new, mixed)

    low = jnp.full((1, tokens), MASKED, F32)
    none = jnp.zeros((1, tokens), F32)
    peak0, total0, peak1, total1, mixed = lax.fori_loop(
        span[0], span[1], step, (low, none, low, none, jnp.zeros((LANES, tokens), F32))
    )
    weight = jnp.concatenate(
        [
            jnp.broadcast_to(1.0 / total0, (HEAD_DIM, tokens)),
            jnp.broadcast_to(1.0 / total1, (HEAD_DIM, tokens)),
        ],
        axis=0,
    )
    out_ref[...] = (mixed * weight).T.astype(BF16)
    lse_ref[0] = jnp.concatenate([peak0 + jnp.log(total0), peak1 + jnp.log(total1)], axis=0)


def attention_forward(span, query, key_pairs, value_pairs, bias):
    tokens, width = query.shape
    keys = bias.shape[0]
    pairs = width // LANES
    per_kv = pairs // KV_HEADS
    pair_spec = pl.BlockSpec((tokens, LANES), lambda j, s: (0, j))
    kv_spec = pl.BlockSpec((1, 2, keys, LANES), lambda j, s: (j // per_kv, 0, 0, 0))
    return pl.pallas_call(
        attention_forward_kernel,
        out_shape=(
            jax.ShapeDtypeStruct((tokens, width), BF16),
            jax.ShapeDtypeStruct((pairs, 2, tokens), F32),
        ),
        grid_spec=pltpu.PrefetchScalarGridSpec(
            num_scalar_prefetch=1,
            grid=(pairs,),
            in_specs=[
                pair_spec,
                kv_spec,
                kv_spec,
                pl.BlockSpec((keys, tokens), lambda j, s: (0, 0)),
            ],
            out_specs=(pair_spec, pl.BlockSpec((1, 2, tokens), lambda j, s: (j, 0, 0))),
        ),
        compiler_params=pltpu.CompilerParams(
            dimension_semantics=("arbitrary",), vmem_limit_bytes=40 << 20
        ),
        cost_estimate=pl.CostEstimate(
            flops=4 * tokens * keys * width,
            transcendentals=tokens * keys * HEADS // 2,
            bytes_accessed=4 * tokens * width + 16 * keys * LANES * KV_HEADS,
        ),
        name="attention_forward",
    )(span, query, key_pairs, value_pairs, bias)


def attention_backward_kernel(
    span, q_ref, do_ref, o_ref, lse_ref, k_ref, v_ref, bias_ref, dq_ref, dk_ref, dv_ref
):
    tokens = q_ref.shape[0]
    per_kv = pl.num_programs(0) // KV_HEADS
    member = lax.rem(pl.program_id(0), per_kv)

    @pl.when(member == 0)
    def _():
        dk_ref[...] = jnp.zeros_like(dk_ref)
        dv_ref[...] = jnp.zeros_like(dv_ref)

    query = q_ref[...]
    grad = do_ref[...]
    lane = lax.broadcasted_iota(jnp.int32, (tokens, LANES), 1)
    none = jnp.zeros_like(query)
    query_stack = jnp.concatenate(
        [jnp.where(lane < HEAD_DIM, query, none), jnp.where(lane < HEAD_DIM, none, query)], axis=0
    )
    grad_stack = jnp.concatenate(
        [jnp.where(lane < HEAD_DIM, grad, none), jnp.where(lane < HEAD_DIM, none, grad)], axis=0
    )
    product = grad.astype(F32) * o_ref[...].astype(F32)
    row = lax.broadcasted_iota(jnp.int32, (8, LANES), 0)
    column = lax.broadcasted_iota(jnp.int32, (8, LANES), 1)
    chooser = jnp.where(row == column // HEAD_DIM, 1.0, 0.0).astype(F32)
    deltas = lax.dot_general(
        chooser,
        product,
        (((1,), (1,)), ((), ())),
        precision=lax.Precision.HIGHEST,
        preferred_element_type=F32,
    )

    def step(index, dquery):
        start = pl.multiple_of(index * KEY_BLOCK, KEY_BLOCK)
        rows = pl.ds(start, KEY_BLOCK)
        bias = bias_ref[rows, :]
        all_probs, all_dscores = [], []
        for side in range(2):
            scores = mm_nt(k_ref[0, side, rows, :], query) + bias
            probs = jnp.exp(scores - lse_ref[0, side : side + 1, :])
            dprobs = mm_nt(v_ref[0, side, rows, :], grad)
            dscores = (probs * (dprobs - deltas[side : side + 1, :])).astype(BF16)
            all_probs.append(probs.astype(BF16))
            all_dscores.append(dscores)
            dquery = dquery + mm_tn(k_ref[0, side, rows, :], dscores)
        dk_ref[0, rows, :] += mm(jnp.concatenate(all_dscores, axis=1), query_stack)
        dv_ref[0, rows, :] += mm(jnp.concatenate(all_probs, axis=1), grad_stack)
        return dquery

    dquery = lax.fori_loop(span[0], span[1], step, jnp.zeros((LANES, tokens), F32))
    dq_ref[...] = dquery.T * (HEAD_DIM**-0.5)


def attention_backward(span, query, grad, attended, lse, key_pairs, value_pairs, bias):
    tokens, width = query.shape
    keys = bias.shape[0]
    pairs = width // LANES
    per_kv = pairs // KV_HEADS
    pair_spec = pl.BlockSpec((tokens, LANES), lambda j, s: (0, j))
    kv_spec = pl.BlockSpec((1, 2, keys, LANES), lambda j, s: (j // per_kv, 0, 0, 0))
    dkv_spec = pl.BlockSpec((1, keys, LANES), lambda j, s: (j // per_kv, 0, 0))
    return pl.pallas_call(
        attention_backward_kernel,
        out_shape=(
            jax.ShapeDtypeStruct((tokens, width), F32),
            jax.ShapeDtypeStruct((KV_HEADS, keys, LANES), F32),
            jax.ShapeDtypeStruct((KV_HEADS, keys, LANES), F32),
        ),
        grid_spec=pltpu.PrefetchScalarGridSpec(
            num_scalar_prefetch=1,
            grid=(pairs,),
            in_specs=[
                pair_spec,
                pair_spec,
                pair_spec,
                pl.BlockSpec((1, 2, tokens), lambda j, s: (j, 0, 0)),
                kv_spec,
                kv_spec,
                pl.BlockSpec((keys, tokens), lambda j, s: (0, 0)),
            ],
            out_specs=(pair_spec, dkv_spec, dkv_spec),
        ),
        compiler_params=pltpu.CompilerParams(
            dimension_semantics=("arbitrary",), vmem_limit_bytes=48 << 20
        ),
        cost_estimate=pl.CostEstimate(
            flops=10 * tokens * keys * width,
            transcendentals=tokens * keys * HEADS // 2,
            bytes_accessed=10 * tokens * width + 24 * keys * LANES * KV_HEADS,
        ),
        name="attention_backward",
    )(span, query, grad, attended, lse, key_pairs, value_pairs, bias)


def side_pairs(array):
    keys = array.shape[0]
    heads = array.reshape(keys, KV_HEADS, HEAD_DIM).transpose(1, 0, 2)
    none = jnp.zeros_like(heads)
    return jnp.stack(
        [jnp.concatenate([heads, none], axis=2), jnp.concatenate([none, heads], axis=2)], axis=1
    )


def join_sides(array):
    summed = array[:, :, :HEAD_DIM] + array[:, :, HEAD_DIM:]
    return summed.transpose(1, 0, 2).reshape(array.shape[1], KV_HEADS * HEAD_DIM)


def exchange_sum(parts):
    received = lax.all_to_all(parts.astype(BF16), "grp", 0, 0, tiled=True)
    return jnp.sum(received.astype(F32), axis=0)


CORE, ACROSS_X, ACROSS_Y = 1, 2, 4


def flip(array, mask):
    members = lax.axis_size("grp")
    return lax.ppermute(array, "grp", [(i, i ^ mask) for i in range(members)])


def flip_group(array):
    groups = lax.axis_size("rep")
    return lax.ppermute(array, "rep", [(i, i ^ 1) for i in range(groups)])


def gather_same_core(weight):
    rows = weight.shape[0] // 2
    parity = lax.axis_index("rep") % 2
    mine = lax.dynamic_slice_in_dim(weight, parity * rows, rows, 0)
    over_x, over_y = yield flip(mine, ACROSS_X), flip(mine, ACROSS_Y)
    both_low = flip(over_x[: rows // 2], ACROSS_Y)
    both_high = flip(over_y[rows // 2 :], ACROSS_X)
    other_x, both_low, both_high, over_y = yield flip_group(over_x), both_low, both_high, over_y
    other_y, *_ = yield (flip_group(over_y),)
    other_both = (flip_group(both_low), flip_group(both_high))
    return (
        ((over_x,), (other_x,)),
        ((over_y,), (other_y,)),
        ((both_low, both_high), other_both),
    )


def tie(value, transfers):
    value, *transfers = lax.optimization_barrier((value, *transfers))
    return value, tuple(transfers)


def times_pieces(mine, other, pieces):
    total = None
    for value, part in zip((mine, other), pieces):
        start = 0
        for piece in part:
            term = mm(value[:, start : start + piece.shape[0]], piece)
            total = term if total is None else total + term
            start += piece.shape[0]
    return total


def times_pieces_flipped(value, pieces):
    return [
        jnp.concatenate([mm_nt(value, piece) for piece in part], axis=1) for part in pieces
    ]


def feed_forward_alone(norm2, sens, gate_up_full, down_full, pieces, masks_of, compact_with):
    ffn_in, switch_right_pieces, lift_right_pieces, down_in, lower_right_pieces = pieces
    narrow = down_in.shape[1]
    hidden_width = down_full.shape[0]
    visible, seen = masks_of(lax.axis_index("grp"))
    mask_two = jnp.concatenate([visible, visible], axis=1)
    latent_gu = (mm(norm2, ffn_in) * mask_two).astype(BF16)
    latent_g, latent_u = latent_gu[:, :narrow], latent_gu[:, narrow:]
    gate_up = mm(norm2, gate_up_full) + LOWRANK_FACTOR * jnp.concatenate(
        [mm(latent_g, switch_right_pieces), mm(latent_u, lift_right_pieces)], axis=1
    )
    gate = gate_up[:, :hidden_width]
    up = gate_up[:, hidden_width:]
    sigma = jax.nn.sigmoid(gate)
    act = (gate * sigma * up).astype(BF16)
    latent_d = (mm(act, down_in) * visible).astype(BF16)
    response_part = mm(act, down_full) + LOWRANK_FACTOR * mm(latent_d, lower_right_pieces)
    dlat_d = (LOWRANK_FACTOR * mm_nt(sens, lower_right_pieces) * visible).astype(BF16)
    dact = mm_nt(sens, down_full) + mm_nt(dlat_d, down_in)
    dgate = (dact * up * (sigma * (1.0 + gate * (1.0 - sigma)))).astype(BF16)
    dup = (dact * gate * sigma).astype(BF16)
    dlat_gu = (
        LOWRANK_FACTOR
        * jnp.concatenate(
            [mm_nt(dgate, switch_right_pieces), mm_nt(dup, lift_right_pieces)], axis=1
        )
        * mask_two
    ).astype(BF16)
    dnorm2 = (
        mm_nt(dgate, gate_up_full[:, :hidden_width])
        + mm_nt(dup, gate_up_full[:, hidden_width:])
        + mm_nt(dlat_gu, ffn_in)
    )
    deep = jnp.concatenate(
        [
            mm_tn(act, compact_with(dlat_d, seen)),
            LOWRANK_FACTOR * mm_tn(dgate, compact_with(latent_g, seen)),
            LOWRANK_FACTOR * mm_tn(dup, compact_with(latent_u, seen)),
        ],
        axis=1,
    ).astype(BF16)
    return response_part, dnorm2, latent_d, dlat_gu, deep


def feed_forward_paired(
    norm2, sens, sens_near, own_weight, far, down_full, pieces, masks_of, compact_with
):
    ffn_in, switch_right_pieces, lift_right_pieces, down_in, lower_right_pieces = pieces
    count, width = norm2.shape
    narrow = down_in.shape[1]
    hidden_width = down_full.shape[0]
    block = own_weight.shape[1]
    member = lax.axis_index("grp")
    parity = lax.axis_index("rep") % 2
    owns_gate = member < ACROSS_Y
    over_x, over_y, over_both = far

    both = jnp.concatenate([norm2, flip(norm2, CORE)], axis=0)
    sens_both = jnp.concatenate([sens, sens_near], axis=0)
    visible, seen = (
        jnp.concatenate(pair, axis=0) for pair in zip(masks_of(member), masks_of(member ^ CORE))
    )
    mask_two = jnp.concatenate([visible, visible], axis=1)
    latent_gu = (mm(both, ffn_in) * mask_two).astype(BF16)
    dlat_d = (LOWRANK_FACTOR * mm_nt(sens_both, lower_right_pieces) * visible).astype(BF16)
    half = width // 2
    mine = lax.dynamic_slice_in_dim(both, parity * half, half, 1)
    other = lax.dynamic_slice_in_dim(both, (1 - parity) * half, half, 1)

    def order(first, second):
        return jnp.where(owns_gate, first, second), jnp.where(owns_gate, second, first)

    latent_one, latent_two = order(latent_gu[:, :narrow], latent_gu[:, narrow:])
    seen_d = compact_with(dlat_d, seen)
    seen_one, seen_two = compact_with(latent_one, seen), compact_with(latent_two, seen)

    response_part, latent_d, dlat_one, dlat_two, deep = 0.0, 0.0, 0.0, 0.0, None
    dnorm_mine, dnorm_other = 0.0, 0.0
    for index in range(2):
        hidden = (member % ACROSS_Y) ^ (0 if index == 0 else ACROSS_X)
        start = hidden * block
        switch_block = lax.dynamic_slice_in_dim(switch_right_pieces, start, block, 1)
        lift_block = lax.dynamic_slice_in_dim(lift_right_pieces, start, block, 1)
        in_block = lax.dynamic_slice_in_dim(down_in, start, block, 0)
        down_block = lax.dynamic_slice_in_dim(down_full, start, block, 0)
        piece_one, piece_two = order(switch_block, lift_block)
        if index == 0:
            first = mm(both, own_weight)
            second = times_pieces(mine, other, over_y)
        else:
            first = times_pieces(mine, other, over_x)
            second = times_pieces(mine, other, over_both)
        first = first + LOWRANK_FACTOR * mm(latent_one, piece_one)
        second = second + LOWRANK_FACTOR * mm(latent_two, piece_two)
        gate, up = order(first, second)
        sigma = jax.nn.sigmoid(gate)
        act = (gate * sigma * up).astype(BF16)
        dact = mm_nt(sens_both, down_block) + mm_nt(dlat_d, in_block)
        dgate = (dact * up * (sigma * (1.0 + gate * (1.0 - sigma)))).astype(BF16)
        dup = (dact * gate * sigma).astype(BF16)
        dfirst, dsecond = order(dgate, dup)
        latent_d = latent_d + mm(act, in_block)
        response_part = response_part + mm(act, down_block)
        dlat_one = dlat_one + mm_nt(dfirst, piece_one)
        dlat_two = dlat_two + mm_nt(dsecond, piece_two)
        if index == 0:
            dnorm_own = mm_nt(dfirst, own_weight)
            terms = [times_pieces_flipped(dsecond, over_y)]
        else:
            terms = [
                times_pieces_flipped(dfirst, over_x),
                times_pieces_flipped(dsecond, over_both),
            ]
        for mine_part, other_part in terms:
            dnorm_mine = dnorm_mine + mine_part
            dnorm_other = dnorm_other + other_part
        grad_one = LOWRANK_FACTOR * mm_tn(dfirst, seen_one)
        grad_two = LOWRANK_FACTOR * mm_tn(dsecond, seen_two)
        rows = jnp.concatenate([mm_tn(act, seen_d), *order(grad_one, grad_two)], axis=1)
        if deep is None:
            deep = jnp.zeros((hidden_width, rows.shape[1]), BF16)
        deep = lax.dynamic_update_slice_in_dim(deep, rows.astype(BF16), start, 0)

    low, high = jnp.where(parity == 0, dnorm_mine, dnorm_other), jnp.where(
        parity == 0, dnorm_other, dnorm_mine
    )
    dnorm2 = dnorm_own + jnp.concatenate([low, high], axis=1)
    dlat_g, dlat_u = order(dlat_one, dlat_two)

    def meet(*parts):
        joined = jnp.concatenate(parts, axis=1)
        near = flip(joined[count:].astype(BF16), CORE)
        return joined[:count] + near.astype(F32)

    backward = meet(dnorm2, dlat_g, dlat_u)
    own_mask = mask_two[:count]
    dlat_gu = (LOWRANK_FACTOR * backward[:, width:] * own_mask).astype(BF16)
    dnorm2 = backward[:, :width] + mm_nt(dlat_gu, ffn_in)
    forward = meet(response_part, latent_d)
    latent_d = (forward[:, width:] * visible[:count]).astype(BF16)
    response_part = forward[:, :width] + LOWRANK_FACTOR * mm(latent_d, lower_right_pieces)
    return response_part, dnorm2, latent_d, dlat_gu, deep


def shards(
    tokens,
    response_sensitivity,
    seq_lengths,
    prefix_lengths,
    adapter_ids,
    attn_gain,
    mlp_gain,
    qkv_weight,
    out_weight,
    gate_up_weight,
    down_weight,
    query_in,
    asking_right_pieces,
    key_in,
    lookup_right_pieces,
    value_in,
    content_right_pieces,
    output_in,
    final_right_pieces,
    gate_in,
    switch_right_pieces,
    up_in,
    lift_right_pieces,
    down_in,
    lower_right_pieces,
):
    count, width = tokens.shape
    members = lax.axis_size("grp")
    groups = lax.axis_size("rep")
    kv_width = lookup_right_pieces.shape[1]
    narrow = query_in.shape[1]
    hidden_width = down_weight.shape[0]
    group = lax.axis_index("rep")
    member = lax.axis_index("grp")
    lengths = lax.dynamic_slice_in_dim(seq_lengths, 2 * group, 2)
    prefixes = lax.dynamic_slice_in_dim(prefix_lengths, 2 * group, 2)
    chosen_ids = lax.dynamic_slice_in_dim(adapter_ids, 2 * group, 2)
    key_count = count * members

    qkv_full = lax.all_gather(qkv_weight, "grp", axis=1, tiled=True)
    out_full = lax.all_gather(out_weight, "grp", axis=1, tiled=True)
    down_full = lax.all_gather(down_weight, "grp", axis=1, tiled=True)
    paired = members == 8 and groups % 2 == 0
    if paired:
        steps = gather_same_core(gate_up_weight)
        qkv_full, transfers = tie(qkv_full, next(steps))
        sens_near = flip(response_sensitivity, CORE)
    else:
        gate_up_full = lax.all_gather(gate_up_weight, "grp", axis=1, tiled=True)

    key_index = jnp.arange(key_count, dtype=jnp.int32)
    key_second = (key_index >= lengths[0]).astype(jnp.int32)
    key_position = key_index - key_second * lengths[0]
    own_index = member * count + jnp.arange(count, dtype=jnp.int32)
    own_second = (own_index >= lengths[0]).astype(jnp.int32)
    position = own_index - own_second * lengths[0]
    prefix = jnp.where(own_second == 0, prefixes[0], prefixes[1])
    allowed = (key_second[:, None] == own_second[None, :]) & (
        (key_position[:, None] <= position[None, :]) | (key_position[:, None] < prefix[None, :])
    )
    bias = jnp.where(allowed, 0.0, MASKED).astype(F32)
    first_key = own_second[0] * lengths[0]
    last_key = jnp.max(own_second * lengths[0] + jnp.maximum(position, prefix - 1))
    span = jnp.stack([first_key // KEY_BLOCK, last_key // KEY_BLOCK + 1]).astype(jnp.int32)

    columns = jnp.arange(narrow, dtype=jnp.int32)
    slots = 2 * RANK
    slot = jnp.arange(slots, dtype=jnp.int32)
    slot_column = chosen_ids[slot // RANK] * RANK + slot % RANK
    pick = (columns[:, None] == slot_column[None, :]).astype(BF16)

    def masks_of(device):
        second = (device * count + jnp.arange(count, dtype=jnp.int32) >= lengths[0]).astype(jnp.int32)
        chosen = jnp.where(second == 0, chosen_ids[0], chosen_ids[1])
        visible = (chosen[:, None] == columns[None, :] // RANK).astype(F32)
        return visible, (second[:, None] == slot[None, :] // RANK).astype(F32)

    visible, slot_visible = masks_of(member)
    mask_three = jnp.concatenate([visible, visible, visible], axis=1)

    def compact_with(latent, seen):
        return (mm(latent, pick) * seen).astype(BF16)

    def compact(latent):
        return compact_with(latent, slot_visible)

    incoming = tokens.astype(F32)
    scale_one = inverse_rms(incoming)
    norm1 = (incoming * scale_one * attn_gain).astype(BF16)
    qkv_in = jnp.concatenate([query_in, key_in, value_in], axis=1)
    latent_qkv = (mm(norm1, qkv_in) * mask_three).astype(BF16)
    latent_q, latent_k, latent_v = (
        latent_qkv[:, :narrow],
        latent_qkv[:, narrow : 2 * narrow],
        latent_qkv[:, 2 * narrow :],
    )
    adapted = LOWRANK_FACTOR * jnp.concatenate(
        [
            mm(latent_q, asking_right_pieces),
            mm(latent_k, lookup_right_pieces),
            mm(latent_v, content_right_pieces),
        ],
        axis=1,
    )
    half = HEAD_DIM // 2
    freqs = 10000.0 ** (-2.0 * jnp.arange(half).astype(F32) / HEAD_DIM)
    angles = position.astype(F32)[:, None] * jnp.concatenate([freqs, freqs])[None, :]
    cosines = jnp.cos(angles)
    sines = jnp.sin(angles)
    wide_cos, wide_sin = jnp.tile(cosines, (1, HEADS)), jnp.tile(sines, (1, HEADS))
    kv_cos, kv_sin = jnp.tile(cosines, (1, KV_HEADS)), jnp.tile(sines, (1, KV_HEADS))

    qkv = mm(norm1, qkv_full) + adapted
    scale = HEAD_DIM**-0.5
    query = (rotate(qkv[:, :width], wide_cos, wide_sin)).astype(BF16) * jnp.asarray(scale, BF16)
    key_own = rotate(qkv[:, width : width + kv_width], kv_cos, kv_sin).astype(BF16)
    value_own = qkv[:, width + kv_width :].astype(BF16)
    key_value = lax.all_gather(
        jnp.concatenate([key_own, value_own], axis=1), "grp", axis=0, tiled=True
    )
    key_pairs = side_pairs(key_value[:, :kv_width])
    value_pairs = side_pairs(key_value[:, kv_width:])
    if paired:
        key_pairs, transfers = tie(key_pairs, steps.send(transfers))
    attended_low, lse = attention_forward(span, query, key_pairs, value_pairs, bias)

    if paired:
        attended_low, transfers = tie(attended_low, steps.send(transfers))
        try:
            steps.send(transfers)
        except StopIteration as stop:
            far = stop.value

    latent_o = (mm(attended_low, output_in) * visible).astype(BF16)
    stream = incoming + (
        mm(attended_low, out_full) + LOWRANK_FACTOR * mm(latent_o, final_right_pieces)
    )
    scale_two = inverse_rms(stream)
    norm2 = (stream * scale_two * mlp_gain).astype(BF16)
    sens = response_sensitivity
    ffn_in = jnp.concatenate([gate_in, up_in], axis=1)
    pieces = (ffn_in, switch_right_pieces, lift_right_pieces, down_in, lower_right_pieces)
    if paired:
        response_part, dnorm2, latent_d, dlat_gu, deep = feed_forward_paired(
            norm2, sens, sens_near, gate_up_weight, far, down_full, pieces, masks_of, compact_with
        )
    else:
        response_part, dnorm2, latent_d, dlat_gu, deep = feed_forward_alone(
            norm2, sens, gate_up_full, down_full, pieces, masks_of, compact_with
        )
    level_response = (stream + response_part).astype(BF16)
    dhidden = sens.astype(F32) + norm_backward(stream, scale_two, mlp_gain, dnorm2)
    dbranch = dhidden.astype(BF16)
    dlat_o = (LOWRANK_FACTOR * mm_nt(dbranch, final_right_pieces) * visible).astype(BF16)
    dattended = (mm_nt(dbranch, out_full) + mm_nt(dlat_o, output_in)).astype(BF16)

    def blocks(array):
        return array.reshape(members, array.shape[0] // members, array.shape[1])

    wide = jnp.concatenate(
        [
            LOWRANK_FACTOR * mm_tn(sens, compact(latent_d)),
            mm_tn(norm2, jnp.concatenate([compact(dlat_gu[:, :narrow]), compact(dlat_gu[:, narrow:])], axis=1)),
            mm_tn(attended_low, compact(dlat_o)),
        ],
        axis=1,
    ).astype(BF16)
    final_part = (LOWRANK_FACTOR * mm_tn(dbranch, compact(latent_o))).astype(BF16)
    wide_rows, deep_rows = width // members, hidden_width // members
    final_blocks = jnp.pad(blocks(final_part), ((0, 0), (0, deep_rows - wide_rows), (0, 0)))
    early = jnp.concatenate(
        [blocks(wide), jnp.concatenate([blocks(deep), final_blocks], axis=2)], axis=1
    )
    early_sum = lax.psum_scatter(early, "grp", scatter_dimension=0, tiled=True)
    early_sum = early_sum.reshape(wide_rows + deep_rows, 4 * slots)
    early_all = lax.all_gather(early_sum, "rep", axis=0)

    dquery, dkeys, dvalues = attention_backward(
        span, query, dattended, attended_low, lse, key_pairs, value_pairs, bias
    )
    dkv = jnp.concatenate([join_sides(dkeys), join_sides(dvalues)], axis=1)
    dkv_own = exchange_sum(dkv.reshape(members, count, 2 * kv_width))
    dq = unrotate(dquery, wide_cos, wide_sin).astype(BF16)
    dk = unrotate(dkv_own[:, :kv_width], kv_cos, kv_sin).astype(BF16)
    dv = dkv_own[:, kv_width:].astype(BF16)
    dlat_qkv = (
        LOWRANK_FACTOR
        * jnp.concatenate(
            [
                mm_nt(dq, asking_right_pieces),
                mm_nt(dk, lookup_right_pieces),
                mm_nt(dv, content_right_pieces),
            ],
            axis=1,
        )
        * mask_three
    ).astype(BF16)
    dqkv = jnp.concatenate([dq, dk, dv], axis=1)
    late_wide = jnp.concatenate(
        [
            mm_tn(
                norm1,
                jnp.concatenate(
                    [compact(dlat_qkv[:, i * narrow : (i + 1) * narrow]) for i in range(3)], axis=1
                ),
            ),
            LOWRANK_FACTOR * mm_tn(dq, compact(latent_q)),
        ],
        axis=1,
    ).astype(BF16)
    late_thin = jnp.concatenate(
        [
            LOWRANK_FACTOR * mm_tn(dk, compact(latent_k)),
            LOWRANK_FACTOR * mm_tn(dv, compact(latent_v)),
        ],
        axis=1,
    ).astype(BF16)
    thin_rows = kv_width // members
    late = jnp.concatenate(
        [blocks(late_wide), jnp.pad(blocks(late_thin), ((0, 0), (0, 0), (0, 2 * slots)))], axis=1
    )
    late_sum = exchange_sum(late).astype(BF16)
    late_all = lax.all_gather(late_sum, "rep", axis=0)
    dnorm1 = mm_nt(dqkv, qkv_full) + mm_nt(dlat_qkv, qkv_in)
    input_grad = (dhidden + norm_backward(incoming, scale_one, attn_gain, dnorm1)).astype(BF16)

    all_slot = jnp.arange(groups * slots, dtype=jnp.int32)
    all_column = adapter_ids[all_slot // RANK] * RANK + all_slot % RANK
    place = (all_column[:, None] == columns[None, :]).astype(BF16)

    def gathered(array, start, rows, index):
        piece = lax.slice_in_dim(array, start, start + rows, axis=1)
        piece = piece[:, :, index * slots : (index + 1) * slots]
        return piece.transpose(1, 0, 2).reshape(rows, groups * slots)

    def as_rows(array, start, rows, index):
        return mm(gathered(array, start, rows, index), place)

    def as_columns(array, start, rows, index):
        return lax.dot_general(
            place,
            gathered(array, start, rows, index),
            (((0,), (1,)), ((), ())),
            preferred_element_type=F32,
        )

    return (
        level_response,
        input_grad,
        as_rows(late_all, 0, wide_rows, 0),
        as_columns(late_all, 0, wide_rows, 3),
        as_rows(late_all, 0, wide_rows, 1),
        as_columns(late_all, wide_rows, thin_rows, 0),
        as_rows(late_all, 0, wide_rows, 2),
        as_columns(late_all, wide_rows, thin_rows, 1),
        as_rows(early_all, 0, wide_rows, 3),
        as_columns(early_all, wide_rows, wide_rows, 3),
        as_rows(early_all, 0, wide_rows, 1),
        as_columns(early_all, wide_rows, deep_rows, 1),
        as_rows(early_all, 0, wide_rows, 2),
        as_columns(early_all, wide_rows, deep_rows, 2),
        as_rows(early_all, wide_rows, deep_rows, 0),
        as_columns(early_all, 0, wide_rows, 0),
    )


def solution(mesh):
    rows = P(("rep", "grp"), None)
    split = P(None, "grp")
    in_specs = (rows, rows, *[P()] * 5, *[split] * 4, *[P()] * 14)
    out_specs = (rows, rows, *[P("grp", None), P(None, "grp")] * 7)
    return jax.shard_map(shards, mesh=mesh, in_specs=in_specs, out_specs=out_specs, check_vma=False)
```

```python
import jax
import jax.numpy as jnp
from jax import lax
from jax.experimental import pallas as pl
from jax.experimental.pallas import tpu as pltpu
from jax.sharding import PartitionSpec as P

HEADS = 32
KV_HEADS = 4
HEAD_DIM = 64
RANK = 16
LANES = 128
KEY_BLOCK = 512

EPS = 1e-05
LOWRANK_FACTOR = 2.0
MASKED = -1e30
F32 = jnp.float32
BF16 = jnp.bfloat16


def mm(left, right):
    return jnp.dot(left, right, preferred_element_type=F32)


def mm_nt(left, right):
    return lax.dot_general(left, right, (((1,), (1,)), ((), ())), preferred_element_type=F32)


def mm_tn(left, right):
    return lax.dot_general(left, right, (((0,), (0,)), ((), ())), preferred_element_type=F32)


def inverse_rms(value):
    return lax.rsqrt(jnp.mean(value * value, axis=-1, keepdims=True) + EPS)


def norm_backward(value, scale, gain, grad):
    scaled = gain * grad
    return scale * scaled - value * (scale * scale * scale) * jnp.mean(
        scaled * value, axis=-1, keepdims=True
    )


def half_turn(value):
    half = HEAD_DIM // 2
    lane = lax.broadcasted_iota(jnp.int32, value.shape, 1) % HEAD_DIM
    return jnp.where(
        lane < half, -jnp.roll(value, -half, axis=1), jnp.roll(value, half, axis=1)
    )


def rotate(value, cosines, sines):
    return value * cosines + half_turn(value) * sines


def unrotate(grad, cosines, sines):
    return grad * cosines - half_turn(grad * sines)


def lane_of(shape):
    return lax.broadcasted_iota(jnp.int32, shape, 1)


def key_rows(span, index):
    return pl.ds(pl.multiple_of((index ^ span[2]) * KEY_BLOCK, KEY_BLOCK), KEY_BLOCK)


def spread_heads(span, odd, source_ref, pair_ref):
    def step(index, carry):
        rows = key_rows(span, index)
        value = source_ref[rows, :].astype(F32)
        turned = pltpu.roll(value, HEAD_DIM, 1)
        low = lane_of(value.shape) < HEAD_DIM
        none = jnp.zeros_like(value)
        pair_ref[0, rows, :] = jnp.where(low, jnp.where(odd, turned, value), none).astype(BF16)
        pair_ref[1, rows, :] = jnp.where(low, none, jnp.where(odd, value, turned)).astype(BF16)
        return carry

    lax.fori_loop(span[0], span[1], step, 0)


def attention_forward_kernel(span, q_ref, key_ref, value_ref, bias_ref, out_ref, lse_ref, k_ref, v_ref):
    tokens = q_ref.shape[0]
    per_kv = pl.num_programs(0) // KV_HEADS
    odd = lax.rem(pl.program_id(0) // per_kv, 2) == 1

    @pl.when(lax.rem(pl.program_id(0), per_kv) == 0)
    def _():
        spread_heads(span, odd, key_ref, k_ref)
        spread_heads(span, odd, value_ref, v_ref)

    query = q_ref[...]

    def step(index, carry):
        rows = key_rows(span, index)
        bias = bias_ref[rows, :]
        mixed = carry[4]
        new, parts, decays = [], [], []
        for side in range(2):
            peak, total = carry[2 * side], carry[2 * side + 1]
            scores = mm_nt(k_ref[side, rows, :], query) + bias
            top = jnp.maximum(peak, jnp.max(scores, axis=0, keepdims=True))
            decay = jnp.exp(peak - top)
            probs = jnp.exp(scores - top)
            total = total * decay + jnp.sum(probs, axis=0, keepdims=True)
            new += [top, total]
            decays.append(jnp.broadcast_to(decay, (HEAD_DIM, tokens)))
            parts.append(mm_tn(v_ref[side, rows, :], probs.astype(BF16)))
        mixed = mixed * jnp.concatenate(decays, axis=0) + (parts[0] + parts[1])
        return (*new, mixed)

    low = jnp.full((1, tokens), MASKED, F32)
    none = jnp.zeros((1, tokens), F32)
    peak0, total0, peak1, total1, mixed = lax.fori_loop(
        span[0], span[1], step, (low, none, low, none, jnp.zeros((LANES, tokens), F32))
    )
    weight = jnp.concatenate(
        [
            jnp.broadcast_to(1.0 / total0, (HEAD_DIM, tokens)),
            jnp.broadcast_to(1.0 / total1, (HEAD_DIM, tokens)),
        ],
        axis=0,
    )
    out_ref[...] = (mixed * weight).T.astype(BF16)
    lse_ref[0] = jnp.concatenate([peak0 + jnp.log(total0), peak1 + jnp.log(total1)], axis=0)


def key_value_specs(keys, per_kv):
    blocks = KV_HEADS * HEAD_DIM // LANES
    heads = LANES // HEAD_DIM
    return [
        pl.BlockSpec((keys, LANES), lambda j, s: (0, j // per_kv // heads)),
        pl.BlockSpec((keys, LANES), lambda j, s: (0, blocks + j // per_kv // heads)),
    ]


def attention_forward(span, query, key_value, bias):
    tokens, width = query.shape
    keys = bias.shape[0]
    pairs = width // LANES
    pair_spec = pl.BlockSpec((tokens, LANES), lambda j, s: (0, j))
    return pl.pallas_call(
        attention_forward_kernel,
        out_shape=(
            jax.ShapeDtypeStruct((tokens, width), BF16),
            jax.ShapeDtypeStruct((pairs, 2, tokens), F32),
        ),
        grid_spec=pltpu.PrefetchScalarGridSpec(
            num_scalar_prefetch=1,
            grid=(pairs,),
            in_specs=[
                pair_spec,
                *key_value_specs(keys, pairs // KV_HEADS),
                pl.BlockSpec((keys, tokens), lambda j, s: (0, 0)),
            ],
            out_specs=(pair_spec, pl.BlockSpec((1, 2, tokens), lambda j, s: (j, 0, 0))),
            scratch_shapes=[pltpu.VMEM((2, keys, LANES), BF16)] * 2,
        ),
        compiler_params=pltpu.CompilerParams(
            dimension_semantics=("arbitrary",), vmem_limit_bytes=40 << 20
        ),
        cost_estimate=pl.CostEstimate(
            flops=4 * tokens * keys * width,
            transcendentals=tokens * keys * HEADS // 2,
            bytes_accessed=4 * tokens * width + 16 * keys * LANES * KV_HEADS,
        ),
        name="attention_forward",
    )(span, query, key_value, key_value, bias)


def attention_backward_kernel(
    span,
    q_ref,
    do_ref,
    o_ref,
    lse_ref,
    key_ref,
    value_ref,
    bias_ref,
    cos_ref,
    sin_ref,
    dq_ref,
    dk_ref,
    dv_ref,
    k_ref,
    v_ref,
    dk_sum,
    dv_sum,
):
    tokens = q_ref.shape[0]
    per_kv = pl.num_programs(0) // KV_HEADS
    member = lax.rem(pl.program_id(0), per_kv)
    odd = lax.rem(pl.program_id(0) // per_kv, LANES // HEAD_DIM) == 1

    @pl.when(member == 0)
    def _():
        spread_heads(span, odd, key_ref, k_ref)
        spread_heads(span, odd, value_ref, v_ref)
        dk_sum[...] = jnp.zeros_like(dk_sum)
        dv_sum[...] = jnp.zeros_like(dv_sum)

    query = q_ref[...]
    grad = do_ref[...]
    low = lane_of((tokens, LANES)) < HEAD_DIM
    none = jnp.zeros_like(query)
    query_stack = jnp.concatenate(
        [jnp.where(low, query, none), jnp.where(low, none, query)], axis=0
    )
    grad_stack = jnp.concatenate([jnp.where(low, grad, none), jnp.where(low, none, grad)], axis=0)
    product = grad.astype(F32) * o_ref[...].astype(F32)
    row = lax.broadcasted_iota(jnp.int32, (8, LANES), 0)
    column = lax.broadcasted_iota(jnp.int32, (8, LANES), 1)
    chooser = jnp.where(row == column // HEAD_DIM, 1.0, 0.0).astype(F32)
    deltas = lax.dot_general(
        chooser,
        product,
        (((1,), (1,)), ((), ())),
        precision=lax.Precision.HIGHEST,
        preferred_element_type=F32,
    )

    def step(index, dquery):
        rows = key_rows(span, index)
        bias = bias_ref[rows, :]
        all_probs, all_dscores = [], []
        for side in range(2):
            scores = mm_nt(k_ref[side, rows, :], query) + bias
            probs = jnp.exp(scores - lse_ref[0, side : side + 1, :])
            dprobs = mm_nt(v_ref[side, rows, :], grad)
            dscores = (probs * (dprobs - deltas[side : side + 1, :])).astype(BF16)
            all_probs.append(probs.astype(BF16))
            all_dscores.append(dscores)
            dquery = dquery + mm_tn(k_ref[side, rows, :], dscores)
        dk_sum[rows, :] += mm(jnp.concatenate(all_dscores, axis=1), query_stack)
        dv_sum[rows, :] += mm(jnp.concatenate(all_probs, axis=1), grad_stack)
        return dquery

    dquery = lax.fori_loop(span[0], span[1], step, jnp.zeros((LANES, tokens), F32))
    dquery = dquery.T * (HEAD_DIM**-0.5)
    turned = dquery * sin_ref[...]
    half = HEAD_DIM // 2
    first = lax.rem(lane_of(turned.shape), HEAD_DIM) < half
    turned = jnp.where(
        first, pltpu.roll(turned, LANES - half, 1), -pltpu.roll(turned, half, 1)
    )
    dq_ref[...] = (dquery * cos_ref[...] + turned).astype(BF16)

    @pl.when(member == per_kv - 1)
    def _():
        def put(index, carry):
            place = pl.ds(pl.multiple_of((index ^ span[3]) * tokens, tokens), tokens)
            for sum_ref, out_ref in ((dk_sum, dk_ref), (dv_sum, dv_ref)):
                total = sum_ref[pl.ds(pl.multiple_of(index * tokens, tokens), tokens), :]
                total = total + pltpu.roll(total, HEAD_DIM, 1)
                keep = jnp.logical_and(odd, lane_of(total.shape) < HEAD_DIM)
                out_ref[place, :] = jnp.where(keep, out_ref[place, :], total.astype(BF16))
            return carry

        lax.fori_loop(0, dk_sum.shape[0] // tokens, put, 0)


def attention_backward(span, query, grad, attended, lse, key_value, bias, cosines, sines):
    tokens, width = query.shape
    keys = bias.shape[0]
    pairs = width // LANES
    per_kv = pairs // KV_HEADS
    heads = LANES // HEAD_DIM
    pair_spec = pl.BlockSpec((tokens, LANES), lambda j, s: (0, j))
    table_spec = pl.BlockSpec((tokens, LANES), lambda j, s: (0, 0))
    dkv_spec = pl.BlockSpec((keys, LANES), lambda j, s: (0, j // per_kv // heads))
    return pl.pallas_call(
        attention_backward_kernel,
        out_shape=(
            jax.ShapeDtypeStruct((tokens, width), BF16),
            jax.ShapeDtypeStruct((keys, KV_HEADS * HEAD_DIM), BF16),
            jax.ShapeDtypeStruct((keys, KV_HEADS * HEAD_DIM), BF16),
        ),
        grid_spec=pltpu.PrefetchScalarGridSpec(
            num_scalar_prefetch=1,
            grid=(pairs,),
            in_specs=[
                pair_spec,
                pair_spec,
                pair_spec,
                pl.BlockSpec((1, 2, tokens), lambda j, s: (j, 0, 0)),
                *key_value_specs(keys, per_kv),
                pl.BlockSpec((keys, tokens), lambda j, s: (0, 0)),
                table_spec,
                table_spec,
            ],
            out_specs=(pair_spec, dkv_spec, dkv_spec),
            scratch_shapes=[pltpu.VMEM((2, keys, LANES), BF16)] * 2
            + [pltpu.VMEM((keys, LANES), F32)] * 2,
        ),
        compiler_params=pltpu.CompilerParams(
            dimension_semantics=("arbitrary",), vmem_limit_bytes=48 << 20
        ),
        cost_estimate=pl.CostEstimate(
            flops=10 * tokens * keys * width,
            transcendentals=tokens * keys * HEADS // 2,
            bytes_accessed=10 * tokens * width + 24 * keys * LANES * KV_HEADS,
        ),
        name="attention_backward",
    )(span, query, grad, attended, lse, key_value, key_value, bias, cosines, sines)


CORE, ACROSS_X, ACROSS_Y = 1, 2, 4


def flip(array, mask):
    members = lax.axis_size("grp")
    return lax.ppermute(array, "grp", [(i, i ^ mask) for i in range(members)])


def flip_group(array):
    groups = lax.axis_size("rep")
    return lax.ppermute(array, "rep", [(i, i ^ 1) for i in range(groups)])


def gather_same_core(weight):
    rows = weight.shape[0] // 4
    parity = lax.axis_index("rep") % 2
    quarters = [
        lax.dynamic_slice_in_dim(weight, ((parity ^ (q // 2)) * 2 + q % 2) * rows, rows, 0)
        for q in range(4)
    ]
    x_low, y_low, next_quarter = yield quarters, (
        flip(quarters[0], ACROSS_X),
        flip(quarters[0], ACROSS_Y),
        quarters[1],
    )
    x_high, y_high, *others = yield (
        flip(next_quarter, ACROSS_X),
        flip(next_quarter, ACROSS_Y),
        flip_group(x_low),
        flip_group(y_low),
    )
    x_low_other, y_low_other = others
    both_low, both_high, x_high_other, y_high_other = yield (
        flip(x_low, ACROSS_Y),
        flip(y_high, ACROSS_X),
        flip_group(x_high),
        flip_group(y_high),
    )
    both_other = yield flip_group(both_low), flip_group(both_high)
    return (
        (x_low, x_high, x_low_other, x_high_other),
        (y_low, y_high, y_low_other, y_high_other),
        (both_low, both_high, *both_other),
    )


def gather_key_values(own):
    pieces = [own, flip(own, ACROSS_X), flip(own, ACROSS_Y), flip(own, ACROSS_X | ACROSS_Y)]
    return jnp.concatenate(
        [part for piece in pieces for part in (piece, flip(piece, CORE))], axis=0
    )


def tie(value, transfers):
    value, *transfers = lax.optimization_barrier((value, *transfers))
    return value, tuple(transfers)


def feed_forward_alone(norm2, sens, gate_up_full, down_full, small, seen):
    ffn_in, switch, lift, down_in, lower = small
    slots, hidden_width = switch.shape
    seen_two = jnp.concatenate([seen, seen], axis=1)
    latent_gu = (mm(norm2, ffn_in) * seen_two).astype(BF16)
    latent_g, latent_u = latent_gu[:, :slots], latent_gu[:, slots:]
    gate_up = mm(norm2, gate_up_full) + LOWRANK_FACTOR * jnp.concatenate(
        [mm(latent_g, switch), mm(latent_u, lift)], axis=1
    )
    gate = gate_up[:, :hidden_width]
    up = gate_up[:, hidden_width:]
    sigma = jax.nn.sigmoid(gate)
    act = (gate * sigma * up).astype(BF16)
    latent_d = (mm_nt(act, down_in) * seen).astype(BF16)
    response_part = mm(act, down_full) + LOWRANK_FACTOR * mm(latent_d, lower)
    dlat_d = (LOWRANK_FACTOR * mm_nt(sens, lower) * seen).astype(BF16)
    dact = mm_nt(sens, down_full) + mm(dlat_d, down_in)
    dgate = (dact * up * (sigma * (1.0 + gate * (1.0 - sigma)))).astype(BF16)
    dup = (dact * gate * sigma).astype(BF16)
    dlat_gu = (
        LOWRANK_FACTOR
        * jnp.concatenate([mm_nt(dgate, switch), mm_nt(dup, lift)], axis=1)
        * seen_two
    ).astype(BF16)
    dnorm2 = (
        mm_nt(dgate, gate_up_full[:, :hidden_width])
        + mm_nt(dup, gate_up_full[:, hidden_width:])
        + mm_nt(dlat_gu, ffn_in)
    )
    deep = jnp.concatenate(
        [
            mm_tn(dlat_d, act),
            LOWRANK_FACTOR * mm_tn(latent_g, dgate),
            LOWRANK_FACTOR * mm_tn(latent_u, dup),
        ],
        axis=0,
    ).astype(BF16)
    return response_part, dnorm2, latent_d, dlat_gu, deep


def feed_forward_kernel(
    meta, x_ref, g_ref, latent_ref, dlat_ref, stack_ref, *refs
):
    weights = [[refs[8 * b + 4 * t : 8 * b + 4 * t + 4] for t in range(2)] for b in range(2)]
    piece_refs = [refs[16 + 2 * b : 18 + 2 * b] for b in range(2)]
    in_refs = refs[20:22]
    down_refs = refs[22:24]
    back_own, back_near, front_own, front_near, deep_ref = refs[24:29]
    dnorm, response, dlat_sum, latent_sum = refs[29:33]
    tokens, width = x_ref.shape
    count = tokens // 2
    slots = dlat_ref.shape[1]
    quarter = width // 4
    parity = meta[0]
    owns_gate = meta[1] == 1
    starts = [
        pl.multiple_of((parity if q < 2 else 1 - parity) * (width // 2) + (q % 2) * quarter, quarter)
        for q in range(4)
    ]

    @pl.when(pl.program_id(0) == 0)
    def _():
        for ref in (dnorm, response, dlat_sum, latent_sum):
            ref[...] = jnp.zeros_like(ref)

    none = jnp.zeros((slots, LANES), BF16)
    firsts, seconds = ([piece_refs[b][t][...] for b in range(2)] for t in range(2))
    pieces = jnp.concatenate(
        [
            jnp.concatenate([firsts[0], none, firsts[1], none], axis=1),
            jnp.concatenate([none, seconds[0], none, seconds[1]], axis=1),
        ],
        axis=0,
    )

    def columns_of(q):
        return jnp.concatenate(
            [weights[b][t][q][...] for b in range(2) for t in range(2)], axis=1
        )

    total = mm(latent_ref[...], pieces)
    for q in range(4):
        total = total + mm(x_ref[:, pl.ds(starts[q], quarter)], columns_of(q))
    first = jnp.concatenate([total[:, :LANES], total[:, 2 * LANES : 3 * LANES]], axis=1)
    second = jnp.concatenate([total[:, LANES : 2 * LANES], total[:, 3 * LANES :]], axis=1)
    gate = jnp.where(owns_gate, first, second)
    up = jnp.where(owns_gate, second, first)
    down_in = jnp.concatenate([ref[...] for ref in in_refs], axis=1)
    sigma = jax.nn.sigmoid(gate)
    act = (gate * sigma * up).astype(BF16)
    dact = mm(dlat_ref[...], down_in)
    parts, _, columns = down_refs[0].shape
    for k in range(parts):
        down = jnp.concatenate([ref[k] for ref in down_refs], axis=0)
        lanes = slice(k * columns, (k + 1) * columns)
        dact = dact + mm_nt(g_ref[:, lanes], down)
        response[:, lanes] += mm(act, down)
    dgate = (dact * up * (sigma * (1.0 + gate * (1.0 - sigma)))).astype(BF16)
    dup = (dact * gate * sigma).astype(BF16)
    latent_sum[:, :slots] += mm_nt(act, down_in)
    act_grad = mm(stack_ref[:slots, :], act)
    dfirst = jnp.where(owns_gate, dgate, dup)
    dsecond = jnp.where(owns_gate, dup, dgate)
    both = jnp.concatenate(
        [dfirst[:, :LANES], dsecond[:, :LANES], dfirst[:, LANES:], dsecond[:, LANES:]], axis=1
    )
    for q in range(4):
        dnorm[:, q * quarter : (q + 1) * quarter] += mm_nt(both, columns_of(q))
    dlat_sum[:, : 2 * slots] += mm_nt(both, pieces)
    piece_grad = mm(stack_ref[slots:, :], both).astype(BF16)
    act_grad = act_grad.astype(BF16)
    for b in range(2):
        deep_ref[b, :slots, :] = act_grad[:, b * LANES : (b + 1) * LANES]
        start = 2 * b * LANES
        deep_ref[b, slots : 2 * slots, :] = piece_grad[:slots, start : start + LANES]
        deep_ref[b, 2 * slots :, :] = piece_grad[slots:, start + LANES : start + 2 * LANES]

    @pl.when(pl.program_id(0) == pl.num_programs(0) - 1)
    def _():
        for q in range(4):
            value = dnorm[:, q * quarter : (q + 1) * quarter]
            back_own[:, pl.ds(starts[q], quarter)] = value[:count]
            back_near[:, pl.ds(starts[q], quarter)] = value[count:].astype(BF16)
        back_own[:, width:] = dlat_sum[:count, :]
        back_near[:, width:] = dlat_sum[count:, :].astype(BF16)
        front_own[:, :width] = response[:count, :]
        front_near[:, :width] = response[count:, :].astype(BF16)
        front_own[:, width:] = latent_sum[:count, :]
        front_near[:, width:] = latent_sum[count:, :].astype(BF16)


def feed_forward_paired(norm2, sens, sens_near, own, far, down_parts, small, seen, seen_near):
    ffn_in, switch, lift, down_in, lower = small
    count, width = norm2.shape
    slots, hidden_width = switch.shape
    block = own[0].shape[1]
    steps = block // LANES
    member = lax.axis_index("grp")
    parity = lax.axis_index("rep") % 2
    owns_gate = member < ACROSS_Y
    hidden = member % ACROSS_Y
    over_x, over_y, over_both = far

    def order(first, second):
        return jnp.where(owns_gate, first, second), jnp.where(owns_gate, second, first)

    both = jnp.concatenate([norm2, flip(norm2, CORE)], axis=0)
    sens_both = jnp.concatenate([sens, sens_near], axis=0)
    seen_both = jnp.concatenate([seen, seen_near], axis=0)
    seen_two = jnp.concatenate([seen_both, seen_both], axis=1)
    latent_gu = (mm(both, ffn_in) * seen_two).astype(BF16)
    latent = jnp.concatenate(order(latent_gu[:, :slots], latent_gu[:, slots:]), axis=1)
    dlat_d = (LOWRANK_FACTOR * mm_nt(sens_both, lower) * seen_both).astype(BF16)
    stack = jnp.concatenate([dlat_d, latent], axis=1).T
    pieces = order(switch, lift)
    meta = jnp.stack([parity, owns_gate.astype(jnp.int32), hidden, hidden ^ ACROSS_X]).astype(
        jnp.int32
    )

    quarter = width // 4
    operands, specs = [], []

    def add(operand, shape, index_map, **how):
        operands.append(operand)
        specs.append(pl.BlockSpec(shape, index_map, **how))

    def whole(operand):
        add(operand, operand.shape, lambda j, m: (0,) * operand.ndim)

    def columns_of(piece):
        add(piece, (quarter, LANES), lambda j, m: (0, j))

    for operand in (both, sens_both, latent * jnp.asarray(LOWRANK_FACTOR, BF16), dlat_d, stack):
        whole(operand)
    for quarters in (own, over_y, over_x, over_both):
        for piece in quarters:
            columns_of(piece)
    for b in range(2):
        for piece in pieces:
            add(piece, (slots, LANES), lambda j, m, b=b: (0, m[2 + b] * steps + j))
    for b in range(2):
        add(down_in, (slots, LANES), lambda j, m, b=b: (0, m[2 + b] * steps + j))
    members, _, part_columns = down_parts.shape
    for b in range(2):
        add(
            down_parts,
            (members, LANES, part_columns),
            lambda j, m, b=b: (0, m[2 + b] * steps + j, 0),
        )
    wide = width + LANES
    result_spec = pl.BlockSpec((count, wide), lambda j, m: (0, 0))
    flops = 2 * 6 * 2 * count * width * 2 * block
    back_own, back_near, front_own, front_near, deep = pl.pallas_call(
        feed_forward_kernel,
        out_shape=(
            jax.ShapeDtypeStruct((count, wide), F32),
            jax.ShapeDtypeStruct((count, wide), BF16),
            jax.ShapeDtypeStruct((count, wide), F32),
            jax.ShapeDtypeStruct((count, wide), BF16),
            jax.ShapeDtypeStruct((2, 3 * slots, block), BF16),
        ),
        grid_spec=pltpu.PrefetchScalarGridSpec(
            num_scalar_prefetch=1,
            grid=(steps,),
            in_specs=specs,
            out_specs=(
                *[result_spec] * 4,
                pl.BlockSpec((2, 3 * slots, LANES), lambda j, m: (0, 0, j)),
            ),
            scratch_shapes=[
                pltpu.VMEM((2 * count, width), F32),
                pltpu.VMEM((2 * count, width), F32),
                pltpu.VMEM((2 * count, LANES), F32),
                pltpu.VMEM((2 * count, LANES), F32),
            ],
        ),
        compiler_params=pltpu.CompilerParams(
            dimension_semantics=("arbitrary",), vmem_limit_bytes=56 << 20
        ),
        cost_estimate=pl.CostEstimate(
            flops=flops,
            transcendentals=4 * count * block,
            bytes_accessed=2 * 6 * width * block + 40 * count * width,
        ),
        name="feed_forward",
    )(meta, *operands)

    backward = back_own + flip(back_near, CORE).astype(F32)
    forward = front_own + flip(front_near, CORE).astype(F32)
    dlat_one, dlat_two = (
        backward[:, width : width + slots],
        backward[:, width + slots : width + 2 * slots],
    )
    dlat_gu = (
        LOWRANK_FACTOR * jnp.concatenate(order(dlat_one, dlat_two), axis=1) * seen_two[:count]
    ).astype(BF16)
    dnorm2 = backward[:, :width] + mm_nt(dlat_gu, ffn_in)
    latent_d = (forward[:, width : width + slots] * seen).astype(BF16)
    response_part = forward[:, :width] + LOWRANK_FACTOR * mm(latent_d, lower)

    two = jnp.asarray(LOWRANK_FACTOR, BF16)
    grads = order(deep[:, slots : 2 * slots] * two, deep[:, 2 * slots :] * two)
    deep = jnp.concatenate([deep[:, :slots], *grads], axis=1)
    placed = jnp.zeros((3 * slots, hidden_width), BF16)
    for b in range(2):
        placed = lax.dynamic_update_slice_in_dim(
            placed, deep[b], (hidden ^ (b * ACROSS_X)) * block, 1
        )
    return response_part, dnorm2, latent_d, dlat_gu, placed


def exchange_sum(parts):
    received = lax.all_to_all(parts.astype(BF16), "grp", 0, 0, tiled=True)
    return jnp.sum(received.astype(F32), axis=0)


def round_groups(array):
    groups = lax.axis_size("rep")
    return [array] + [
        lax.ppermute(array, "rep", [(i, (i + shift) % groups) for i in range(groups)])
        for shift in range(1, groups)
    ]


def shards(
    tokens,
    response_sensitivity,
    seq_lengths,
    prefix_lengths,
    adapter_ids,
    attn_gain,
    mlp_gain,
    qkv_weight,
    out_weight,
    gate_up_weight,
    down_weight,
    query_in,
    asking_right_pieces,
    key_in,
    lookup_right_pieces,
    value_in,
    content_right_pieces,
    output_in,
    final_right_pieces,
    gate_in,
    switch_right_pieces,
    up_in,
    lift_right_pieces,
    down_in,
    lower_right_pieces,
):
    count, width = tokens.shape
    members = lax.axis_size("grp")
    groups = lax.axis_size("rep")
    kv_width = lookup_right_pieces.shape[1]
    narrow = query_in.shape[1]
    group = lax.axis_index("rep")
    member = lax.axis_index("grp")
    lengths = lax.dynamic_slice_in_dim(seq_lengths, 2 * group, 2)
    prefixes = lax.dynamic_slice_in_dim(prefix_lengths, 2 * group, 2)
    chosen_ids = lax.dynamic_slice_in_dim(adapter_ids, 2 * group, 2)
    key_count = count * members
    sens = response_sensitivity

    paired = members == 8 and groups % 2 == 0
    qkv_full = lax.all_gather(qkv_weight, "grp", axis=1, tiled=True)
    if paired:
        steps = gather_same_core(gate_up_weight)
        own, transfers = next(steps)
        sens_near = flip(sens, CORE)
    else:
        out_full = lax.all_gather(out_weight, "grp", axis=1, tiled=True)
        down_full = lax.all_gather(down_weight, "grp", axis=1, tiled=True)
        gate_up_full = lax.all_gather(gate_up_weight, "grp", axis=1, tiled=True)

    turn = member if paired else 0
    key_index = jnp.arange(key_count, dtype=jnp.int32)
    key_index = (key_index // count ^ turn) * count + key_index % count
    key_second = (key_index >= lengths[0]).astype(jnp.int32)
    key_position = key_index - key_second * lengths[0]
    own_index = member * count + jnp.arange(count, dtype=jnp.int32)
    own_second = (own_index >= lengths[0]).astype(jnp.int32)
    position = own_index - own_second * lengths[0]
    prefix = jnp.where(own_second == 0, prefixes[0], prefixes[1])
    allowed = (key_second[:, None] == own_second[None, :]) & (
        (key_position[:, None] <= position[None, :]) | (key_position[:, None] < prefix[None, :])
    )
    bias = jnp.where(allowed, 0.0, MASKED).astype(F32)
    first_key = own_second[0] * lengths[0]
    last_key = jnp.max(own_second * lengths[0] + jnp.maximum(position, prefix - 1))
    span = jnp.stack(
        [first_key // KEY_BLOCK, last_key // KEY_BLOCK + 1, turn * count // KEY_BLOCK, turn]
    ).astype(jnp.int32)

    slots = 2 * RANK
    columns = jnp.arange(narrow, dtype=jnp.int32)
    slot = jnp.arange(slots, dtype=jnp.int32)
    slot_column = chosen_ids[slot // RANK] * RANK + slot % RANK
    pick = (columns[:, None] == slot_column[None, :]).astype(BF16)

    def seen_by(device):
        index = device * count + jnp.arange(count, dtype=jnp.int32)
        second = (index >= lengths[0]).astype(jnp.int32)
        return (second[:, None] == slot[None, :] // RANK).astype(F32)

    def pick_in(weight):
        return mm(weight, pick).astype(BF16)

    def pick_right(weight):
        return mm_tn(pick, weight).astype(BF16)

    seen = seen_by(member)
    seen_three = jnp.concatenate([seen, seen, seen], axis=1)
    qkv_in = jnp.concatenate([pick_in(query_in), pick_in(key_in), pick_in(value_in)], axis=1)
    asking = pick_right(asking_right_pieces)
    lookup = pick_right(lookup_right_pieces)
    content = pick_right(content_right_pieces)
    none = jnp.zeros_like(lookup)
    kv_right = jnp.concatenate(
        [jnp.concatenate([lookup, none], axis=1), jnp.concatenate([none, content], axis=1)], axis=0
    )
    out_in = pick_in(output_in)
    final = pick_right(final_right_pieces)
    lower = pick_right(lower_right_pieces)
    small = (
        jnp.concatenate([pick_in(gate_in), pick_in(up_in)], axis=1),
        pick_right(switch_right_pieces),
        pick_right(lift_right_pieces),
        lax.dot_general(
            pick, down_in, (((0,), (1,)), ((), ())), preferred_element_type=F32
        ).astype(BF16),
        lower,
    )

    incoming = tokens.astype(F32)
    scale_one = inverse_rms(incoming)
    norm1 = (incoming * scale_one * attn_gain).astype(BF16)
    if paired:
        norm1, transfers = tie(norm1, transfers)
        qkv_full, transfers = tie(qkv_full, steps.send(transfers))
        out_full = lax.all_gather(out_weight, "grp", axis=1, tiled=True)
        down_full = lax.all_gather(down_weight, "grp", axis=0)
    latent_qkv = (mm(norm1, qkv_in) * seen_three).astype(BF16)
    latent_q, latent_kv = latent_qkv[:, :slots], latent_qkv[:, slots:]
    half = HEAD_DIM // 2
    freqs = 10000.0 ** (-2.0 * jnp.arange(half).astype(F32) / HEAD_DIM)
    freqs = jnp.tile(freqs, LANES // half)
    angles = position.astype(F32)[:, None] * freqs[None, :]
    cosines, sines = jnp.cos(angles), jnp.sin(angles)

    def widen(table, size):
        return jnp.tile(table, (1, size // LANES))

    qkv = mm(norm1, qkv_full)
    query = qkv[:, :width] + LOWRANK_FACTOR * mm(latent_q, asking)
    own_kv = qkv[:, width:] + LOWRANK_FACTOR * mm(latent_kv, kv_right)
    query = rotate(query, widen(cosines, width), widen(sines, width)).astype(BF16)
    query = query * jnp.asarray(HEAD_DIM**-0.5, BF16)
    key_own = rotate(own_kv[:, :kv_width], widen(cosines, kv_width), widen(sines, kv_width))
    key_value = jnp.concatenate([key_own, own_kv[:, kv_width:]], axis=1).astype(BF16)
    if paired:
        key_value, transfers = tie(gather_key_values(key_value), steps.send(transfers))
    else:
        key_value = lax.all_gather(key_value, "grp", axis=0, tiled=True)
    attended_low, lse = attention_forward(span, query, key_value, bias)
    if paired:
        attended_low, transfers = tie(attended_low, steps.send(transfers))
        try:
            steps.send(transfers)
        except StopIteration as stop:
            far = stop.value

    latent_o = (mm(attended_low, out_in) * seen).astype(BF16)
    stream = incoming + (mm(attended_low, out_full) + LOWRANK_FACTOR * mm(latent_o, final))
    scale_two = inverse_rms(stream)
    norm2 = (stream * scale_two * mlp_gain).astype(BF16)
    if paired:
        response_part, dnorm2, latent_d, dlat_gu, deep = feed_forward_paired(
            norm2, sens, sens_near, own, far, down_full, small, seen, seen_by(member ^ CORE)
        )
    else:
        response_part, dnorm2, latent_d, dlat_gu, deep = feed_forward_alone(
            norm2, sens, gate_up_full, down_full, small, seen
        )
    level_response = (stream + response_part).astype(BF16)
    dhidden = sens.astype(F32) + norm_backward(stream, scale_two, mlp_gain, dnorm2)
    dbranch = dhidden.astype(BF16)
    dlat_o = (LOWRANK_FACTOR * mm_nt(dbranch, final) * seen).astype(BF16)
    dattended = (mm_nt(dbranch, out_full) + mm_nt(dlat_o, out_in)).astype(BF16)

    wide = jnp.concatenate(
        [
            LOWRANK_FACTOR * mm_tn(latent_d, sens),
            mm_tn(dlat_gu, norm2),
            mm_tn(dlat_o, attended_low),
            LOWRANK_FACTOR * mm_tn(latent_o, dbranch),
        ],
        axis=0,
    ).astype(BF16)
    deep_sum = lax.psum_scatter(deep, "grp", scatter_dimension=1, tiled=True)

    dq, dk_all, dv_all = attention_backward(
        span, query, dattended, attended_low, lse, key_value, bias, cosines, sines
    )
    dk_all, (deep_sum,) = tie(dk_all, (deep_sum,))
    dkv_all = jnp.concatenate([dk_all, dv_all], axis=1)
    dkv = exchange_sum(dkv_all.reshape(members, count, 2 * kv_width))
    dlat_q = (LOWRANK_FACTOR * mm_nt(dq, asking) * seen).astype(BF16)
    dnorm_q = mm_nt(dq, qkv_full[:, :width]) + mm_nt(dlat_q, qkv_in[:, :slots])
    late_q = jnp.concatenate(
        [mm_tn(dlat_q, norm1), LOWRANK_FACTOR * mm_tn(latent_q, dq)], axis=0
    ).astype(BF16)
    dk = unrotate(dkv[:, :kv_width], widen(cosines, kv_width), widen(sines, kv_width))
    dkv = jnp.concatenate([dk, dkv[:, kv_width:]], axis=1).astype(BF16)
    dlat_kv = (LOWRANK_FACTOR * mm_nt(dkv, kv_right) * seen_three[:, : 2 * slots]).astype(BF16)
    late_kv = mm_tn(dlat_kv, norm1).astype(BF16)
    thin = (
        LOWRANK_FACTOR
        * jnp.concatenate(
            [
                mm_tn(latent_kv[:, :slots], dkv[:, :kv_width]),
                mm_tn(latent_kv[:, slots:], dkv[:, kv_width:]),
            ],
            axis=0,
        )
    ).astype(BF16)

    def blocks(array):
        rows, size = array.shape
        return array.reshape(rows, members, size // members).transpose(1, 0, 2)

    share, thin_share = width // members, kv_width // members
    thin_rows = 2 * slots * thin_share // share
    late = jnp.concatenate(
        [
            blocks(jnp.concatenate([late_q, late_kv, wide], axis=0)),
            blocks(thin).reshape(members, thin_rows, share),
        ],
        axis=1,
    )
    late, (deep_sum,) = tie(late, (deep_sum,))
    late_sum = round_groups(exchange_sum(late).astype(BF16))
    deep_sum = round_groups(deep_sum)
    dnorm1 = dnorm_q + mm_nt(dkv, qkv_full[:, width:]) + mm_nt(dlat_kv, qkv_in[:, slots:])
    input_grad = (dhidden + norm_backward(incoming, scale_one, attn_gain, dnorm1)).astype(BF16)

    turn = jnp.arange(groups * slots, dtype=jnp.int32)
    source = (group - turn // slots) % groups
    all_column = adapter_ids[2 * source + turn % slots // RANK] * RANK + turn % RANK
    place = (all_column[:, None] == columns[None, :]).astype(BF16)

    def rows_of(arrays, index):
        return jnp.concatenate(
            [array[index * slots : (index + 1) * slots] for array in arrays], axis=0
        )

    def in_grad(arrays, index):
        return mm_tn(rows_of(arrays, index), place)

    def right_grad(arrays, index):
        return mm_tn(place, rows_of(arrays, index))

    thin_sum = [array[9 * slots :].reshape(2 * slots, thin_share) for array in late_sum]
    return (
        level_response,
        input_grad,
        in_grad(late_sum, 0),
        right_grad(late_sum, 1),
        in_grad(late_sum, 2),
        right_grad(thin_sum, 0),
        in_grad(late_sum, 3),
        right_grad(thin_sum, 1),
        in_grad(late_sum, 7),
        right_grad(late_sum, 8),
        in_grad(late_sum, 5),
        right_grad(deep_sum, 1),
        in_grad(late_sum, 6),
        right_grad(deep_sum, 2),
        in_grad(deep_sum, 0),
        right_grad(late_sum, 4),
    )


def solution(mesh):
    rows = P(("rep", "grp"), None)
    split = P(None, "grp")
    in_specs = (rows, rows, *[P()] * 5, *[split] * 4, *[P()] * 14)
    out_specs = (rows, rows, *[P("grp", None), P(None, "grp")] * 7)
    return jax.shard_map(shards, mesh=mesh, in_specs=in_specs, out_specs=out_specs, check_vma=False)
```

```python
import functools

import jax
import jax.numpy as jnp
from jax import lax
from jax.experimental import pallas as pl
from jax.experimental.pallas import tpu as pltpu
from jax.sharding import PartitionSpec as P

HEADS = 32
KV_HEADS = 4
HEAD_DIM = 64
RANK = 16
LANES = 128
KEY_BLOCK = 1024
PAIRS = 4

EPS = 1e-05
LOWRANK_FACTOR = 2.0
MASKED = -1e30
F32 = jnp.float32
BF16 = jnp.bfloat16


def mm(left, right):
    return jnp.dot(left, right, preferred_element_type=F32)


def mm_nt(left, right):
    return lax.dot_general(left, right, (((1,), (1,)), ((), ())), preferred_element_type=F32)


def mm_tn(left, right):
    return lax.dot_general(left, right, (((0,), (0,)), ((), ())), preferred_element_type=F32)


def inverse_rms(value):
    return lax.rsqrt(jnp.mean(value * value, axis=-1, keepdims=True) + EPS)


def norm_backward(value, scale, gain, grad):
    scaled = gain * grad
    return scale * scaled - value * (scale * scale * scale) * jnp.mean(
        scaled * value, axis=-1, keepdims=True
    )


def half_turn(value):
    half = HEAD_DIM // 2
    lane = lax.broadcasted_iota(jnp.int32, value.shape, 1) % HEAD_DIM
    return jnp.where(
        lane < half, -jnp.roll(value, -half, axis=1), jnp.roll(value, half, axis=1)
    )


def rotate(value, cosines, sines):
    return value * cosines + half_turn(value) * sines


def unrotate(grad, cosines, sines):
    return grad * cosines - half_turn(grad * sines)


def lane_of(shape):
    return lax.broadcasted_iota(jnp.int32, shape, 1)


def key_rows(span, index):
    return pl.ds(pl.multiple_of((index ^ span[2]) * KEY_BLOCK, KEY_BLOCK), KEY_BLOCK)


def spread_heads(span, odd, source_ref, pair_ref):
    def step(index, carry):
        rows = key_rows(span, index)
        value = source_ref[rows, :].astype(F32)
        turned = pltpu.roll(value, HEAD_DIM, 1)
        low = lane_of(value.shape) < HEAD_DIM
        none = jnp.zeros_like(value)
        pair_ref[0, rows, :] = jnp.where(low, jnp.where(odd, turned, value), none).astype(BF16)
        pair_ref[1, rows, :] = jnp.where(low, none, jnp.where(odd, value, turned)).astype(BF16)
        return carry

    lax.fori_loop(span[0], span[1], step, 0)


def attention_forward_kernel(
    per_kv, span, q_ref, key_ref, value_ref, bias_ref, out_ref, lse_ref, k_ref, v_ref
):
    tokens = q_ref.shape[0]
    odd = lax.rem(pl.program_id(0) // per_kv, LANES // HEAD_DIM) == 1

    @pl.when(lax.rem(pl.program_id(0), per_kv) == 0)
    def _():
        spread_heads(span, odd, key_ref, k_ref)
        spread_heads(span, odd, value_ref, v_ref)

    queries = [q_ref[:, pair * LANES : (pair + 1) * LANES] for pair in range(PAIRS)]

    def step(index, carry):
        rows = key_rows(span, index)
        bias = bias_ref[rows, :]
        new = []
        for pair, (peaks, totals, mixed) in enumerate(carry):
            tops, sums, parts, decays = [], [], [], []
            for side in range(2):
                scores = mm_nt(k_ref[side, rows, :], queries[pair]) + bias
                top = jnp.maximum(peaks[side], jnp.max(scores, axis=0, keepdims=True))
                decay = jnp.exp(peaks[side] - top)
                probs = jnp.exp(scores - top)
                tops.append(top)
                sums.append(totals[side] * decay + jnp.sum(probs, axis=0, keepdims=True))
                decays.append(jnp.broadcast_to(decay, (HEAD_DIM, tokens)))
                parts.append(mm_tn(v_ref[side, rows, :], probs.astype(BF16)))
            mixed = mixed * jnp.concatenate(decays, axis=0) + (parts[0] + parts[1])
            new.append((tuple(tops), tuple(sums), mixed))
        return tuple(new)

    low = jnp.full((1, tokens), MASKED, F32)
    none = jnp.zeros((1, tokens), F32)
    start = ((low, low), (none, none), jnp.zeros((LANES, tokens), F32))
    result = lax.fori_loop(span[0], span[1], step, (start,) * PAIRS)
    for pair, (peaks, totals, mixed) in enumerate(result):
        weight = jnp.concatenate(
            [jnp.broadcast_to(1.0 / total, (HEAD_DIM, tokens)) for total in totals], axis=0
        )
        out_ref[:, pair * LANES : (pair + 1) * LANES] = (mixed * weight).T.astype(BF16)
        lse_ref[pair] = jnp.concatenate(
            [peak + jnp.log(total) for peak, total in zip(peaks, totals)], axis=0
        )


def key_value_specs(keys, per_kv):
    blocks = KV_HEADS * HEAD_DIM // LANES
    heads = LANES // HEAD_DIM
    return [
        pl.BlockSpec((keys, LANES), lambda j, s: (0, j // per_kv // heads)),
        pl.BlockSpec((keys, LANES), lambda j, s: (0, blocks + j // per_kv // heads)),
    ]


def attention_forward(span, query, key_value, bias):
    tokens, width = query.shape
    keys = bias.shape[0]
    pairs = width // LANES
    steps = pairs // PAIRS
    pair_spec = pl.BlockSpec((tokens, PAIRS * LANES), lambda j, s: (0, j))
    return pl.pallas_call(
        functools.partial(attention_forward_kernel, steps // KV_HEADS),
        out_shape=(
            jax.ShapeDtypeStruct((tokens, width), BF16),
            jax.ShapeDtypeStruct((pairs, 2, tokens), F32),
        ),
        grid_spec=pltpu.PrefetchScalarGridSpec(
            num_scalar_prefetch=1,
            grid=(steps,),
            in_specs=[
                pair_spec,
                *key_value_specs(keys, steps // KV_HEADS),
                pl.BlockSpec((keys, tokens), lambda j, s: (0, 0)),
            ],
            out_specs=(pair_spec, pl.BlockSpec((PAIRS, 2, tokens), lambda j, s: (j, 0, 0))),
            scratch_shapes=[pltpu.VMEM((2, keys, LANES), BF16)] * 2,
        ),
        compiler_params=pltpu.CompilerParams(
            dimension_semantics=("arbitrary",), vmem_limit_bytes=40 << 20
        ),
        cost_estimate=pl.CostEstimate(
            flops=4 * tokens * keys * width,
            transcendentals=tokens * keys * HEADS // 2,
            bytes_accessed=4 * tokens * width + 16 * keys * LANES * KV_HEADS,
        ),
        name="attention_forward",
    )(span, query, key_value, key_value, bias)


def attention_backward_kernel(
    per_kv,
    span,
    q_ref,
    do_ref,
    o_ref,
    lse_ref,
    key_ref,
    value_ref,
    bias_ref,
    cos_ref,
    sin_ref,
    dq_ref,
    dkv_ref,
    k_ref,
    v_ref,
    dk_sum,
    dv_sum,
):
    tokens = q_ref.shape[0]
    member = lax.rem(pl.program_id(0), per_kv)
    odd = lax.rem(pl.program_id(0) // per_kv, LANES // HEAD_DIM) == 1

    @pl.when(member == 0)
    def _():
        spread_heads(span, odd, key_ref, k_ref)
        spread_heads(span, odd, value_ref, v_ref)
        dk_sum[...] = jnp.zeros_like(dk_sum)
        dv_sum[...] = jnp.zeros_like(dv_sum)

    low = lane_of((tokens, LANES)) < HEAD_DIM
    row = lax.broadcasted_iota(jnp.int32, (8, LANES), 0)
    column = lax.broadcasted_iota(jnp.int32, (8, LANES), 1)
    chooser = jnp.where(row == column // HEAD_DIM, 1.0, 0.0).astype(F32)
    queries, grads, deltas, query_stack, grad_stack = [], [], [], [], []
    for pair in range(PAIRS):
        lanes = slice(pair * LANES, (pair + 1) * LANES)
        query, grad = q_ref[:, lanes], do_ref[:, lanes]
        none = jnp.zeros_like(query)
        queries.append(query)
        grads.append(grad)
        query_stack += [jnp.where(low, query, none), jnp.where(low, none, query)]
        grad_stack += [jnp.where(low, grad, none), jnp.where(low, none, grad)]
        deltas.append(
            lax.dot_general(
                chooser,
                grad.astype(F32) * o_ref[:, lanes].astype(F32),
                (((1,), (1,)), ((), ())),
                precision=lax.Precision.HIGHEST,
                preferred_element_type=F32,
            )
        )
    query_stack = jnp.concatenate(query_stack, axis=0)
    grad_stack = jnp.concatenate(grad_stack, axis=0)

    def step(index, dqueries):
        rows = key_rows(span, index)
        bias = bias_ref[rows, :]
        all_probs, all_dscores, new = [], [], []
        for pair, dquery in enumerate(dqueries):
            for side in range(2):
                scores = mm_nt(k_ref[side, rows, :], queries[pair]) + bias
                probs = jnp.exp(scores - lse_ref[pair, side : side + 1, :])
                dprobs = mm_nt(v_ref[side, rows, :], grads[pair])
                delta = deltas[pair][side : side + 1, :]
                dscores = (probs * (dprobs - delta)).astype(BF16)
                all_probs.append(probs.astype(BF16))
                all_dscores.append(dscores)
                dquery = dquery + mm_tn(k_ref[side, rows, :], dscores)
            new.append(dquery)
        dk_sum[rows, :] += mm(jnp.concatenate(all_dscores, axis=1), query_stack)
        dv_sum[rows, :] += mm(jnp.concatenate(all_probs, axis=1), grad_stack)
        return tuple(new)

    dqueries = lax.fori_loop(
        span[0], span[1], step, (jnp.zeros((LANES, tokens), F32),) * PAIRS
    )
    half = HEAD_DIM // 2
    for pair, dquery in enumerate(dqueries):
        dquery = dquery.T * (HEAD_DIM**-0.5)
        turned = dquery * sin_ref[...]
        first = lax.rem(lane_of(turned.shape), HEAD_DIM) < half
        turned = jnp.where(
            first, pltpu.roll(turned, LANES - half, 1), -pltpu.roll(turned, half, 1)
        )
        dq_ref[:, pair * LANES : (pair + 1) * LANES] = (dquery * cos_ref[...] + turned).astype(BF16)

    @pl.when(member == per_kv - 1)
    def _():
        block = pl.program_id(0) // per_kv // (LANES // HEAD_DIM)

        def put(index, carry):
            target = index ^ span[3]
            for sum_ref, first in ((dk_sum, 0), (dv_sum, KV_HEADS * HEAD_DIM // LANES)):
                total = sum_ref[pl.ds(pl.multiple_of(index * tokens, tokens), tokens), :]
                total = total + pltpu.roll(total, HEAD_DIM, 1)
                keep = jnp.logical_and(odd, lane_of(total.shape) < HEAD_DIM)
                lanes = pl.ds(pl.multiple_of((first + block) * LANES, LANES), LANES)
                dkv_ref[target, :, lanes] = jnp.where(
                    keep, dkv_ref[target, :, lanes], total.astype(BF16)
                )
            return carry

        lax.fori_loop(0, dkv_ref.shape[0], put, 0)


def attention_backward(span, query, grad, attended, lse, key_value, bias, cosines, sines):
    tokens, width = query.shape
    keys, kv_two = key_value.shape
    pairs = width // LANES
    steps = pairs // PAIRS
    per_kv = steps // KV_HEADS
    pair_spec = pl.BlockSpec((tokens, PAIRS * LANES), lambda j, s: (0, j))
    table_spec = pl.BlockSpec((tokens, LANES), lambda j, s: (0, 0))
    return pl.pallas_call(
        functools.partial(attention_backward_kernel, per_kv),
        out_shape=(
            jax.ShapeDtypeStruct((tokens, width), BF16),
            jax.ShapeDtypeStruct((keys // tokens, tokens, kv_two), BF16),
        ),
        grid_spec=pltpu.PrefetchScalarGridSpec(
            num_scalar_prefetch=1,
            grid=(steps,),
            in_specs=[
                pair_spec,
                pair_spec,
                pair_spec,
                pl.BlockSpec((PAIRS, 2, tokens), lambda j, s: (j, 0, 0)),
                *key_value_specs(keys, per_kv),
                pl.BlockSpec((keys, tokens), lambda j, s: (0, 0)),
                table_spec,
                table_spec,
            ],
            out_specs=(
                pair_spec,
                pl.BlockSpec((keys // tokens, tokens, kv_two), lambda j, s: (0, 0, 0)),
            ),
            scratch_shapes=[pltpu.VMEM((2, keys, LANES), BF16)] * 2
            + [pltpu.VMEM((keys, LANES), F32)] * 2,
        ),
        compiler_params=pltpu.CompilerParams(
            dimension_semantics=("arbitrary",), vmem_limit_bytes=48 << 20
        ),
        cost_estimate=pl.CostEstimate(
            flops=10 * tokens * keys * width,
            transcendentals=tokens * keys * HEADS // 2,
            bytes_accessed=10 * tokens * width + 8 * keys * kv_two,
        ),
        name="attention_backward",
    )(span, query, grad, attended, lse, key_value, key_value, bias, cosines, sines)


CORE, ACROSS_X, ACROSS_Y = 1, 2, 4


def flip(array, mask):
    members = lax.axis_size("grp")
    return lax.ppermute(array, "grp", [(i, i ^ mask) for i in range(members)])


def flip_group(array):
    groups = lax.axis_size("rep")
    return lax.ppermute(array, "rep", [(i, i ^ 1) for i in range(groups)])


def gather_hidden_block(gate_up_weight, down_weight):
    rows = gate_up_weight.shape[0] // 4
    block = gate_up_weight.shape[1]
    member = lax.axis_index("grp")
    parity = lax.axis_index("rep") % 2
    own = [
        lax.dynamic_slice_in_dim(gate_up_weight, ((parity ^ (q // 2)) * 2 + q % 2) * rows, rows, 0)
        for q in range(4)
    ]

    def down_rows(mask):
        start = ((member ^ mask) % ACROSS_Y) * block
        return lax.dynamic_slice_in_dim(down_weight, start, block, 0)

    low, next_quarter, *near = yield (
        flip(own[0], ACROSS_Y),
        own[1],
        flip(down_rows(ACROSS_X), ACROSS_X),
        flip(down_rows(CORE), CORE),
        flip(down_rows(ACROSS_X | CORE), ACROSS_X | CORE),
    )
    down_own = jnp.stack([down_rows(0), near[1], near[0], near[2]])
    high, low_other, down_own = yield flip(next_quarter, ACROSS_Y), flip_group(low), down_own
    mine, second = (
        lax.dynamic_slice_in_dim(down_own, 2 * parity + index, 1, 0) for index in range(2)
    )
    down_mine, high_other, second = yield flip(mine, ACROSS_Y), flip_group(high), second
    down_second, down_other = yield flip(second, ACROSS_Y), flip_group(down_mine)
    (second_other,) = yield (flip_group(down_second),)
    return {
        "own": own,
        "over_y": (low, high, low_other, high_other),
        "down": (down_own, down_mine, down_second, down_other, second_other),
    }


def gather_key_values(own):
    over_y = flip(own, ACROSS_Y)
    pieces = [own, flip(own, ACROSS_X), over_y, flip(over_y, ACROSS_X)]
    return jnp.concatenate(
        [part for piece in pieces for part in (piece, flip(piece, CORE))], axis=0
    )


def tie(value, transfers):
    value, *transfers = lax.optimization_barrier((value, *transfers))
    return value, tuple(transfers)


def feed_forward_alone(norm2, sens, gate_up_full, down_full, small, seen):
    ffn_in, switch, lift, down_in, lower = small
    slots, hidden_width = switch.shape
    seen_two = jnp.concatenate([seen, seen], axis=1)
    latent_gu = (mm(norm2, ffn_in) * seen_two).astype(BF16)
    latent_g, latent_u = latent_gu[:, :slots], latent_gu[:, slots:]
    gate_up = mm(norm2, gate_up_full) + LOWRANK_FACTOR * jnp.concatenate(
        [mm(latent_g, switch), mm(latent_u, lift)], axis=1
    )
    gate = gate_up[:, :hidden_width]
    up = gate_up[:, hidden_width:]
    sigma = jax.nn.sigmoid(gate)
    act = (gate * sigma * up).astype(BF16)
    latent_d = (mm_nt(act, down_in) * seen).astype(BF16)
    response_part = mm(act, down_full) + LOWRANK_FACTOR * mm(latent_d, lower)
    dlat_d = (LOWRANK_FACTOR * mm_nt(sens, lower) * seen).astype(BF16)
    dact = mm_nt(sens, down_full) + mm(dlat_d, down_in)
    dgate = (dact * up * (sigma * (1.0 + gate * (1.0 - sigma)))).astype(BF16)
    dup = (dact * gate * sigma).astype(BF16)
    dlat_gu = (
        LOWRANK_FACTOR
        * jnp.concatenate([mm_nt(dgate, switch), mm_nt(dup, lift)], axis=1)
        * seen_two
    ).astype(BF16)
    dnorm2 = (
        mm_nt(dgate, gate_up_full[:, :hidden_width])
        + mm_nt(dup, gate_up_full[:, hidden_width:])
        + mm_nt(dlat_gu, ffn_in)
    )
    deep = jnp.concatenate(
        [
            mm_tn(dlat_d, act),
            LOWRANK_FACTOR * mm_tn(latent_g, dgate),
            LOWRANK_FACTOR * mm_tn(latent_u, dup),
        ],
        axis=0,
    ).astype(BF16)
    members = lax.axis_size("grp")
    deep = deep.reshape(3 * slots, members, hidden_width // members).transpose(1, 0, 2)
    return response_part, dnorm2, latent_d, dlat_gu, deep


def feed_forward_kernel(
    meta,
    own_x,
    near_x,
    own_g,
    near_g,
    own_seen,
    near_seen,
    lower_ref,
    switch_ref,
    lift_ref,
    in_ref,
    *refs,
):
    whole_refs, whole_down = refs[:8], refs[8:13]
    back_own, back_near, front_own, front_near, deep_ref = refs[13:18]
    x_turned, g_turned, latents, dlats, stack, acts, firsts, seconds, dacts, dlat_sum = refs[18:28]
    kept, kept_down, semaphores = refs[28:]
    count, width = own_g.shape
    tokens = 2 * count
    slots, block = in_ref.shape
    quarter = width // 4
    part = width // kept_down.shape[0]
    parity = meta[0]
    owns_gate = meta[1] == 1
    member = meta[2]
    starts = [
        pl.multiple_of((parity if q < 2 else 1 - parity) * (width // 2) + (q % 2) * quarter, quarter)
        for q in range(4)
    ]
    bases = [0, 1, 2, 3, *(4 + 2 * parity + k for k in (0, 1)), *(6 - 2 * parity + k for k in (0, 1))]
    columns = [pl.ds(pl.multiple_of((member ^ base) * part, part), part) for base in bases]
    down_copies = [
        pltpu.make_async_copy(ref, kept_down.at[pl.ds(start, size)], semaphores.at[8 + index])
        for index, (ref, start, size) in enumerate(zip(whole_down, (0, 4, 5, 6, 7), (4, 1, 1, 1, 1)))
    ]
    copies = [
        pltpu.make_async_copy(ref, kept.at[index], semaphores.at[index])
        for index, ref in enumerate(whole_refs)
    ]
    for copy in down_copies + copies:
        copy.start()
    dlat_sum[...] = jnp.zeros_like(dlat_sum)
    for index, (x_ref, g_ref, seen_ref) in enumerate(
        ((own_x, own_g, own_seen), (near_x, near_g, near_seen))
    ):
        rows = slice(index * count, (index + 1) * count)
        for q in range(4):
            x_turned[rows, q * quarter : (q + 1) * quarter] = x_ref[:, pl.ds(starts[q], quarter)]
        for k, lanes in enumerate(columns):
            g_turned[rows, k * part : (k + 1) * part] = g_ref[:, lanes]
        latents[rows, :] = x_ref[:, width : width + 2 * slots]
        dlat = LOWRANK_FACTOR * mm_nt(g_ref[...], lower_ref[...]) * seen_ref[...]
        dlats[rows, :] = dlat.astype(BF16)
        stack[:slots, rows] = dlat.T.astype(BF16)
        latent = x_ref[:, width : width + LANES].astype(F32).T[: 2 * slots]
        stack[slots:, rows] = latent.astype(BF16)

    def dact_part(start, size):
        here = pl.ds(start, size)
        down = jnp.concatenate([kept_down[k, here, :] for k in range(len(columns))], axis=1)
        dacts[:, here] = mm_nt(g_turned[...], down) + mm(dlats[...], in_ref[:, here])

    def dact_step(index, carry):
        dact_part(pl.multiple_of(index * 2 * LANES, 2 * LANES), 2 * LANES)
        return carry

    for copy in down_copies:
        copy.wait()
    lax.fori_loop(0, block // (2 * LANES), dact_step, 0)
    if block % (2 * LANES):
        dact_part(block // (2 * LANES) * 2 * LANES, block % (2 * LANES))
    for copy in copies:
        copy.wait()

    def hidden_part(start, size):
        here = pl.ds(start, size)
        none = jnp.zeros((slots, size), BF16)
        switch, lift = switch_ref[:, here], lift_ref[:, here]
        pieces = jnp.where(
            owns_gate,
            jnp.concatenate(
                [jnp.concatenate([switch, none], axis=1), jnp.concatenate([none, lift], axis=1)],
                axis=0,
            ),
            jnp.concatenate(
                [jnp.concatenate([none, switch], axis=1), jnp.concatenate([lift, none], axis=1)],
                axis=0,
            ),
        )
        weight = jnp.concatenate(
            [
                jnp.concatenate([kept[q, :, here], kept[4 + q, :, here]], axis=1)
                for q in range(4)
            ],
            axis=0,
        )
        total = mm(x_turned[...], weight)
        total = total + LOWRANK_FACTOR * mm(latents[...], pieces)
        gate = jnp.where(owns_gate, total[:, :size], total[:, size:])
        up = jnp.where(owns_gate, total[:, size:], total[:, :size])
        sigma = jax.nn.sigmoid(gate)
        act = (gate * sigma * up).astype(BF16)
        dact = dacts[:, here]
        dgate = (dact * up * (sigma * (1.0 + gate * (1.0 - sigma)))).astype(BF16)
        dup = (dact * gate * sigma).astype(BF16)
        dfirst, dsecond = jnp.where(owns_gate, dgate, dup), jnp.where(owns_gate, dup, dgate)
        acts[:, here] = act
        firsts[:, here] = dfirst
        seconds[:, here] = dsecond
        both = jnp.concatenate([dfirst, dsecond], axis=1)
        dlat_sum[:, : 2 * slots] += mm_nt(both, pieces)
        piece_grad = LOWRANK_FACTOR * mm(stack[slots:, :], both)
        low, high = piece_grad[:, :size], piece_grad[:, size:]
        deep_ref[:slots, here] = mm(stack[:slots, :], act)
        deep_ref[slots : 2 * slots, here] = jnp.where(owns_gate, low, high)[:slots]
        deep_ref[2 * slots :, here] = jnp.where(owns_gate, high, low)[slots:]

    def hidden_step(index, carry):
        hidden_part(pl.multiple_of(index * 2 * LANES, 2 * LANES), 2 * LANES)
        return carry

    lax.fori_loop(0, block // (2 * LANES), hidden_step, 0)
    if block % (2 * LANES):
        hidden_part(block // (2 * LANES) * 2 * LANES, block % (2 * LANES))

    def back(q, carry):
        value = mm_nt(firsts[...], kept[q]) + mm_nt(seconds[...], kept[4 + q])
        start = ((q // 2) ^ parity) * (width // 2) + lax.rem(q, 2) * quarter
        lanes = pl.ds(pl.multiple_of(start, quarter), quarter)
        back_own[:, lanes] = value[:count]
        back_near[:, lanes] = value[count:].astype(BF16)
        return carry

    def front(index, carry):
        value = mm(acts[...], kept_down[index])
        half = (index - 4) // 2 ^ parity
        base = jnp.where(index < 4, index, 4 + 2 * half + lax.rem(index, 2))
        lanes = pl.ds(pl.multiple_of((member ^ base) * part, part), part)
        front_own[:, lanes] = value[:count].astype(front_own.dtype)
        front_near[:, lanes] = value[count:].astype(BF16)
        return carry

    lax.fori_loop(0, 4, back, 0)
    lax.fori_loop(0, kept_down.shape[0], front, 0)
    back_own[:, width:] = dlat_sum[:count, :]
    back_near[:, width:] = dlat_sum[count:, :].astype(BF16)
    latent = mm_nt(acts[...], in_ref[...])
    latent = jnp.concatenate([latent, jnp.zeros((tokens, LANES - slots), F32)], axis=1)
    front_own[:, width:] = latent[:count, :].astype(front_own.dtype)
    front_near[:, width:] = latent[count:, :].astype(BF16)


def feed_forward_pair(meta, rows, sens, seen, weights, pieces, front_type):
    count, width = sens[0].shape
    slots, block = pieces[-1].shape
    wide, tokens = width + LANES, 2 * count
    operands = (*rows, *sens, *seen, *pieces)
    arrays = (*weights["own"], *weights["over_y"], *weights["down"])
    return pl.pallas_call(
        feed_forward_kernel,
        out_shape=(
            jax.ShapeDtypeStruct((count, wide), F32),
            jax.ShapeDtypeStruct((count, wide), BF16),
            jax.ShapeDtypeStruct((count, wide), front_type),
            jax.ShapeDtypeStruct((count, wide), BF16),
            jax.ShapeDtypeStruct((3 * slots, block), F32),
        ),
        in_specs=[pl.BlockSpec(memory_space=pltpu.SMEM)]
        + [pl.BlockSpec(memory_space=pltpu.VMEM)] * len(operands)
        + [pl.BlockSpec(memory_space=pl.ANY)] * len(arrays),
        scratch_shapes=[
            pltpu.VMEM((tokens, width), BF16),
            pltpu.VMEM((tokens, width), BF16),
            pltpu.VMEM((tokens, 2 * slots), BF16),
            pltpu.VMEM((tokens, slots), BF16),
            pltpu.VMEM((3 * slots, tokens), BF16),
            pltpu.VMEM((tokens, block), BF16),
            pltpu.VMEM((tokens, block), BF16),
            pltpu.VMEM((tokens, block), BF16),
            pltpu.VMEM((tokens, block), F32),
            pltpu.VMEM((tokens, LANES), F32),
            pltpu.VMEM((8, width // 4, block), BF16),
            pltpu.VMEM((8, block, width // 8), BF16),
            pltpu.SemaphoreType.DMA((13,)),
        ],
        compiler_params=pltpu.CompilerParams(vmem_limit_bytes=46 << 20),
        cost_estimate=pl.CostEstimate(
            flops=2 * 6 * tokens * width * block,
            transcendentals=tokens * block,
            bytes_accessed=6 * width * block + 20 * tokens * width,
        ),
        name="feed_forward",
    )(meta, *operands, *arrays)


def feed_forward_shared(norm2, sens_pairs, weights, small, seen_by):
    ffn_in, switch, lift, down_in, lower = small
    width = norm2.shape[1]
    slots, hidden_width = switch.shape
    block = weights["own"][0].shape[1]
    member = lax.axis_index("grp")
    parity = lax.axis_index("rep") % 2
    owns_gate = member < ACROSS_Y
    hidden = member % ACROSS_Y

    meta = jnp.stack([parity, owns_gate.astype(jnp.int32), member]).astype(jnp.int32)
    pieces = (
        lower,
        *(
            lax.dynamic_slice_in_dim(piece, hidden * block, block, 1)
            for piece in (switch, lift, down_in)
        ),
    )
    seen = seen_by(member)
    seen_two = jnp.concatenate([seen, seen], axis=1)
    latent_gu = (mm(norm2, ffn_in) * seen_two).astype(BF16)
    pad = jnp.zeros((norm2.shape[0], LANES - 2 * slots), BF16)
    rows = jnp.concatenate([norm2, latent_gu, pad], axis=1)
    across = flip(rows, ACROSS_X)
    results = []
    for index, sens_pair in enumerate(sens_pairs):
        first = member ^ (index * ACROSS_X)
        if index == 1:
            result, (across,) = tie(results[0][1], (across,))
            results[0][1] = result
            rows = across
        seen_pair = (seen_by(first), seen_by(first ^ CORE))
        row_pair = (rows, flip(rows, CORE))
        results.append(
            list(
                feed_forward_pair(
                    meta, row_pair, sens_pair, seen_pair, weights, pieces, (F32, BF16)[index]
                )
            )
        )

    chips = [result[0] + flip(result[1], CORE).astype(F32) for result in results]
    deep = (results[0][4] + results[1][4]).astype(BF16)
    members = lax.axis_size("grp")
    owners = members * block // hidden_width
    deep = deep.reshape(3 * slots, owners, block // owners).transpose(1, 0, 2)
    placed = jnp.zeros((members, 3 * slots, block // owners), BF16)
    placed = lax.dynamic_update_slice_in_dim(placed, deep, hidden * owners, 0)
    across, (placed,) = tie(flip(chips[1].astype(BF16), ACROSS_X), (placed,))
    backward = chips[0] + across.astype(F32)
    dlat_gu = (LOWRANK_FACTOR * backward[:, width : width + 2 * slots] * seen_two).astype(BF16)
    dnorm2 = backward[:, :width] + mm_nt(dlat_gu, ffn_in)
    forwards = [part for result in results for part in result[2:4]]
    dnorm2, forwards = tie(dnorm2, forwards)
    forward = forwards[0]
    for part, mask in zip(forwards[1:], (CORE, ACROSS_X, ACROSS_X | CORE)):
        forward = forward + flip(part, mask).astype(F32)
    latent_d = (forward[:, width : width + slots] * seen).astype(BF16)
    response_part = forward[:, :width] + LOWRANK_FACTOR * mm(latent_d, lower)
    return response_part, dnorm2, latent_d, dlat_gu, placed


def exchange_sum(parts):
    received = lax.all_to_all(parts.astype(BF16), "grp", 0, 0, tiled=True)
    return jnp.sum(received.astype(F32), axis=0)


def simple_call(kernel, name, out_shape, operands, flops):
    return pl.pallas_call(
        kernel,
        out_shape=out_shape,
        compiler_params=pltpu.CompilerParams(vmem_limit_bytes=32 << 20),
        cost_estimate=pl.CostEstimate(
            flops=flops,
            transcendentals=0,
            bytes_accessed=sum(array.size * array.dtype.itemsize for array in operands),
        ),
        name=name,
    )(*operands)


def early_gradients_kernel(
    dq_ref,
    asking_ref,
    seen_ref,
    latent_q_ref,
    norm1_ref,
    latent_d_ref,
    sens_ref,
    dlat_gu_ref,
    norm2_ref,
    dlat_o_ref,
    attended_ref,
    latent_o_ref,
    dbranch_ref,
    dlat_q_ref,
    early_ref,
):
    dlat_q = (LOWRANK_FACTOR * mm_nt(dq_ref[...], asking_ref[...]) * seen_ref[...]).astype(BF16)
    dlat_q_ref[...] = dlat_q
    two = LOWRANK_FACTOR
    start = 0
    for factor, small, large in (
        (1.0, dlat_q, norm1_ref),
        (two, latent_q_ref[...], dq_ref),
        (two, latent_d_ref[...], sens_ref),
        (1.0, dlat_gu_ref[...], norm2_ref),
        (1.0, dlat_o_ref[...], attended_ref),
        (two, latent_o_ref[...], dbranch_ref),
    ):
        rows = small.shape[1]
        early_ref[start : start + rows, :] = (factor * mm_tn(small, large[...])).astype(BF16)
        start += rows


def early_gradients(*operands):
    count, width = operands[0].shape
    slots = operands[1].shape[0]
    return simple_call(
        early_gradients_kernel,
        "early_gradients",
        (
            jax.ShapeDtypeStruct((count, slots), BF16),
            jax.ShapeDtypeStruct((7 * slots, width), BF16),
        ),
        operands,
        2 * count * width * 8 * slots,
    )


def key_value_gradients_kernel(
    received_ref,
    early_ref,
    cos_ref,
    sin_ref,
    right_ref,
    seen_ref,
    latent_ref,
    norm_ref,
    dkv_ref,
    dlat_ref,
    pack_ref,
):
    half = HEAD_DIM // 2
    total = received_ref[0].astype(F32)
    for source in range(1, received_ref.shape[0]):
        total = total + received_ref[source].astype(F32)
    kv_width = total.shape[1] // 2
    pieces = []
    for start in range(0, kv_width, LANES):
        value = total[:, start : start + LANES]
        turned = value * sin_ref[...]
        first = lax.rem(lane_of(turned.shape), HEAD_DIM) < half
        turned = jnp.where(
            first, pltpu.roll(turned, LANES - half, 1), -pltpu.roll(turned, half, 1)
        )
        pieces.append((value * cos_ref[...] + turned).astype(BF16))
    dkv = jnp.concatenate([*pieces, total[:, kv_width:].astype(BF16)], axis=1)
    dkv_ref[...] = dkv
    dlat = (LOWRANK_FACTOR * mm_nt(dkv, right_ref[...]) * seen_ref[...]).astype(BF16)
    dlat_ref[...] = dlat
    late = mm_tn(dlat, norm_ref[...]).astype(BF16)
    thin = (LOWRANK_FACTOR * mm_tn(latent_ref[...], dkv)).astype(BF16)
    rows, head = late.shape[0], early_ref.shape[0]
    thin = jnp.concatenate([thin[: rows // 2, :kv_width], thin[rows // 2 :, kv_width:]], axis=0)
    share = pack_ref.shape[2]
    for target in range(pack_ref.shape[0]):
        columns = slice(target * share, (target + 1) * share)
        pack_ref[target, :head, :] = early_ref[:, columns]
        pack_ref[target, head : head + rows, :] = late[:, columns]
        for index, start in enumerate(range(0, kv_width, share)):
            place = head + (index + 1) * rows
            pack_ref[target, place : place + rows, :] = thin[:, start : start + share]


def key_value_gradients(received, early, cosines, sines, kv_right, seen_two, latent_kv, norm1):
    members, count, kv_two = received.shape
    rows = kv_right.shape[0]
    share = norm1.shape[1] // members
    packed = early.shape[0] + rows * (1 + kv_two // 2 // share)
    return simple_call(
        key_value_gradients_kernel,
        "key_value_gradients",
        (
            jax.ShapeDtypeStruct((count, kv_two), BF16),
            jax.ShapeDtypeStruct((count, rows), BF16),
            jax.ShapeDtypeStruct((members, packed, share), BF16),
        ),
        (received, early, cosines, sines, kv_right, seen_two, latent_kv, norm1),
        2 * count * rows * (norm1.shape[1] + 2 * kv_two),
    )


def place_kernel(jobs, groups, slots, *refs):
    place_ref, refs = refs[0], refs[1:]
    outs = refs[len(refs) - len(jobs) :]
    for (source, index, is_right), out_ref in zip(jobs, outs):
        value = jnp.concatenate(
            [
                refs[source * groups + g][index * slots : (index + 1) * slots, :]
                for g in range(groups)
            ],
            axis=0,
        )
        if is_right:
            out_ref[...] = mm_tn(place_ref[...], value)
        else:
            out_ref[...] = mm_tn(value, place_ref[...])


def place_gradients(place, sources, slots, jobs):
    groups = len(sources[0])
    narrow = place.shape[1]
    shapes = []
    for source, _, is_right in jobs:
        size = sources[source][0].shape[1]
        shapes.append(
            jax.ShapeDtypeStruct((narrow, size) if is_right else (size, narrow), F32)
        )
    return pl.pallas_call(
        functools.partial(place_kernel, jobs, groups, slots),
        out_shape=tuple(shapes),
        compiler_params=pltpu.CompilerParams(vmem_limit_bytes=32 << 20),
        cost_estimate=pl.CostEstimate(
            flops=2 * sum(shape.size for shape in shapes) * place.shape[0],
            transcendentals=0,
            bytes_accessed=4 * sum(shape.size for shape in shapes),
        ),
        name="place_gradients",
    )(place, *[array for source in sources for array in source])


def round_groups(array):
    groups = lax.axis_size("rep")
    return [array] + [
        lax.ppermute(array, "rep", [(i, (i + shift) % groups) for i in range(groups)])
        for shift in range(1, groups)
    ]


def shards(
    tokens,
    response_sensitivity,
    seq_lengths,
    prefix_lengths,
    adapter_ids,
    attn_gain,
    mlp_gain,
    qkv_weight,
    out_weight,
    gate_up_weight,
    down_weight,
    query_in,
    asking_right_pieces,
    key_in,
    lookup_right_pieces,
    value_in,
    content_right_pieces,
    output_in,
    final_right_pieces,
    gate_in,
    switch_right_pieces,
    up_in,
    lift_right_pieces,
    down_in,
    lower_right_pieces,
):
    count, width = tokens.shape
    members = lax.axis_size("grp")
    groups = lax.axis_size("rep")
    kv_width = lookup_right_pieces.shape[1]
    narrow = query_in.shape[1]
    group = lax.axis_index("rep")
    member = lax.axis_index("grp")
    lengths = lax.dynamic_slice_in_dim(seq_lengths, 2 * group, 2)
    prefixes = lax.dynamic_slice_in_dim(prefix_lengths, 2 * group, 2)
    chosen_ids = lax.dynamic_slice_in_dim(adapter_ids, 2 * group, 2)
    key_count = count * members
    sens = response_sensitivity

    paired = members == 8 and groups % 2 == 0
    qkv_full = lax.all_gather(qkv_weight, "grp", axis=1, tiled=True)
    if paired:
        steps = gather_hidden_block(gate_up_weight, down_weight)
        transfers = next(steps)
    else:
        out_full = lax.all_gather(out_weight, "grp", axis=1, tiled=True)
        down_full = lax.all_gather(down_weight, "grp", axis=1, tiled=True)
        gate_up_full = lax.all_gather(gate_up_weight, "grp", axis=1, tiled=True)

    turn = member if paired else 0
    key_index = jnp.arange(key_count, dtype=jnp.int32)
    key_index = (key_index // count ^ turn) * count + key_index % count
    key_second = (key_index >= lengths[0]).astype(jnp.int32)
    key_position = key_index - key_second * lengths[0]
    own_index = member * count + jnp.arange(count, dtype=jnp.int32)
    own_second = (own_index >= lengths[0]).astype(jnp.int32)
    position = own_index - own_second * lengths[0]
    prefix = jnp.where(own_second == 0, prefixes[0], prefixes[1])
    allowed = (key_second[:, None] == own_second[None, :]) & (
        (key_position[:, None] <= position[None, :]) | (key_position[:, None] < prefix[None, :])
    )
    bias = jnp.where(allowed, 0.0, MASKED).astype(F32)
    first_key = own_second[0] * lengths[0]
    last_key = jnp.max(own_second * lengths[0] + jnp.maximum(position, prefix - 1))
    span = jnp.stack(
        [first_key // KEY_BLOCK, last_key // KEY_BLOCK + 1, turn * count // KEY_BLOCK, turn]
    ).astype(jnp.int32)

    slots = 2 * RANK
    columns = jnp.arange(narrow, dtype=jnp.int32)
    slot = jnp.arange(slots, dtype=jnp.int32)
    slot_column = chosen_ids[slot // RANK] * RANK + slot % RANK
    pick = (columns[:, None] == slot_column[None, :]).astype(BF16)

    def seen_by(device):
        index = device * count + jnp.arange(count, dtype=jnp.int32)
        second = (index >= lengths[0]).astype(jnp.int32)
        return (second[:, None] == slot[None, :] // RANK).astype(F32)

    def pick_in(weight):
        return mm(weight, pick).astype(BF16)

    def pick_right(weight):
        return mm_tn(pick, weight).astype(BF16)

    seen = seen_by(member)
    seen_three = jnp.concatenate([seen, seen, seen], axis=1)
    qkv_in = jnp.concatenate([pick_in(query_in), pick_in(key_in), pick_in(value_in)], axis=1)
    asking = pick_right(asking_right_pieces)
    lookup = pick_right(lookup_right_pieces)
    content = pick_right(content_right_pieces)
    none = jnp.zeros_like(lookup)
    kv_right = jnp.concatenate(
        [jnp.concatenate([lookup, none], axis=1), jnp.concatenate([none, content], axis=1)], axis=0
    )
    out_in = pick_in(output_in)
    final = pick_right(final_right_pieces)
    lower = pick_right(lower_right_pieces)
    small = (
        jnp.concatenate([pick_in(gate_in), pick_in(up_in)], axis=1),
        pick_right(switch_right_pieces),
        pick_right(lift_right_pieces),
        lax.dot_general(
            pick, down_in, (((0,), (1,)), ((), ())), preferred_element_type=F32
        ).astype(BF16),
        lower,
    )

    incoming = tokens.astype(F32)
    scale_one = inverse_rms(incoming)
    norm1 = (incoming * scale_one * attn_gain).astype(BF16)
    if paired:
        norm1, transfers = tie(norm1, transfers)
        transfers = steps.send(transfers)
        out_full = lax.all_gather(out_weight, "grp", axis=1, tiled=True)
    latent_qkv = (mm(norm1, qkv_in) * seen_three).astype(BF16)
    latent_q, latent_kv = latent_qkv[:, :slots], latent_qkv[:, slots:]
    half = HEAD_DIM // 2
    freqs = 10000.0 ** (-2.0 * jnp.arange(half).astype(F32) / HEAD_DIM)
    freqs = jnp.tile(freqs, LANES // half)
    angles = position.astype(F32)[:, None] * freqs[None, :]
    cosines, sines = jnp.cos(angles), jnp.sin(angles)

    def widen(table, size):
        return jnp.tile(table, (1, size // LANES))

    qkv = mm(norm1, qkv_full)
    query = qkv[:, :width] + LOWRANK_FACTOR * mm(latent_q, asking)
    own_kv = qkv[:, width:] + LOWRANK_FACTOR * mm(latent_kv, kv_right)
    query = rotate(query, widen(cosines, width), widen(sines, width)).astype(BF16)
    query = query * jnp.asarray(HEAD_DIM**-0.5, BF16)
    key_own = rotate(own_kv[:, :kv_width], widen(cosines, kv_width), widen(sines, kv_width))
    key_value = jnp.concatenate([key_own, own_kv[:, kv_width:]], axis=1).astype(BF16)
    if paired:
        key_value, transfers = tie(key_value, transfers)
        key_value, (ready, *transfers) = tie(gather_key_values(key_value), (sens, *transfers))
        transfers = steps.send(transfers)
        sens_near, sens_across = flip(ready, CORE), flip(ready, ACROSS_X)
    else:
        key_value = lax.all_gather(key_value, "grp", axis=0, tiled=True)
    attended_low, lse = attention_forward(span, query, key_value, bias)
    if paired:
        attended_low, (sens_near, sens_across, *transfers) = tie(
            attended_low, (sens_near, sens_across, *transfers)
        )
        sens_pairs = [(sens, sens_near), (sens_across, flip(sens_across, CORE))]
        out_full, transfers = tie(out_full, steps.send(transfers))
        transfers = steps.send(transfers)

    latent_o = (mm(attended_low, out_in) * seen).astype(BF16)
    stream = incoming + (mm(attended_low, out_full) + LOWRANK_FACTOR * mm(latent_o, final))
    scale_two = inverse_rms(stream)
    norm2 = (stream * scale_two * mlp_gain).astype(BF16)
    if paired:
        norm2, transfers = tie(norm2, transfers)
        try:
            steps.send(transfers)
        except StopIteration as stop:
            weights = stop.value
        response_part, dnorm2, latent_d, dlat_gu, deep = feed_forward_shared(
            norm2, sens_pairs, weights, small, seen_by
        )
    else:
        response_part, dnorm2, latent_d, dlat_gu, deep = feed_forward_alone(
            norm2, sens, gate_up_full, down_full, small, seen
        )
    level_response = (stream + response_part).astype(BF16)
    dhidden = sens.astype(F32) + norm_backward(stream, scale_two, mlp_gain, dnorm2)
    dbranch = dhidden.astype(BF16)
    dlat_o = (LOWRANK_FACTOR * mm_nt(dbranch, final) * seen).astype(BF16)
    dattended = (mm_nt(dbranch, out_full) + mm_nt(dlat_o, out_in)).astype(BF16)

    dattended, (deep,) = tie(dattended, (deep,))
    deep_sum = lax.psum_scatter(deep, "grp", scatter_dimension=0, tiled=True)[0]

    dq, dkv_all = attention_backward(
        span, query, dattended, attended_low, lse, key_value, bias, cosines, sines
    )
    dkv_all, (deep_sum,) = tie(dkv_all, (deep_sum,))
    received = lax.all_to_all(dkv_all, "grp", 0, 0, tiled=True)
    dlat_q, early = early_gradients(
        dq,
        asking,
        seen,
        latent_q,
        norm1,
        latent_d,
        sens,
        dlat_gu,
        norm2,
        dlat_o,
        attended_low,
        latent_o,
        dbranch,
    )
    dnorm_q = mm_nt(dq, qkv_full[:, :width]) + mm_nt(dlat_q, qkv_in[:, :slots])
    dkv, dlat_kv, late = key_value_gradients(
        received, early, cosines, sines, kv_right, seen_three[:, : 2 * slots], latent_kv, norm1
    )
    deep_sum = round_groups(deep_sum)
    late_sum = round_groups(exchange_sum(late).astype(BF16))
    dnorm1 = dnorm_q + mm_nt(dkv, qkv_full[:, width:]) + mm_nt(dlat_kv, qkv_in[:, slots:])
    input_grad = (dhidden + norm_backward(incoming, scale_one, attn_gain, dnorm1)).astype(BF16)

    cycle = jnp.arange(groups * slots, dtype=jnp.int32)
    source = (group - cycle // slots) % groups
    all_column = adapter_ids[2 * source + cycle % slots // RANK] * RANK + cycle % RANK
    place = (all_column[:, None] == columns[None, :]).astype(BF16)
    share = width // members
    pieces = kv_width // share
    thin_start = 9 * slots
    thin_sum = [
        jnp.concatenate(
            [
                array[thin_start + 2 * slots * i : thin_start + 2 * slots * (i + 1)]
                for i in range(pieces)
            ],
            axis=1,
        )
        for array in late_sum
    ]
    jobs = (
        (0, 0, False),
        (0, 1, True),
        (0, 7, False),
        (2, 0, True),
        (0, 8, False),
        (2, 1, True),
        (0, 5, False),
        (0, 6, True),
        (0, 3, False),
        (1, 1, True),
        (0, 4, False),
        (1, 2, True),
        (1, 0, False),
        (0, 2, True),
    )
    grads = list(place_gradients(place, (late_sum, deep_sum, thin_sum), slots, jobs))
    own = kv_width // members
    for index in (3, 5):
        grads[index] = lax.dynamic_slice_in_dim(grads[index], member * own, own, 1)
    return (level_response, input_grad, *grads)


def solution(mesh):
    rows = P(("rep", "grp"), None)
    split = P(None, "grp")
    in_specs = (rows, rows, *[P()] * 5, *[split] * 4, *[P()] * 14)
    out_specs = (rows, rows, *[P("grp", None), P(None, "grp")] * 7)
    return jax.shard_map(shards, mesh=mesh, in_specs=in_specs, out_specs=out_specs, check_vma=False)
```

```python
import functools

import jax
import jax.numpy as jnp
from jax import lax
from jax.experimental import pallas as pl
from jax.experimental.pallas import tpu as pltpu
from jax.sharding import PartitionSpec as P

HEADS = 32
KV_HEADS = 4
HEAD_DIM = 64
RANK = 16
LANES = 128
KEY_BLOCK = 1024
PAIRS = 4

EPS = 1e-05
LOWRANK_FACTOR = 2.0
MASKED = -1e30
F32 = jnp.float32
BF16 = jnp.bfloat16


def mm(left, right):
    return jnp.dot(left, right, preferred_element_type=F32)


def mm_nt(left, right):
    return lax.dot_general(left, right, (((1,), (1,)), ((), ())), preferred_element_type=F32)


def mm_tn(left, right):
    return lax.dot_general(left, right, (((0,), (0,)), ((), ())), preferred_element_type=F32)


def inverse_rms(value):
    return lax.rsqrt(jnp.mean(value * value, axis=-1, keepdims=True) + EPS)


def norm_backward(value, scale, gain, grad):
    scaled = gain * grad
    return scale * scaled - value * (scale * scale * scale) * jnp.mean(
        scaled * value, axis=-1, keepdims=True
    )


def half_turn(value):
    half = HEAD_DIM // 2
    lane = lax.broadcasted_iota(jnp.int32, value.shape, 1) % HEAD_DIM
    return jnp.where(
        lane < half, -jnp.roll(value, -half, axis=1), jnp.roll(value, half, axis=1)
    )


def rotate(value, cosines, sines):
    return value * cosines + half_turn(value) * sines


def unrotate(grad, cosines, sines):
    return grad * cosines - half_turn(grad * sines)


def lane_of(shape):
    return lax.broadcasted_iota(jnp.int32, shape, 1)


def key_rows(span, index):
    return pl.ds(pl.multiple_of((index ^ span[2]) * KEY_BLOCK, KEY_BLOCK), KEY_BLOCK)


def spread_heads(span, odd, source_ref, pair_ref):
    def step(index, carry):
        rows = key_rows(span, index)
        value = source_ref[rows, :].astype(F32)
        turned = pltpu.roll(value, HEAD_DIM, 1)
        low = lane_of(value.shape) < HEAD_DIM
        none = jnp.zeros_like(value)
        pair_ref[0, rows, :] = jnp.where(low, jnp.where(odd, turned, value), none).astype(BF16)
        pair_ref[1, rows, :] = jnp.where(low, none, jnp.where(odd, value, turned)).astype(BF16)
        return carry

    lax.fori_loop(span[0], span[1], step, 0)


def attention_forward_kernel(
    per_kv, span, q_ref, key_ref, value_ref, bias_ref, out_ref, lse_ref, k_ref, v_ref
):
    tokens = q_ref.shape[0]
    odd = lax.rem(pl.program_id(0) // per_kv, LANES // HEAD_DIM) == 1

    @pl.when(lax.rem(pl.program_id(0), per_kv) == 0)
    def _():
        spread_heads(span, odd, key_ref, k_ref)
        spread_heads(span, odd, value_ref, v_ref)

    queries = [q_ref[:, pair * LANES : (pair + 1) * LANES] for pair in range(PAIRS)]

    def step(index, carry):
        rows = key_rows(span, index)
        bias = bias_ref[rows, :]
        new = []
        for pair, (peaks, totals, mixed) in enumerate(carry):
            tops, sums, parts, decays = [], [], [], []
            for side in range(2):
                scores = mm_nt(k_ref[side, rows, :], queries[pair]) + bias
                top = jnp.maximum(peaks[side], jnp.max(scores, axis=0, keepdims=True))
                decay = jnp.exp(peaks[side] - top)
                probs = jnp.exp(scores - top)
                tops.append(top)
                sums.append(totals[side] * decay + jnp.sum(probs, axis=0, keepdims=True))
                decays.append(jnp.broadcast_to(decay, (HEAD_DIM, tokens)))
                parts.append(mm_tn(v_ref[side, rows, :], probs.astype(BF16)))
            mixed = mixed * jnp.concatenate(decays, axis=0) + (parts[0] + parts[1])
            new.append((tuple(tops), tuple(sums), mixed))
        return tuple(new)

    low = jnp.full((1, tokens), MASKED, F32)
    none = jnp.zeros((1, tokens), F32)
    start = ((low, low), (none, none), jnp.zeros((LANES, tokens), F32))
    result = lax.fori_loop(span[0], span[1], step, (start,) * PAIRS)
    for pair, (peaks, totals, mixed) in enumerate(result):
        weight = jnp.concatenate(
            [jnp.broadcast_to(1.0 / total, (HEAD_DIM, tokens)) for total in totals], axis=0
        )
        out_ref[:, pair * LANES : (pair + 1) * LANES] = (mixed * weight).T.astype(BF16)
        lse_ref[pair] = jnp.concatenate(
            [peak + jnp.log(total) for peak, total in zip(peaks, totals)], axis=0
        )


def key_value_specs(keys, per_kv):
    blocks = KV_HEADS * HEAD_DIM // LANES
    heads = LANES // HEAD_DIM
    return [
        pl.BlockSpec((keys, LANES), lambda j, s: (0, j // per_kv // heads)),
        pl.BlockSpec((keys, LANES), lambda j, s: (0, blocks + j // per_kv // heads)),
    ]


def attention_forward(span, query, key_value, bias):
    tokens, width = query.shape
    keys = bias.shape[0]
    pairs = width // LANES
    steps = pairs // PAIRS
    pair_spec = pl.BlockSpec((tokens, PAIRS * LANES), lambda j, s: (0, j))
    return pl.pallas_call(
        functools.partial(attention_forward_kernel, steps // KV_HEADS),
        out_shape=(
            jax.ShapeDtypeStruct((tokens, width), BF16),
            jax.ShapeDtypeStruct((pairs, 2, tokens), F32),
        ),
        grid_spec=pltpu.PrefetchScalarGridSpec(
            num_scalar_prefetch=1,
            grid=(steps,),
            in_specs=[
                pair_spec,
                *key_value_specs(keys, steps // KV_HEADS),
                pl.BlockSpec((keys, tokens), lambda j, s: (0, 0)),
            ],
            out_specs=(pair_spec, pl.BlockSpec((PAIRS, 2, tokens), lambda j, s: (j, 0, 0))),
            scratch_shapes=[pltpu.VMEM((2, keys, LANES), BF16)] * 2,
        ),
        compiler_params=pltpu.CompilerParams(
            dimension_semantics=("arbitrary",), vmem_limit_bytes=30 << 20
        ),
        cost_estimate=pl.CostEstimate(
            flops=4 * tokens * keys * width,
            transcendentals=tokens * keys * HEADS // 2,
            bytes_accessed=4 * tokens * width + 16 * keys * LANES * KV_HEADS,
        ),
        name="attention_forward",
    )(span, query, key_value, key_value, bias)


def attention_backward_kernel(
    per_kv,
    span,
    q_ref,
    do_ref,
    o_ref,
    lse_ref,
    key_ref,
    value_ref,
    bias_ref,
    cos_ref,
    sin_ref,
    dq_ref,
    dkv_ref,
    k_ref,
    v_ref,
    dk_sum,
    dv_sum,
):
    tokens = q_ref.shape[0]
    member = lax.rem(pl.program_id(0), per_kv)
    odd = lax.rem(pl.program_id(0) // per_kv, LANES // HEAD_DIM) == 1

    @pl.when(member == 0)
    def _():
        spread_heads(span, odd, key_ref, k_ref)
        spread_heads(span, odd, value_ref, v_ref)
        dk_sum[...] = jnp.zeros_like(dk_sum)
        dv_sum[...] = jnp.zeros_like(dv_sum)

    low = lane_of((tokens, LANES)) < HEAD_DIM
    row = lax.broadcasted_iota(jnp.int32, (8, LANES), 0)
    column = lax.broadcasted_iota(jnp.int32, (8, LANES), 1)
    chooser = jnp.where(row == column // HEAD_DIM, 1.0, 0.0).astype(F32)
    queries, grads, deltas, query_stack, grad_stack = [], [], [], [], []
    for pair in range(PAIRS):
        lanes = slice(pair * LANES, (pair + 1) * LANES)
        query, grad = q_ref[:, lanes], do_ref[:, lanes]
        none = jnp.zeros_like(query)
        queries.append(query)
        grads.append(grad)
        query_stack += [jnp.where(low, query, none), jnp.where(low, none, query)]
        grad_stack += [jnp.where(low, grad, none), jnp.where(low, none, grad)]
        deltas.append(
            lax.dot_general(
                chooser,
                grad.astype(F32) * o_ref[:, lanes].astype(F32),
                (((1,), (1,)), ((), ())),
                precision=lax.Precision.HIGHEST,
                preferred_element_type=F32,
            )
        )
    query_stack = jnp.concatenate(query_stack, axis=0)
    grad_stack = jnp.concatenate(grad_stack, axis=0)

    def step(index, dqueries):
        rows = key_rows(span, index)
        bias = bias_ref[rows, :]
        all_probs, all_dscores, new = [], [], []
        for pair, dquery in enumerate(dqueries):
            for side in range(2):
                scores = mm_nt(k_ref[side, rows, :], queries[pair]) + bias
                probs = jnp.exp(scores - lse_ref[pair, side : side + 1, :])
                dprobs = mm_nt(v_ref[side, rows, :], grads[pair])
                delta = deltas[pair][side : side + 1, :]
                dscores = (probs * (dprobs - delta)).astype(BF16)
                all_probs.append(probs.astype(BF16))
                all_dscores.append(dscores)
                dquery = dquery + mm_tn(k_ref[side, rows, :], dscores)
            new.append(dquery)
        dk_sum[rows, :] += mm(jnp.concatenate(all_dscores, axis=1), query_stack)
        dv_sum[rows, :] += mm(jnp.concatenate(all_probs, axis=1), grad_stack)
        return tuple(new)

    dqueries = lax.fori_loop(
        span[0], span[1], step, (jnp.zeros((LANES, tokens), F32),) * PAIRS
    )
    half = HEAD_DIM // 2
    for pair, dquery in enumerate(dqueries):
        dquery = dquery.T * (HEAD_DIM**-0.5)
        turned = dquery * sin_ref[...]
        first = lax.rem(lane_of(turned.shape), HEAD_DIM) < half
        turned = jnp.where(
            first, pltpu.roll(turned, LANES - half, 1), -pltpu.roll(turned, half, 1)
        )
        dq_ref[:, pair * LANES : (pair + 1) * LANES] = (dquery * cos_ref[...] + turned).astype(BF16)

    @pl.when(member == per_kv - 1)
    def _():
        block = pl.program_id(0) // per_kv // (LANES // HEAD_DIM)

        def put(index, carry):
            target = index ^ span[3]
            for sum_ref, first in ((dk_sum, 0), (dv_sum, KV_HEADS * HEAD_DIM // LANES)):
                total = sum_ref[pl.ds(pl.multiple_of(index * tokens, tokens), tokens), :]
                total = total + pltpu.roll(total, HEAD_DIM, 1)
                keep = jnp.logical_and(odd, lane_of(total.shape) < HEAD_DIM)
                lanes = pl.ds(pl.multiple_of((first + block) * LANES, LANES), LANES)
                dkv_ref[target, :, lanes] = jnp.where(
                    keep, dkv_ref[target, :, lanes], total.astype(BF16)
                )
            return carry

        lax.fori_loop(0, dkv_ref.shape[0], put, 0)


def attention_backward(span, query, grad, attended, lse, key_value, bias, cosines, sines):
    tokens, width = query.shape
    keys, kv_two = key_value.shape
    pairs = width // LANES
    steps = pairs // PAIRS
    per_kv = steps // KV_HEADS
    pair_spec = pl.BlockSpec((tokens, PAIRS * LANES), lambda j, s: (0, j))
    table_spec = pl.BlockSpec((tokens, LANES), lambda j, s: (0, 0))
    return pl.pallas_call(
        functools.partial(attention_backward_kernel, per_kv),
        out_shape=(
            jax.ShapeDtypeStruct((tokens, width), BF16),
            jax.ShapeDtypeStruct((keys // tokens, tokens, kv_two), BF16),
        ),
        grid_spec=pltpu.PrefetchScalarGridSpec(
            num_scalar_prefetch=1,
            grid=(steps,),
            in_specs=[
                pair_spec,
                pair_spec,
                pair_spec,
                pl.BlockSpec((PAIRS, 2, tokens), lambda j, s: (j, 0, 0)),
                *key_value_specs(keys, per_kv),
                pl.BlockSpec((keys, tokens), lambda j, s: (0, 0)),
                table_spec,
                table_spec,
            ],
            out_specs=(
                pair_spec,
                pl.BlockSpec((keys // tokens, tokens, kv_two), lambda j, s: (0, 0, 0)),
            ),
            scratch_shapes=[pltpu.VMEM((2, keys, LANES), BF16)] * 2
            + [pltpu.VMEM((keys, LANES), F32)] * 2,
        ),
        compiler_params=pltpu.CompilerParams(
            dimension_semantics=("arbitrary",), vmem_limit_bytes=46 << 20
        ),
        cost_estimate=pl.CostEstimate(
            flops=10 * tokens * keys * width,
            transcendentals=tokens * keys * HEADS // 2,
            bytes_accessed=10 * tokens * width + 8 * keys * kv_two,
        ),
        name="attention_backward",
    )(span, query, grad, attended, lse, key_value, key_value, bias, cosines, sines)


CORE, ACROSS_X, ACROSS_Y = 1, 2, 4


def flip(array, mask):
    members = lax.axis_size("grp")
    return lax.ppermute(array, "grp", [(i, i ^ mask) for i in range(members)])


def flip_group(array):
    groups = lax.axis_size("rep")
    return lax.ppermute(array, "rep", [(i, i ^ 1) for i in range(groups)])


def gather_hidden_block(gate_up_weight, down_weight):
    rows = gate_up_weight.shape[0] // 4
    block = gate_up_weight.shape[1]
    member = lax.axis_index("grp")
    parity = lax.axis_index("rep") % 2
    own = [
        lax.dynamic_slice_in_dim(gate_up_weight, ((parity ^ (q // 2)) * 2 + q % 2) * rows, rows, 0)
        for q in range(4)
    ]

    def down_rows(mask):
        start = ((member ^ mask) % ACROSS_Y) * block
        return lax.dynamic_slice_in_dim(down_weight, start, block, 0)

    low, next_quarter, *near = yield (
        flip(own[0], ACROSS_Y),
        own[1],
        flip(down_rows(ACROSS_X), ACROSS_X),
        flip(down_rows(CORE), CORE),
        flip(down_rows(ACROSS_X | CORE), ACROSS_X | CORE),
    )
    down_own = jnp.stack([down_rows(0), near[1], near[0], near[2]])
    high, low_other, down_own = yield flip(next_quarter, ACROSS_Y), flip_group(low), down_own
    mine, second = (
        lax.dynamic_slice_in_dim(down_own, 2 * parity + index, 1, 0) for index in range(2)
    )
    down_mine, high_other, second = yield flip(mine, ACROSS_Y), flip_group(high), second
    down_second, down_other = yield flip(second, ACROSS_Y), flip_group(down_mine)
    (second_other,) = yield (flip_group(down_second),)
    return {
        "own": own,
        "over_y": (low, high, low_other, high_other),
        "down": (down_own, down_mine, down_second, down_other, second_other),
    }


def gather_key_values(own):
    over_y = flip(own, ACROSS_Y)
    pieces = [own, flip(own, ACROSS_X), over_y, flip(over_y, ACROSS_X)]
    return jnp.concatenate(
        [part for piece in pieces for part in (piece, flip(piece, CORE))], axis=0
    )


def tie(value, transfers):
    value, *transfers = lax.optimization_barrier((value, *transfers))
    return value, tuple(transfers)


def feed_forward_alone(norm2, sens, gate_up_full, down_full, small, seen):
    ffn_in, switch, lift, down_in, lower = small
    slots, hidden_width = switch.shape
    seen_two = jnp.concatenate([seen, seen], axis=1)
    latent_gu = (mm(norm2, ffn_in) * seen_two).astype(BF16)
    latent_g, latent_u = latent_gu[:, :slots], latent_gu[:, slots:]
    gate_up = mm(norm2, gate_up_full) + LOWRANK_FACTOR * jnp.concatenate(
        [mm(latent_g, switch), mm(latent_u, lift)], axis=1
    )
    gate = gate_up[:, :hidden_width]
    up = gate_up[:, hidden_width:]
    sigma = jax.nn.sigmoid(gate)
    act = (gate * sigma * up).astype(BF16)
    latent_d = (mm_nt(act, down_in) * seen).astype(BF16)
    response_part = mm(act, down_full) + LOWRANK_FACTOR * mm(latent_d, lower)
    dlat_d = (LOWRANK_FACTOR * mm_nt(sens, lower) * seen).astype(BF16)
    dact = mm_nt(sens, down_full) + mm(dlat_d, down_in)
    dgate = (dact * up * (sigma * (1.0 + gate * (1.0 - sigma)))).astype(BF16)
    dup = (dact * gate * sigma).astype(BF16)
    dlat_gu = (
        LOWRANK_FACTOR
        * jnp.concatenate([mm_nt(dgate, switch), mm_nt(dup, lift)], axis=1)
        * seen_two
    ).astype(BF16)
    dnorm2 = (
        mm_nt(dgate, gate_up_full[:, :hidden_width])
        + mm_nt(dup, gate_up_full[:, hidden_width:])
        + mm_nt(dlat_gu, ffn_in)
    )
    deep = jnp.concatenate(
        [
            mm_tn(dlat_d, act),
            LOWRANK_FACTOR * mm_tn(latent_g, dgate),
            LOWRANK_FACTOR * mm_tn(latent_u, dup),
        ],
        axis=0,
    ).astype(BF16)
    members = lax.axis_size("grp")
    deep = deep.reshape(3 * slots, members, hidden_width // members).transpose(1, 0, 2)
    return response_part, dnorm2, latent_d, dlat_gu, deep


def feed_forward_kernel(
    meta,
    own_x,
    near_x,
    own_g,
    near_g,
    own_seen,
    near_seen,
    lower_ref,
    switch_ref,
    lift_ref,
    in_ref,
    *refs,
):
    whole_refs, whole_down = refs[:8], refs[8:13]
    back_own, back_near, acts, deep_ref = refs[13:17]
    x_turned, g_turned, latents, dlats, stack, firsts, seconds, dacts, dlat_sum = refs[17:26]
    kept, kept_down, semaphores = refs[26:]
    count, width = own_g.shape
    tokens = 2 * count
    slots, block = in_ref.shape
    quarter = width // 4
    part = width // kept_down.shape[0]
    parity = meta[0]
    owns_gate = meta[1] == 1
    member = meta[2]
    starts = [
        pl.multiple_of((parity if q < 2 else 1 - parity) * (width // 2) + (q % 2) * quarter, quarter)
        for q in range(4)
    ]
    bases = [0, 1, 2, 3, *(4 + 2 * parity + k for k in (0, 1)), *(6 - 2 * parity + k for k in (0, 1))]
    columns = [pl.ds(pl.multiple_of((member ^ base) * part, part), part) for base in bases]
    down_copies = [
        pltpu.make_async_copy(ref, kept_down.at[pl.ds(start, size)], semaphores.at[8 + index])
        for index, (ref, start, size) in enumerate(zip(whole_down, (0, 4, 5, 6, 7), (4, 1, 1, 1, 1)))
    ]
    copies = [
        pltpu.make_async_copy(ref, kept.at[index], semaphores.at[index])
        for index, ref in enumerate(whole_refs)
    ]
    for copy in down_copies + copies:
        copy.start()
    dlat_sum[...] = jnp.zeros_like(dlat_sum)
    for index, (x_ref, g_ref, seen_ref) in enumerate(
        ((own_x, own_g, own_seen), (near_x, near_g, near_seen))
    ):
        rows = slice(index * count, (index + 1) * count)
        for q in range(4):
            x_turned[rows, q * quarter : (q + 1) * quarter] = x_ref[:, pl.ds(starts[q], quarter)]
        for k, lanes in enumerate(columns):
            g_turned[rows, k * part : (k + 1) * part] = g_ref[:, lanes]
        latents[rows, :] = x_ref[:, width : width + 2 * slots]
        dlat = LOWRANK_FACTOR * mm_nt(g_ref[...], lower_ref[...]) * seen_ref[...]
        dlats[rows, :] = dlat.astype(BF16)
        stack[:slots, rows] = dlat.T.astype(BF16)
        latent = x_ref[:, width : width + LANES].astype(F32).T[: 2 * slots]
        stack[slots:, rows] = latent.astype(BF16)

    def dact_part(start, size):
        here = pl.ds(start, size)
        down = jnp.concatenate([kept_down[k, here, :] for k in range(len(columns))], axis=1)
        dacts[:, here] = mm_nt(g_turned[...], down) + mm(dlats[...], in_ref[:, here])

    def dact_step(index, carry):
        dact_part(pl.multiple_of(index * 2 * LANES, 2 * LANES), 2 * LANES)
        return carry

    for copy in down_copies:
        copy.wait()
    lax.fori_loop(0, block // (2 * LANES), dact_step, 0)
    if block % (2 * LANES):
        dact_part(block // (2 * LANES) * 2 * LANES, block % (2 * LANES))
    for copy in copies:
        copy.wait()

    def hidden_part(start, size):
        here = pl.ds(start, size)
        none = jnp.zeros((slots, size), BF16)
        switch, lift = switch_ref[:, here], lift_ref[:, here]
        pieces = jnp.where(
            owns_gate,
            jnp.concatenate(
                [jnp.concatenate([switch, none], axis=1), jnp.concatenate([none, lift], axis=1)],
                axis=0,
            ),
            jnp.concatenate(
                [jnp.concatenate([none, switch], axis=1), jnp.concatenate([lift, none], axis=1)],
                axis=0,
            ),
        )
        weight = jnp.concatenate(
            [
                jnp.concatenate([kept[q, :, here], kept[4 + q, :, here]], axis=1)
                for q in range(4)
            ],
            axis=0,
        )
        total = mm(x_turned[...], weight)
        total = total + LOWRANK_FACTOR * mm(latents[...], pieces)
        gate = jnp.where(owns_gate, total[:, :size], total[:, size:])
        up = jnp.where(owns_gate, total[:, size:], total[:, :size])
        sigma = jax.nn.sigmoid(gate)
        act = (gate * sigma * up).astype(BF16)
        dact = dacts[:, here]
        dgate = (dact * up * (sigma * (1.0 + gate * (1.0 - sigma)))).astype(BF16)
        dup = (dact * gate * sigma).astype(BF16)
        dfirst, dsecond = jnp.where(owns_gate, dgate, dup), jnp.where(owns_gate, dup, dgate)
        acts[:, here] = act
        firsts[:, here] = dfirst
        seconds[:, here] = dsecond
        both = jnp.concatenate([dfirst, dsecond], axis=1)
        dlat_sum[:, : 2 * slots] += mm_nt(both, pieces)
        piece_grad = LOWRANK_FACTOR * mm(stack[slots:, :], both)
        low, high = piece_grad[:, :size], piece_grad[:, size:]
        deep_ref[:slots, here] = mm(stack[:slots, :], act)
        deep_ref[slots : 2 * slots, here] = jnp.where(owns_gate, low, high)[:slots]
        deep_ref[2 * slots :, here] = jnp.where(owns_gate, high, low)[slots:]

    def hidden_step(index, carry):
        hidden_part(pl.multiple_of(index * 2 * LANES, 2 * LANES), 2 * LANES)
        return carry

    lax.fori_loop(0, block // (2 * LANES), hidden_step, 0)
    if block % (2 * LANES):
        hidden_part(block // (2 * LANES) * 2 * LANES, block % (2 * LANES))

    def back(q, carry):
        value = mm_nt(firsts[...], kept[q]) + mm_nt(seconds[...], kept[4 + q])
        start = ((q // 2) ^ parity) * (width // 2) + lax.rem(q, 2) * quarter
        lanes = pl.ds(pl.multiple_of(start, quarter), quarter)
        back_own[:, lanes] = value[:count]
        back_near[:, lanes] = value[count:].astype(BF16)
        return carry

    lax.fori_loop(0, 4, back, 0)
    back_own[:, width:] = dlat_sum[:count, :]
    back_near[:, width:] = dlat_sum[count:, :].astype(BF16)


def down_kernel(meta, in_ref, *refs):
    acts_refs, whole_down = refs[:2], refs[2:7]
    results = (refs[7:9], refs[9:11])
    kept_down, semaphores = refs[11:]
    slots = in_ref.shape[0]
    parts, _, part = kept_down.shape
    width = parts * part
    parity, member = meta[0], meta[2]
    copies = [
        pltpu.make_async_copy(ref, kept_down.at[pl.ds(start, size)], semaphores.at[index])
        for index, (ref, start, size) in enumerate(zip(whole_down, (0, 4, 5, 6, 7), (4, 1, 1, 1, 1)))
    ]
    for copy in copies:
        copy.start()
    for acts, outs in zip(acts_refs, results):
        latent = mm_nt(acts[...], in_ref[...])
        pad = jnp.zeros((latent.shape[0], LANES - slots), F32)
        latent = jnp.concatenate([latent, pad], axis=1)
        for index, out in enumerate(outs):
            rows = slice(index * out.shape[0], (index + 1) * out.shape[0])
            out[:, width:] = latent[rows].astype(out.dtype)
    for copy in copies:
        copy.wait()

    def columns(index, carry):
        half = (index - 4) // 2 ^ parity
        base = jnp.where(index < 4, index, 4 + 2 * half + lax.rem(index, 2))
        lanes = pl.ds(pl.multiple_of((member ^ base) * part, part), part)
        for acts, outs in zip(acts_refs, results):
            value = mm(acts[...], kept_down[index])
            for side, out in enumerate(outs):
                rows = slice(side * out.shape[0], (side + 1) * out.shape[0])
                out[:, lanes] = value[rows].astype(out.dtype)
        return carry

    lax.fori_loop(0, parts, columns, 0)


def down_projection(meta, acts, down_in, weights):
    tokens, block = acts[0].shape
    slots = down_in.shape[0]
    width = 8 * weights["down"][0].shape[2]
    wide, count = width + LANES, tokens // 2
    kept = jax.ShapeDtypeStruct((count, wide), F32)
    sent = jax.ShapeDtypeStruct((count, wide), BF16)
    return pl.pallas_call(
        down_kernel,
        out_shape=(kept, sent, sent, sent),
        in_specs=[pl.BlockSpec(memory_space=pltpu.SMEM)]
        + [pl.BlockSpec(memory_space=pltpu.VMEM)] * 3
        + [pl.BlockSpec(memory_space=pl.ANY)] * 5,
        scratch_shapes=[
            pltpu.VMEM((8, block, width // 8), BF16),
            pltpu.SemaphoreType.DMA((5,)),
        ],
        compiler_params=pltpu.CompilerParams(vmem_limit_bytes=24 << 20),
        cost_estimate=pl.CostEstimate(
            flops=4 * tokens * width * block,
            transcendentals=0,
            bytes_accessed=2 * width * block + 8 * tokens * width,
        ),
        name="down_projection",
    )(meta, down_in, *acts, *weights["down"])


def feed_forward_pair(meta, rows, sens, seen, weights, pieces):
    count, width = sens[0].shape
    slots, block = pieces[-1].shape
    wide, tokens = width + LANES, 2 * count
    operands = (*rows, *sens, *seen, *pieces)
    arrays = (*weights["own"], *weights["over_y"], *weights["down"])
    return pl.pallas_call(
        feed_forward_kernel,
        out_shape=(
            jax.ShapeDtypeStruct((count, wide), F32),
            jax.ShapeDtypeStruct((count, wide), BF16),
            jax.ShapeDtypeStruct((tokens, block), BF16),
            jax.ShapeDtypeStruct((3 * slots, block), F32),
        ),
        in_specs=[pl.BlockSpec(memory_space=pltpu.SMEM)]
        + [pl.BlockSpec(memory_space=pltpu.VMEM)] * len(operands)
        + [pl.BlockSpec(memory_space=pl.ANY)] * len(arrays),
        scratch_shapes=[
            pltpu.VMEM((tokens, width), BF16),
            pltpu.VMEM((tokens, width), BF16),
            pltpu.VMEM((tokens, 2 * slots), BF16),
            pltpu.VMEM((tokens, slots), BF16),
            pltpu.VMEM((3 * slots, tokens), BF16),
            pltpu.VMEM((tokens, block), BF16),
            pltpu.VMEM((tokens, block), BF16),
            pltpu.VMEM((tokens, block), F32),
            pltpu.VMEM((tokens, LANES), F32),
            pltpu.VMEM((8, width // 4, block), BF16),
            pltpu.VMEM((8, block, width // 8), BF16),
            pltpu.SemaphoreType.DMA((13,)),
        ],
        compiler_params=pltpu.CompilerParams(vmem_limit_bytes=50 << 20),
        cost_estimate=pl.CostEstimate(
            flops=2 * 5 * tokens * width * block,
            transcendentals=tokens * block,
            bytes_accessed=6 * width * block + 20 * tokens * width,
        ),
        name="feed_forward",
    )(meta, *operands, *arrays)


def feed_forward_shared(norm2, sens_pairs, weights, small, all_seen):
    ffn_in, *pieces = small
    lower = pieces[0]
    width = norm2.shape[1]
    slots, block = pieces[-1].shape
    hidden_width = block * ACROSS_Y
    member = lax.axis_index("grp")
    parity = lax.axis_index("rep") % 2
    owns_gate = member < ACROSS_Y
    hidden = member % ACROSS_Y
    meta = jnp.stack([parity, owns_gate.astype(jnp.int32), member]).astype(jnp.int32)
    seen = all_seen[0]
    seen_two = jnp.concatenate([seen, seen], axis=1)
    latent_gu = (mm(norm2, ffn_in) * seen_two).astype(BF16)
    pad = jnp.zeros((norm2.shape[0], LANES - 2 * slots), BF16)
    rows = jnp.concatenate([norm2, latent_gu, pad], axis=1)
    across = flip(rows, ACROSS_X)
    results = []
    for index, sens_pair in enumerate(sens_pairs):
        if index == 1:
            result, (across,) = tie(results[0][1], (across,))
            results[0][1] = result
            rows = across
        seen_pair = all_seen[2 * index : 2 * index + 2]
        row_pair = (rows, flip(rows, CORE))
        results.append(
            list(feed_forward_pair(meta, row_pair, sens_pair, seen_pair, weights, pieces))
        )

    chips = [result[0] + flip(result[1], CORE).astype(F32) for result in results]
    deep = (results[0][3] + results[1][3]).astype(BF16)
    members = lax.axis_size("grp")
    owners = members * block // hidden_width
    deep = deep.reshape(3 * slots, owners, block // owners).transpose(1, 0, 2)
    placed = jnp.zeros((members, 3 * slots, block // owners), BF16)
    placed = lax.dynamic_update_slice_in_dim(placed, deep, hidden * owners, 0)
    forwards = down_projection(meta, [result[2] for result in results], pieces[-1], weights)
    across = flip(chips[1].astype(BF16), ACROSS_X)
    across, (placed, *forwards) = tie(across, (placed, *forwards))
    backward = chips[0] + across.astype(F32)
    dlat_gu = (LOWRANK_FACTOR * backward[:, width : width + 2 * slots] * seen_two).astype(BF16)
    dnorm2 = backward[:, :width] + mm_nt(dlat_gu, ffn_in)
    dnorm2, forwards = tie(dnorm2, forwards)
    forward = forwards[0]
    for part, mask in zip(forwards[1:], (CORE, ACROSS_X, ACROSS_X | CORE)):
        forward = forward + flip(part, mask).astype(F32)
    latent_d = (forward[:, width : width + slots] * seen).astype(BF16)
    response_part = forward[:, :width] + LOWRANK_FACTOR * mm(latent_d, lower)
    return response_part, dnorm2, latent_d, dlat_gu, placed


def exchange_sum(parts):
    received = lax.all_to_all(parts.astype(BF16), "grp", 0, 0, tiled=True)
    return jnp.sum(received.astype(F32), axis=0)


def simple_call(kernel, name, out_shape, operands, flops):
    return pl.pallas_call(
        kernel,
        out_shape=out_shape,
        compiler_params=pltpu.CompilerParams(vmem_limit_bytes=32 << 20),
        cost_estimate=pl.CostEstimate(
            flops=flops,
            transcendentals=0,
            bytes_accessed=sum(array.size * array.dtype.itemsize for array in operands),
        ),
        name=name,
    )(*operands)


def early_gradients_kernel(
    dq_ref,
    asking_ref,
    seen_ref,
    latent_q_ref,
    norm1_ref,
    latent_d_ref,
    sens_ref,
    dlat_gu_ref,
    norm2_ref,
    dlat_o_ref,
    attended_ref,
    latent_o_ref,
    dbranch_ref,
    dlat_q_ref,
    early_ref,
):
    dlat_q = (LOWRANK_FACTOR * mm_nt(dq_ref[...], asking_ref[...]) * seen_ref[...]).astype(BF16)
    dlat_q_ref[...] = dlat_q
    two = LOWRANK_FACTOR
    start = 0
    for factor, small, large in (
        (1.0, dlat_q, norm1_ref),
        (two, latent_q_ref[...], dq_ref),
        (two, latent_d_ref[...], sens_ref),
        (1.0, dlat_gu_ref[...], norm2_ref),
        (1.0, dlat_o_ref[...], attended_ref),
        (two, latent_o_ref[...], dbranch_ref),
    ):
        rows = small.shape[1]
        early_ref[start : start + rows, :] = (factor * mm_tn(small, large[...])).astype(BF16)
        start += rows


def early_gradients(*operands):
    count, width = operands[0].shape
    slots = operands[1].shape[0]
    return simple_call(
        early_gradients_kernel,
        "early_gradients",
        (
            jax.ShapeDtypeStruct((count, slots), BF16),
            jax.ShapeDtypeStruct((7 * slots, width), BF16),
        ),
        operands,
        2 * count * width * 8 * slots,
    )


def key_value_gradients_kernel(
    received_ref,
    early_ref,
    cos_ref,
    sin_ref,
    right_ref,
    seen_ref,
    latent_ref,
    norm_ref,
    dkv_ref,
    dlat_ref,
    pack_ref,
):
    half = HEAD_DIM // 2
    total = received_ref[0].astype(F32)
    for source in range(1, received_ref.shape[0]):
        total = total + received_ref[source].astype(F32)
    kv_width = total.shape[1] // 2
    pieces = []
    for start in range(0, kv_width, LANES):
        value = total[:, start : start + LANES]
        turned = value * sin_ref[...]
        first = lax.rem(lane_of(turned.shape), HEAD_DIM) < half
        turned = jnp.where(
            first, pltpu.roll(turned, LANES - half, 1), -pltpu.roll(turned, half, 1)
        )
        pieces.append((value * cos_ref[...] + turned).astype(BF16))
    dkv = jnp.concatenate([*pieces, total[:, kv_width:].astype(BF16)], axis=1)
    dkv_ref[...] = dkv
    dlat = (LOWRANK_FACTOR * mm_nt(dkv, right_ref[...]) * seen_ref[...]).astype(BF16)
    dlat_ref[...] = dlat
    late = mm_tn(dlat, norm_ref[...]).astype(BF16)
    thin = (LOWRANK_FACTOR * mm_tn(latent_ref[...], dkv)).astype(BF16)
    rows, head = late.shape[0], early_ref.shape[0]
    thin = jnp.concatenate([thin[: rows // 2, :kv_width], thin[rows // 2 :, kv_width:]], axis=0)
    share = pack_ref.shape[2]
    for target in range(pack_ref.shape[0]):
        columns = slice(target * share, (target + 1) * share)
        pack_ref[target, :head, :] = early_ref[:, columns]
        pack_ref[target, head : head + rows, :] = late[:, columns]
        for index, start in enumerate(range(0, kv_width, share)):
            place = head + (index + 1) * rows
            pack_ref[target, place : place + rows, :] = thin[:, start : start + share]


def key_value_gradients(received, early, cosines, sines, kv_right, seen_two, latent_kv, norm1):
    members, count, kv_two = received.shape
    rows = kv_right.shape[0]
    share = norm1.shape[1] // members
    packed = early.shape[0] + rows * (1 + kv_two // 2 // share)
    return simple_call(
        key_value_gradients_kernel,
        "key_value_gradients",
        (
            jax.ShapeDtypeStruct((count, kv_two), BF16),
            jax.ShapeDtypeStruct((count, rows), BF16),
            jax.ShapeDtypeStruct((members, packed, share), BF16),
        ),
        (received, early, cosines, sines, kv_right, seen_two, latent_kv, norm1),
        2 * count * rows * (norm1.shape[1] + 2 * kv_two),
    )


def place_kernel(jobs, groups, slots, *refs):
    place_ref, refs = refs[0], refs[1:]
    outs = refs[len(refs) - len(jobs) :]
    for (source, index, is_right), out_ref in zip(jobs, outs):
        value = jnp.concatenate(
            [
                refs[source * groups + g][index * slots : (index + 1) * slots, :]
                for g in range(groups)
            ],
            axis=0,
        )
        if is_right:
            out_ref[...] = mm_tn(place_ref[...], value)
        else:
            out_ref[...] = mm_tn(value, place_ref[...])


def place_gradients(place, sources, slots, jobs):
    groups = len(sources[0])
    narrow = place.shape[1]
    shapes = []
    for source, _, is_right in jobs:
        size = sources[source][0].shape[1]
        shapes.append(
            jax.ShapeDtypeStruct((narrow, size) if is_right else (size, narrow), F32)
        )
    return pl.pallas_call(
        functools.partial(place_kernel, jobs, groups, slots),
        out_shape=tuple(shapes),
        compiler_params=pltpu.CompilerParams(vmem_limit_bytes=32 << 20),
        cost_estimate=pl.CostEstimate(
            flops=2 * sum(shape.size for shape in shapes) * place.shape[0],
            transcendentals=0,
            bytes_accessed=4 * sum(shape.size for shape in shapes),
        ),
        name="place_gradients",
    )(place, *[array for source in sources for array in source])


def round_groups(array):
    groups = lax.axis_size("rep")
    return [array] + [
        lax.ppermute(array, "rep", [(i, (i + shift) % groups) for i in range(groups)])
        for shift in range(1, groups)
    ]


def shards(
    tokens,
    response_sensitivity,
    seq_lengths,
    prefix_lengths,
    adapter_ids,
    attn_gain,
    mlp_gain,
    qkv_weight,
    out_weight,
    gate_up_weight,
    down_weight,
    query_in,
    asking_right_pieces,
    key_in,
    lookup_right_pieces,
    value_in,
    content_right_pieces,
    output_in,
    final_right_pieces,
    gate_in,
    switch_right_pieces,
    up_in,
    lift_right_pieces,
    down_in,
    lower_right_pieces,
):
    count, width = tokens.shape
    members = lax.axis_size("grp")
    groups = lax.axis_size("rep")
    kv_width = lookup_right_pieces.shape[1]
    narrow = query_in.shape[1]
    group = lax.axis_index("rep")
    member = lax.axis_index("grp")
    lengths = lax.dynamic_slice_in_dim(seq_lengths, 2 * group, 2)
    prefixes = lax.dynamic_slice_in_dim(prefix_lengths, 2 * group, 2)
    chosen_ids = lax.dynamic_slice_in_dim(adapter_ids, 2 * group, 2)
    key_count = count * members
    sens = response_sensitivity

    paired = members == 8 and groups % 2 == 0
    qkv_full = lax.all_gather(qkv_weight, "grp", axis=1, tiled=True)
    if paired:
        steps = gather_hidden_block(gate_up_weight, down_weight)
        transfers = next(steps)
    else:
        out_full = lax.all_gather(out_weight, "grp", axis=1, tiled=True)
        down_full = lax.all_gather(down_weight, "grp", axis=1, tiled=True)
        gate_up_full = lax.all_gather(gate_up_weight, "grp", axis=1, tiled=True)

    turn = member if paired else 0
    key_index = jnp.arange(key_count, dtype=jnp.int32)
    key_index = (key_index // count ^ turn) * count + key_index % count
    key_second = (key_index >= lengths[0]).astype(jnp.int32)
    key_position = key_index - key_second * lengths[0]
    own_index = member * count + jnp.arange(count, dtype=jnp.int32)
    own_second = (own_index >= lengths[0]).astype(jnp.int32)
    position = own_index - own_second * lengths[0]
    prefix = jnp.where(own_second == 0, prefixes[0], prefixes[1])
    allowed = (key_second[:, None] == own_second[None, :]) & (
        (key_position[:, None] <= position[None, :]) | (key_position[:, None] < prefix[None, :])
    )
    bias = jnp.where(allowed, 0.0, MASKED).astype(F32)
    first_key = own_second[0] * lengths[0]
    last_key = jnp.max(own_second * lengths[0] + jnp.maximum(position, prefix - 1))
    span = jnp.stack(
        [first_key // KEY_BLOCK, last_key // KEY_BLOCK + 1, turn * count // KEY_BLOCK, turn]
    ).astype(jnp.int32)

    slots = 2 * RANK
    columns = jnp.arange(narrow, dtype=jnp.int32)
    slot = jnp.arange(slots, dtype=jnp.int32)
    slot_column = jnp.where(slot < RANK, chosen_ids[0], chosen_ids[1]) * RANK + slot % RANK
    pick = (columns[:, None] == slot_column[None, :]).astype(BF16)

    def seen_by(device):
        index = device * count + jnp.arange(count, dtype=jnp.int32)
        second = (index >= lengths[0]).astype(jnp.int32)
        return (second[:, None] == slot[None, :] // RANK).astype(F32)

    def pick_in(weight):
        return mm(weight, pick).astype(BF16)

    def pick_right(weight):
        return mm_tn(pick, weight).astype(BF16)

    seen = seen_by(member)
    seen_three = jnp.concatenate([seen, seen, seen], axis=1)
    qkv_in = jnp.concatenate([pick_in(query_in), pick_in(key_in), pick_in(value_in)], axis=1)
    asking = pick_right(asking_right_pieces)
    lookup = pick_right(lookup_right_pieces)
    content = pick_right(content_right_pieces)
    none = jnp.zeros_like(lookup)
    kv_right = jnp.concatenate(
        [jnp.concatenate([lookup, none], axis=1), jnp.concatenate([none, content], axis=1)], axis=0
    )
    out_in = pick_in(output_in)
    final = pick_right(final_right_pieces)
    lower = pick_right(lower_right_pieces)
    small = (
        jnp.concatenate([pick_in(gate_in), pick_in(up_in)], axis=1),
        pick_right(switch_right_pieces),
        pick_right(lift_right_pieces),
        lax.dot_general(
            pick, down_in, (((0,), (1,)), ((), ())), preferred_element_type=F32
        ).astype(BF16),
        lower,
    )

    cycle = jnp.arange(groups * slots, dtype=jnp.int32)
    source = (group - cycle // slots) % groups
    sequence = 2 * source + cycle % slots // RANK
    sequences = jnp.arange(adapter_ids.shape[0], dtype=jnp.int32)
    theirs = jnp.where(sequence[:, None] == sequences[None, :], adapter_ids[None, :], 0)
    all_column = jnp.sum(theirs, axis=1) * RANK + cycle % RANK
    place = (all_column[:, None] == columns[None, :]).astype(BF16)
    incoming = tokens.astype(F32)
    scale_one = inverse_rms(incoming)
    norm1 = (incoming * scale_one * attn_gain).astype(BF16)
    if paired:
        block = down_weight.shape[0] // ACROSS_Y
        start = member % ACROSS_Y * block
        pieces = [lax.dynamic_slice_in_dim(piece, start, block, 1) for piece in small[1:4]]
        others = (seen_by(member ^ mask) for mask in (CORE, ACROSS_X, ACROSS_X | CORE))
        ready = (*transfers, asking, kv_right, out_in, final, lower, place, small[0], *pieces)
        norm1, ready = tie(norm1, (*ready, *others))
        transfers = ready[: len(transfers)]
        asking, kv_right, out_in, final, lower, place, ffn_in, *ready = ready[len(transfers) :]
        small = (ffn_in, lower, *ready[:3])
        all_seen = (seen, *ready[3:])
        transfers = steps.send(transfers)
        out_full = lax.all_gather(out_weight, "grp", axis=1, tiled=True)
    latent_qkv = (mm(norm1, qkv_in) * seen_three).astype(BF16)
    latent_q, latent_kv = latent_qkv[:, :slots], latent_qkv[:, slots:]
    half = HEAD_DIM // 2
    freqs = 10000.0 ** (-2.0 * jnp.arange(half).astype(F32) / HEAD_DIM)
    freqs = jnp.tile(freqs, LANES // half)
    angles = position.astype(F32)[:, None] * freqs[None, :]
    cosines, sines = jnp.cos(angles), jnp.sin(angles)

    def widen(table, size):
        return jnp.tile(table, (1, size // LANES))

    qkv = mm(norm1, qkv_full)
    query = qkv[:, :width] + LOWRANK_FACTOR * mm(latent_q, asking)
    own_kv = qkv[:, width:] + LOWRANK_FACTOR * mm(latent_kv, kv_right)
    query = rotate(query, widen(cosines, width), widen(sines, width)).astype(BF16)
    query = query * jnp.asarray(HEAD_DIM**-0.5, BF16)
    key_own = rotate(own_kv[:, :kv_width], widen(cosines, kv_width), widen(sines, kv_width))
    key_value = jnp.concatenate([key_own, own_kv[:, kv_width:]], axis=1).astype(BF16)
    if paired:
        key_value, transfers = tie(key_value, transfers)
        key_value, (ready, *transfers) = tie(gather_key_values(key_value), (sens, *transfers))
        transfers = steps.send(transfers)
        sens_near, sens_across = flip(ready, CORE), flip(ready, ACROSS_X)
    else:
        key_value = lax.all_gather(key_value, "grp", axis=0, tiled=True)
    attended_low, lse = attention_forward(span, query, key_value, bias)
    if paired:
        attended_low, (sens_near, sens_across, *transfers) = tie(
            attended_low, (sens_near, sens_across, *transfers)
        )
        out_full, (sens_last, *transfers) = tie(
            out_full, (flip(sens_across, CORE), *steps.send(transfers))
        )
        sens_pairs = [(sens, sens_near), (sens_across, sens_last)]
        transfers = steps.send(transfers)

    latent_o = (mm(attended_low, out_in) * seen).astype(BF16)
    stream = incoming + (mm(attended_low, out_full) + LOWRANK_FACTOR * mm(latent_o, final))
    scale_two = inverse_rms(stream)
    norm2 = (stream * scale_two * mlp_gain).astype(BF16)
    if paired:
        norm2, transfers = tie(norm2, transfers)
        try:
            steps.send(transfers)
        except StopIteration as stop:
            weights = stop.value
        response_part, dnorm2, latent_d, dlat_gu, deep = feed_forward_shared(
            norm2, sens_pairs, weights, small, all_seen
        )
    else:
        response_part, dnorm2, latent_d, dlat_gu, deep = feed_forward_alone(
            norm2, sens, gate_up_full, down_full, small, seen
        )
    level_response = (stream + response_part).astype(BF16)
    dhidden = sens.astype(F32) + norm_backward(stream, scale_two, mlp_gain, dnorm2)
    dbranch = dhidden.astype(BF16)
    dlat_o = (LOWRANK_FACTOR * mm_nt(dbranch, final) * seen).astype(BF16)
    dattended = (mm_nt(dbranch, out_full) + mm_nt(dlat_o, out_in)).astype(BF16)

    dattended, (deep,) = tie(dattended, (deep,))
    deep_sum = lax.psum_scatter(deep, "grp", scatter_dimension=0, tiled=True)[0]

    dq, dkv_all = attention_backward(
        span, query, dattended, attended_low, lse, key_value, bias, cosines, sines
    )
    dkv_all, (deep_sum,) = tie(dkv_all, (deep_sum,))
    received = lax.all_to_all(dkv_all, "grp", 0, 0, tiled=True)
    dlat_q, early = early_gradients(
        dq,
        asking,
        seen,
        latent_q,
        norm1,
        latent_d,
        sens,
        dlat_gu,
        norm2,
        dlat_o,
        attended_low,
        latent_o,
        dbranch,
    )
    dnorm_q = mm_nt(dq, qkv_full[:, :width]) + mm_nt(dlat_q, qkv_in[:, :slots])
    dkv, dlat_kv, late = key_value_gradients(
        received, early, cosines, sines, kv_right, seen_three[:, : 2 * slots], latent_kv, norm1
    )
    deep_sum = round_groups(deep_sum)
    late_sum = round_groups(exchange_sum(late).astype(BF16))
    dnorm1 = dnorm_q + mm_nt(dkv, qkv_full[:, width:]) + mm_nt(dlat_kv, qkv_in[:, slots:])
    input_grad = (dhidden + norm_backward(incoming, scale_one, attn_gain, dnorm1)).astype(BF16)

    share = width // members
    pieces = kv_width // share
    thin_start = 9 * slots
    thin_sum = [
        jnp.concatenate(
            [
                array[thin_start + 2 * slots * i : thin_start + 2 * slots * (i + 1)]
                for i in range(pieces)
            ],
            axis=1,
        )
        for array in late_sum
    ]
    jobs = (
        (0, 0, False),
        (0, 1, True),
        (0, 7, False),
        (2, 0, True),
        (0, 8, False),
        (2, 1, True),
        (0, 5, False),
        (0, 6, True),
        (0, 3, False),
        (1, 1, True),
        (0, 4, False),
        (1, 2, True),
        (1, 0, False),
        (0, 2, True),
    )
    grads = list(place_gradients(place, (late_sum, deep_sum, thin_sum), slots, jobs))
    own = kv_width // members
    for index in (3, 5):
        grads[index] = lax.dynamic_slice_in_dim(grads[index], member * own, own, 1)
    return (level_response, input_grad, *grads)


def solution(mesh):
    rows = P(("rep", "grp"), None)
    split = P(None, "grp")
    in_specs = (rows, rows, *[P()] * 5, *[split] * 4, *[P()] * 14)
    out_specs = (rows, rows, *[P("grp", None), P(None, "grp")] * 7)
    return jax.shard_map(shards, mesh=mesh, in_specs=in_specs, out_specs=out_specs, check_vma=False)
```

```python
import functools

import jax
import jax.numpy as jnp
from jax import lax
from jax.experimental import pallas as pl
from jax.experimental.pallas import tpu as pltpu
from jax.sharding import PartitionSpec as P

HEADS = 32
KV_HEADS = 4
HEAD_DIM = 64
RANK = 16
LANES = 128
KEY_BLOCK = 1024
PAIRS = 4

EPS = 1e-05
LOWRANK_FACTOR = 2.0
MASKED = -1e30
F32 = jnp.float32
BF16 = jnp.bfloat16


def mm(left, right):
    return jnp.dot(left, right, preferred_element_type=F32)


def mm_nt(left, right):
    return lax.dot_general(left, right, (((1,), (1,)), ((), ())), preferred_element_type=F32)


def mm_tn(left, right):
    return lax.dot_general(left, right, (((0,), (0,)), ((), ())), preferred_element_type=F32)


def inverse_rms(value):
    return lax.rsqrt(jnp.mean(value * value, axis=-1, keepdims=True) + EPS)


def norm_backward(value, scale, gain, grad):
    scaled = gain * grad
    return scale * scaled - value * (scale * scale * scale) * jnp.mean(
        scaled * value, axis=-1, keepdims=True
    )


def half_turn(value):
    half = HEAD_DIM // 2
    lane = lax.broadcasted_iota(jnp.int32, value.shape, 1) % HEAD_DIM
    return jnp.where(
        lane < half, -jnp.roll(value, -half, axis=1), jnp.roll(value, half, axis=1)
    )


def rotate(value, cosines, sines):
    return value * cosines + half_turn(value) * sines


def unrotate(grad, cosines, sines):
    return grad * cosines - half_turn(grad * sines)


def lane_of(shape):
    return lax.broadcasted_iota(jnp.int32, shape, 1)


def key_rows(span, index):
    return pl.ds(pl.multiple_of((index ^ span[2]) * KEY_BLOCK, KEY_BLOCK), KEY_BLOCK)


def spread_heads(span, odd, source_ref, pair_ref):
    def step(index, carry):
        rows = key_rows(span, index)
        value = source_ref[rows, :].astype(F32)
        turned = pltpu.roll(value, HEAD_DIM, 1)
        low = lane_of(value.shape) < HEAD_DIM
        none = jnp.zeros_like(value)
        pair_ref[0, rows, :] = jnp.where(low, jnp.where(odd, turned, value), none).astype(BF16)
        pair_ref[1, rows, :] = jnp.where(low, none, jnp.where(odd, value, turned)).astype(BF16)
        return carry

    lax.fori_loop(span[0], span[1], step, 0)


def attention_forward_kernel(
    per_kv, span, q_ref, key_ref, value_ref, bias_ref, out_ref, lse_ref, k_ref, v_ref
):
    tokens = q_ref.shape[0]
    odd = lax.rem(pl.program_id(0) // per_kv, LANES // HEAD_DIM) == 1

    @pl.when(lax.rem(pl.program_id(0), per_kv) == 0)
    def _():
        spread_heads(span, odd, key_ref, k_ref)
        spread_heads(span, odd, value_ref, v_ref)

    queries = [q_ref[:, pair * LANES : (pair + 1) * LANES] for pair in range(PAIRS)]

    def step(index, carry):
        rows = key_rows(span, index)
        bias = bias_ref[rows, :]
        new = []
        flat = jnp.concatenate([v_ref[0, rows, :], v_ref[1, rows, :]], axis=0).T
        for pair, (peaks, totals, mixed) in enumerate(carry):
            tops, sums, parts, decays = [], [], [], []
            for side in range(2):
                scores = mm_nt(k_ref[side, rows, :], queries[pair]) + bias
                top = jnp.maximum(peaks[side], jnp.max(scores, axis=0, keepdims=True))
                decay = jnp.exp(peaks[side] - top)
                probs = jnp.exp(scores - top)
                tops.append(top)
                sums.append(totals[side] * decay + jnp.sum(probs, axis=0, keepdims=True))
                decays.append(jnp.broadcast_to(decay, (HEAD_DIM, tokens)))
                parts.append(probs.astype(BF16))
            mixed = mixed * jnp.concatenate(decays, axis=0)
            mixed = mixed + mm(flat, jnp.concatenate(parts, axis=0))
            new.append((tuple(tops), tuple(sums), mixed))
        return tuple(new)

    low = jnp.full((1, tokens), MASKED, F32)
    none = jnp.zeros((1, tokens), F32)
    start = ((low, low), (none, none), jnp.zeros((LANES, tokens), F32))
    result = lax.fori_loop(span[0], span[1], step, (start,) * PAIRS)
    for pair, (peaks, totals, mixed) in enumerate(result):
        weight = jnp.concatenate(
            [jnp.broadcast_to(1.0 / total, (HEAD_DIM, tokens)) for total in totals], axis=0
        )
        out_ref[:, pair * LANES : (pair + 1) * LANES] = (mixed * weight).T.astype(BF16)
        lse_ref[pair] = jnp.concatenate(
            [peak + jnp.log(total) for peak, total in zip(peaks, totals)], axis=0
        )


def key_value_specs(keys, per_kv):
    blocks = KV_HEADS * HEAD_DIM // LANES
    heads = LANES // HEAD_DIM
    return [
        pl.BlockSpec((keys, LANES), lambda j, s: (0, j // per_kv // heads)),
        pl.BlockSpec((keys, LANES), lambda j, s: (0, blocks + j // per_kv // heads)),
    ]


def attention_forward(span, query, key_value, bias):
    tokens, width = query.shape
    keys = bias.shape[0]
    pairs = width // LANES
    steps = pairs // PAIRS
    pair_spec = pl.BlockSpec((tokens, PAIRS * LANES), lambda j, s: (0, j))
    return pl.pallas_call(
        functools.partial(attention_forward_kernel, steps // KV_HEADS),
        out_shape=(
            jax.ShapeDtypeStruct((tokens, width), BF16),
            jax.ShapeDtypeStruct((pairs, 2, tokens), F32),
        ),
        grid_spec=pltpu.PrefetchScalarGridSpec(
            num_scalar_prefetch=1,
            grid=(steps,),
            in_specs=[
                pair_spec,
                *key_value_specs(keys, steps // KV_HEADS),
                pl.BlockSpec((keys, tokens), lambda j, s: (0, 0)),
            ],
            out_specs=(pair_spec, pl.BlockSpec((PAIRS, 2, tokens), lambda j, s: (j, 0, 0))),
            scratch_shapes=[pltpu.VMEM((2, keys, LANES), BF16)] * 2,
        ),
        compiler_params=pltpu.CompilerParams(
            dimension_semantics=("arbitrary",), vmem_limit_bytes=30 << 20
        ),
        cost_estimate=pl.CostEstimate(
            flops=4 * tokens * keys * width,
            transcendentals=tokens * keys * HEADS // 2,
            bytes_accessed=4 * tokens * width + 16 * keys * LANES * KV_HEADS,
        ),
        name="attention_forward",
    )(span, query, key_value, key_value, bias)


def attention_backward_kernel(
    per_kv,
    span,
    q_ref,
    do_ref,
    o_ref,
    lse_ref,
    key_ref,
    value_ref,
    bias_ref,
    cos_ref,
    sin_ref,
    dq_ref,
    dkv_ref,
    k_ref,
    v_ref,
    dk_sum,
    dv_sum,
):
    tokens = q_ref.shape[0]
    member = lax.rem(pl.program_id(0), per_kv)
    odd = lax.rem(pl.program_id(0) // per_kv, LANES // HEAD_DIM) == 1

    @pl.when(member == 0)
    def _():
        spread_heads(span, odd, key_ref, k_ref)
        spread_heads(span, odd, value_ref, v_ref)
        dk_sum[...] = jnp.zeros_like(dk_sum)
        dv_sum[...] = jnp.zeros_like(dv_sum)

    low = lane_of((tokens, LANES)) < HEAD_DIM
    row = lax.broadcasted_iota(jnp.int32, (8, LANES), 0)
    column = lax.broadcasted_iota(jnp.int32, (8, LANES), 1)
    chooser = jnp.where(row == column // HEAD_DIM, 1.0, 0.0).astype(F32)
    queries, grads, deltas, query_stack, grad_stack = [], [], [], [], []
    for pair in range(PAIRS):
        lanes = slice(pair * LANES, (pair + 1) * LANES)
        query, grad = q_ref[:, lanes], do_ref[:, lanes]
        none = jnp.zeros_like(query)
        queries.append(query)
        grads.append(grad)
        query_stack += [jnp.where(low, query, none), jnp.where(low, none, query)]
        grad_stack += [jnp.where(low, grad, none), jnp.where(low, none, grad)]
        deltas.append(
            lax.dot_general(
                chooser,
                grad.astype(F32) * o_ref[:, lanes].astype(F32),
                (((1,), (1,)), ((), ())),
                precision=lax.Precision.HIGHEST,
                preferred_element_type=F32,
            )
        )
    query_stack = jnp.concatenate(query_stack, axis=0)
    grad_stack = jnp.concatenate(grad_stack, axis=0)

    def step(index, dqueries):
        rows = key_rows(span, index)
        bias = bias_ref[rows, :]
        all_probs, all_dscores, new = [], [], []
        flat = jnp.concatenate([k_ref[0, rows, :], k_ref[1, rows, :]], axis=0).T
        for pair, dquery in enumerate(dqueries):
            for side in range(2):
                scores = mm_nt(k_ref[side, rows, :], queries[pair]) + bias
                probs = jnp.exp(scores - lse_ref[pair, side : side + 1, :])
                dprobs = mm_nt(v_ref[side, rows, :], grads[pair])
                delta = deltas[pair][side : side + 1, :]
                dscores = (probs * (dprobs - delta)).astype(BF16)
                all_probs.append(probs.astype(BF16))
                all_dscores.append(dscores)
            new.append(dquery + mm(flat, jnp.concatenate(all_dscores[-2:], axis=0)))
        dk_sum[rows, :] += mm(jnp.concatenate(all_dscores, axis=1), query_stack)
        dv_sum[rows, :] += mm(jnp.concatenate(all_probs, axis=1), grad_stack)
        return tuple(new)

    dqueries = lax.fori_loop(
        span[0], span[1], step, (jnp.zeros((LANES, tokens), F32),) * PAIRS
    )
    half = HEAD_DIM // 2
    for pair, dquery in enumerate(dqueries):
        dquery = dquery.T * (HEAD_DIM**-0.5)
        turned = dquery * sin_ref[...]
        first = lax.rem(lane_of(turned.shape), HEAD_DIM) < half
        turned = jnp.where(
            first, pltpu.roll(turned, LANES - half, 1), -pltpu.roll(turned, half, 1)
        )
        dq_ref[:, pair * LANES : (pair + 1) * LANES] = (dquery * cos_ref[...] + turned).astype(BF16)

    @pl.when(member == per_kv - 1)
    def _():
        block = pl.program_id(0) // per_kv // (LANES // HEAD_DIM)

        def put(index, carry):
            target = index ^ span[3]
            for sum_ref, first in ((dk_sum, 0), (dv_sum, KV_HEADS * HEAD_DIM // LANES)):
                total = sum_ref[pl.ds(pl.multiple_of(index * tokens, tokens), tokens), :]
                total = total + pltpu.roll(total, HEAD_DIM, 1)
                keep = jnp.logical_and(odd, lane_of(total.shape) < HEAD_DIM)
                lanes = pl.ds(pl.multiple_of((first + block) * LANES, LANES), LANES)
                dkv_ref[target, :, lanes] = jnp.where(
                    keep, dkv_ref[target, :, lanes], total.astype(BF16)
                )
            return carry

        lax.fori_loop(0, dkv_ref.shape[0], put, 0)


def attention_backward(span, query, grad, attended, lse, key_value, bias, cosines, sines):
    tokens, width = query.shape
    keys, kv_two = key_value.shape
    pairs = width // LANES
    steps = pairs // PAIRS
    per_kv = steps // KV_HEADS
    pair_spec = pl.BlockSpec((tokens, PAIRS * LANES), lambda j, s: (0, j))
    table_spec = pl.BlockSpec((tokens, LANES), lambda j, s: (0, 0))
    return pl.pallas_call(
        functools.partial(attention_backward_kernel, per_kv),
        out_shape=(
            jax.ShapeDtypeStruct((tokens, width), BF16),
            jax.ShapeDtypeStruct((keys // tokens, tokens, kv_two), BF16),
        ),
        grid_spec=pltpu.PrefetchScalarGridSpec(
            num_scalar_prefetch=1,
            grid=(steps,),
            in_specs=[
                pair_spec,
                pair_spec,
                pair_spec,
                pl.BlockSpec((PAIRS, 2, tokens), lambda j, s: (j, 0, 0)),
                *key_value_specs(keys, per_kv),
                pl.BlockSpec((keys, tokens), lambda j, s: (0, 0)),
                table_spec,
                table_spec,
            ],
            out_specs=(
                pair_spec,
                pl.BlockSpec((keys // tokens, tokens, kv_two), lambda j, s: (0, 0, 0)),
            ),
            scratch_shapes=[pltpu.VMEM((2, keys, LANES), BF16)] * 2
            + [pltpu.VMEM((keys, LANES), F32)] * 2,
        ),
        compiler_params=pltpu.CompilerParams(
            dimension_semantics=("arbitrary",), vmem_limit_bytes=46 << 20
        ),
        cost_estimate=pl.CostEstimate(
            flops=10 * tokens * keys * width,
            transcendentals=tokens * keys * HEADS // 2,
            bytes_accessed=10 * tokens * width + 8 * keys * kv_two,
        ),
        name="attention_backward",
    )(span, query, grad, attended, lse, key_value, key_value, bias, cosines, sines)


CORE, ACROSS_X, ACROSS_Y = 1, 2, 4


def flip(array, mask):
    members = lax.axis_size("grp")
    return lax.ppermute(array, "grp", [(i, i ^ mask) for i in range(members)])


def flip_group(array):
    groups = lax.axis_size("rep")
    return lax.ppermute(array, "rep", [(i, i ^ 1) for i in range(groups)])


def gather_hidden_block(gate_up_weight, down_weight):
    rows = gate_up_weight.shape[0] // 4
    block = gate_up_weight.shape[1]
    member = lax.axis_index("grp")
    parity = lax.axis_index("rep") % 2
    own = [
        lax.dynamic_slice_in_dim(gate_up_weight, ((parity ^ (q // 2)) * 2 + q % 2) * rows, rows, 0)
        for q in range(4)
    ]

    def down_rows(mask):
        start = ((member ^ mask) % ACROSS_Y) * block
        return lax.dynamic_slice_in_dim(down_weight, start, block, 0)

    low, next_quarter, *near = yield (
        flip(own[0], ACROSS_Y),
        own[1],
        flip(down_rows(ACROSS_X), ACROSS_X),
        flip(down_rows(CORE), CORE),
        flip(down_rows(ACROSS_X | CORE), ACROSS_X | CORE),
    )
    down_own = jnp.stack([down_rows(0), near[1], near[0], near[2]])
    high, low_other, down_own = yield flip(next_quarter, ACROSS_Y), flip_group(low), down_own
    mine, second = (
        lax.dynamic_slice_in_dim(down_own, 2 * parity + index, 1, 0) for index in range(2)
    )
    down_mine, high_other, second = yield flip(mine, ACROSS_Y), flip_group(high), second
    down_second, down_other = yield flip(second, ACROSS_Y), flip_group(down_mine)
    (second_other,) = yield (flip_group(down_second),)
    return {
        "own": own,
        "over_y": (low, high, low_other, high_other),
        "down": (down_own, down_mine, down_second, down_other, second_other),
    }


def gather_key_values(own):
    over_y = flip(own, ACROSS_Y)
    pieces = [own, flip(own, ACROSS_X), over_y, flip(over_y, ACROSS_X)]
    return jnp.concatenate(
        [part for piece in pieces for part in (piece, flip(piece, CORE))], axis=0
    )


def tie(value, transfers):
    value, *transfers = lax.optimization_barrier((value, *transfers))
    return value, tuple(transfers)


def feed_forward_alone(norm2, sens, gate_up_full, down_full, small, seen):
    ffn_in, switch, lift, down_in, lower = small
    slots, hidden_width = switch.shape
    seen_two = jnp.concatenate([seen, seen], axis=1)
    latent_gu = (mm(norm2, ffn_in) * seen_two).astype(BF16)
    latent_g, latent_u = latent_gu[:, :slots], latent_gu[:, slots:]
    gate_up = mm(norm2, gate_up_full) + LOWRANK_FACTOR * jnp.concatenate(
        [mm(latent_g, switch), mm(latent_u, lift)], axis=1
    )
    gate = gate_up[:, :hidden_width]
    up = gate_up[:, hidden_width:]
    sigma = jax.nn.sigmoid(gate)
    act = (gate * sigma * up).astype(BF16)
    latent_d = (mm_nt(act, down_in) * seen).astype(BF16)
    response_part = mm(act, down_full) + LOWRANK_FACTOR * mm(latent_d, lower)
    dlat_d = (LOWRANK_FACTOR * mm_nt(sens, lower) * seen).astype(BF16)
    dact = mm_nt(sens, down_full) + mm(dlat_d, down_in)
    dgate = (dact * up * (sigma * (1.0 + gate * (1.0 - sigma)))).astype(BF16)
    dup = (dact * gate * sigma).astype(BF16)
    dlat_gu = (
        LOWRANK_FACTOR
        * jnp.concatenate([mm_nt(dgate, switch), mm_nt(dup, lift)], axis=1)
        * seen_two
    ).astype(BF16)
    dnorm2 = (
        mm_nt(dgate, gate_up_full[:, :hidden_width])
        + mm_nt(dup, gate_up_full[:, hidden_width:])
        + mm_nt(dlat_gu, ffn_in)
    )
    deep = jnp.concatenate(
        [
            mm_tn(dlat_d, act),
            LOWRANK_FACTOR * mm_tn(latent_g, dgate),
            LOWRANK_FACTOR * mm_tn(latent_u, dup),
        ],
        axis=0,
    ).astype(BF16)
    members = lax.axis_size("grp")
    deep = deep.reshape(3 * slots, members, hidden_width // members).transpose(1, 0, 2)
    return response_part, dnorm2, latent_d, dlat_gu, deep


def feed_forward_kernel(
    meta,
    own_x,
    near_x,
    own_g,
    near_g,
    own_seen,
    near_seen,
    lower_ref,
    switch_ref,
    lift_ref,
    in_ref,
    *refs,
):
    whole_refs, whole_down = refs[:8], refs[8:13]
    back_own, back_near, acts, deep_ref = refs[13:17]
    x_turned, g_turned, latents, dlats, stack, firsts, seconds, dacts, dlat_sum = refs[17:26]
    kept, kept_down, semaphores = refs[26:]
    count, width = own_g.shape
    tokens = 2 * count
    slots, block = in_ref.shape
    quarter = width // 4
    part = width // kept_down.shape[0]
    parity = meta[0]
    owns_gate = meta[1] == 1
    member = meta[2]
    starts = [
        pl.multiple_of((parity if q < 2 else 1 - parity) * (width // 2) + (q % 2) * quarter, quarter)
        for q in range(4)
    ]
    bases = [0, 1, 2, 3, *(4 + 2 * parity + k for k in (0, 1)), *(6 - 2 * parity + k for k in (0, 1))]
    columns = [pl.ds(pl.multiple_of((member ^ base) * part, part), part) for base in bases]
    down_copies = [
        pltpu.make_async_copy(ref, kept_down.at[pl.ds(start, size)], semaphores.at[8 + index])
        for index, (ref, start, size) in enumerate(zip(whole_down, (0, 4, 5, 6, 7), (4, 1, 1, 1, 1)))
    ]
    copies = [
        pltpu.make_async_copy(ref, kept.at[index], semaphores.at[index])
        for index, ref in enumerate(whole_refs)
    ]
    for copy in down_copies + copies:
        copy.start()
    dlat_sum[...] = jnp.zeros_like(dlat_sum)
    for index, (x_ref, g_ref, seen_ref) in enumerate(
        ((own_x, own_g, own_seen), (near_x, near_g, near_seen))
    ):
        rows = slice(index * count, (index + 1) * count)
        for q in range(4):
            x_turned[rows, q * quarter : (q + 1) * quarter] = x_ref[:, pl.ds(starts[q], quarter)]
        for k, lanes in enumerate(columns):
            g_turned[rows, k * part : (k + 1) * part] = g_ref[:, lanes]
        latents[rows, :] = x_ref[:, width : width + 2 * slots]
        dlat = LOWRANK_FACTOR * mm_nt(g_ref[...], lower_ref[...]) * seen_ref[...]
        dlats[rows, :] = dlat.astype(BF16)
        stack[:slots, rows] = dlat.T.astype(BF16)
        latent = x_ref[:, width : width + LANES].astype(F32).T[: 2 * slots]
        stack[slots:, rows] = latent.astype(BF16)

    def dact_part(start, size):
        here = pl.ds(start, size)
        down = jnp.concatenate([kept_down[k, here, :] for k in range(len(columns))], axis=1)
        dacts[:, here] = mm_nt(g_turned[...], down) + mm(dlats[...], in_ref[:, here])

    def dact_step(index, carry):
        dact_part(pl.multiple_of(index * 2 * LANES, 2 * LANES), 2 * LANES)
        return carry

    for copy in down_copies:
        copy.wait()
    lax.fori_loop(0, block // (2 * LANES), dact_step, 0)
    if block % (2 * LANES):
        dact_part(block // (2 * LANES) * 2 * LANES, block % (2 * LANES))
    for copy in copies:
        copy.wait()

    def hidden_part(start, size):
        here = pl.ds(start, size)
        none = jnp.zeros((slots, size), BF16)
        switch, lift = switch_ref[:, here], lift_ref[:, here]
        pieces = jnp.where(
            owns_gate,
            jnp.concatenate(
                [jnp.concatenate([switch, none], axis=1), jnp.concatenate([none, lift], axis=1)],
                axis=0,
            ),
            jnp.concatenate(
                [jnp.concatenate([none, switch], axis=1), jnp.concatenate([lift, none], axis=1)],
                axis=0,
            ),
        )
        weight = jnp.concatenate(
            [
                jnp.concatenate([kept[q, :, here], kept[4 + q, :, here]], axis=1)
                for q in range(4)
            ],
            axis=0,
        )
        total = mm(x_turned[...], weight)
        total = total + LOWRANK_FACTOR * mm(latents[...], pieces)
        gate = jnp.where(owns_gate, total[:, :size], total[:, size:])
        up = jnp.where(owns_gate, total[:, size:], total[:, :size])
        sigma = jax.nn.sigmoid(gate)
        act = (gate * sigma * up).astype(BF16)
        dact = dacts[:, here]
        dgate = (dact * up * (sigma * (1.0 + gate * (1.0 - sigma)))).astype(BF16)
        dup = (dact * gate * sigma).astype(BF16)
        dfirst, dsecond = jnp.where(owns_gate, dgate, dup), jnp.where(owns_gate, dup, dgate)
        acts[:, here] = act
        firsts[:, here] = dfirst
        seconds[:, here] = dsecond
        both = jnp.concatenate([dfirst, dsecond], axis=1)
        dlat_sum[:, : 2 * slots] += mm_nt(both, pieces)
        piece_grad = LOWRANK_FACTOR * mm(stack[slots:, :], both)
        low, high = piece_grad[:, :size], piece_grad[:, size:]
        deep_ref[:slots, here] = mm(stack[:slots, :], act)
        deep_ref[slots : 2 * slots, here] = jnp.where(owns_gate, low, high)[:slots]
        deep_ref[2 * slots :, here] = jnp.where(owns_gate, high, low)[slots:]

    def hidden_step(index, carry):
        hidden_part(pl.multiple_of(index * 2 * LANES, 2 * LANES), 2 * LANES)
        return carry

    lax.fori_loop(0, block // (2 * LANES), hidden_step, 0)
    if block % (2 * LANES):
        hidden_part(block // (2 * LANES) * 2 * LANES, block % (2 * LANES))

    def back(q, carry):
        value = mm_nt(firsts[...], kept[q]) + mm_nt(seconds[...], kept[4 + q])
        start = ((q // 2) ^ parity) * (width // 2) + lax.rem(q, 2) * quarter
        lanes = pl.ds(pl.multiple_of(start, quarter), quarter)
        back_own[:, lanes] = value[:count]
        back_near[:, lanes] = value[count:].astype(BF16)
        return carry

    lax.fori_loop(0, 4, back, 0)
    back_own[:, width:] = dlat_sum[:count, :]
    back_near[:, width:] = dlat_sum[count:, :].astype(BF16)


def down_kernel(meta, in_ref, *refs):
    acts_refs, whole_down = refs[:2], refs[2:7]
    results = (refs[7:9], refs[9:11])
    kept_down, semaphores = refs[11:]
    slots = in_ref.shape[0]
    parts, _, part = kept_down.shape
    width = parts * part
    parity, member = meta[0], meta[2]
    copies = [
        pltpu.make_async_copy(ref, kept_down.at[pl.ds(start, size)], semaphores.at[index])
        for index, (ref, start, size) in enumerate(zip(whole_down, (0, 4, 5, 6, 7), (4, 1, 1, 1, 1)))
    ]
    for copy in copies:
        copy.start()
    for acts, outs in zip(acts_refs, results):
        latent = mm_nt(acts[...], in_ref[...])
        pad = jnp.zeros((latent.shape[0], LANES - slots), F32)
        latent = jnp.concatenate([latent, pad], axis=1)
        for index, out in enumerate(outs):
            rows = slice(index * out.shape[0], (index + 1) * out.shape[0])
            out[:, width:] = latent[rows].astype(out.dtype)
    for copy in copies:
        copy.wait()

    def columns(index, carry):
        half = (index - 4) // 2 ^ parity
        base = jnp.where(index < 4, index, 4 + 2 * half + lax.rem(index, 2))
        lanes = pl.ds(pl.multiple_of((member ^ base) * part, part), part)
        for acts, outs in zip(acts_refs, results):
            value = mm(acts[...], kept_down[index])
            for side, out in enumerate(outs):
                rows = slice(side * out.shape[0], (side + 1) * out.shape[0])
                out[:, lanes] = value[rows].astype(out.dtype)
        return carry

    lax.fori_loop(0, parts, columns, 0)


def down_projection(meta, acts, down_in, weights):
    tokens, block = acts[0].shape
    slots = down_in.shape[0]
    width = 8 * weights["down"][0].shape[2]
    wide, count = width + LANES, tokens // 2
    kept = jax.ShapeDtypeStruct((count, wide), F32)
    sent = jax.ShapeDtypeStruct((count, wide), BF16)
    return pl.pallas_call(
        down_kernel,
        out_shape=(kept, sent, sent, sent),
        in_specs=[pl.BlockSpec(memory_space=pltpu.SMEM)]
        + [pl.BlockSpec(memory_space=pltpu.VMEM)] * 3
        + [pl.BlockSpec(memory_space=pl.ANY)] * 5,
        scratch_shapes=[
            pltpu.VMEM((8, block, width // 8), BF16),
            pltpu.SemaphoreType.DMA((5,)),
        ],
        compiler_params=pltpu.CompilerParams(vmem_limit_bytes=24 << 20),
        cost_estimate=pl.CostEstimate(
            flops=4 * tokens * width * block,
            transcendentals=0,
            bytes_accessed=2 * width * block + 8 * tokens * width,
        ),
        name="down_projection",
    )(meta, down_in, *acts, *weights["down"])


def feed_forward_pair(meta, rows, sens, seen, weights, pieces):
    count, width = sens[0].shape
    slots, block = pieces[-1].shape
    wide, tokens = width + LANES, 2 * count
    operands = (*rows, *sens, *seen, *pieces)
    arrays = (*weights["own"], *weights["over_y"], *weights["down"])
    return pl.pallas_call(
        feed_forward_kernel,
        out_shape=(
            jax.ShapeDtypeStruct((count, wide), F32),
            jax.ShapeDtypeStruct((count, wide), BF16),
            jax.ShapeDtypeStruct((tokens, block), BF16),
            jax.ShapeDtypeStruct((3 * slots, block), F32),
        ),
        in_specs=[pl.BlockSpec(memory_space=pltpu.SMEM)]
        + [pl.BlockSpec(memory_space=pltpu.VMEM)] * len(operands)
        + [pl.BlockSpec(memory_space=pl.ANY)] * len(arrays),
        scratch_shapes=[
            pltpu.VMEM((tokens, width), BF16),
            pltpu.VMEM((tokens, width), BF16),
            pltpu.VMEM((tokens, 2 * slots), BF16),
            pltpu.VMEM((tokens, slots), BF16),
            pltpu.VMEM((3 * slots, tokens), BF16),
            pltpu.VMEM((tokens, block), BF16),
            pltpu.VMEM((tokens, block), BF16),
            pltpu.VMEM((tokens, block), F32),
            pltpu.VMEM((tokens, LANES), F32),
            pltpu.VMEM((8, width // 4, block), BF16),
            pltpu.VMEM((8, block, width // 8), BF16),
            pltpu.SemaphoreType.DMA((13,)),
        ],
        compiler_params=pltpu.CompilerParams(vmem_limit_bytes=50 << 20),
        cost_estimate=pl.CostEstimate(
            flops=2 * 5 * tokens * width * block,
            transcendentals=tokens * block,
            bytes_accessed=6 * width * block + 20 * tokens * width,
        ),
        name="feed_forward",
    )(meta, *operands, *arrays)


def feed_forward_shared(norm2, sens_pairs, weights, small, all_seen):
    ffn_in, *pieces = small
    lower = pieces[0]
    width = norm2.shape[1]
    slots, block = pieces[-1].shape
    hidden_width = block * ACROSS_Y
    member = lax.axis_index("grp")
    parity = lax.axis_index("rep") % 2
    owns_gate = member < ACROSS_Y
    hidden = member % ACROSS_Y
    meta = jnp.stack([parity, owns_gate.astype(jnp.int32), member]).astype(jnp.int32)
    seen = all_seen[0]
    seen_two = jnp.concatenate([seen, seen], axis=1)
    latent_gu = (mm(norm2, ffn_in) * seen_two).astype(BF16)
    pad = jnp.zeros((norm2.shape[0], LANES - 2 * slots), BF16)
    rows = jnp.concatenate([norm2, latent_gu, pad], axis=1)
    across = flip(rows, ACROSS_X)
    results = []
    for index, sens_pair in enumerate(sens_pairs):
        if index == 1:
            result, (across,) = tie(results[0][1], (across,))
            results[0][1] = result
            rows = across
        seen_pair = all_seen[2 * index : 2 * index + 2]
        row_pair = (rows, flip(rows, CORE))
        results.append(
            list(feed_forward_pair(meta, row_pair, sens_pair, seen_pair, weights, pieces))
        )

    chips = [result[0] + flip(result[1], CORE).astype(F32) for result in results]
    deep = (results[0][3] + results[1][3]).astype(BF16)
    members = lax.axis_size("grp")
    owners = members * block // hidden_width
    deep = deep.reshape(3 * slots, owners, block // owners).transpose(1, 0, 2)
    placed = jnp.zeros((members, 3 * slots, block // owners), BF16)
    placed = lax.dynamic_update_slice_in_dim(placed, deep, hidden * owners, 0)
    forwards = down_projection(meta, [result[2] for result in results], pieces[-1], weights)
    across = flip(chips[1].astype(BF16), ACROSS_X)
    across, (placed, *forwards) = tie(across, (placed, *forwards))
    backward = chips[0] + across.astype(F32)
    dlat_gu = (LOWRANK_FACTOR * backward[:, width : width + 2 * slots] * seen_two).astype(BF16)
    dnorm2 = backward[:, :width] + mm_nt(dlat_gu, ffn_in)
    dnorm2, forwards = tie(dnorm2, forwards)
    forward = forwards[0]
    for part, mask in zip(forwards[1:], (CORE, ACROSS_X, ACROSS_X | CORE)):
        forward = forward + flip(part, mask).astype(F32)
    latent_d = (forward[:, width : width + slots] * seen).astype(BF16)
    response_part = forward[:, :width] + LOWRANK_FACTOR * mm(latent_d, lower)
    return response_part, dnorm2, latent_d, dlat_gu, placed


def exchange_sum(parts):
    received = lax.all_to_all(parts.astype(BF16), "grp", 0, 0, tiled=True)
    return jnp.sum(received.astype(F32), axis=0)


def simple_call(kernel, name, out_shape, operands, flops):
    return pl.pallas_call(
        kernel,
        out_shape=out_shape,
        compiler_params=pltpu.CompilerParams(vmem_limit_bytes=32 << 20),
        cost_estimate=pl.CostEstimate(
            flops=flops,
            transcendentals=0,
            bytes_accessed=sum(array.size * array.dtype.itemsize for array in operands),
        ),
        name=name,
    )(*operands)


def early_gradients_kernel(
    dq_ref,
    asking_ref,
    seen_ref,
    latent_q_ref,
    norm1_ref,
    latent_d_ref,
    sens_ref,
    dlat_gu_ref,
    norm2_ref,
    dlat_o_ref,
    attended_ref,
    latent_o_ref,
    dbranch_ref,
    dlat_q_ref,
    early_ref,
):
    dlat_q = (LOWRANK_FACTOR * mm_nt(dq_ref[...], asking_ref[...]) * seen_ref[...]).astype(BF16)
    dlat_q_ref[...] = dlat_q
    two = LOWRANK_FACTOR
    start = 0
    for factor, small, large in (
        (1.0, dlat_q, norm1_ref),
        (two, latent_q_ref[...], dq_ref),
        (two, latent_d_ref[...], sens_ref),
        (1.0, dlat_gu_ref[...], norm2_ref),
        (1.0, dlat_o_ref[...], attended_ref),
        (two, latent_o_ref[...], dbranch_ref),
    ):
        rows = small.shape[1]
        early_ref[start : start + rows, :] = (factor * mm_tn(small, large[...])).astype(BF16)
        start += rows


def early_gradients(*operands):
    count, width = operands[0].shape
    slots = operands[1].shape[0]
    return simple_call(
        early_gradients_kernel,
        "early_gradients",
        (
            jax.ShapeDtypeStruct((count, slots), BF16),
            jax.ShapeDtypeStruct((7 * slots, width), BF16),
        ),
        operands,
        2 * count * width * 8 * slots,
    )


def key_value_gradients_kernel(
    received_ref,
    early_ref,
    cos_ref,
    sin_ref,
    right_ref,
    seen_ref,
    latent_ref,
    norm_ref,
    dkv_ref,
    dlat_ref,
    pack_ref,
):
    half = HEAD_DIM // 2
    total = received_ref[0].astype(F32)
    for source in range(1, received_ref.shape[0]):
        total = total + received_ref[source].astype(F32)
    kv_width = total.shape[1] // 2
    pieces = []
    for start in range(0, kv_width, LANES):
        value = total[:, start : start + LANES]
        turned = value * sin_ref[...]
        first = lax.rem(lane_of(turned.shape), HEAD_DIM) < half
        turned = jnp.where(
            first, pltpu.roll(turned, LANES - half, 1), -pltpu.roll(turned, half, 1)
        )
        pieces.append((value * cos_ref[...] + turned).astype(BF16))
    dkv = jnp.concatenate([*pieces, total[:, kv_width:].astype(BF16)], axis=1)
    dkv_ref[...] = dkv
    dlat = (LOWRANK_FACTOR * mm_nt(dkv, right_ref[...]) * seen_ref[...]).astype(BF16)
    dlat_ref[...] = dlat
    late = mm_tn(dlat, norm_ref[...]).astype(BF16)
    thin = (LOWRANK_FACTOR * mm_tn(latent_ref[...], dkv)).astype(BF16)
    rows, head = late.shape[0], early_ref.shape[0]
    thin = jnp.concatenate([thin[: rows // 2, :kv_width], thin[rows // 2 :, kv_width:]], axis=0)
    share = pack_ref.shape[2]
    for target in range(pack_ref.shape[0]):
        columns = slice(target * share, (target + 1) * share)
        pack_ref[target, :head, :] = early_ref[:, columns]
        pack_ref[target, head : head + rows, :] = late[:, columns]
        for index, start in enumerate(range(0, kv_width, share)):
            place = head + (index + 1) * rows
            pack_ref[target, place : place + rows, :] = thin[:, start : start + share]


def key_value_gradients(received, early, cosines, sines, kv_right, seen_two, latent_kv, norm1):
    members, count, kv_two = received.shape
    rows = kv_right.shape[0]
    share = norm1.shape[1] // members
    packed = early.shape[0] + rows * (1 + kv_two // 2 // share)
    return simple_call(
        key_value_gradients_kernel,
        "key_value_gradients",
        (
            jax.ShapeDtypeStruct((count, kv_two), BF16),
            jax.ShapeDtypeStruct((count, rows), BF16),
            jax.ShapeDtypeStruct((members, packed, share), BF16),
        ),
        (received, early, cosines, sines, kv_right, seen_two, latent_kv, norm1),
        2 * count * rows * (norm1.shape[1] + 2 * kv_two),
    )


def place_kernel(jobs, groups, slots, *refs):
    place_ref, refs = refs[0], refs[1:]
    outs = refs[len(refs) - len(jobs) :]
    for (source, index, is_right), out_ref in zip(jobs, outs):
        value = jnp.concatenate(
            [
                refs[source * groups + g][index * slots : (index + 1) * slots, :]
                for g in range(groups)
            ],
            axis=0,
        )
        if is_right:
            out_ref[...] = mm_tn(place_ref[...], value)
        else:
            out_ref[...] = mm_tn(value, place_ref[...])


def place_gradients(place, sources, slots, jobs):
    groups = len(sources[0])
    narrow = place.shape[1]
    shapes = []
    for source, _, is_right in jobs:
        size = sources[source][0].shape[1]
        shapes.append(
            jax.ShapeDtypeStruct((narrow, size) if is_right else (size, narrow), F32)
        )
    return pl.pallas_call(
        functools.partial(place_kernel, jobs, groups, slots),
        out_shape=tuple(shapes),
        compiler_params=pltpu.CompilerParams(vmem_limit_bytes=32 << 20),
        cost_estimate=pl.CostEstimate(
            flops=2 * sum(shape.size for shape in shapes) * place.shape[0],
            transcendentals=0,
            bytes_accessed=4 * sum(shape.size for shape in shapes),
        ),
        name="place_gradients",
    )(place, *[array for source in sources for array in source])


def round_groups(array):
    groups = lax.axis_size("rep")
    return [array] + [
        lax.ppermute(array, "rep", [(i, (i + shift) % groups) for i in range(groups)])
        for shift in range(1, groups)
    ]


def shards(
    tokens,
    response_sensitivity,
    seq_lengths,
    prefix_lengths,
    adapter_ids,
    attn_gain,
    mlp_gain,
    qkv_weight,
    out_weight,
    gate_up_weight,
    down_weight,
    query_in,
    asking_right_pieces,
    key_in,
    lookup_right_pieces,
    value_in,
    content_right_pieces,
    output_in,
    final_right_pieces,
    gate_in,
    switch_right_pieces,
    up_in,
    lift_right_pieces,
    down_in,
    lower_right_pieces,
):
    count, width = tokens.shape
    members = lax.axis_size("grp")
    groups = lax.axis_size("rep")
    kv_width = lookup_right_pieces.shape[1]
    narrow = query_in.shape[1]
    group = lax.axis_index("rep")
    member = lax.axis_index("grp")
    lengths = lax.dynamic_slice_in_dim(seq_lengths, 2 * group, 2)
    prefixes = lax.dynamic_slice_in_dim(prefix_lengths, 2 * group, 2)
    chosen_ids = lax.dynamic_slice_in_dim(adapter_ids, 2 * group, 2)
    key_count = count * members
    sens = response_sensitivity

    paired = members == 8 and groups % 2 == 0
    qkv_full = lax.all_gather(qkv_weight, "grp", axis=1, tiled=True)
    if paired:
        steps = gather_hidden_block(gate_up_weight, down_weight)
        transfers = next(steps)
    else:
        out_full = lax.all_gather(out_weight, "grp", axis=1, tiled=True)
        down_full = lax.all_gather(down_weight, "grp", axis=1, tiled=True)
        gate_up_full = lax.all_gather(gate_up_weight, "grp", axis=1, tiled=True)

    turn = member if paired else 0
    key_index = jnp.arange(key_count, dtype=jnp.int32)
    key_index = (key_index // count ^ turn) * count + key_index % count
    key_second = (key_index >= lengths[0]).astype(jnp.int32)
    key_position = key_index - key_second * lengths[0]
    own_index = member * count + jnp.arange(count, dtype=jnp.int32)
    own_second = (own_index >= lengths[0]).astype(jnp.int32)
    position = own_index - own_second * lengths[0]
    prefix = jnp.where(own_second == 0, prefixes[0], prefixes[1])
    allowed = (key_second[:, None] == own_second[None, :]) & (
        (key_position[:, None] <= position[None, :]) | (key_position[:, None] < prefix[None, :])
    )
    bias = jnp.where(allowed, 0.0, MASKED).astype(F32)
    first_key = own_second[0] * lengths[0]
    last_key = jnp.max(own_second * lengths[0] + jnp.maximum(position, prefix - 1))
    span = jnp.stack(
        [first_key // KEY_BLOCK, last_key // KEY_BLOCK + 1, turn * count // KEY_BLOCK, turn]
    ).astype(jnp.int32)

    slots = 2 * RANK
    columns = jnp.arange(narrow, dtype=jnp.int32)
    slot = jnp.arange(slots, dtype=jnp.int32)
    slot_column = jnp.where(slot < RANK, chosen_ids[0], chosen_ids[1]) * RANK + slot % RANK
    pick = (columns[:, None] == slot_column[None, :]).astype(BF16)

    def seen_by(device):
        index = device * count + jnp.arange(count, dtype=jnp.int32)
        second = (index >= lengths[0]).astype(jnp.int32)
        return (second[:, None] == slot[None, :] // RANK).astype(F32)

    def pick_in(weight):
        return mm(weight, pick).astype(BF16)

    def pick_right(weight):
        return mm_tn(pick, weight).astype(BF16)

    seen = seen_by(member)
    seen_three = jnp.concatenate([seen, seen, seen], axis=1)
    qkv_in = jnp.concatenate([pick_in(query_in), pick_in(key_in), pick_in(value_in)], axis=1)
    asking = pick_right(asking_right_pieces)
    lookup = pick_right(lookup_right_pieces)
    content = pick_right(content_right_pieces)
    none = jnp.zeros_like(lookup)
    kv_right = jnp.concatenate(
        [jnp.concatenate([lookup, none], axis=1), jnp.concatenate([none, content], axis=1)], axis=0
    )
    out_in = pick_in(output_in)
    final = pick_right(final_right_pieces)
    lower = pick_right(lower_right_pieces)
    small = (
        jnp.concatenate([pick_in(gate_in), pick_in(up_in)], axis=1),
        pick_right(switch_right_pieces),
        pick_right(lift_right_pieces),
        lax.dot_general(
            pick, down_in, (((0,), (1,)), ((), ())), preferred_element_type=F32
        ).astype(BF16),
        lower,
    )

    cycle = jnp.arange(groups * slots, dtype=jnp.int32)
    source = (group - cycle // slots) % groups
    sequence = 2 * source + cycle % slots // RANK
    sequences = jnp.arange(adapter_ids.shape[0], dtype=jnp.int32)
    theirs = jnp.where(sequence[:, None] == sequences[None, :], adapter_ids[None, :], 0)
    all_column = jnp.sum(theirs, axis=1) * RANK + cycle % RANK
    place = (all_column[:, None] == columns[None, :]).astype(BF16)
    incoming = tokens.astype(F32)
    scale_one = inverse_rms(incoming)
    norm1 = (incoming * scale_one * attn_gain).astype(BF16)
    if paired:
        block = down_weight.shape[0] // ACROSS_Y
        start = member % ACROSS_Y * block
        pieces = [lax.dynamic_slice_in_dim(piece, start, block, 1) for piece in small[1:4]]
        others = (seen_by(member ^ mask) for mask in (CORE, ACROSS_X, ACROSS_X | CORE))
        ready = (*transfers, asking, kv_right, out_in, final, lower, place, small[0], *pieces)
        norm1, ready = tie(norm1, (*ready, *others))
        transfers = ready[: len(transfers)]
        asking, kv_right, out_in, final, lower, place, ffn_in, *ready = ready[len(transfers) :]
        small = (ffn_in, lower, *ready[:3])
        all_seen = (seen, *ready[3:])
        transfers = steps.send(transfers)
        out_full = lax.all_gather(out_weight, "grp", axis=1, tiled=True)
    latent_qkv = (mm(norm1, qkv_in) * seen_three).astype(BF16)
    latent_q, latent_kv = latent_qkv[:, :slots], latent_qkv[:, slots:]
    half = HEAD_DIM // 2
    freqs = 10000.0 ** (-2.0 * jnp.arange(half).astype(F32) / HEAD_DIM)
    freqs = jnp.tile(freqs, LANES // half)
    angles = position.astype(F32)[:, None] * freqs[None, :]
    cosines, sines = jnp.cos(angles), jnp.sin(angles)

    def widen(table, size):
        return jnp.tile(table, (1, size // LANES))

    qkv = mm(norm1, qkv_full)
    query = qkv[:, :width] + LOWRANK_FACTOR * mm(latent_q, asking)
    own_kv = qkv[:, width:] + LOWRANK_FACTOR * mm(latent_kv, kv_right)
    query = rotate(query, widen(cosines, width), widen(sines, width)).astype(BF16)
    query = query * jnp.asarray(HEAD_DIM**-0.5, BF16)
    key_own = rotate(own_kv[:, :kv_width], widen(cosines, kv_width), widen(sines, kv_width))
    key_value = jnp.concatenate([key_own, own_kv[:, kv_width:]], axis=1).astype(BF16)
    if paired:
        key_value, transfers = tie(key_value, transfers)
        key_value, (ready, *transfers) = tie(gather_key_values(key_value), (sens, *transfers))
        transfers = steps.send(transfers)
        sens_near, sens_across = flip(ready, CORE), flip(ready, ACROSS_X)
    else:
        key_value = lax.all_gather(key_value, "grp", axis=0, tiled=True)
    attended_low, lse = attention_forward(span, query, key_value, bias)
    if paired:
        attended_low, (sens_near, sens_across, *transfers) = tie(
            attended_low, (sens_near, sens_across, *transfers)
        )
        out_full, (sens_last, *transfers) = tie(
            out_full, (flip(sens_across, CORE), *steps.send(transfers))
        )
        sens_pairs = [(sens, sens_near), (sens_across, sens_last)]
        transfers = steps.send(transfers)

    latent_o = (mm(attended_low, out_in) * seen).astype(BF16)
    stream = incoming + (mm(attended_low, out_full) + LOWRANK_FACTOR * mm(latent_o, final))
    scale_two = inverse_rms(stream)
    norm2 = (stream * scale_two * mlp_gain).astype(BF16)
    if paired:
        norm2, transfers = tie(norm2, transfers)
        try:
            steps.send(transfers)
        except StopIteration as stop:
            weights = stop.value
        response_part, dnorm2, latent_d, dlat_gu, deep = feed_forward_shared(
            norm2, sens_pairs, weights, small, all_seen
        )
    else:
        response_part, dnorm2, latent_d, dlat_gu, deep = feed_forward_alone(
            norm2, sens, gate_up_full, down_full, small, seen
        )
    level_response = (stream + response_part).astype(BF16)
    dhidden = sens.astype(F32) + norm_backward(stream, scale_two, mlp_gain, dnorm2)
    dbranch = dhidden.astype(BF16)
    dlat_o = (LOWRANK_FACTOR * mm_nt(dbranch, final) * seen).astype(BF16)
    dattended = (mm_nt(dbranch, out_full) + mm_nt(dlat_o, out_in)).astype(BF16)

    dattended, (deep,) = tie(dattended, (deep,))
    deep_sum = lax.psum_scatter(deep, "grp", scatter_dimension=0, tiled=True)[0]

    dq, dkv_all = attention_backward(
        span, query, dattended, attended_low, lse, key_value, bias, cosines, sines
    )
    dkv_all, (deep_sum,) = tie(dkv_all, (deep_sum,))
    received = lax.all_to_all(dkv_all, "grp", 0, 0, tiled=True)
    dlat_q, early = early_gradients(
        dq,
        asking,
        seen,
        latent_q,
        norm1,
        latent_d,
        sens,
        dlat_gu,
        norm2,
        dlat_o,
        attended_low,
        latent_o,
        dbranch,
    )
    dnorm_q = mm_nt(dq, qkv_full[:, :width]) + mm_nt(dlat_q, qkv_in[:, :slots])
    dkv, dlat_kv, late = key_value_gradients(
        received, early, cosines, sines, kv_right, seen_three[:, : 2 * slots], latent_kv, norm1
    )
    deep_sum = round_groups(deep_sum)
    late_sum = round_groups(exchange_sum(late).astype(BF16))
    dnorm1 = dnorm_q + mm_nt(dkv, qkv_full[:, width:]) + mm_nt(dlat_kv, qkv_in[:, slots:])
    input_grad = (dhidden + norm_backward(incoming, scale_one, attn_gain, dnorm1)).astype(BF16)

    share = width // members
    pieces = kv_width // share
    thin_start = 9 * slots
    thin_sum = [
        jnp.concatenate(
            [
                array[thin_start + 2 * slots * i : thin_start + 2 * slots * (i + 1)]
                for i in range(pieces)
            ],
            axis=1,
        )
        for array in late_sum
    ]
    jobs = (
        (0, 0, False),
        (0, 1, True),
        (0, 7, False),
        (2, 0, True),
        (0, 8, False),
        (2, 1, True),
        (0, 5, False),
        (0, 6, True),
        (0, 3, False),
        (1, 1, True),
        (0, 4, False),
        (1, 2, True),
        (1, 0, False),
        (0, 2, True),
    )
    grads = list(place_gradients(place, (late_sum, deep_sum, thin_sum), slots, jobs))
    own = kv_width // members
    for index in (3, 5):
        grads[index] = lax.dynamic_slice_in_dim(grads[index], member * own, own, 1)
    return (level_response, input_grad, *grads)


def solution(mesh):
    rows = P(("rep", "grp"), None)
    split = P(None, "grp")
    in_specs = (rows, rows, *[P()] * 5, *[split] * 4, *[P()] * 14)
    out_specs = (rows, rows, *[P("grp", None), P(None, "grp")] * 7)
    return jax.shard_map(shards, mesh=mesh, in_specs=in_specs, out_specs=out_specs, check_vma=False)
```

```python
import functools

import jax
import jax.numpy as jnp
from jax import lax
from jax.experimental import pallas as pl
from jax.experimental.pallas import tpu as pltpu
from jax.sharding import PartitionSpec as P

HEADS = 32
KV_HEADS = 4
HEAD_DIM = 64
RANK = 16
LANES = 128
KEY_BLOCK = 1024
PAIRS = 4

EPS = 1e-05
LOWRANK_FACTOR = 2.0
MASKED = -1e30
F32 = jnp.float32
BF16 = jnp.bfloat16


def mm(left, right):
    return jnp.dot(left, right, preferred_element_type=F32)


def mm_nt(left, right):
    return lax.dot_general(left, right, (((1,), (1,)), ((), ())), preferred_element_type=F32)


def mm_tn(left, right):
    return lax.dot_general(left, right, (((0,), (0,)), ((), ())), preferred_element_type=F32)


def inverse_rms(value):
    return lax.rsqrt(jnp.mean(value * value, axis=-1, keepdims=True) + EPS)


def norm_backward(value, scale, gain, grad):
    scaled = gain * grad
    return scale * scaled - value * (scale * scale * scale) * jnp.mean(
        scaled * value, axis=-1, keepdims=True
    )


def half_turn(value):
    half = HEAD_DIM // 2
    lane = lax.broadcasted_iota(jnp.int32, value.shape, 1) % HEAD_DIM
    return jnp.where(
        lane < half, -jnp.roll(value, -half, axis=1), jnp.roll(value, half, axis=1)
    )


def rotate(value, cosines, sines):
    return value * cosines + half_turn(value) * sines


def unrotate(grad, cosines, sines):
    return grad * cosines - half_turn(grad * sines)


def lane_of(shape):
    return lax.broadcasted_iota(jnp.int32, shape, 1)


def key_rows(span, index):
    return pl.ds(pl.multiple_of((index ^ span[2]) * KEY_BLOCK, KEY_BLOCK), KEY_BLOCK)


def spread_heads(span, odd, source_ref, pair_ref):
    def step(index, carry):
        rows = key_rows(span, index)
        value = source_ref[rows, :].astype(F32)
        turned = pltpu.roll(value, HEAD_DIM, 1)
        low = lane_of(value.shape) < HEAD_DIM
        none = jnp.zeros_like(value)
        pair_ref[0, rows, :] = jnp.where(low, jnp.where(odd, turned, value), none).astype(BF16)
        pair_ref[1, rows, :] = jnp.where(low, none, jnp.where(odd, value, turned)).astype(BF16)
        return carry

    lax.fori_loop(span[0], span[1], step, 0)


def attention_forward_kernel(
    per_kv, span, q_ref, key_ref, value_ref, bias_ref, out_ref, lse_ref, k_ref, v_ref
):
    tokens = q_ref.shape[0]
    odd = lax.rem(pl.program_id(0) // per_kv, LANES // HEAD_DIM) == 1

    @pl.when(lax.rem(pl.program_id(0), per_kv) == 0)
    def _():
        spread_heads(span, odd, key_ref, k_ref)
        spread_heads(span, odd, value_ref, v_ref)

    queries = [q_ref[:, pair * LANES : (pair + 1) * LANES] for pair in range(PAIRS)]

    def step(index, carry):
        rows = key_rows(span, index)
        bias = bias_ref[rows, :]
        new = []
        flat = jnp.concatenate([v_ref[0, rows, :], v_ref[1, rows, :]], axis=0).T
        for pair, (peaks, totals, mixed) in enumerate(carry):
            tops, sums, parts, decays = [], [], [], []
            for side in range(2):
                scores = mm_nt(k_ref[side, rows, :], queries[pair]) + bias
                top = jnp.maximum(peaks[side], jnp.max(scores, axis=0, keepdims=True))
                decay = jnp.exp(peaks[side] - top)
                probs = jnp.exp(scores - top)
                tops.append(top)
                sums.append(totals[side] * decay + jnp.sum(probs, axis=0, keepdims=True))
                decays.append(jnp.broadcast_to(decay, (HEAD_DIM, tokens)))
                parts.append(probs.astype(BF16))
            mixed = mixed * jnp.concatenate(decays, axis=0)
            mixed = mixed + mm(flat, jnp.concatenate(parts, axis=0))
            new.append((tuple(tops), tuple(sums), mixed))
        return tuple(new)

    low = jnp.full((1, tokens), MASKED, F32)
    none = jnp.zeros((1, tokens), F32)
    start = ((low, low), (none, none), jnp.zeros((LANES, tokens), F32))
    result = lax.fori_loop(span[0], span[1], step, (start,) * PAIRS)
    for pair, (peaks, totals, mixed) in enumerate(result):
        weight = jnp.concatenate(
            [jnp.broadcast_to(1.0 / total, (HEAD_DIM, tokens)) for total in totals], axis=0
        )
        out_ref[:, pair * LANES : (pair + 1) * LANES] = (mixed * weight).T.astype(BF16)
        lse_ref[pair] = jnp.concatenate(
            [peak + jnp.log(total) for peak, total in zip(peaks, totals)], axis=0
        )


def key_value_specs(keys, per_kv):
    blocks = KV_HEADS * HEAD_DIM // LANES
    heads = LANES // HEAD_DIM
    return [
        pl.BlockSpec((keys, LANES), lambda j, s: (0, j // per_kv // heads)),
        pl.BlockSpec((keys, LANES), lambda j, s: (0, blocks + j // per_kv // heads)),
    ]


def attention_forward(span, query, key_value, bias):
    tokens, width = query.shape
    keys = bias.shape[0]
    pairs = width // LANES
    steps = pairs // PAIRS
    pair_spec = pl.BlockSpec((tokens, PAIRS * LANES), lambda j, s: (0, j))
    return pl.pallas_call(
        functools.partial(attention_forward_kernel, steps // KV_HEADS),
        out_shape=(
            jax.ShapeDtypeStruct((tokens, width), BF16),
            jax.ShapeDtypeStruct((pairs, 2, tokens), F32),
        ),
        grid_spec=pltpu.PrefetchScalarGridSpec(
            num_scalar_prefetch=1,
            grid=(steps,),
            in_specs=[
                pair_spec,
                *key_value_specs(keys, steps // KV_HEADS),
                pl.BlockSpec((keys, tokens), lambda j, s: (0, 0)),
            ],
            out_specs=(pair_spec, pl.BlockSpec((PAIRS, 2, tokens), lambda j, s: (j, 0, 0))),
            scratch_shapes=[pltpu.VMEM((2, keys, LANES), BF16)] * 2,
        ),
        compiler_params=pltpu.CompilerParams(
            dimension_semantics=("arbitrary",), vmem_limit_bytes=30 << 20
        ),
        cost_estimate=pl.CostEstimate(
            flops=4 * tokens * keys * width,
            transcendentals=tokens * keys * HEADS // 2,
            bytes_accessed=4 * tokens * width + 16 * keys * LANES * KV_HEADS,
        ),
        name="attention_forward",
    )(span, query, key_value, key_value, bias)


def attention_backward_kernel(
    per_kv,
    span,
    q_ref,
    do_ref,
    o_ref,
    lse_ref,
    key_ref,
    value_ref,
    bias_ref,
    cos_ref,
    sin_ref,
    dq_ref,
    even_ref,
    odd_ref,
    k_ref,
    v_ref,
    dk_sum,
    dv_sum,
):
    tokens = q_ref.shape[0]
    member = lax.rem(pl.program_id(0), per_kv)
    odd = lax.rem(pl.program_id(0) // per_kv, LANES // HEAD_DIM) == 1

    @pl.when(member == 0)
    def _():
        spread_heads(span, odd, key_ref, k_ref)
        spread_heads(span, odd, value_ref, v_ref)
        dk_sum[...] = jnp.zeros_like(dk_sum)
        dv_sum[...] = jnp.zeros_like(dv_sum)

    low = lane_of((tokens, LANES)) < HEAD_DIM
    row = lax.broadcasted_iota(jnp.int32, (8, LANES), 0)
    column = lax.broadcasted_iota(jnp.int32, (8, LANES), 1)
    chooser = jnp.where(row == column // HEAD_DIM, 1.0, 0.0).astype(F32)
    queries, grads, deltas, query_stack, grad_stack = [], [], [], [], []
    for pair in range(PAIRS):
        lanes = slice(pair * LANES, (pair + 1) * LANES)
        query, grad = q_ref[:, lanes], do_ref[:, lanes]
        none = jnp.zeros_like(query)
        queries.append(query)
        grads.append(grad)
        query_stack += [jnp.where(low, query, none), jnp.where(low, none, query)]
        grad_stack += [jnp.where(low, grad, none), jnp.where(low, none, grad)]
        deltas.append(
            lax.dot_general(
                chooser,
                grad.astype(F32) * o_ref[:, lanes].astype(F32),
                (((1,), (1,)), ((), ())),
                precision=lax.Precision.HIGHEST,
                preferred_element_type=F32,
            )
        )
    query_stack = jnp.concatenate(query_stack, axis=0)
    grad_stack = jnp.concatenate(grad_stack, axis=0)

    def step(index, dqueries):
        rows = key_rows(span, index)
        bias = bias_ref[rows, :]
        all_probs, all_dscores, new = [], [], []
        flat = jnp.concatenate([k_ref[0, rows, :], k_ref[1, rows, :]], axis=0).T
        for pair, dquery in enumerate(dqueries):
            for side in range(2):
                scores = mm_nt(k_ref[side, rows, :], queries[pair]) + bias
                probs = jnp.exp(scores - lse_ref[pair, side : side + 1, :])
                dprobs = mm_nt(v_ref[side, rows, :], grads[pair])
                delta = deltas[pair][side : side + 1, :]
                dscores = (probs * (dprobs - delta)).astype(BF16)
                all_probs.append(probs.astype(BF16))
                all_dscores.append(dscores)
            new.append(dquery + mm(flat, jnp.concatenate(all_dscores[-2:], axis=0)))
        dk_sum[rows, :] += mm(jnp.concatenate(all_dscores, axis=1), query_stack)
        dv_sum[rows, :] += mm(jnp.concatenate(all_probs, axis=1), grad_stack)
        return tuple(new)

    dqueries = lax.fori_loop(
        span[0], span[1], step, (jnp.zeros((LANES, tokens), F32),) * PAIRS
    )
    half = HEAD_DIM // 2
    for pair, dquery in enumerate(dqueries):
        dquery = dquery.T * (HEAD_DIM**-0.5)
        turned = dquery * sin_ref[...]
        first = lax.rem(lane_of(turned.shape), HEAD_DIM) < half
        turned = jnp.where(
            first, pltpu.roll(turned, LANES - half, 1), -pltpu.roll(turned, half, 1)
        )
        dq_ref[:, pair * LANES : (pair + 1) * LANES] = (dquery * cos_ref[...] + turned).astype(BF16)

    @pl.when(member == per_kv - 1)
    def _():
        block = pl.program_id(0) // per_kv // (LANES // HEAD_DIM)

        def put(index, carry):
            for side, out_ref in enumerate((even_ref, odd_ref)):
                rows = pl.ds(pl.multiple_of((2 * index + side) * tokens, tokens), tokens)
                for sum_ref, first in ((dk_sum, 0), (dv_sum, KV_HEADS * HEAD_DIM // LANES)):
                    total = sum_ref[rows, :]
                    total = total + pltpu.roll(total, HEAD_DIM, 1)
                    keep = jnp.logical_and(odd, lane_of(total.shape) < HEAD_DIM)
                    lanes = pl.ds(pl.multiple_of((first + block) * LANES, LANES), LANES)
                    out_ref[index, :, lanes] = jnp.where(
                        keep, out_ref[index, :, lanes], total.astype(BF16)
                    )
            return carry

        lax.fori_loop(0, even_ref.shape[0], put, 0)


def attention_backward(span, query, grad, attended, lse, key_value, bias, cosines, sines):
    tokens, width = query.shape
    keys, kv_two = key_value.shape
    pairs = width // LANES
    steps = pairs // PAIRS
    per_kv = steps // KV_HEADS
    pair_spec = pl.BlockSpec((tokens, PAIRS * LANES), lambda j, s: (0, j))
    table_spec = pl.BlockSpec((tokens, LANES), lambda j, s: (0, 0))
    return pl.pallas_call(
        functools.partial(attention_backward_kernel, per_kv),
        out_shape=(
            jax.ShapeDtypeStruct((tokens, width), BF16),
            *[jax.ShapeDtypeStruct((keys // tokens // 2, tokens, kv_two), BF16)] * 2,
        ),
        grid_spec=pltpu.PrefetchScalarGridSpec(
            num_scalar_prefetch=1,
            grid=(steps,),
            in_specs=[
                pair_spec,
                pair_spec,
                pair_spec,
                pl.BlockSpec((PAIRS, 2, tokens), lambda j, s: (j, 0, 0)),
                *key_value_specs(keys, per_kv),
                pl.BlockSpec((keys, tokens), lambda j, s: (0, 0)),
                table_spec,
                table_spec,
            ],
            out_specs=(
                pair_spec,
                *[pl.BlockSpec((keys // tokens // 2, tokens, kv_two), lambda j, s: (0, 0, 0))] * 2,
            ),
            scratch_shapes=[pltpu.VMEM((2, keys, LANES), BF16)] * 2
            + [pltpu.VMEM((keys, LANES), F32)] * 2,
        ),
        compiler_params=pltpu.CompilerParams(
            dimension_semantics=("arbitrary",), vmem_limit_bytes=46 << 20
        ),
        cost_estimate=pl.CostEstimate(
            flops=10 * tokens * keys * width,
            transcendentals=tokens * keys * HEADS // 2,
            bytes_accessed=10 * tokens * width + 8 * keys * kv_two,
        ),
        name="attention_backward",
    )(span, query, grad, attended, lse, key_value, key_value, bias, cosines, sines)


CORE, ACROSS_X, ACROSS_Y = 1, 2, 4


def flip(array, mask):
    members = lax.axis_size("grp")
    return lax.ppermute(array, "grp", [(i, i ^ mask) for i in range(members)])


def flip_group(array):
    groups = lax.axis_size("rep")
    return lax.ppermute(array, "rep", [(i, i ^ 1) for i in range(groups)])


def gather_hidden_block(gate_up_weight, down_weight):
    rows = gate_up_weight.shape[0] // 4
    block = gate_up_weight.shape[1]
    member = lax.axis_index("grp")
    parity = lax.axis_index("rep") % 2
    own = [
        lax.dynamic_slice_in_dim(gate_up_weight, ((parity ^ (q // 2)) * 2 + q % 2) * rows, rows, 0)
        for q in range(4)
    ]

    def down_rows(mask):
        start = ((member ^ mask) % ACROSS_Y) * block
        return lax.dynamic_slice_in_dim(down_weight, start, block, 0)

    low, next_quarter, *near = yield (
        flip(own[0], ACROSS_Y),
        own[1],
        flip(down_rows(ACROSS_X), ACROSS_X),
        flip(down_rows(CORE), CORE),
        flip(down_rows(ACROSS_X | CORE), ACROSS_X | CORE),
    )
    down_own = jnp.stack([down_rows(0), near[1], near[0], near[2]])
    high, low_other, down_own = yield flip(next_quarter, ACROSS_Y), flip_group(low), down_own
    mine, second = (
        lax.dynamic_slice_in_dim(down_own, 2 * parity + index, 1, 0) for index in range(2)
    )
    down_mine, high_other, second = yield flip(mine, ACROSS_Y), flip_group(high), second
    down_second, down_other = yield flip(second, ACROSS_Y), flip_group(down_mine)
    (second_other,) = yield (flip_group(down_second),)
    return {
        "own": own,
        "over_y": (low, high, low_other, high_other),
        "down": (down_own, down_mine, down_second, down_other, second_other),
    }


def gather_key_values(own):
    over_y = flip(own, ACROSS_Y)
    pieces = [own, flip(own, ACROSS_X), over_y, flip(over_y, ACROSS_X)]
    return jnp.concatenate(
        [part for piece in pieces for part in (piece, flip(piece, CORE))], axis=0
    )


def tie(value, transfers):
    value, *transfers = lax.optimization_barrier((value, *transfers))
    return value, tuple(transfers)


def feed_forward_alone(norm2, sens, gate_up_full, down_full, small, seen):
    ffn_in, switch, lift, down_in, lower = small
    slots, hidden_width = switch.shape
    seen_two = jnp.concatenate([seen, seen], axis=1)
    latent_gu = (mm(norm2, ffn_in) * seen_two).astype(BF16)
    latent_g, latent_u = latent_gu[:, :slots], latent_gu[:, slots:]
    gate_up = mm(norm2, gate_up_full) + LOWRANK_FACTOR * jnp.concatenate(
        [mm(latent_g, switch), mm(latent_u, lift)], axis=1
    )
    gate = gate_up[:, :hidden_width]
    up = gate_up[:, hidden_width:]
    sigma = jax.nn.sigmoid(gate)
    act = (gate * sigma * up).astype(BF16)
    latent_d = (mm_nt(act, down_in) * seen).astype(BF16)
    response_part = mm(act, down_full) + LOWRANK_FACTOR * mm(latent_d, lower)
    dlat_d = (LOWRANK_FACTOR * mm_nt(sens, lower) * seen).astype(BF16)
    dact = mm_nt(sens, down_full) + mm(dlat_d, down_in)
    dgate = (dact * up * (sigma * (1.0 + gate * (1.0 - sigma)))).astype(BF16)
    dup = (dact * gate * sigma).astype(BF16)
    dlat_gu = (
        LOWRANK_FACTOR
        * jnp.concatenate([mm_nt(dgate, switch), mm_nt(dup, lift)], axis=1)
        * seen_two
    ).astype(BF16)
    dnorm2 = (
        mm_nt(dgate, gate_up_full[:, :hidden_width])
        + mm_nt(dup, gate_up_full[:, hidden_width:])
        + mm_nt(dlat_gu, ffn_in)
    )
    deep = jnp.concatenate(
        [
            mm_tn(dlat_d, act),
            LOWRANK_FACTOR * mm_tn(latent_g, dgate),
            LOWRANK_FACTOR * mm_tn(latent_u, dup),
        ],
        axis=0,
    ).astype(BF16)
    members = lax.axis_size("grp")
    deep = deep.reshape(3 * slots, members, hidden_width // members).transpose(1, 0, 2)
    return (lambda shares: shares[0], (response_part,)), dnorm2, latent_d, dlat_gu, deep


def feed_forward_kernel(
    meta,
    own_x,
    near_x,
    own_g,
    near_g,
    own_seen,
    near_seen,
    lower_ref,
    switch_ref,
    lift_ref,
    in_ref,
    *refs,
):
    whole_refs, whole_down = refs[:8], refs[8:13]
    back_own, back_near, acts, deep_ref = refs[13:17]
    x_turned, g_turned, latents, dlats, stack, firsts, seconds, dacts, dlat_sum = refs[17:26]
    kept, kept_down, semaphores = refs[26:]
    count, width = own_g.shape
    tokens = 2 * count
    slots, block = in_ref.shape
    quarter = width // 4
    part = width // kept_down.shape[0]
    parity = meta[0]
    owns_gate = meta[1] == 1
    member = meta[2]
    starts = [
        pl.multiple_of((parity if q < 2 else 1 - parity) * (width // 2) + (q % 2) * quarter, quarter)
        for q in range(4)
    ]
    bases = [0, 1, 2, 3, *(4 + 2 * parity + k for k in (0, 1)), *(6 - 2 * parity + k for k in (0, 1))]
    columns = [pl.ds(pl.multiple_of((member ^ base) * part, part), part) for base in bases]
    down_copies = [
        pltpu.make_async_copy(ref, kept_down.at[pl.ds(start, size)], semaphores.at[8 + index])
        for index, (ref, start, size) in enumerate(zip(whole_down, (0, 4, 5, 6, 7), (4, 1, 1, 1, 1)))
    ]
    copies = [
        pltpu.make_async_copy(ref, kept.at[index], semaphores.at[index])
        for index, ref in enumerate(whole_refs)
    ]
    for copy in down_copies + copies:
        copy.start()
    dlat_sum[...] = jnp.zeros_like(dlat_sum)
    for index, (x_ref, g_ref, seen_ref) in enumerate(
        ((own_x, own_g, own_seen), (near_x, near_g, near_seen))
    ):
        rows = slice(index * count, (index + 1) * count)
        for q in range(4):
            x_turned[rows, q * quarter : (q + 1) * quarter] = x_ref[:, pl.ds(starts[q], quarter)]
        for k, lanes in enumerate(columns):
            g_turned[rows, k * part : (k + 1) * part] = g_ref[:, lanes]
        latents[rows, :] = x_ref[:, width : width + 2 * slots]
        dlat = LOWRANK_FACTOR * mm_nt(g_ref[...], lower_ref[...]) * seen_ref[...]
        dlats[rows, :] = dlat.astype(BF16)
        stack[:slots, rows] = dlat.T.astype(BF16)
        latent = x_ref[:, width : width + LANES].astype(F32).T[: 2 * slots]
        stack[slots:, rows] = latent.astype(BF16)

    def dact_part(start, size):
        here = pl.ds(start, size)
        down = jnp.concatenate([kept_down[k, here, :] for k in range(len(columns))], axis=1)
        dacts[:, here] = mm_nt(g_turned[...], down) + mm(dlats[...], in_ref[:, here])

    def dact_step(index, carry):
        dact_part(pl.multiple_of(index * 2 * LANES, 2 * LANES), 2 * LANES)
        return carry

    for copy in down_copies:
        copy.wait()
    lax.fori_loop(0, block // (2 * LANES), dact_step, 0)
    if block % (2 * LANES):
        dact_part(block // (2 * LANES) * 2 * LANES, block % (2 * LANES))
    for copy in copies:
        copy.wait()

    def hidden_part(start, size):
        here = pl.ds(start, size)
        none = jnp.zeros((slots, size), BF16)
        switch, lift = switch_ref[:, here], lift_ref[:, here]
        pieces = jnp.where(
            owns_gate,
            jnp.concatenate(
                [jnp.concatenate([switch, none], axis=1), jnp.concatenate([none, lift], axis=1)],
                axis=0,
            ),
            jnp.concatenate(
                [jnp.concatenate([none, switch], axis=1), jnp.concatenate([lift, none], axis=1)],
                axis=0,
            ),
        )
        weight = jnp.concatenate(
            [
                jnp.concatenate([kept[q, :, here], kept[4 + q, :, here]], axis=1)
                for q in range(4)
            ],
            axis=0,
        )
        total = mm(x_turned[...], weight)
        total = total + LOWRANK_FACTOR * mm(latents[...], pieces)
        gate = jnp.where(owns_gate, total[:, :size], total[:, size:])
        up = jnp.where(owns_gate, total[:, size:], total[:, :size])
        sigma = jax.nn.sigmoid(gate)
        act = (gate * sigma * up).astype(BF16)
        dact = dacts[:, here]
        dgate = (dact * up * (sigma * (1.0 + gate * (1.0 - sigma)))).astype(BF16)
        dup = (dact * gate * sigma).astype(BF16)
        dfirst, dsecond = jnp.where(owns_gate, dgate, dup), jnp.where(owns_gate, dup, dgate)
        acts[:, here] = act
        firsts[:, here] = dfirst
        seconds[:, here] = dsecond
        both = jnp.concatenate([dfirst, dsecond], axis=1)
        dlat_sum[:, : 2 * slots] += mm_nt(both, pieces)
        piece_grad = LOWRANK_FACTOR * mm(stack[slots:, :], both)
        low, high = piece_grad[:, :size], piece_grad[:, size:]
        deep_ref[:slots, here] = mm(stack[:slots, :], act)
        deep_ref[slots : 2 * slots, here] = jnp.where(owns_gate, low, high)[:slots]
        deep_ref[2 * slots :, here] = jnp.where(owns_gate, high, low)[slots:]

    def hidden_step(index, carry):
        hidden_part(pl.multiple_of(index * 2 * LANES, 2 * LANES), 2 * LANES)
        return carry

    lax.fori_loop(0, block // (2 * LANES), hidden_step, 0)
    if block % (2 * LANES):
        hidden_part(block // (2 * LANES) * 2 * LANES, block % (2 * LANES))

    def back(q, carry):
        value = mm_nt(firsts[...], kept[q]) + mm_nt(seconds[...], kept[4 + q])
        start = ((q // 2) ^ parity) * (width // 2) + lax.rem(q, 2) * quarter
        lanes = pl.ds(pl.multiple_of(start, quarter), quarter)
        back_own[:, lanes] = value[:count]
        back_near[:, lanes] = value[count:].astype(BF16)
        return carry

    lax.fori_loop(0, 4, back, 0)
    dlat_sum[:, 2 * slots : 3 * slots] = mm_nt(acts[...], in_ref[...])
    back_own[:, width:] = dlat_sum[:count, :]
    back_near[:, width:] = dlat_sum[count:, :].astype(BF16)


def down_kernel(meta, *refs):
    acts_refs, whole_down = refs[:2], refs[2:7]
    results = (refs[7:9], refs[9:11])
    kept_down, semaphores = refs[11:]
    parts, _, part = kept_down.shape
    parity, member = meta[0], meta[2]
    copies = [
        pltpu.make_async_copy(ref, kept_down.at[pl.ds(start, size)], semaphores.at[index])
        for index, (ref, start, size) in enumerate(zip(whole_down, (0, 4, 5, 6, 7), (4, 1, 1, 1, 1)))
    ]
    for copy in copies:
        copy.start()
    for copy in copies:
        copy.wait()

    def columns(index, carry):
        half = (index - 4) // 2 ^ parity
        base = jnp.where(index < 4, index, 4 + 2 * half + lax.rem(index, 2))
        lanes = pl.ds(pl.multiple_of((member ^ base) * part, part), part)
        for acts, outs in zip(acts_refs, results):
            value = mm(acts[...], kept_down[index])
            for side, out in enumerate(outs):
                rows = slice(side * out.shape[0], (side + 1) * out.shape[0])
                out[:, lanes] = value[rows].astype(out.dtype)
        return carry

    lax.fori_loop(0, parts, columns, 0)


def down_projection(meta, acts, weights):
    tokens, block = acts[0].shape
    width = 8 * weights["down"][0].shape[2]
    count = tokens // 2
    kept = jax.ShapeDtypeStruct((count, width), F32)
    sent = jax.ShapeDtypeStruct((count, width), BF16)
    return pl.pallas_call(
        down_kernel,
        out_shape=(kept, sent, sent, sent),
        in_specs=[pl.BlockSpec(memory_space=pltpu.SMEM)]
        + [pl.BlockSpec(memory_space=pltpu.VMEM)] * 2
        + [pl.BlockSpec(memory_space=pl.ANY)] * 5,
        scratch_shapes=[
            pltpu.VMEM((8, block, width // 8), BF16),
            pltpu.SemaphoreType.DMA((5,)),
        ],
        compiler_params=pltpu.CompilerParams(vmem_limit_bytes=24 << 20),
        cost_estimate=pl.CostEstimate(
            flops=4 * tokens * width * block,
            transcendentals=0,
            bytes_accessed=2 * width * block + 8 * tokens * width,
        ),
        name="down_projection",
    )(meta, *acts, *weights["down"])


def feed_forward_pair(meta, rows, sens, seen, weights, pieces):
    count, width = sens[0].shape
    slots, block = pieces[-1].shape
    wide, tokens = width + LANES, 2 * count
    operands = (*rows, *sens, *seen, *pieces)
    arrays = (*weights["own"], *weights["over_y"], *weights["down"])
    return pl.pallas_call(
        feed_forward_kernel,
        out_shape=(
            jax.ShapeDtypeStruct((count, wide), F32),
            jax.ShapeDtypeStruct((count, wide), BF16),
            jax.ShapeDtypeStruct((tokens, block), BF16),
            jax.ShapeDtypeStruct((3 * slots, block), F32),
        ),
        in_specs=[pl.BlockSpec(memory_space=pltpu.SMEM)]
        + [pl.BlockSpec(memory_space=pltpu.VMEM)] * len(operands)
        + [pl.BlockSpec(memory_space=pl.ANY)] * len(arrays),
        scratch_shapes=[
            pltpu.VMEM((tokens, width), BF16),
            pltpu.VMEM((tokens, width), BF16),
            pltpu.VMEM((tokens, 2 * slots), BF16),
            pltpu.VMEM((tokens, slots), BF16),
            pltpu.VMEM((3 * slots, tokens), BF16),
            pltpu.VMEM((tokens, block), BF16),
            pltpu.VMEM((tokens, block), BF16),
            pltpu.VMEM((tokens, block), F32),
            pltpu.VMEM((tokens, LANES), F32),
            pltpu.VMEM((8, width // 4, block), BF16),
            pltpu.VMEM((8, block, width // 8), BF16),
            pltpu.SemaphoreType.DMA((13,)),
        ],
        compiler_params=pltpu.CompilerParams(vmem_limit_bytes=50 << 20),
        cost_estimate=pl.CostEstimate(
            flops=2 * 5 * tokens * width * block,
            transcendentals=tokens * block,
            bytes_accessed=6 * width * block + 20 * tokens * width,
        ),
        name="feed_forward",
    )(meta, *operands, *arrays)


def feed_forward_shared(norm2, sens_pairs, weights, small, all_seen):
    ffn_in, *pieces = small
    lower = pieces[0]
    width = norm2.shape[1]
    slots, block = pieces[-1].shape
    hidden_width = block * ACROSS_Y
    member = lax.axis_index("grp")
    parity = lax.axis_index("rep") % 2
    owns_gate = member < ACROSS_Y
    hidden = member % ACROSS_Y
    meta = jnp.stack([parity, owns_gate.astype(jnp.int32), member]).astype(jnp.int32)
    seen = all_seen[0]
    seen_two = jnp.concatenate([seen, seen], axis=1)
    latent_gu = (mm(norm2, ffn_in) * seen_two).astype(BF16)
    pad = jnp.zeros((norm2.shape[0], LANES - 2 * slots), BF16)
    rows = jnp.concatenate([norm2, latent_gu, pad], axis=1)
    across = flip(rows, ACROSS_X)
    results = []
    for index, sens_pair in enumerate(sens_pairs):
        if index == 1:
            result, (across,) = tie(results[0][1], (across,))
            results[0][1] = result
            rows = across
        seen_pair = all_seen[2 * index : 2 * index + 2]
        row_pair = (rows, flip(rows, CORE))
        results.append(
            list(feed_forward_pair(meta, row_pair, sens_pair, seen_pair, weights, pieces))
        )

    chips = [result[0] + flip(result[1], CORE).astype(F32) for result in results]
    deep = (results[0][3] + results[1][3]).astype(BF16)
    members = lax.axis_size("grp")
    owners = members * block // hidden_width
    deep = deep.reshape(3 * slots, owners, block // owners).transpose(1, 0, 2)
    placed = jnp.zeros((members, 3 * slots, block // owners), BF16)
    placed = lax.dynamic_update_slice_in_dim(placed, deep, hidden * owners, 0)
    forwards = down_projection(meta, [result[2] for result in results], weights)
    across = flip(chips[1].astype(BF16), ACROSS_X)
    across, (placed, *forwards) = tie(across, (placed, *forwards))
    backward = chips[0] + across.astype(F32)
    dlat_gu = (LOWRANK_FACTOR * backward[:, width : width + 2 * slots] * seen_two).astype(BF16)
    dnorm2 = backward[:, :width] + mm_nt(dlat_gu, ffn_in)
    latent_d = (backward[:, width + 2 * slots : width + 3 * slots] * seen).astype(BF16)

    dnorm2, (mine, near, other, other_near) = tie(dnorm2, forwards)
    other = (other.astype(F32) + flip(other_near, CORE).astype(F32)).astype(BF16)
    shares = (mine, flip(near, CORE), flip(other, ACROSS_X))

    def finish(shares):
        mine, near, other = shares
        response_part = mine + near.astype(F32) + other.astype(F32)
        return response_part + LOWRANK_FACTOR * mm(latent_d, lower)

    return (finish, shares), dnorm2, latent_d, dlat_gu, placed


def exchange(evens, odds, by_permutes, later=None):
    if by_permutes:
        total = (evens.astype(F32) + flip(odds, CORE).astype(F32)).astype(BF16)
        if later is not None:
            total, (later,) = tie(total, (later,))
        masks = (ACROSS_X, ACROSS_Y, ACROSS_X | ACROSS_Y)
        return [total[0], *(flip(total[i], mask) for i, mask in enumerate(masks, start=1))], later
    parts = jnp.stack([evens, odds], axis=1).reshape(-1, *evens.shape[1:])
    received = lax.all_to_all(parts, "grp", 0, 0, tiled=True)
    return [received[i] for i in range(received.shape[0])], later


def simple_call(kernel, name, out_shape, operands, flops):
    return pl.pallas_call(
        kernel,
        out_shape=out_shape,
        compiler_params=pltpu.CompilerParams(vmem_limit_bytes=32 << 20),
        cost_estimate=pl.CostEstimate(
            flops=flops,
            transcendentals=0,
            bytes_accessed=sum(array.size * array.dtype.itemsize for array in operands),
        ),
        name=name,
    )(*operands)


def early_gradients_kernel(
    dq_ref,
    asking_ref,
    seen_ref,
    latent_q_ref,
    norm1_ref,
    latent_d_ref,
    sens_ref,
    dlat_gu_ref,
    norm2_ref,
    dlat_o_ref,
    attended_ref,
    latent_o_ref,
    dbranch_ref,
    dlat_q_ref,
    early_ref,
):
    dlat_q = (LOWRANK_FACTOR * mm_nt(dq_ref[...], asking_ref[...]) * seen_ref[...]).astype(BF16)
    dlat_q_ref[...] = dlat_q
    two = LOWRANK_FACTOR
    start = 0
    for factor, small, large in (
        (1.0, dlat_q, norm1_ref),
        (two, latent_q_ref[...], dq_ref),
        (two, latent_d_ref[...], sens_ref),
        (1.0, dlat_gu_ref[...], norm2_ref),
        (1.0, dlat_o_ref[...], attended_ref),
        (two, latent_o_ref[...], dbranch_ref),
    ):
        rows = small.shape[1]
        early_ref[start : start + rows, :] = (factor * mm_tn(small, large[...])).astype(BF16)
        start += rows


def early_gradients(*operands):
    count, width = operands[0].shape
    slots = operands[1].shape[0]
    return simple_call(
        early_gradients_kernel,
        "early_gradients",
        (
            jax.ShapeDtypeStruct((count, slots), BF16),
            jax.ShapeDtypeStruct((7 * slots, width), BF16),
        ),
        operands,
        2 * count * width * 8 * slots,
    )


def key_value_gradients_kernel(turn_ref, *refs):
    received, refs = refs[:-12], refs[-12:]
    early_ref, cos_ref, sin_ref, right_ref, seen_ref, latent_ref, norm_ref = refs[:7]
    dkv_ref, dlat_ref, even_ref, odd_ref, late_ref = refs[7:12]
    half = HEAD_DIM // 2
    total = received[0][...].astype(F32)
    for source in received[1:]:
        total = total + source[...].astype(F32)
    kv_width = total.shape[1] // 2
    pieces = []
    for start in range(0, kv_width, LANES):
        value = total[:, start : start + LANES]
        turned = value * sin_ref[...]
        first = lax.rem(lane_of(turned.shape), HEAD_DIM) < half
        turned = jnp.where(
            first, pltpu.roll(turned, LANES - half, 1), -pltpu.roll(turned, half, 1)
        )
        pieces.append((value * cos_ref[...] + turned).astype(BF16))
    dkv = jnp.concatenate([*pieces, total[:, kv_width:].astype(BF16)], axis=1)
    dkv_ref[...] = dkv
    dlat = (LOWRANK_FACTOR * mm_nt(dkv, right_ref[...]) * seen_ref[...]).astype(BF16)
    dlat_ref[...] = dlat
    late_ref[...] = mm_tn(dlat, norm_ref[...]).astype(BF16)
    thin = (LOWRANK_FACTOR * mm_tn(latent_ref[...], dkv)).astype(BF16)
    rows, head = late_ref.shape[0], early_ref.shape[0]
    thin = jnp.concatenate([thin[: rows // 2, :kv_width], thin[rows // 2 :, kv_width:]], axis=0)
    share = even_ref.shape[2]
    for place in range(2 * even_ref.shape[0]):
        pack_ref = (even_ref, odd_ref)[place % 2]
        columns = pl.ds(pl.multiple_of((place ^ turn_ref[0]) * share, share), share)
        pack_ref[place // 2, :head, :] = early_ref[:, columns]
        pack_ref[place // 2, head : head + rows, :] = late_ref[:, columns]
        for index, start in enumerate(range(0, kv_width, share)):
            first = head + (index + 1) * rows
            pack_ref[place // 2, first : first + rows, :] = thin[:, start : start + share]


def key_value_gradients(turn, received, early, cosines, sines, kv_right, seen_two, latent_kv, norm1):
    members = lax.axis_size("grp")
    count, kv_two = received[0].shape
    rows, width = kv_right.shape[0], norm1.shape[1]
    share = width // members
    packed = early.shape[0] + rows * (1 + kv_two // 2 // share)
    operands = (*received, early, cosines, sines, kv_right, seen_two, latent_kv, norm1)
    pack = jax.ShapeDtypeStruct((members // 2, packed, share), BF16)
    return pl.pallas_call(
        key_value_gradients_kernel,
        out_shape=(
            jax.ShapeDtypeStruct((count, kv_two), BF16),
            jax.ShapeDtypeStruct((count, rows), BF16),
            pack,
            pack,
        ),
        in_specs=[pl.BlockSpec(memory_space=pltpu.SMEM)]
        + [pl.BlockSpec(memory_space=pltpu.VMEM)] * len(operands),
        scratch_shapes=[pltpu.VMEM((rows, width), BF16)],
        compiler_params=pltpu.CompilerParams(vmem_limit_bytes=32 << 20),
        cost_estimate=pl.CostEstimate(
            flops=2 * count * rows * (width + 2 * kv_two),
            transcendentals=0,
            bytes_accessed=sum(array.size * array.dtype.itemsize for array in operands),
        ),
        name="key_value_gradients",
    )(turn, *operands)


def place_kernel(jobs, groups, slots, *refs):
    place_ref, refs = refs[0], refs[1:]
    outs = refs[len(refs) - len(jobs) :]
    for (source, index, is_right), out_ref in zip(jobs, outs):
        value = jnp.concatenate(
            [
                refs[source * groups + g][index * slots : (index + 1) * slots, :]
                for g in range(groups)
            ],
            axis=0,
        )
        if is_right:
            out_ref[...] = mm_tn(place_ref[...], value)
        else:
            out_ref[...] = mm_tn(value, place_ref[...])


def place_gradients(place, sources, slots, jobs):
    groups = len(sources[0])
    narrow = place.shape[1]
    shapes = []
    for source, _, is_right in jobs:
        size = sources[source][0].shape[1]
        shapes.append(
            jax.ShapeDtypeStruct((narrow, size) if is_right else (size, narrow), F32)
        )
    return pl.pallas_call(
        functools.partial(place_kernel, jobs, groups, slots),
        out_shape=tuple(shapes),
        compiler_params=pltpu.CompilerParams(vmem_limit_bytes=32 << 20),
        cost_estimate=pl.CostEstimate(
            flops=2 * sum(shape.size for shape in shapes) * place.shape[0],
            transcendentals=0,
            bytes_accessed=4 * sum(shape.size for shape in shapes),
        ),
        name="place_gradients",
    )(place, *[array for source in sources for array in source])


def round_groups(array):
    groups = lax.axis_size("rep")
    return [array] + [
        lax.ppermute(array, "rep", [(i, (i + shift) % groups) for i in range(groups)])
        for shift in range(1, groups)
    ]


def shards(
    tokens,
    response_sensitivity,
    seq_lengths,
    prefix_lengths,
    adapter_ids,
    attn_gain,
    mlp_gain,
    qkv_weight,
    out_weight,
    gate_up_weight,
    down_weight,
    query_in,
    asking_right_pieces,
    key_in,
    lookup_right_pieces,
    value_in,
    content_right_pieces,
    output_in,
    final_right_pieces,
    gate_in,
    switch_right_pieces,
    up_in,
    lift_right_pieces,
    down_in,
    lower_right_pieces,
):
    count, width = tokens.shape
    members = lax.axis_size("grp")
    groups = lax.axis_size("rep")
    kv_width = lookup_right_pieces.shape[1]
    narrow = query_in.shape[1]
    group = lax.axis_index("rep")
    member = lax.axis_index("grp")
    lengths = lax.dynamic_slice_in_dim(seq_lengths, 2 * group, 2)
    prefixes = lax.dynamic_slice_in_dim(prefix_lengths, 2 * group, 2)
    chosen_ids = lax.dynamic_slice_in_dim(adapter_ids, 2 * group, 2)
    key_count = count * members
    sens = response_sensitivity

    paired = members == 8 and groups % 2 == 0
    qkv_full = lax.all_gather(qkv_weight, "grp", axis=1, tiled=True)
    if paired:
        steps = gather_hidden_block(gate_up_weight, down_weight)
        transfers = next(steps)
    else:
        out_full = lax.all_gather(out_weight, "grp", axis=1, tiled=True)
        down_full = lax.all_gather(down_weight, "grp", axis=1, tiled=True)
        gate_up_full = lax.all_gather(gate_up_weight, "grp", axis=1, tiled=True)

    turn = member if paired else 0
    key_index = jnp.arange(key_count, dtype=jnp.int32)
    key_index = (key_index // count ^ turn) * count + key_index % count
    key_second = (key_index >= lengths[0]).astype(jnp.int32)
    key_position = key_index - key_second * lengths[0]
    own_index = member * count + jnp.arange(count, dtype=jnp.int32)
    own_second = (own_index >= lengths[0]).astype(jnp.int32)
    position = own_index - own_second * lengths[0]
    prefix = jnp.where(own_second == 0, prefixes[0], prefixes[1])
    allowed = (key_second[:, None] == own_second[None, :]) & (
        (key_position[:, None] <= position[None, :]) | (key_position[:, None] < prefix[None, :])
    )
    bias = jnp.where(allowed, 0.0, MASKED).astype(F32)
    first_key = own_second[0] * lengths[0]
    last_key = jnp.max(own_second * lengths[0] + jnp.maximum(position, prefix - 1))
    span = jnp.stack(
        [first_key // KEY_BLOCK, last_key // KEY_BLOCK + 1, turn * count // KEY_BLOCK]
    ).astype(jnp.int32)

    slots = 2 * RANK
    columns = jnp.arange(narrow, dtype=jnp.int32)
    slot = jnp.arange(slots, dtype=jnp.int32)
    slot_column = jnp.where(slot < RANK, chosen_ids[0], chosen_ids[1]) * RANK + slot % RANK
    pick = (columns[:, None] == slot_column[None, :]).astype(BF16)

    def seen_by(device):
        index = device * count + jnp.arange(count, dtype=jnp.int32)
        second = (index >= lengths[0]).astype(jnp.int32)
        return (second[:, None] == slot[None, :] // RANK).astype(F32)

    def pick_in(weight):
        return mm(weight, pick).astype(BF16)

    def pick_right(weight):
        return mm_tn(pick, weight).astype(BF16)

    seen = seen_by(member)
    seen_three = jnp.concatenate([seen, seen, seen], axis=1)
    qkv_in = jnp.concatenate([pick_in(query_in), pick_in(key_in), pick_in(value_in)], axis=1)
    asking = pick_right(asking_right_pieces)
    lookup = pick_right(lookup_right_pieces)
    content = pick_right(content_right_pieces)
    none = jnp.zeros_like(lookup)
    kv_right = jnp.concatenate(
        [jnp.concatenate([lookup, none], axis=1), jnp.concatenate([none, content], axis=1)], axis=0
    )
    out_in = pick_in(output_in)
    final = pick_right(final_right_pieces)
    lower = pick_right(lower_right_pieces)
    small = (
        jnp.concatenate([pick_in(gate_in), pick_in(up_in)], axis=1),
        pick_right(switch_right_pieces),
        pick_right(lift_right_pieces),
        lax.dot_general(
            pick, down_in, (((0,), (1,)), ((), ())), preferred_element_type=F32
        ).astype(BF16),
        lower,
    )

    cycle = jnp.arange(groups * slots, dtype=jnp.int32)
    source = (group - cycle // slots) % groups
    sequence = 2 * source + cycle % slots // RANK
    sequences = jnp.arange(adapter_ids.shape[0], dtype=jnp.int32)
    theirs = jnp.where(sequence[:, None] == sequences[None, :], adapter_ids[None, :], 0)
    all_column = jnp.sum(theirs, axis=1) * RANK + cycle % RANK
    place = (all_column[:, None] == columns[None, :]).astype(BF16)
    incoming = tokens.astype(F32)
    scale_one = inverse_rms(incoming)
    norm1 = (incoming * scale_one * attn_gain).astype(BF16)
    if paired:
        block = down_weight.shape[0] // ACROSS_Y
        start = member % ACROSS_Y * block
        pieces = [lax.dynamic_slice_in_dim(piece, start, block, 1) for piece in small[1:4]]
        others = (seen_by(member ^ mask) for mask in (CORE, ACROSS_X, ACROSS_X | CORE))
        ready = (*transfers, asking, kv_right, out_in, final, lower, place, small[0], *pieces)
        norm1, ready = tie(norm1, (*ready, *others))
        transfers = ready[: len(transfers)]
        asking, kv_right, out_in, final, lower, place, ffn_in, *ready = ready[len(transfers) :]
        small = (ffn_in, lower, *ready[:3])
        all_seen = (seen, *ready[3:])
        transfers = steps.send(transfers)
        out_full = lax.all_gather(out_weight, "grp", axis=1, tiled=True)
    latent_qkv = (mm(norm1, qkv_in) * seen_three).astype(BF16)
    latent_q, latent_kv = latent_qkv[:, :slots], latent_qkv[:, slots:]
    half = HEAD_DIM // 2
    freqs = 10000.0 ** (-2.0 * jnp.arange(half).astype(F32) / HEAD_DIM)
    freqs = jnp.tile(freqs, LANES // half)
    angles = position.astype(F32)[:, None] * freqs[None, :]
    cosines, sines = jnp.cos(angles), jnp.sin(angles)

    def widen(table, size):
        return jnp.tile(table, (1, size // LANES))

    qkv = mm(norm1, qkv_full)
    query = qkv[:, :width] + LOWRANK_FACTOR * mm(latent_q, asking)
    own_kv = qkv[:, width:] + LOWRANK_FACTOR * mm(latent_kv, kv_right)
    query = rotate(query, widen(cosines, width), widen(sines, width)).astype(BF16)
    query = query * jnp.asarray(HEAD_DIM**-0.5, BF16)
    key_own = rotate(own_kv[:, :kv_width], widen(cosines, kv_width), widen(sines, kv_width))
    key_value = jnp.concatenate([key_own, own_kv[:, kv_width:]], axis=1).astype(BF16)
    if paired:
        key_value, transfers = tie(key_value, transfers)
        key_value, (ready, *transfers) = tie(gather_key_values(key_value), (sens, *transfers))
        transfers = steps.send(transfers)
        sens_near, sens_across = flip(ready, CORE), flip(ready, ACROSS_X)
    else:
        key_value = lax.all_gather(key_value, "grp", axis=0, tiled=True)
    attended_low, lse = attention_forward(span, query, key_value, bias)
    if paired:
        attended_low, (sens_near, sens_across, *transfers) = tie(
            attended_low, (sens_near, sens_across, *transfers)
        )
        out_full, (sens_last, *transfers) = tie(
            out_full, (flip(sens_across, CORE), *steps.send(transfers))
        )
        sens_pairs = [(sens, sens_near), (sens_across, sens_last)]
        transfers = steps.send(transfers)

    latent_o = (mm(attended_low, out_in) * seen).astype(BF16)
    stream = incoming + (mm(attended_low, out_full) + LOWRANK_FACTOR * mm(latent_o, final))
    scale_two = inverse_rms(stream)
    norm2 = (stream * scale_two * mlp_gain).astype(BF16)
    if paired:
        norm2, transfers = tie(norm2, transfers)
        try:
            steps.send(transfers)
        except StopIteration as stop:
            weights = stop.value
        (finish, shares), dnorm2, latent_d, dlat_gu, deep = feed_forward_shared(
            norm2, sens_pairs, weights, small, all_seen
        )
    else:
        (finish, shares), dnorm2, latent_d, dlat_gu, deep = feed_forward_alone(
            norm2, sens, gate_up_full, down_full, small, seen
        )
    dhidden = sens.astype(F32) + norm_backward(stream, scale_two, mlp_gain, dnorm2)
    dbranch = dhidden.astype(BF16)
    dlat_o = (LOWRANK_FACTOR * mm_nt(dbranch, final) * seen).astype(BF16)
    dattended = (mm_nt(dbranch, out_full) + mm_nt(dlat_o, out_in)).astype(BF16)

    dattended, (deep,) = tie(dattended, (deep,))
    deep_sum = lax.psum_scatter(deep, "grp", scatter_dimension=0, tiled=True)[0]

    dq, dkv_even, dkv_odd = attention_backward(
        span, query, dattended, attended_low, lse, key_value, bias, cosines, sines
    )
    dkv_odd, (deep_sum, *shares) = tie(dkv_odd, (deep_sum, *shares))
    received, dq = exchange(dkv_even, dkv_odd, paired, dq)
    dlat_q, early = early_gradients(
        dq,
        asking,
        seen,
        latent_q,
        norm1,
        latent_d,
        sens,
        dlat_gu,
        norm2,
        dlat_o,
        attended_low,
        latent_o,
        dbranch,
    )
    dnorm_q = mm_nt(dq, qkv_full[:, :width]) + mm_nt(dlat_q, qkv_in[:, :slots])
    turns = jnp.full((1,), turn, jnp.int32)
    dkv, dlat_kv, late_even, late_odd = key_value_gradients(
        turns, received, early, cosines, sines, kv_right, seen_three[:, : 2 * slots], latent_kv, norm1
    )
    deep_sum = round_groups(deep_sum)
    late_parts = [part.astype(F32) for part in exchange(late_even, late_odd, paired)[0]]
    late_sum = round_groups(sum(late_parts[1:], late_parts[0]).astype(BF16))
    level_response = (stream + finish(shares)).astype(BF16)
    dnorm1 = dnorm_q + mm_nt(dkv, qkv_full[:, width:]) + mm_nt(dlat_kv, qkv_in[:, slots:])
    input_grad = (dhidden + norm_backward(incoming, scale_one, attn_gain, dnorm1)).astype(BF16)

    share = width // members
    pieces = kv_width // share
    thin_start = 9 * slots
    thin_sum = [
        jnp.concatenate(
            [
                array[thin_start + 2 * slots * i : thin_start + 2 * slots * (i + 1)]
                for i in range(pieces)
            ],
            axis=1,
        )
        for array in late_sum
    ]
    jobs = (
        (0, 0, False),
        (0, 1, True),
        (0, 7, False),
        (2, 0, True),
        (0, 8, False),
        (2, 1, True),
        (0, 5, False),
        (0, 6, True),
        (0, 3, False),
        (1, 1, True),
        (0, 4, False),
        (1, 2, True),
        (1, 0, False),
        (0, 2, True),
    )
    grads = list(place_gradients(place, (late_sum, deep_sum, thin_sum), slots, jobs))
    own = kv_width // members
    for index in (3, 5):
        grads[index] = lax.dynamic_slice_in_dim(grads[index], member * own, own, 1)
    return (level_response, input_grad, *grads)


def solution(mesh):
    rows = P(("rep", "grp"), None)
    split = P(None, "grp")
    in_specs = (rows, rows, *[P()] * 5, *[split] * 4, *[P()] * 14)
    out_specs = (rows, rows, *[P("grp", None), P(None, "grp")] * 7)
    return jax.shard_map(shards, mesh=mesh, in_specs=in_specs, out_specs=out_specs, check_vma=False)
```

```python
import functools

import jax
import jax.numpy as jnp
from jax import lax
from jax.experimental import pallas as pl
from jax.experimental.pallas import tpu as pltpu
from jax.sharding import PartitionSpec as P

HEADS = 32
KV_HEADS = 4
HEAD_DIM = 64
RANK = 16
LANES = 128
KEY_BLOCK = 1024
PAIRS = 4

EPS = 1e-05
LOWRANK_FACTOR = 2.0
MASKED = -1e30
F32 = jnp.float32
BF16 = jnp.bfloat16


def mm(left, right):
    return jnp.dot(left, right, preferred_element_type=F32)


def mm_nt(left, right):
    return lax.dot_general(left, right, (((1,), (1,)), ((), ())), preferred_element_type=F32)


def mm_tn(left, right):
    return lax.dot_general(left, right, (((0,), (0,)), ((), ())), preferred_element_type=F32)


def inverse_rms(value):
    return lax.rsqrt(jnp.mean(value * value, axis=-1, keepdims=True) + EPS)


def norm_backward(value, scale, gain, grad):
    scaled = gain * grad
    return scale * scaled - value * (scale * scale * scale) * jnp.mean(
        scaled * value, axis=-1, keepdims=True
    )


def half_turn(value):
    half = HEAD_DIM // 2
    lane = lax.broadcasted_iota(jnp.int32, value.shape, 1) % HEAD_DIM
    return jnp.where(
        lane < half, -jnp.roll(value, -half, axis=1), jnp.roll(value, half, axis=1)
    )


def rotate(value, cosines, sines):
    return value * cosines + half_turn(value) * sines


def unrotate(grad, cosines, sines):
    return grad * cosines - half_turn(grad * sines)


def lane_of(shape):
    return lax.broadcasted_iota(jnp.int32, shape, 1)


def key_rows(span, index):
    return pl.ds(pl.multiple_of((index ^ span[2]) * KEY_BLOCK, KEY_BLOCK), KEY_BLOCK)


def spread_heads(span, odd, source_ref, pair_ref):
    def step(index, carry):
        rows = key_rows(span, index)
        value = source_ref[rows, :].astype(F32)
        turned = pltpu.roll(value, HEAD_DIM, 1)
        low = lane_of(value.shape) < HEAD_DIM
        none = jnp.zeros_like(value)
        pair_ref[0, rows, :] = jnp.where(low, jnp.where(odd, turned, value), none).astype(BF16)
        pair_ref[1, rows, :] = jnp.where(low, none, jnp.where(odd, value, turned)).astype(BF16)
        return carry

    lax.fori_loop(span[0], span[1], step, 0)


def attention_forward_kernel(
    per_kv, span, q_ref, key_ref, value_ref, bias_ref, out_ref, lse_ref, k_ref, v_ref
):
    tokens = q_ref.shape[0]
    odd = lax.rem(pl.program_id(0) // per_kv, LANES // HEAD_DIM) == 1

    @pl.when(lax.rem(pl.program_id(0), per_kv) == 0)
    def _():
        spread_heads(span, odd, key_ref, k_ref)
        spread_heads(span, odd, value_ref, v_ref)

    queries = [q_ref[:, pair * LANES : (pair + 1) * LANES] for pair in range(PAIRS)]

    def step(index, carry):
        rows = key_rows(span, index)
        bias = bias_ref[rows, :]
        new = []
        flat = jnp.concatenate([v_ref[0, rows, :], v_ref[1, rows, :]], axis=0).T
        for pair, (peaks, totals, mixed) in enumerate(carry):
            tops, sums, parts, decays = [], [], [], []
            for side in range(2):
                scores = mm_nt(k_ref[side, rows, :], queries[pair]) + bias
                top = jnp.maximum(peaks[side], jnp.max(scores, axis=0, keepdims=True))
                decay = jnp.exp(peaks[side] - top)
                probs = jnp.exp(scores - top)
                tops.append(top)
                sums.append(totals[side] * decay + jnp.sum(probs, axis=0, keepdims=True))
                decays.append(jnp.broadcast_to(decay, (HEAD_DIM, tokens)))
                parts.append(probs.astype(BF16))
            mixed = mixed * jnp.concatenate(decays, axis=0)
            mixed = mixed + mm(flat, jnp.concatenate(parts, axis=0))
            new.append((tuple(tops), tuple(sums), mixed))
        return tuple(new)

    low = jnp.full((1, tokens), MASKED, F32)
    none = jnp.zeros((1, tokens), F32)
    start = ((low, low), (none, none), jnp.zeros((LANES, tokens), F32))
    result = lax.fori_loop(span[0], span[1], step, (start,) * PAIRS)
    for pair, (peaks, totals, mixed) in enumerate(result):
        weight = jnp.concatenate(
            [jnp.broadcast_to(1.0 / total, (HEAD_DIM, tokens)) for total in totals], axis=0
        )
        out_ref[:, pair * LANES : (pair + 1) * LANES] = (mixed * weight).T.astype(BF16)
        lse_ref[pair] = jnp.concatenate(
            [peak + jnp.log(total) for peak, total in zip(peaks, totals)], axis=0
        )


def key_value_specs(keys, per_kv):
    blocks = KV_HEADS * HEAD_DIM // LANES
    heads = LANES // HEAD_DIM
    return [
        pl.BlockSpec((keys, LANES), lambda j, s: (0, j // per_kv // heads)),
        pl.BlockSpec((keys, LANES), lambda j, s: (0, blocks + j // per_kv // heads)),
    ]


def attention_forward(span, query, key_value, bias):
    tokens, width = query.shape
    keys = bias.shape[0]
    pairs = width // LANES
    steps = pairs // PAIRS
    pair_spec = pl.BlockSpec((tokens, PAIRS * LANES), lambda j, s: (0, j))
    return pl.pallas_call(
        functools.partial(attention_forward_kernel, steps // KV_HEADS),
        out_shape=(
            jax.ShapeDtypeStruct((tokens, width), BF16),
            jax.ShapeDtypeStruct((pairs, 2, tokens), F32),
        ),
        grid_spec=pltpu.PrefetchScalarGridSpec(
            num_scalar_prefetch=1,
            grid=(steps,),
            in_specs=[
                pair_spec,
                *key_value_specs(keys, steps // KV_HEADS),
                pl.BlockSpec((keys, tokens), lambda j, s: (0, 0)),
            ],
            out_specs=(pair_spec, pl.BlockSpec((PAIRS, 2, tokens), lambda j, s: (j, 0, 0))),
            scratch_shapes=[pltpu.VMEM((2, keys, LANES), BF16)] * 2,
        ),
        compiler_params=pltpu.CompilerParams(
            dimension_semantics=("arbitrary",), vmem_limit_bytes=30 << 20
        ),
        cost_estimate=pl.CostEstimate(
            flops=4 * tokens * keys * width,
            transcendentals=tokens * keys * HEADS // 2,
            bytes_accessed=4 * tokens * width + 16 * keys * LANES * KV_HEADS,
        ),
        name="attention_forward",
    )(span, query, key_value, key_value, bias)


def attention_backward_kernel(
    per_kv,
    span,
    q_ref,
    do_ref,
    o_ref,
    lse_ref,
    key_ref,
    value_ref,
    bias_ref,
    cos_ref,
    sin_ref,
    dq_ref,
    even_ref,
    odd_ref,
    k_ref,
    v_ref,
    dk_sum,
    dv_sum,
):
    tokens = q_ref.shape[0]
    member = lax.rem(pl.program_id(0), per_kv)
    odd = lax.rem(pl.program_id(0) // per_kv, LANES // HEAD_DIM) == 1

    @pl.when(member == 0)
    def _():
        spread_heads(span, odd, key_ref, k_ref)
        spread_heads(span, odd, value_ref, v_ref)
        dk_sum[...] = jnp.zeros_like(dk_sum)
        dv_sum[...] = jnp.zeros_like(dv_sum)

    low = lane_of((tokens, LANES)) < HEAD_DIM
    row = lax.broadcasted_iota(jnp.int32, (8, LANES), 0)
    column = lax.broadcasted_iota(jnp.int32, (8, LANES), 1)
    chooser = jnp.where(row == column // HEAD_DIM, 1.0, 0.0).astype(F32)
    queries, grads, deltas, query_stack, grad_stack = [], [], [], [], []
    for pair in range(PAIRS):
        lanes = slice(pair * LANES, (pair + 1) * LANES)
        query, grad = q_ref[:, lanes], do_ref[:, lanes]
        none = jnp.zeros_like(query)
        queries.append(query)
        grads.append(grad)
        query_stack += [jnp.where(low, query, none), jnp.where(low, none, query)]
        grad_stack += [jnp.where(low, grad, none), jnp.where(low, none, grad)]
        deltas.append(
            lax.dot_general(
                chooser,
                grad.astype(F32) * o_ref[:, lanes].astype(F32),
                (((1,), (1,)), ((), ())),
                precision=lax.Precision.HIGHEST,
                preferred_element_type=F32,
            )
        )
    query_stack = jnp.concatenate(query_stack, axis=0)
    grad_stack = jnp.concatenate(grad_stack, axis=0)

    def step(index, dqueries):
        rows = key_rows(span, index)
        bias = bias_ref[rows, :]
        all_probs, all_dscores, new = [], [], []
        flat = jnp.concatenate([k_ref[0, rows, :], k_ref[1, rows, :]], axis=0).T
        for pair, dquery in enumerate(dqueries):
            for side in range(2):
                scores = mm_nt(k_ref[side, rows, :], queries[pair]) + bias
                probs = jnp.exp(scores - lse_ref[pair, side : side + 1, :])
                dprobs = mm_nt(v_ref[side, rows, :], grads[pair])
                delta = deltas[pair][side : side + 1, :]
                dscores = (probs * (dprobs - delta)).astype(BF16)
                all_probs.append(probs.astype(BF16))
                all_dscores.append(dscores)
            new.append(dquery + mm(flat, jnp.concatenate(all_dscores[-2:], axis=0)))
        dk_sum[rows, :] += mm(jnp.concatenate(all_dscores, axis=1), query_stack)
        dv_sum[rows, :] += mm(jnp.concatenate(all_probs, axis=1), grad_stack)
        return tuple(new)

    dqueries = lax.fori_loop(
        span[0], span[1], step, (jnp.zeros((LANES, tokens), F32),) * PAIRS
    )
    half = HEAD_DIM // 2
    for pair, dquery in enumerate(dqueries):
        dquery = dquery.T * (HEAD_DIM**-0.5)
        turned = dquery * sin_ref[...]
        first = lax.rem(lane_of(turned.shape), HEAD_DIM) < half
        turned = jnp.where(
            first, pltpu.roll(turned, LANES - half, 1), -pltpu.roll(turned, half, 1)
        )
        dq_ref[:, pair * LANES : (pair + 1) * LANES] = (dquery * cos_ref[...] + turned).astype(BF16)

    @pl.when(member == per_kv - 1)
    def _():
        block = pl.program_id(0) // per_kv // (LANES // HEAD_DIM)

        def put(index, carry):
            for side, out_ref in enumerate((even_ref, odd_ref)):
                rows = pl.ds(pl.multiple_of((2 * index + side) * tokens, tokens), tokens)
                for sum_ref, first in ((dk_sum, 0), (dv_sum, KV_HEADS * HEAD_DIM // LANES)):
                    total = sum_ref[rows, :]
                    total = total + pltpu.roll(total, HEAD_DIM, 1)
                    keep = jnp.logical_and(odd, lane_of(total.shape) < HEAD_DIM)
                    lanes = pl.ds(pl.multiple_of((first + block) * LANES, LANES), LANES)
                    out_ref[index, :, lanes] = jnp.where(
                        keep, out_ref[index, :, lanes], total.astype(BF16)
                    )
            return carry

        lax.fori_loop(0, even_ref.shape[0], put, 0)


def attention_backward(span, query, grad, attended, lse, key_value, bias, cosines, sines):
    tokens, width = query.shape
    keys, kv_two = key_value.shape
    pairs = width // LANES
    steps = pairs // PAIRS
    per_kv = steps // KV_HEADS
    pair_spec = pl.BlockSpec((tokens, PAIRS * LANES), lambda j, s: (0, j))
    table_spec = pl.BlockSpec((tokens, LANES), lambda j, s: (0, 0))
    return pl.pallas_call(
        functools.partial(attention_backward_kernel, per_kv),
        out_shape=(
            jax.ShapeDtypeStruct((tokens, width), BF16),
            *[jax.ShapeDtypeStruct((keys // tokens // 2, tokens, kv_two), BF16)] * 2,
        ),
        grid_spec=pltpu.PrefetchScalarGridSpec(
            num_scalar_prefetch=1,
            grid=(steps,),
            in_specs=[
                pair_spec,
                pair_spec,
                pair_spec,
                pl.BlockSpec((PAIRS, 2, tokens), lambda j, s: (j, 0, 0)),
                *key_value_specs(keys, per_kv),
                pl.BlockSpec((keys, tokens), lambda j, s: (0, 0)),
                table_spec,
                table_spec,
            ],
            out_specs=(
                pair_spec,
                *[pl.BlockSpec((keys // tokens // 2, tokens, kv_two), lambda j, s: (0, 0, 0))] * 2,
            ),
            scratch_shapes=[pltpu.VMEM((2, keys, LANES), BF16)] * 2
            + [pltpu.VMEM((keys, LANES), F32)] * 2,
        ),
        compiler_params=pltpu.CompilerParams(
            dimension_semantics=("arbitrary",), vmem_limit_bytes=46 << 20
        ),
        cost_estimate=pl.CostEstimate(
            flops=10 * tokens * keys * width,
            transcendentals=tokens * keys * HEADS // 2,
            bytes_accessed=10 * tokens * width + 8 * keys * kv_two,
        ),
        name="attention_backward",
    )(span, query, grad, attended, lse, key_value, key_value, bias, cosines, sines)


CORE, ACROSS_X, ACROSS_Y = 1, 2, 4


def flip(array, mask):
    members = lax.axis_size("grp")
    return lax.ppermute(array, "grp", [(i, i ^ mask) for i in range(members)])


def flip_group(array):
    groups = lax.axis_size("rep")
    return lax.ppermute(array, "rep", [(i, i ^ 1) for i in range(groups)])


def gather_hidden_block(gate_up_weight, down_weight):
    rows = gate_up_weight.shape[0] // 4
    block = gate_up_weight.shape[1]
    member = lax.axis_index("grp")
    parity = lax.axis_index("rep") % 2
    own = [
        lax.dynamic_slice_in_dim(gate_up_weight, ((parity ^ (q // 2)) * 2 + q % 2) * rows, rows, 0)
        for q in range(4)
    ]

    def down_rows(mask):
        start = ((member ^ mask) % ACROSS_Y) * block
        return lax.dynamic_slice_in_dim(down_weight, start, block, 0)

    low, next_quarter, *near = yield (
        flip(own[0], ACROSS_Y),
        own[1],
        flip(down_rows(ACROSS_X), ACROSS_X),
        flip(down_rows(CORE), CORE),
        flip(down_rows(ACROSS_X | CORE), ACROSS_X | CORE),
    )
    down_own = jnp.stack([down_rows(0), near[1], near[0], near[2]])
    high, low_other, down_own = yield flip(next_quarter, ACROSS_Y), flip_group(low), down_own
    mine, second = (
        lax.dynamic_slice_in_dim(down_own, 2 * parity + index, 1, 0) for index in range(2)
    )
    down_mine, high_other, second = yield flip(mine, ACROSS_Y), flip_group(high), second
    down_second, down_other = yield flip(second, ACROSS_Y), flip_group(down_mine)
    (second_other,) = yield (flip_group(down_second),)
    return {
        "own": own,
        "over_y": (low, high, low_other, high_other),
        "down": (down_own, down_mine, down_second, down_other, second_other),
    }


def gather_key_values(own):
    over_y = flip(own, ACROSS_Y)
    pieces = [own, flip(own, ACROSS_X), over_y, flip(over_y, ACROSS_X)]
    return jnp.concatenate(
        [part for piece in pieces for part in (piece, flip(piece, CORE))], axis=0
    )


def tie(value, transfers):
    value, *transfers = lax.optimization_barrier((value, *transfers))
    return value, tuple(transfers)


def feed_forward_alone(norm2, sens, gate_up_full, down_full, small, seen):
    ffn_in, switch, lift, down_in, lower = small
    slots, hidden_width = switch.shape
    seen_two = jnp.concatenate([seen, seen], axis=1)
    latent_gu = (mm(norm2, ffn_in) * seen_two).astype(BF16)
    latent_g, latent_u = latent_gu[:, :slots], latent_gu[:, slots:]
    gate_up = mm(norm2, gate_up_full) + LOWRANK_FACTOR * jnp.concatenate(
        [mm(latent_g, switch), mm(latent_u, lift)], axis=1
    )
    gate = gate_up[:, :hidden_width]
    up = gate_up[:, hidden_width:]
    sigma = jax.nn.sigmoid(gate)
    act = (gate * sigma * up).astype(BF16)
    latent_d = (mm_nt(act, down_in) * seen).astype(BF16)
    response_part = mm(act, down_full) + LOWRANK_FACTOR * mm(latent_d, lower)
    dlat_d = (LOWRANK_FACTOR * mm_nt(sens, lower) * seen).astype(BF16)
    dact = mm_nt(sens, down_full) + mm(dlat_d, down_in)
    dgate = (dact * up * (sigma * (1.0 + gate * (1.0 - sigma)))).astype(BF16)
    dup = (dact * gate * sigma).astype(BF16)
    dlat_gu = (
        LOWRANK_FACTOR
        * jnp.concatenate([mm_nt(dgate, switch), mm_nt(dup, lift)], axis=1)
        * seen_two
    ).astype(BF16)
    dnorm2 = (
        mm_nt(dgate, gate_up_full[:, :hidden_width])
        + mm_nt(dup, gate_up_full[:, hidden_width:])
        + mm_nt(dlat_gu, ffn_in)
    )
    deep = jnp.concatenate(
        [
            mm_tn(dlat_d, act),
            LOWRANK_FACTOR * mm_tn(latent_g, dgate),
            LOWRANK_FACTOR * mm_tn(latent_u, dup),
        ],
        axis=0,
    ).astype(BF16)
    members = lax.axis_size("grp")
    deep = deep.reshape(3 * slots, members, hidden_width // members).transpose(1, 0, 2)
    return (lambda shares: shares[0], (response_part,)), dnorm2, latent_d, dlat_gu, deep


def feed_forward_kernel(
    meta,
    own_x,
    near_x,
    own_g,
    near_g,
    own_seen,
    near_seen,
    lower_ref,
    switch_ref,
    lift_ref,
    in_ref,
    *refs,
):
    whole_refs, whole_down = refs[:8], refs[8:13]
    back_own, back_near, acts, deep_ref = refs[13:17]
    x_turned, g_turned, latents, dlats, stack, firsts, seconds, dacts, dlat_sum = refs[17:26]
    kept, kept_down, semaphores = refs[26:]
    count, width = own_g.shape
    tokens = 2 * count
    slots, block = in_ref.shape
    quarter = width // 4
    part = width // kept_down.shape[0]
    parity = meta[0]
    owns_gate = meta[1] == 1
    member = meta[2]
    starts = [
        pl.multiple_of((parity if q < 2 else 1 - parity) * (width // 2) + (q % 2) * quarter, quarter)
        for q in range(4)
    ]
    bases = [0, 1, 2, 3, *(4 + 2 * parity + k for k in (0, 1)), *(6 - 2 * parity + k for k in (0, 1))]
    columns = [pl.ds(pl.multiple_of((member ^ base) * part, part), part) for base in bases]
    down_copies = [
        pltpu.make_async_copy(ref, kept_down.at[pl.ds(start, size)], semaphores.at[8 + index])
        for index, (ref, start, size) in enumerate(zip(whole_down, (0, 4, 5, 6, 7), (4, 1, 1, 1, 1)))
    ]
    copies = [
        pltpu.make_async_copy(ref, kept.at[index], semaphores.at[index])
        for index, ref in enumerate(whole_refs)
    ]
    for copy in down_copies + copies:
        copy.start()
    dlat_sum[...] = jnp.zeros_like(dlat_sum)
    for index, (x_ref, g_ref, seen_ref) in enumerate(
        ((own_x, own_g, own_seen), (near_x, near_g, near_seen))
    ):
        rows = slice(index * count, (index + 1) * count)
        for q in range(4):
            x_turned[rows, q * quarter : (q + 1) * quarter] = x_ref[:, pl.ds(starts[q], quarter)]
        for k, lanes in enumerate(columns):
            g_turned[rows, k * part : (k + 1) * part] = g_ref[:, lanes]
        latents[rows, :] = x_ref[:, width : width + 2 * slots]
        dlat = LOWRANK_FACTOR * mm_nt(g_ref[...], lower_ref[...]) * seen_ref[...]
        dlats[rows, :] = dlat.astype(BF16)
        stack[:slots, rows] = dlat.T.astype(BF16)
        latent = x_ref[:, width : width + LANES].astype(F32).T[: 2 * slots]
        stack[slots:, rows] = latent.astype(BF16)

    def dact_part(start, size):
        here = pl.ds(start, size)
        down = jnp.concatenate([kept_down[k, here, :] for k in range(len(columns))], axis=1)
        dacts[:, here] = mm_nt(g_turned[...], down) + mm(dlats[...], in_ref[:, here])

    def dact_step(index, carry):
        dact_part(pl.multiple_of(index * 2 * LANES, 2 * LANES), 2 * LANES)
        return carry

    for copy in down_copies:
        copy.wait()
    lax.fori_loop(0, block // (2 * LANES), dact_step, 0)
    if block % (2 * LANES):
        dact_part(block // (2 * LANES) * 2 * LANES, block % (2 * LANES))
    for copy in copies:
        copy.wait()

    def hidden_part(start, size):
        here = pl.ds(start, size)
        none = jnp.zeros((slots, size), BF16)
        switch, lift = switch_ref[:, here], lift_ref[:, here]
        pieces = jnp.where(
            owns_gate,
            jnp.concatenate(
                [jnp.concatenate([switch, none], axis=1), jnp.concatenate([none, lift], axis=1)],
                axis=0,
            ),
            jnp.concatenate(
                [jnp.concatenate([none, switch], axis=1), jnp.concatenate([lift, none], axis=1)],
                axis=0,
            ),
        )
        weight = jnp.concatenate(
            [
                jnp.concatenate([kept[q, :, here], kept[4 + q, :, here]], axis=1)
                for q in range(4)
            ],
            axis=0,
        )
        total = mm(x_turned[...], weight)
        total = total + LOWRANK_FACTOR * mm(latents[...], pieces)
        gate = jnp.where(owns_gate, total[:, :size], total[:, size:])
        up = jnp.where(owns_gate, total[:, size:], total[:, :size])
        sigma = jax.nn.sigmoid(gate)
        act = (gate * sigma * up).astype(BF16)
        dact = dacts[:, here]
        dgate = (dact * up * (sigma * (1.0 + gate * (1.0 - sigma)))).astype(BF16)
        dup = (dact * gate * sigma).astype(BF16)
        dfirst, dsecond = jnp.where(owns_gate, dgate, dup), jnp.where(owns_gate, dup, dgate)
        acts[:, here] = act
        firsts[:, here] = dfirst
        seconds[:, here] = dsecond
        both = jnp.concatenate([dfirst, dsecond], axis=1)
        dlat_sum[:, : 2 * slots] += mm_nt(both, pieces)
        piece_grad = LOWRANK_FACTOR * mm(stack[slots:, :], both)
        low, high = piece_grad[:, :size], piece_grad[:, size:]
        deep_ref[:slots, here] = mm(stack[:slots, :], act)
        deep_ref[slots : 2 * slots, here] = jnp.where(owns_gate, low, high)[:slots]
        deep_ref[2 * slots :, here] = jnp.where(owns_gate, high, low)[slots:]

    def hidden_step(index, carry):
        hidden_part(pl.multiple_of(index * 2 * LANES, 2 * LANES), 2 * LANES)
        return carry

    lax.fori_loop(0, block // (2 * LANES), hidden_step, 0)
    if block % (2 * LANES):
        hidden_part(block // (2 * LANES) * 2 * LANES, block % (2 * LANES))

    def back(q, carry):
        value = mm_nt(firsts[...], kept[q]) + mm_nt(seconds[...], kept[4 + q])
        start = ((q // 2) ^ parity) * (width // 2) + lax.rem(q, 2) * quarter
        lanes = pl.ds(pl.multiple_of(start, quarter), quarter)
        back_own[:, lanes] = value[:count]
        back_near[:, lanes] = value[count:].astype(BF16)
        return carry

    lax.fori_loop(0, 4, back, 0)
    dlat_sum[:, 2 * slots : 3 * slots] = mm_nt(acts[...], in_ref[...])
    back_own[:, width:] = dlat_sum[:count, :]
    back_near[:, width:] = dlat_sum[count:, :].astype(BF16)


def down_kernel(meta, *refs):
    acts_refs, whole_down = refs[:2], refs[2:7]
    results = (refs[7:9], refs[9:11])
    kept_down, semaphores = refs[11:]
    parts, _, part = kept_down.shape
    parity, member = meta[0], meta[2]
    copies = [
        pltpu.make_async_copy(ref, kept_down.at[pl.ds(start, size)], semaphores.at[index])
        for index, (ref, start, size) in enumerate(zip(whole_down, (0, 4, 5, 6, 7), (4, 1, 1, 1, 1)))
    ]
    for copy in copies:
        copy.start()
    for copy in copies:
        copy.wait()

    def columns(index, carry):
        half = (index - 4) // 2 ^ parity
        base = jnp.where(index < 4, index, 4 + 2 * half + lax.rem(index, 2))
        lanes = pl.ds(pl.multiple_of((member ^ base) * part, part), part)
        for acts, outs in zip(acts_refs, results):
            value = mm(acts[...], kept_down[index])
            for side, out in enumerate(outs):
                rows = slice(side * out.shape[0], (side + 1) * out.shape[0])
                out[:, lanes] = value[rows].astype(out.dtype)
        return carry

    lax.fori_loop(0, parts, columns, 0)


def down_projection(meta, acts, weights):
    tokens, block = acts[0].shape
    width = 8 * weights["down"][0].shape[2]
    count = tokens // 2
    kept = jax.ShapeDtypeStruct((count, width), F32)
    sent = jax.ShapeDtypeStruct((count, width), BF16)
    return pl.pallas_call(
        down_kernel,
        out_shape=(kept, sent, sent, sent),
        in_specs=[pl.BlockSpec(memory_space=pltpu.SMEM)]
        + [pl.BlockSpec(memory_space=pltpu.VMEM)] * 2
        + [pl.BlockSpec(memory_space=pl.ANY)] * 5,
        scratch_shapes=[
            pltpu.VMEM((8, block, width // 8), BF16),
            pltpu.SemaphoreType.DMA((5,)),
        ],
        compiler_params=pltpu.CompilerParams(vmem_limit_bytes=24 << 20),
        cost_estimate=pl.CostEstimate(
            flops=4 * tokens * width * block,
            transcendentals=0,
            bytes_accessed=2 * width * block + 8 * tokens * width,
        ),
        name="down_projection",
    )(meta, *acts, *weights["down"])


def feed_forward_pair(meta, rows, sens, seen, weights, pieces):
    count, width = sens[0].shape
    slots, block = pieces[-1].shape
    wide, tokens = width + LANES, 2 * count
    operands = (*rows, *sens, *seen, *pieces)
    arrays = (*weights["own"], *weights["over_y"], *weights["down"])
    return pl.pallas_call(
        feed_forward_kernel,
        out_shape=(
            jax.ShapeDtypeStruct((count, wide), F32),
            jax.ShapeDtypeStruct((count, wide), BF16),
            jax.ShapeDtypeStruct((tokens, block), BF16),
            jax.ShapeDtypeStruct((3 * slots, block), F32),
        ),
        in_specs=[pl.BlockSpec(memory_space=pltpu.SMEM)]
        + [pl.BlockSpec(memory_space=pltpu.VMEM)] * len(operands)
        + [pl.BlockSpec(memory_space=pl.ANY)] * len(arrays),
        scratch_shapes=[
            pltpu.VMEM((tokens, width), BF16),
            pltpu.VMEM((tokens, width), BF16),
            pltpu.VMEM((tokens, 2 * slots), BF16),
            pltpu.VMEM((tokens, slots), BF16),
            pltpu.VMEM((3 * slots, tokens), BF16),
            pltpu.VMEM((tokens, block), BF16),
            pltpu.VMEM((tokens, block), BF16),
            pltpu.VMEM((tokens, block), F32),
            pltpu.VMEM((tokens, LANES), F32),
            pltpu.VMEM((8, width // 4, block), BF16),
            pltpu.VMEM((8, block, width // 8), BF16),
            pltpu.SemaphoreType.DMA((13,)),
        ],
        compiler_params=pltpu.CompilerParams(vmem_limit_bytes=50 << 20),
        cost_estimate=pl.CostEstimate(
            flops=2 * 5 * tokens * width * block,
            transcendentals=tokens * block,
            bytes_accessed=6 * width * block + 20 * tokens * width,
        ),
        name="feed_forward",
    )(meta, *operands, *arrays)


def feed_forward_shared(norm2, sens_pairs, weights, small, all_seen):
    ffn_in, *pieces = small
    lower = pieces[0]
    width = norm2.shape[1]
    slots, block = pieces[-1].shape
    hidden_width = block * ACROSS_Y
    member = lax.axis_index("grp")
    parity = lax.axis_index("rep") % 2
    owns_gate = member < ACROSS_Y
    hidden = member % ACROSS_Y
    meta = jnp.stack([parity, owns_gate.astype(jnp.int32), member]).astype(jnp.int32)
    seen = all_seen[0]
    seen_two = jnp.concatenate([seen, seen], axis=1)
    latent_gu = (mm(norm2, ffn_in) * seen_two).astype(BF16)
    pad = jnp.zeros((norm2.shape[0], LANES - 2 * slots), BF16)
    rows = jnp.concatenate([norm2, latent_gu, pad], axis=1)
    across = flip(rows, ACROSS_X)
    results = []
    for index, sens_pair in enumerate(sens_pairs):
        if index == 1:
            result, (across,) = tie(results[0][1], (across,))
            results[0][1] = result
            rows = across
        seen_pair = all_seen[2 * index : 2 * index + 2]
        row_pair = (rows, flip(rows, CORE))
        results.append(
            list(feed_forward_pair(meta, row_pair, sens_pair, seen_pair, weights, pieces))
        )

    chips = [result[0] + flip(result[1], CORE).astype(F32) for result in results]
    deep = (results[0][3] + results[1][3]).astype(BF16)
    members = lax.axis_size("grp")
    owners = members * block // hidden_width
    deep = deep.reshape(3 * slots, owners, block // owners).transpose(1, 0, 2)
    placed = jnp.zeros((members, 3 * slots, block // owners), BF16)
    placed = lax.dynamic_update_slice_in_dim(placed, deep, hidden * owners, 0)
    forwards = down_projection(meta, [result[2] for result in results], weights)
    across = flip(chips[1].astype(BF16), ACROSS_X)
    across, (placed, *forwards) = tie(across, (placed, *forwards))
    backward = chips[0] + across.astype(F32)
    dlat_gu = (LOWRANK_FACTOR * backward[:, width : width + 2 * slots] * seen_two).astype(BF16)
    dnorm2 = backward[:, :width] + mm_nt(dlat_gu, ffn_in)
    latent_d = (backward[:, width + 2 * slots : width + 3 * slots] * seen).astype(BF16)

    dnorm2, (mine, near, other, other_near) = tie(dnorm2, forwards)
    other = (other.astype(F32) + flip(other_near, CORE).astype(F32)).astype(BF16)
    shares = (mine, flip(near, CORE), flip(other, ACROSS_X))

    def finish(shares):
        mine, near, other = shares
        response_part = mine + near.astype(F32) + other.astype(F32)
        return response_part + LOWRANK_FACTOR * mm(latent_d, lower)

    return (finish, shares), dnorm2, latent_d, dlat_gu, placed


def exchange(evens, odds, by_permutes, later=None):
    if by_permutes:
        total = (evens.astype(F32) + flip(odds, CORE).astype(F32)).astype(BF16)
        if later is not None:
            total, (later,) = tie(total, (later,))
        masks = (ACROSS_X, ACROSS_Y, ACROSS_X | ACROSS_Y)
        return [total[0], *(flip(total[i], mask) for i, mask in enumerate(masks, start=1))], later
    parts = jnp.stack([evens, odds], axis=1).reshape(-1, *evens.shape[1:])
    received = lax.all_to_all(parts, "grp", 0, 0, tiled=True)
    return [received[i] for i in range(received.shape[0])], later


def simple_call(kernel, name, out_shape, operands, flops):
    return pl.pallas_call(
        kernel,
        out_shape=out_shape,
        compiler_params=pltpu.CompilerParams(vmem_limit_bytes=32 << 20),
        cost_estimate=pl.CostEstimate(
            flops=flops,
            transcendentals=0,
            bytes_accessed=sum(array.size * array.dtype.itemsize for array in operands),
        ),
        name=name,
    )(*operands)


def early_gradients_kernel(
    dq_ref,
    asking_ref,
    seen_ref,
    latent_q_ref,
    norm1_ref,
    latent_d_ref,
    sens_ref,
    dlat_gu_ref,
    norm2_ref,
    dlat_o_ref,
    attended_ref,
    latent_o_ref,
    dbranch_ref,
    dlat_q_ref,
    early_ref,
):
    dlat_q = (LOWRANK_FACTOR * mm_nt(dq_ref[...], asking_ref[...]) * seen_ref[...]).astype(BF16)
    dlat_q_ref[...] = dlat_q
    two = LOWRANK_FACTOR
    start = 0
    for factor, small, large in (
        (1.0, dlat_q, norm1_ref),
        (two, latent_q_ref[...], dq_ref),
        (two, latent_d_ref[...], sens_ref),
        (1.0, dlat_gu_ref[...], norm2_ref),
        (1.0, dlat_o_ref[...], attended_ref),
        (two, latent_o_ref[...], dbranch_ref),
    ):
        rows = small.shape[1]
        early_ref[start : start + rows, :] = (factor * mm_tn(small, large[...])).astype(BF16)
        start += rows


def early_gradients(*operands):
    count, width = operands[0].shape
    slots = operands[1].shape[0]
    return simple_call(
        early_gradients_kernel,
        "early_gradients",
        (
            jax.ShapeDtypeStruct((count, slots), BF16),
            jax.ShapeDtypeStruct((7 * slots, width), BF16),
        ),
        operands,
        2 * count * width * 8 * slots,
    )


def key_value_gradients_kernel(turn_ref, *refs):
    received, refs = refs[:-12], refs[-12:]
    early_ref, cos_ref, sin_ref, right_ref, seen_ref, latent_ref, norm_ref = refs[:7]
    dkv_ref, dlat_ref, even_ref, odd_ref, late_ref = refs[7:12]
    half = HEAD_DIM // 2
    total = received[0][...].astype(F32)
    for source in received[1:]:
        total = total + source[...].astype(F32)
    kv_width = total.shape[1] // 2
    pieces = []
    for start in range(0, kv_width, LANES):
        value = total[:, start : start + LANES]
        turned = value * sin_ref[...]
        first = lax.rem(lane_of(turned.shape), HEAD_DIM) < half
        turned = jnp.where(
            first, pltpu.roll(turned, LANES - half, 1), -pltpu.roll(turned, half, 1)
        )
        pieces.append((value * cos_ref[...] + turned).astype(BF16))
    dkv = jnp.concatenate([*pieces, total[:, kv_width:].astype(BF16)], axis=1)
    dkv_ref[...] = dkv
    dlat = (LOWRANK_FACTOR * mm_nt(dkv, right_ref[...]) * seen_ref[...]).astype(BF16)
    dlat_ref[...] = dlat
    late_ref[...] = mm_tn(dlat, norm_ref[...]).astype(BF16)
    thin = (LOWRANK_FACTOR * mm_tn(latent_ref[...], dkv)).astype(BF16)
    rows, head = late_ref.shape[0], early_ref.shape[0]
    thin = jnp.concatenate([thin[: rows // 2, :kv_width], thin[rows // 2 :, kv_width:]], axis=0)
    share = even_ref.shape[2]
    for place in range(2 * even_ref.shape[0]):
        pack_ref = (even_ref, odd_ref)[place % 2]
        columns = pl.ds(pl.multiple_of((place ^ turn_ref[0]) * share, share), share)
        pack_ref[place // 2, :head, :] = early_ref[:, columns]
        pack_ref[place // 2, head : head + rows, :] = late_ref[:, columns]
        for index, start in enumerate(range(0, kv_width, share)):
            first = head + (index + 1) * rows
            pack_ref[place // 2, first : first + rows, :] = thin[:, start : start + share]


def key_value_gradients(turn, received, early, cosines, sines, kv_right, seen_two, latent_kv, norm1):
    members = lax.axis_size("grp")
    count, kv_two = received[0].shape
    rows, width = kv_right.shape[0], norm1.shape[1]
    share = width // members
    packed = early.shape[0] + rows * (1 + kv_two // 2 // share)
    operands = (*received, early, cosines, sines, kv_right, seen_two, latent_kv, norm1)
    pack = jax.ShapeDtypeStruct((members // 2, packed, share), BF16)
    return pl.pallas_call(
        key_value_gradients_kernel,
        out_shape=(
            jax.ShapeDtypeStruct((count, kv_two), BF16),
            jax.ShapeDtypeStruct((count, rows), BF16),
            pack,
            pack,
        ),
        in_specs=[pl.BlockSpec(memory_space=pltpu.SMEM)]
        + [pl.BlockSpec(memory_space=pltpu.VMEM)] * len(operands),
        scratch_shapes=[pltpu.VMEM((rows, width), BF16)],
        compiler_params=pltpu.CompilerParams(vmem_limit_bytes=32 << 20),
        cost_estimate=pl.CostEstimate(
            flops=2 * count * rows * (width + 2 * kv_two),
            transcendentals=0,
            bytes_accessed=sum(array.size * array.dtype.itemsize for array in operands),
        ),
        name="key_value_gradients",
    )(turn, *operands)


def place_kernel(jobs, groups, slots, *refs):
    place_ref, refs = refs[0], refs[1:]
    outs = refs[len(refs) - len(jobs) :]
    for (source, index, is_right), out_ref in zip(jobs, outs):
        value = jnp.concatenate(
            [
                refs[source * groups + g][index * slots : (index + 1) * slots, :]
                for g in range(groups)
            ],
            axis=0,
        )
        if is_right:
            out_ref[...] = mm_tn(place_ref[...], value)
        else:
            out_ref[...] = mm_tn(value, place_ref[...])


def place_gradients(place, sources, slots, jobs):
    groups = len(sources[0])
    narrow = place.shape[1]
    shapes = []
    for source, _, is_right in jobs:
        size = sources[source][0].shape[1]
        shapes.append(
            jax.ShapeDtypeStruct((narrow, size) if is_right else (size, narrow), F32)
        )
    return pl.pallas_call(
        functools.partial(place_kernel, jobs, groups, slots),
        out_shape=tuple(shapes),
        compiler_params=pltpu.CompilerParams(vmem_limit_bytes=32 << 20),
        cost_estimate=pl.CostEstimate(
            flops=2 * sum(shape.size for shape in shapes) * place.shape[0],
            transcendentals=0,
            bytes_accessed=4 * sum(shape.size for shape in shapes),
        ),
        name="place_gradients",
    )(place, *[array for source in sources for array in source])


def round_groups(array):
    groups = lax.axis_size("rep")
    return [array] + [
        lax.ppermute(array, "rep", [(i, (i + shift) % groups) for i in range(groups)])
        for shift in range(1, groups)
    ]


def shards(
    tokens,
    response_sensitivity,
    seq_lengths,
    prefix_lengths,
    adapter_ids,
    attn_gain,
    mlp_gain,
    qkv_weight,
    out_weight,
    gate_up_weight,
    down_weight,
    query_in,
    asking_right_pieces,
    key_in,
    lookup_right_pieces,
    value_in,
    content_right_pieces,
    output_in,
    final_right_pieces,
    gate_in,
    switch_right_pieces,
    up_in,
    lift_right_pieces,
    down_in,
    lower_right_pieces,
):
    count, width = tokens.shape
    members = lax.axis_size("grp")
    groups = lax.axis_size("rep")
    kv_width = lookup_right_pieces.shape[1]
    narrow = query_in.shape[1]
    group = lax.axis_index("rep")
    member = lax.axis_index("grp")
    lengths = lax.dynamic_slice_in_dim(seq_lengths, 2 * group, 2)
    prefixes = lax.dynamic_slice_in_dim(prefix_lengths, 2 * group, 2)
    chosen_ids = lax.dynamic_slice_in_dim(adapter_ids, 2 * group, 2)
    key_count = count * members
    sens = response_sensitivity

    paired = members == 8 and groups % 2 == 0
    qkv_full = lax.all_gather(qkv_weight, "grp", axis=1, tiled=True)
    if paired:
        steps = gather_hidden_block(gate_up_weight, down_weight)
        transfers = next(steps)
    else:
        out_full = lax.all_gather(out_weight, "grp", axis=1, tiled=True)
        down_full = lax.all_gather(down_weight, "grp", axis=1, tiled=True)
        gate_up_full = lax.all_gather(gate_up_weight, "grp", axis=1, tiled=True)

    turn = member if paired else 0
    key_index = jnp.arange(key_count, dtype=jnp.int32)
    key_index = (key_index // count ^ turn) * count + key_index % count
    key_second = (key_index >= lengths[0]).astype(jnp.int32)
    key_position = key_index - key_second * lengths[0]
    own_index = member * count + jnp.arange(count, dtype=jnp.int32)
    own_second = (own_index >= lengths[0]).astype(jnp.int32)
    position = own_index - own_second * lengths[0]
    prefix = jnp.where(own_second == 0, prefixes[0], prefixes[1])
    allowed = (key_second[:, None] == own_second[None, :]) & (
        (key_position[:, None] <= position[None, :]) | (key_position[:, None] < prefix[None, :])
    )
    bias = jnp.where(allowed, 0.0, MASKED).astype(F32)
    first_key = own_second[0] * lengths[0]
    last_key = jnp.max(own_second * lengths[0] + jnp.maximum(position, prefix - 1))
    span = jnp.stack(
        [first_key // KEY_BLOCK, last_key // KEY_BLOCK + 1, turn * count // KEY_BLOCK]
    ).astype(jnp.int32)

    slots = 2 * RANK
    columns = jnp.arange(narrow, dtype=jnp.int32)
    slot = jnp.arange(slots, dtype=jnp.int32)
    slot_column = jnp.where(slot < RANK, chosen_ids[0], chosen_ids[1]) * RANK + slot % RANK
    pick = (columns[:, None] == slot_column[None, :]).astype(BF16)

    def seen_by(device):
        index = device * count + jnp.arange(count, dtype=jnp.int32)
        second = (index >= lengths[0]).astype(jnp.int32)
        return (second[:, None] == slot[None, :] // RANK).astype(F32)

    def pick_in(weight):
        return mm(weight, pick).astype(BF16)

    def pick_right(weight):
        return mm_tn(pick, weight).astype(BF16)

    seen = seen_by(member)
    seen_three = jnp.concatenate([seen, seen, seen], axis=1)
    qkv_in = jnp.concatenate([pick_in(query_in), pick_in(key_in), pick_in(value_in)], axis=1)
    asking = pick_right(asking_right_pieces)
    lookup = pick_right(lookup_right_pieces)
    content = pick_right(content_right_pieces)
    none = jnp.zeros_like(lookup)
    kv_right = jnp.concatenate(
        [jnp.concatenate([lookup, none], axis=1), jnp.concatenate([none, content], axis=1)], axis=0
    )
    out_in = pick_in(output_in)
    final = pick_right(final_right_pieces)
    lower = pick_right(lower_right_pieces)
    small = (
        jnp.concatenate([pick_in(gate_in), pick_in(up_in)], axis=1),
        pick_right(switch_right_pieces),
        pick_right(lift_right_pieces),
        lax.dot_general(
            pick, down_in, (((0,), (1,)), ((), ())), preferred_element_type=F32
        ).astype(BF16),
        lower,
    )

    cycle = jnp.arange(groups * slots, dtype=jnp.int32)
    source = (group - cycle // slots) % groups
    sequence = 2 * source + cycle % slots // RANK
    sequences = jnp.arange(adapter_ids.shape[0], dtype=jnp.int32)
    theirs = jnp.where(sequence[:, None] == sequences[None, :], adapter_ids[None, :], 0)
    all_column = jnp.sum(theirs, axis=1) * RANK + cycle % RANK
    place = (all_column[:, None] == columns[None, :]).astype(BF16)
    incoming = tokens.astype(F32)
    scale_one = inverse_rms(incoming)
    norm1 = (incoming * scale_one * attn_gain).astype(BF16)
    if paired:
        block = down_weight.shape[0] // ACROSS_Y
        start = member % ACROSS_Y * block
        pieces = [lax.dynamic_slice_in_dim(piece, start, block, 1) for piece in small[1:4]]
        others = (seen_by(member ^ mask) for mask in (CORE, ACROSS_X, ACROSS_X | CORE))
        ready = (*transfers, asking, kv_right, out_in, final, lower, place, small[0], *pieces)
        norm1, ready = tie(norm1, (*ready, *others))
        transfers = ready[: len(transfers)]
        asking, kv_right, out_in, final, lower, place, ffn_in, *ready = ready[len(transfers) :]
        small = (ffn_in, lower, *ready[:3])
        all_seen = (seen, *ready[3:])
        transfers = steps.send(transfers)
        out_full = lax.all_gather(out_weight, "grp", axis=1, tiled=True)
    latent_qkv = (mm(norm1, qkv_in) * seen_three).astype(BF16)
    latent_q, latent_kv = latent_qkv[:, :slots], latent_qkv[:, slots:]
    half = HEAD_DIM // 2
    freqs = 10000.0 ** (-2.0 * jnp.arange(half).astype(F32) / HEAD_DIM)
    freqs = jnp.tile(freqs, LANES // half)
    angles = position.astype(F32)[:, None] * freqs[None, :]
    cosines, sines = jnp.cos(angles), jnp.sin(angles)

    def widen(table, size):
        return jnp.tile(table, (1, size // LANES))

    qkv = mm(norm1, qkv_full)
    query = qkv[:, :width] + LOWRANK_FACTOR * mm(latent_q, asking)
    own_kv = qkv[:, width:] + LOWRANK_FACTOR * mm(latent_kv, kv_right)
    query = rotate(query, widen(cosines, width), widen(sines, width)).astype(BF16)
    query = query * jnp.asarray(HEAD_DIM**-0.5, BF16)
    key_own = rotate(own_kv[:, :kv_width], widen(cosines, kv_width), widen(sines, kv_width))
    key_value = jnp.concatenate([key_own, own_kv[:, kv_width:]], axis=1).astype(BF16)
    if paired:
        key_value, transfers = tie(key_value, transfers)
        key_value, (ready, *transfers) = tie(gather_key_values(key_value), (sens, *transfers))
        transfers = steps.send(transfers)
        sens_near, sens_across = flip(ready, CORE), flip(ready, ACROSS_X)
    else:
        key_value = lax.all_gather(key_value, "grp", axis=0, tiled=True)
    attended_low, lse = attention_forward(span, query, key_value, bias)
    if paired:
        attended_low, (sens_near, *transfers) = tie(attended_low, (sens_near, *transfers))
        transfers = (sens_across, *steps.send(transfers))

    latent_o = (mm(attended_low, out_in) * seen).astype(BF16)
    stream = incoming + (mm(attended_low, out_full) + LOWRANK_FACTOR * mm(latent_o, final))
    scale_two = inverse_rms(stream)
    norm2 = (stream * scale_two * mlp_gain).astype(BF16)
    if paired:
        norm2, (sens_across, *transfers) = tie(norm2, transfers)
        sens_pairs = [(sens, sens_near), (sens_across, flip(sens_across, CORE))]
        transfers = steps.send(transfers)
        try:
            steps.send(transfers)
        except StopIteration as stop:
            weights = stop.value
        (finish, shares), dnorm2, latent_d, dlat_gu, deep = feed_forward_shared(
            norm2, sens_pairs, weights, small, all_seen
        )
    else:
        (finish, shares), dnorm2, latent_d, dlat_gu, deep = feed_forward_alone(
            norm2, sens, gate_up_full, down_full, small, seen
        )
    dhidden = sens.astype(F32) + norm_backward(stream, scale_two, mlp_gain, dnorm2)
    dbranch = dhidden.astype(BF16)
    dlat_o = (LOWRANK_FACTOR * mm_nt(dbranch, final) * seen).astype(BF16)
    dattended = (mm_nt(dbranch, out_full) + mm_nt(dlat_o, out_in)).astype(BF16)

    dattended, (deep,) = tie(dattended, (deep,))
    deep_sum = lax.psum_scatter(deep, "grp", scatter_dimension=0, tiled=True)[0]

    dq, dkv_even, dkv_odd = attention_backward(
        span, query, dattended, attended_low, lse, key_value, bias, cosines, sines
    )
    dkv_odd, (deep_sum, *shares) = tie(dkv_odd, (deep_sum, *shares))
    received, dq = exchange(dkv_even, dkv_odd, paired, dq)
    dlat_q, early = early_gradients(
        dq,
        asking,
        seen,
        latent_q,
        norm1,
        latent_d,
        sens,
        dlat_gu,
        norm2,
        dlat_o,
        attended_low,
        latent_o,
        dbranch,
    )
    dnorm_q = mm_nt(dq, qkv_full[:, :width]) + mm_nt(dlat_q, qkv_in[:, :slots])
    turns = jnp.full((1,), turn, jnp.int32)
    dkv, dlat_kv, late_even, late_odd = key_value_gradients(
        turns, received, early, cosines, sines, kv_right, seen_three[:, : 2 * slots], latent_kv, norm1
    )
    deep_sum = round_groups(deep_sum)
    late_parts = [part.astype(F32) for part in exchange(late_even, late_odd, paired)[0]]
    late_sum = round_groups(sum(late_parts[1:], late_parts[0]).astype(BF16))
    level_response = (stream + finish(shares)).astype(BF16)
    dnorm1 = dnorm_q + mm_nt(dkv, qkv_full[:, width:]) + mm_nt(dlat_kv, qkv_in[:, slots:])
    input_grad = (dhidden + norm_backward(incoming, scale_one, attn_gain, dnorm1)).astype(BF16)

    share = width // members
    pieces = kv_width // share
    thin_start = 9 * slots
    thin_sum = [
        jnp.concatenate(
            [
                array[thin_start + 2 * slots * i : thin_start + 2 * slots * (i + 1)]
                for i in range(pieces)
            ],
            axis=1,
        )
        for array in late_sum
    ]
    jobs = (
        (0, 0, False),
        (0, 1, True),
        (0, 7, False),
        (2, 0, True),
        (0, 8, False),
        (2, 1, True),
        (0, 5, False),
        (0, 6, True),
        (0, 3, False),
        (1, 1, True),
        (0, 4, False),
        (1, 2, True),
        (1, 0, False),
        (0, 2, True),
    )
    grads = list(place_gradients(place, (late_sum, deep_sum, thin_sum), slots, jobs))
    own = kv_width // members
    for index in (3, 5):
        grads[index] = lax.dynamic_slice_in_dim(grads[index], member * own, own, 1)
    return (level_response, input_grad, *grads)


def solution(mesh):
    rows = P(("rep", "grp"), None)
    split = P(None, "grp")
    in_specs = (rows, rows, *[P()] * 5, *[split] * 4, *[P()] * 14)
    out_specs = (rows, rows, *[P("grp", None), P(None, "grp")] * 7)
    return jax.shard_map(shards, mesh=mesh, in_specs=in_specs, out_specs=out_specs, check_vma=False)
```

```python
import functools

import jax
import jax.numpy as jnp
from jax import lax
from jax.experimental import pallas as pl
from jax.experimental.pallas import tpu as pltpu
from jax.sharding import PartitionSpec as P

HEADS = 32
KV_HEADS = 4
HEAD_DIM = 64
RANK = 16
LANES = 128
KEY_BLOCK = 1024
PAIRS = 4

EPS = 1e-05
LOWRANK_FACTOR = 2.0
MASKED = -1e30
F32 = jnp.float32
BF16 = jnp.bfloat16


def mm(left, right):
    return jnp.dot(left, right, preferred_element_type=F32)


def mm_nt(left, right):
    return lax.dot_general(left, right, (((1,), (1,)), ((), ())), preferred_element_type=F32)


def mm_tn(left, right):
    return lax.dot_general(left, right, (((0,), (0,)), ((), ())), preferred_element_type=F32)


def inverse_rms(value):
    return lax.rsqrt(jnp.mean(value * value, axis=-1, keepdims=True) + EPS)


def norm_backward(value, scale, gain, grad):
    scaled = gain * grad
    return scale * scaled - value * (scale * scale * scale) * jnp.mean(
        scaled * value, axis=-1, keepdims=True
    )


def half_turn(value):
    half = HEAD_DIM // 2
    lane = lax.broadcasted_iota(jnp.int32, value.shape, 1) % HEAD_DIM
    return jnp.where(
        lane < half, -jnp.roll(value, -half, axis=1), jnp.roll(value, half, axis=1)
    )


def rotate(value, cosines, sines):
    return value * cosines + half_turn(value) * sines


def unrotate(grad, cosines, sines):
    return grad * cosines - half_turn(grad * sines)


def lane_of(shape):
    return lax.broadcasted_iota(jnp.int32, shape, 1)


def key_rows(span, index):
    return pl.ds(pl.multiple_of((index ^ span[2]) * KEY_BLOCK, KEY_BLOCK), KEY_BLOCK)


def spread_heads(span, odd, source_ref, pair_ref):
    def step(index, carry):
        rows = key_rows(span, index)
        value = source_ref[rows, :].astype(F32)
        turned = pltpu.roll(value, HEAD_DIM, 1)
        low = lane_of(value.shape) < HEAD_DIM
        none = jnp.zeros_like(value)
        pair_ref[0, rows, :] = jnp.where(low, jnp.where(odd, turned, value), none).astype(BF16)
        pair_ref[1, rows, :] = jnp.where(low, none, jnp.where(odd, value, turned)).astype(BF16)
        return carry

    lax.fori_loop(span[0], span[1], step, 0)


def attention_forward_kernel(
    per_kv, span, q_ref, key_ref, value_ref, bias_ref, out_ref, lse_ref, k_ref, v_ref
):
    tokens = q_ref.shape[0]
    odd = lax.rem(pl.program_id(0) // per_kv, LANES // HEAD_DIM) == 1

    @pl.when(lax.rem(pl.program_id(0), per_kv) == 0)
    def _():
        spread_heads(span, odd, key_ref, k_ref)
        spread_heads(span, odd, value_ref, v_ref)

    queries = [q_ref[:, pair * LANES : (pair + 1) * LANES] for pair in range(PAIRS)]

    def step(index, carry):
        rows = key_rows(span, index)
        bias = bias_ref[rows, :]
        new = []
        flat = jnp.concatenate([v_ref[0, rows, :], v_ref[1, rows, :]], axis=0).T
        for pair, (peaks, totals, mixed) in enumerate(carry):
            tops, sums, parts, decays = [], [], [], []
            for side in range(2):
                scores = mm_nt(k_ref[side, rows, :], queries[pair]) + bias
                top = jnp.maximum(peaks[side], jnp.max(scores, axis=0, keepdims=True))
                decay = jnp.exp(peaks[side] - top)
                probs = jnp.exp(scores - top)
                tops.append(top)
                sums.append(totals[side] * decay + jnp.sum(probs, axis=0, keepdims=True))
                decays.append(jnp.broadcast_to(decay, (HEAD_DIM, tokens)))
                parts.append(probs.astype(BF16))
            mixed = mixed * jnp.concatenate(decays, axis=0)
            mixed = mixed + mm(flat, jnp.concatenate(parts, axis=0))
            new.append((tuple(tops), tuple(sums), mixed))
        return tuple(new)

    low = jnp.full((1, tokens), MASKED, F32)
    none = jnp.zeros((1, tokens), F32)
    start = ((low, low), (none, none), jnp.zeros((LANES, tokens), F32))
    result = lax.fori_loop(span[0], span[1], step, (start,) * PAIRS)
    for pair, (peaks, totals, mixed) in enumerate(result):
        weight = jnp.concatenate(
            [jnp.broadcast_to(1.0 / total, (HEAD_DIM, tokens)) for total in totals], axis=0
        )
        out_ref[:, pair * LANES : (pair + 1) * LANES] = (mixed * weight).T.astype(BF16)
        lse_ref[pair] = jnp.concatenate(
            [peak + jnp.log(total) for peak, total in zip(peaks, totals)], axis=0
        )


def key_value_specs(keys, per_kv):
    blocks = KV_HEADS * HEAD_DIM // LANES
    heads = LANES // HEAD_DIM
    return [
        pl.BlockSpec((keys, LANES), lambda j, s: (0, j // per_kv // heads)),
        pl.BlockSpec((keys, LANES), lambda j, s: (0, blocks + j // per_kv // heads)),
    ]


def attention_forward(span, query, key_value, bias):
    tokens, width = query.shape
    keys = bias.shape[0]
    pairs = width // LANES
    steps = pairs // PAIRS
    pair_spec = pl.BlockSpec((tokens, PAIRS * LANES), lambda j, s: (0, j))
    return pl.pallas_call(
        functools.partial(attention_forward_kernel, steps // KV_HEADS),
        out_shape=(
            jax.ShapeDtypeStruct((tokens, width), BF16),
            jax.ShapeDtypeStruct((pairs, 2, tokens), F32),
        ),
        grid_spec=pltpu.PrefetchScalarGridSpec(
            num_scalar_prefetch=1,
            grid=(steps,),
            in_specs=[
                pair_spec,
                *key_value_specs(keys, steps // KV_HEADS),
                pl.BlockSpec((keys, tokens), lambda j, s: (0, 0)),
            ],
            out_specs=(pair_spec, pl.BlockSpec((PAIRS, 2, tokens), lambda j, s: (j, 0, 0))),
            scratch_shapes=[pltpu.VMEM((2, keys, LANES), BF16)] * 2,
        ),
        compiler_params=pltpu.CompilerParams(
            dimension_semantics=("arbitrary",), vmem_limit_bytes=30 << 20
        ),
        cost_estimate=pl.CostEstimate(
            flops=4 * tokens * keys * width,
            transcendentals=tokens * keys * HEADS // 2,
            bytes_accessed=4 * tokens * width + 16 * keys * LANES * KV_HEADS,
        ),
        name="attention_forward",
    )(span, query, key_value, key_value, bias)


def attention_backward_kernel(
    per_kv,
    span,
    q_ref,
    do_ref,
    o_ref,
    lse_ref,
    key_ref,
    value_ref,
    bias_ref,
    cos_ref,
    sin_ref,
    dq_ref,
    even_ref,
    odd_ref,
    k_ref,
    v_ref,
    dk_sum,
    dv_sum,
):
    tokens = q_ref.shape[0]
    member = lax.rem(pl.program_id(0), per_kv)
    odd = lax.rem(pl.program_id(0) // per_kv, LANES // HEAD_DIM) == 1

    @pl.when(member == 0)
    def _():
        spread_heads(span, odd, key_ref, k_ref)
        spread_heads(span, odd, value_ref, v_ref)
        dk_sum[...] = jnp.zeros_like(dk_sum)
        dv_sum[...] = jnp.zeros_like(dv_sum)

    low = lane_of((tokens, LANES)) < HEAD_DIM
    row = lax.broadcasted_iota(jnp.int32, (8, LANES), 0)
    column = lax.broadcasted_iota(jnp.int32, (8, LANES), 1)
    chooser = jnp.where(row == column // HEAD_DIM, 1.0, 0.0).astype(F32)
    queries, grads, deltas, query_stack, grad_stack = [], [], [], [], []
    for pair in range(PAIRS):
        lanes = slice(pair * LANES, (pair + 1) * LANES)
        query, grad = q_ref[:, lanes], do_ref[:, lanes]
        none = jnp.zeros_like(query)
        queries.append(query)
        grads.append(grad)
        query_stack += [jnp.where(low, query, none), jnp.where(low, none, query)]
        grad_stack += [jnp.where(low, grad, none), jnp.where(low, none, grad)]
        deltas.append(
            lax.dot_general(
                chooser,
                grad.astype(F32) * o_ref[:, lanes].astype(F32),
                (((1,), (1,)), ((), ())),
                precision=lax.Precision.HIGHEST,
                preferred_element_type=F32,
            )
        )
    query_stack = jnp.concatenate(query_stack, axis=0)
    grad_stack = jnp.concatenate(grad_stack, axis=0)

    def step(index, dqueries):
        rows = key_rows(span, index)
        bias = bias_ref[rows, :]
        all_probs, all_dscores, new = [], [], []
        flat = jnp.concatenate([k_ref[0, rows, :], k_ref[1, rows, :]], axis=0).T
        for pair, dquery in enumerate(dqueries):
            for side in range(2):
                scores = mm_nt(k_ref[side, rows, :], queries[pair]) + bias
                probs = jnp.exp(scores - lse_ref[pair, side : side + 1, :])
                dprobs = mm_nt(v_ref[side, rows, :], grads[pair])
                delta = deltas[pair][side : side + 1, :]
                dscores = (probs * (dprobs - delta)).astype(BF16)
                all_probs.append(probs.astype(BF16))
                all_dscores.append(dscores)
            new.append(dquery + mm(flat, jnp.concatenate(all_dscores[-2:], axis=0)))
        dk_sum[rows, :] += mm(jnp.concatenate(all_dscores, axis=1), query_stack)
        dv_sum[rows, :] += mm(jnp.concatenate(all_probs, axis=1), grad_stack)
        return tuple(new)

    dqueries = lax.fori_loop(
        span[0], span[1], step, (jnp.zeros((LANES, tokens), F32),) * PAIRS
    )
    half = HEAD_DIM // 2
    for pair, dquery in enumerate(dqueries):
        dquery = dquery.T * (HEAD_DIM**-0.5)
        turned = dquery * sin_ref[...]
        first = lax.rem(lane_of(turned.shape), HEAD_DIM) < half
        turned = jnp.where(
            first, pltpu.roll(turned, LANES - half, 1), -pltpu.roll(turned, half, 1)
        )
        dq_ref[:, pair * LANES : (pair + 1) * LANES] = (dquery * cos_ref[...] + turned).astype(BF16)

    @pl.when(member == per_kv - 1)
    def _():
        block = pl.program_id(0) // per_kv // (LANES // HEAD_DIM)

        def put(index, carry):
            for side, out_ref in enumerate((even_ref, odd_ref)):
                rows = pl.ds(pl.multiple_of((2 * index + side) * tokens, tokens), tokens)
                for sum_ref, first in ((dk_sum, 0), (dv_sum, KV_HEADS * HEAD_DIM // LANES)):
                    total = sum_ref[rows, :]
                    total = total + pltpu.roll(total, HEAD_DIM, 1)
                    keep = jnp.logical_and(odd, lane_of(total.shape) < HEAD_DIM)
                    lanes = pl.ds(pl.multiple_of((first + block) * LANES, LANES), LANES)
                    out_ref[index, :, lanes] = jnp.where(
                        keep, out_ref[index, :, lanes], total.astype(BF16)
                    )
            return carry

        lax.fori_loop(0, even_ref.shape[0], put, 0)


def attention_backward(span, query, grad, attended, lse, key_value, bias, cosines, sines):
    tokens, width = query.shape
    keys, kv_two = key_value.shape
    pairs = width // LANES
    steps = pairs // PAIRS
    per_kv = steps // KV_HEADS
    pair_spec = pl.BlockSpec((tokens, PAIRS * LANES), lambda j, s: (0, j))
    table_spec = pl.BlockSpec((tokens, LANES), lambda j, s: (0, 0))
    return pl.pallas_call(
        functools.partial(attention_backward_kernel, per_kv),
        out_shape=(
            jax.ShapeDtypeStruct((tokens, width), BF16),
            *[jax.ShapeDtypeStruct((keys // tokens // 2, tokens, kv_two), BF16)] * 2,
        ),
        grid_spec=pltpu.PrefetchScalarGridSpec(
            num_scalar_prefetch=1,
            grid=(steps,),
            in_specs=[
                pair_spec,
                pair_spec,
                pair_spec,
                pl.BlockSpec((PAIRS, 2, tokens), lambda j, s: (j, 0, 0)),
                *key_value_specs(keys, per_kv),
                pl.BlockSpec((keys, tokens), lambda j, s: (0, 0)),
                table_spec,
                table_spec,
            ],
            out_specs=(
                pair_spec,
                *[pl.BlockSpec((keys // tokens // 2, tokens, kv_two), lambda j, s: (0, 0, 0))] * 2,
            ),
            scratch_shapes=[pltpu.VMEM((2, keys, LANES), BF16)] * 2
            + [pltpu.VMEM((keys, LANES), F32)] * 2,
        ),
        compiler_params=pltpu.CompilerParams(
            dimension_semantics=("arbitrary",), vmem_limit_bytes=46 << 20
        ),
        cost_estimate=pl.CostEstimate(
            flops=10 * tokens * keys * width,
            transcendentals=tokens * keys * HEADS // 2,
            bytes_accessed=10 * tokens * width + 8 * keys * kv_two,
        ),
        name="attention_backward",
    )(span, query, grad, attended, lse, key_value, key_value, bias, cosines, sines)


CORE, ACROSS_X, ACROSS_Y = 1, 2, 4


def flip(array, mask):
    members = lax.axis_size("grp")
    return lax.ppermute(array, "grp", [(i, i ^ mask) for i in range(members)])


def flip_group(array):
    groups = lax.axis_size("rep")
    return lax.ppermute(array, "rep", [(i, i ^ 1) for i in range(groups)])


def gather_hidden_block(gate_up_weight, down_weight):
    rows = gate_up_weight.shape[0] // 4
    block = gate_up_weight.shape[1]
    member = lax.axis_index("grp")
    parity = lax.axis_index("rep") % 2
    own = [
        lax.dynamic_slice_in_dim(gate_up_weight, ((parity ^ (q // 2)) * 2 + q % 2) * rows, rows, 0)
        for q in range(4)
    ]

    def down_rows(mask):
        start = ((member ^ mask) % ACROSS_Y) * block
        return lax.dynamic_slice_in_dim(down_weight, start, block, 0)

    low, next_quarter, *near = yield (
        flip(own[0], ACROSS_Y),
        own[1],
        flip(down_rows(ACROSS_X), ACROSS_X),
        flip(down_rows(CORE), CORE),
        flip(down_rows(ACROSS_X | CORE), ACROSS_X | CORE),
    )
    down_own = jnp.stack([down_rows(0), near[1], near[0], near[2]])
    high, low_other, down_own = yield flip(next_quarter, ACROSS_Y), flip_group(low), down_own
    mine, second = (
        lax.dynamic_slice_in_dim(down_own, 2 * parity + index, 1, 0) for index in range(2)
    )
    down_mine, high_other, second = yield flip(mine, ACROSS_Y), flip_group(high), second
    down_second, down_other = yield flip(second, ACROSS_Y), flip_group(down_mine)
    (second_other,) = yield (flip_group(down_second),)
    return {
        "own": own,
        "over_y": (low, high, low_other, high_other),
        "down": (down_own, down_mine, down_second, down_other, second_other),
    }


def gather_key_values(own):
    over_y = flip(own, ACROSS_Y)
    pieces = [own, flip(own, ACROSS_X), over_y, flip(over_y, ACROSS_X)]
    return jnp.concatenate(
        [part for piece in pieces for part in (piece, flip(piece, CORE))], axis=0
    )


def tie(value, transfers):
    value, *transfers = lax.optimization_barrier((value, *transfers))
    return value, tuple(transfers)


def feed_forward_alone(norm2, sens, gate_up_full, down_full, small, seen):
    ffn_in, switch, lift, down_in, lower = small
    slots, hidden_width = switch.shape
    seen_two = jnp.concatenate([seen, seen], axis=1)
    latent_gu = (mm(norm2, ffn_in) * seen_two).astype(BF16)
    latent_g, latent_u = latent_gu[:, :slots], latent_gu[:, slots:]
    gate_up = mm(norm2, gate_up_full) + LOWRANK_FACTOR * jnp.concatenate(
        [mm(latent_g, switch), mm(latent_u, lift)], axis=1
    )
    gate = gate_up[:, :hidden_width]
    up = gate_up[:, hidden_width:]
    sigma = jax.nn.sigmoid(gate)
    act = (gate * sigma * up).astype(BF16)
    latent_d = (mm_nt(act, down_in) * seen).astype(BF16)
    response_part = mm(act, down_full) + LOWRANK_FACTOR * mm(latent_d, lower)
    dlat_d = (LOWRANK_FACTOR * mm_nt(sens, lower) * seen).astype(BF16)
    dact = mm_nt(sens, down_full) + mm(dlat_d, down_in)
    dgate = (dact * up * (sigma * (1.0 + gate * (1.0 - sigma)))).astype(BF16)
    dup = (dact * gate * sigma).astype(BF16)
    dlat_gu = (
        LOWRANK_FACTOR
        * jnp.concatenate([mm_nt(dgate, switch), mm_nt(dup, lift)], axis=1)
        * seen_two
    ).astype(BF16)
    dnorm2 = (
        mm_nt(dgate, gate_up_full[:, :hidden_width])
        + mm_nt(dup, gate_up_full[:, hidden_width:])
        + mm_nt(dlat_gu, ffn_in)
    )
    deep = jnp.concatenate(
        [
            mm_tn(dlat_d, act),
            LOWRANK_FACTOR * mm_tn(latent_g, dgate),
            LOWRANK_FACTOR * mm_tn(latent_u, dup),
        ],
        axis=0,
    ).astype(BF16)
    members = lax.axis_size("grp")
    deep = deep.reshape(3 * slots, members, hidden_width // members).transpose(1, 0, 2)
    return (lambda shares: shares[0], (response_part,)), dnorm2, latent_d, dlat_gu, deep


def feed_forward_kernel(
    meta,
    own_x,
    near_x,
    own_g,
    near_g,
    own_seen,
    near_seen,
    lower_ref,
    switch_ref,
    lift_ref,
    in_ref,
    *refs,
):
    whole_refs, whole_down = refs[:8], refs[8:13]
    back_own, back_near, acts, deep_ref = refs[13:17]
    x_turned, g_turned, latents, dlats, stack, firsts, seconds, dacts, dlat_sum = refs[17:26]
    kept, kept_down, semaphores = refs[26:]
    count, width = own_g.shape
    tokens = 2 * count
    slots, block = in_ref.shape
    quarter = width // 4
    part = width // kept_down.shape[0]
    parity = meta[0]
    owns_gate = meta[1] == 1
    member = meta[2]
    starts = [
        pl.multiple_of((parity if q < 2 else 1 - parity) * (width // 2) + (q % 2) * quarter, quarter)
        for q in range(4)
    ]
    bases = [0, 1, 2, 3, *(4 + 2 * parity + k for k in (0, 1)), *(6 - 2 * parity + k for k in (0, 1))]
    columns = [pl.ds(pl.multiple_of((member ^ base) * part, part), part) for base in bases]
    down_copies = [
        pltpu.make_async_copy(ref, kept_down.at[pl.ds(start, size)], semaphores.at[8 + index])
        for index, (ref, start, size) in enumerate(zip(whole_down, (0, 4, 5, 6, 7), (4, 1, 1, 1, 1)))
    ]
    copies = [
        pltpu.make_async_copy(ref, kept.at[index], semaphores.at[index])
        for index, ref in enumerate(whole_refs)
    ]
    for copy in down_copies + copies:
        copy.start()
    dlat_sum[...] = jnp.zeros_like(dlat_sum)
    for index, (x_ref, g_ref, seen_ref) in enumerate(
        ((own_x, own_g, own_seen), (near_x, near_g, near_seen))
    ):
        rows = slice(index * count, (index + 1) * count)
        for q in range(4):
            x_turned[rows, q * quarter : (q + 1) * quarter] = x_ref[:, pl.ds(starts[q], quarter)]
        for k, lanes in enumerate(columns):
            g_turned[rows, k * part : (k + 1) * part] = g_ref[:, lanes]
        latents[rows, :] = x_ref[:, width : width + 2 * slots]
        dlat = LOWRANK_FACTOR * mm_nt(g_ref[...], lower_ref[...]) * seen_ref[...]
        dlats[rows, :] = dlat.astype(BF16)
        stack[:slots, rows] = dlat.T.astype(BF16)
        latent = x_ref[:, width : width + LANES].astype(F32).T[: 2 * slots]
        stack[slots:, rows] = latent.astype(BF16)

    def dact_part(start, size):
        here = pl.ds(start, size)
        down = jnp.concatenate([kept_down[k, here, :] for k in range(len(columns))], axis=1)
        dacts[:, here] = mm_nt(g_turned[...], down) + mm(dlats[...], in_ref[:, here])

    def dact_step(index, carry):
        dact_part(pl.multiple_of(index * 2 * LANES, 2 * LANES), 2 * LANES)
        return carry

    for copy in down_copies:
        copy.wait()
    lax.fori_loop(0, block // (2 * LANES), dact_step, 0)
    if block % (2 * LANES):
        dact_part(block // (2 * LANES) * 2 * LANES, block % (2 * LANES))
    for copy in copies:
        copy.wait()

    def hidden_part(start, size):
        here = pl.ds(start, size)
        none = jnp.zeros((slots, size), BF16)
        switch, lift = switch_ref[:, here], lift_ref[:, here]
        pieces = jnp.where(
            owns_gate,
            jnp.concatenate(
                [jnp.concatenate([switch, none], axis=1), jnp.concatenate([none, lift], axis=1)],
                axis=0,
            ),
            jnp.concatenate(
                [jnp.concatenate([none, switch], axis=1), jnp.concatenate([lift, none], axis=1)],
                axis=0,
            ),
        )
        weight = jnp.concatenate(
            [
                jnp.concatenate([kept[q, :, here], kept[4 + q, :, here]], axis=1)
                for q in range(4)
            ],
            axis=0,
        )
        total = mm(x_turned[...], weight)
        total = total + LOWRANK_FACTOR * mm(latents[...], pieces)
        gate = jnp.where(owns_gate, total[:, :size], total[:, size:])
        up = jnp.where(owns_gate, total[:, size:], total[:, :size])
        sigma = jax.nn.sigmoid(gate)
        act = (gate * sigma * up).astype(BF16)
        dact = dacts[:, here]
        dgate = (dact * up * (sigma * (1.0 + gate * (1.0 - sigma)))).astype(BF16)
        dup = (dact * gate * sigma).astype(BF16)
        dfirst, dsecond = jnp.where(owns_gate, dgate, dup), jnp.where(owns_gate, dup, dgate)
        acts[:, here] = act
        firsts[:, here] = dfirst
        seconds[:, here] = dsecond
        both = jnp.concatenate([dfirst, dsecond], axis=1)
        dlat_sum[:, : 2 * slots] += mm_nt(both, pieces)
        piece_grad = LOWRANK_FACTOR * mm(stack[slots:, :], both)
        low, high = piece_grad[:, :size], piece_grad[:, size:]
        deep_ref[:slots, here] = mm(stack[:slots, :], act)
        deep_ref[slots : 2 * slots, here] = jnp.where(owns_gate, low, high)[:slots]
        deep_ref[2 * slots :, here] = jnp.where(owns_gate, high, low)[slots:]

    def hidden_step(index, carry):
        hidden_part(pl.multiple_of(index * 2 * LANES, 2 * LANES), 2 * LANES)
        return carry

    lax.fori_loop(0, block // (2 * LANES), hidden_step, 0)
    if block % (2 * LANES):
        hidden_part(block // (2 * LANES) * 2 * LANES, block % (2 * LANES))

    def back(q, carry):
        value = mm_nt(firsts[...], kept[q]) + mm_nt(seconds[...], kept[4 + q])
        start = ((q // 2) ^ parity) * (width // 2) + lax.rem(q, 2) * quarter
        lanes = pl.ds(pl.multiple_of(start, quarter), quarter)
        back_own[:, lanes] = value[:count]
        back_near[:, lanes] = value[count:].astype(BF16)
        return carry

    lax.fori_loop(0, 4, back, 0)
    dlat_sum[:, 2 * slots : 3 * slots] = mm_nt(acts[...], in_ref[...])
    back_own[:, width:] = dlat_sum[:count, :]
    back_near[:, width:] = dlat_sum[count:, :].astype(BF16)


def down_kernel(meta, *refs):
    acts_refs, whole_down = refs[:2], refs[2:7]
    results = (refs[7:9], refs[9:11])
    kept_down, semaphores = refs[11:]
    parts, _, part = kept_down.shape
    parity, member = meta[0], meta[2]
    copies = [
        pltpu.make_async_copy(ref, kept_down.at[pl.ds(start, size)], semaphores.at[index])
        for index, (ref, start, size) in enumerate(zip(whole_down, (0, 4, 5, 6, 7), (4, 1, 1, 1, 1)))
    ]
    for copy in copies:
        copy.start()
    for copy in copies:
        copy.wait()

    def columns(index, carry):
        half = (index - 4) // 2 ^ parity
        base = jnp.where(index < 4, index, 4 + 2 * half + lax.rem(index, 2))
        lanes = pl.ds(pl.multiple_of((member ^ base) * part, part), part)
        for acts, outs in zip(acts_refs, results):
            value = mm(acts[...], kept_down[index])
            for side, out in enumerate(outs):
                rows = slice(side * out.shape[0], (side + 1) * out.shape[0])
                out[:, lanes] = value[rows].astype(out.dtype)
        return carry

    lax.fori_loop(0, parts, columns, 0)


def down_projection(meta, acts, weights):
    tokens, block = acts[0].shape
    width = 8 * weights["down"][0].shape[2]
    count = tokens // 2
    kept = jax.ShapeDtypeStruct((count, width), F32)
    sent = jax.ShapeDtypeStruct((count, width), BF16)
    return pl.pallas_call(
        down_kernel,
        out_shape=(kept, sent, sent, sent),
        in_specs=[pl.BlockSpec(memory_space=pltpu.SMEM)]
        + [pl.BlockSpec(memory_space=pltpu.VMEM)] * 2
        + [pl.BlockSpec(memory_space=pl.ANY)] * 5,
        scratch_shapes=[
            pltpu.VMEM((8, block, width // 8), BF16),
            pltpu.SemaphoreType.DMA((5,)),
        ],
        compiler_params=pltpu.CompilerParams(vmem_limit_bytes=24 << 20),
        cost_estimate=pl.CostEstimate(
            flops=4 * tokens * width * block,
            transcendentals=0,
            bytes_accessed=2 * width * block + 8 * tokens * width,
        ),
        name="down_projection",
    )(meta, *acts, *weights["down"])


def feed_forward_pair(meta, rows, sens, seen, weights, pieces):
    count, width = sens[0].shape
    slots, block = pieces[-1].shape
    wide, tokens = width + LANES, 2 * count
    operands = (*rows, *sens, *seen, *pieces)
    arrays = (*weights["own"], *weights["over_y"], *weights["down"])
    return pl.pallas_call(
        feed_forward_kernel,
        out_shape=(
            jax.ShapeDtypeStruct((count, wide), F32),
            jax.ShapeDtypeStruct((count, wide), BF16),
            jax.ShapeDtypeStruct((tokens, block), BF16),
            jax.ShapeDtypeStruct((3 * slots, block), F32),
        ),
        in_specs=[pl.BlockSpec(memory_space=pltpu.SMEM)]
        + [pl.BlockSpec(memory_space=pltpu.VMEM)] * len(operands)
        + [pl.BlockSpec(memory_space=pl.ANY)] * len(arrays),
        scratch_shapes=[
            pltpu.VMEM((tokens, width), BF16),
            pltpu.VMEM((tokens, width), BF16),
            pltpu.VMEM((tokens, 2 * slots), BF16),
            pltpu.VMEM((tokens, slots), BF16),
            pltpu.VMEM((3 * slots, tokens), BF16),
            pltpu.VMEM((tokens, block), BF16),
            pltpu.VMEM((tokens, block), BF16),
            pltpu.VMEM((tokens, block), F32),
            pltpu.VMEM((tokens, LANES), F32),
            pltpu.VMEM((8, width // 4, block), BF16),
            pltpu.VMEM((8, block, width // 8), BF16),
            pltpu.SemaphoreType.DMA((13,)),
        ],
        compiler_params=pltpu.CompilerParams(vmem_limit_bytes=50 << 20),
        cost_estimate=pl.CostEstimate(
            flops=2 * 5 * tokens * width * block,
            transcendentals=tokens * block,
            bytes_accessed=6 * width * block + 20 * tokens * width,
        ),
        name="feed_forward",
    )(meta, *operands, *arrays)


def feed_forward_shared(norm2, sens_pairs, weights, small, all_seen):
    ffn_in, *pieces = small
    lower = pieces[0]
    width = norm2.shape[1]
    slots, block = pieces[-1].shape
    hidden_width = block * ACROSS_Y
    member = lax.axis_index("grp")
    parity = lax.axis_index("rep") % 2
    owns_gate = member < ACROSS_Y
    hidden = member % ACROSS_Y
    meta = jnp.stack([parity, owns_gate.astype(jnp.int32), member]).astype(jnp.int32)
    seen = all_seen[0]
    seen_two = jnp.concatenate([seen, seen], axis=1)
    latent_gu = (mm(norm2, ffn_in) * seen_two).astype(BF16)
    pad = jnp.zeros((norm2.shape[0], LANES - 2 * slots), BF16)
    rows = jnp.concatenate([norm2, latent_gu, pad], axis=1)
    rows, (last,) = tie(rows, (sens_pairs[1][1],))
    sens_pairs = [sens_pairs[0], (sens_pairs[1][0], last)]
    across = flip(rows, ACROSS_X)
    results = []
    for index, sens_pair in enumerate(sens_pairs):
        if index == 1:
            result, (across,) = tie(results[0][1], (across,))
            results[0][1] = result
            rows = across
        seen_pair = all_seen[2 * index : 2 * index + 2]
        row_pair = (rows, flip(rows, CORE))
        results.append(
            list(feed_forward_pair(meta, row_pair, sens_pair, seen_pair, weights, pieces))
        )

    chips = [result[0] + flip(result[1], CORE).astype(F32) for result in results]
    deep = (results[0][3] + results[1][3]).astype(BF16)
    members = lax.axis_size("grp")
    owners = members * block // hidden_width
    deep = deep.reshape(3 * slots, owners, block // owners).transpose(1, 0, 2)
    placed = jnp.zeros((members, 3 * slots, block // owners), BF16)
    placed = lax.dynamic_update_slice_in_dim(placed, deep, hidden * owners, 0)
    forwards = down_projection(meta, [result[2] for result in results], weights)
    across = flip(chips[1].astype(BF16), ACROSS_X)
    across, (placed, *forwards) = tie(across, (placed, *forwards))
    backward = chips[0] + across.astype(F32)
    dlat_gu = (LOWRANK_FACTOR * backward[:, width : width + 2 * slots] * seen_two).astype(BF16)
    dnorm2 = backward[:, :width] + mm_nt(dlat_gu, ffn_in)
    latent_d = (backward[:, width + 2 * slots : width + 3 * slots] * seen).astype(BF16)

    dnorm2, (mine, near, other, other_near) = tie(dnorm2, forwards)
    other = (other.astype(F32) + flip(other_near, CORE).astype(F32)).astype(BF16)
    shares = (mine, flip(near, CORE), flip(other, ACROSS_X))

    def finish(shares):
        mine, near, other = shares
        response_part = mine + near.astype(F32) + other.astype(F32)
        return response_part + LOWRANK_FACTOR * mm(latent_d, lower)

    return (finish, shares), dnorm2, latent_d, dlat_gu, placed


def exchange(evens, odds, by_permutes, later=None):
    if by_permutes:
        total = (evens.astype(F32) + flip(odds, CORE).astype(F32)).astype(BF16)
        if later is not None:
            total, (later,) = tie(total, (later,))
        masks = (ACROSS_X, ACROSS_Y, ACROSS_X | ACROSS_Y)
        return [total[0], *(flip(total[i], mask) for i, mask in enumerate(masks, start=1))], later
    parts = jnp.stack([evens, odds], axis=1).reshape(-1, *evens.shape[1:])
    received = lax.all_to_all(parts, "grp", 0, 0, tiled=True)
    return [received[i] for i in range(received.shape[0])], later


def simple_call(kernel, name, out_shape, operands, flops):
    return pl.pallas_call(
        kernel,
        out_shape=out_shape,
        compiler_params=pltpu.CompilerParams(vmem_limit_bytes=32 << 20),
        cost_estimate=pl.CostEstimate(
            flops=flops,
            transcendentals=0,
            bytes_accessed=sum(array.size * array.dtype.itemsize for array in operands),
        ),
        name=name,
    )(*operands)


def early_gradients_kernel(
    dq_ref,
    asking_ref,
    seen_ref,
    latent_q_ref,
    norm1_ref,
    latent_d_ref,
    sens_ref,
    dlat_gu_ref,
    norm2_ref,
    dlat_o_ref,
    attended_ref,
    latent_o_ref,
    dbranch_ref,
    dlat_q_ref,
    early_ref,
):
    dlat_q = (LOWRANK_FACTOR * mm_nt(dq_ref[...], asking_ref[...]) * seen_ref[...]).astype(BF16)
    dlat_q_ref[...] = dlat_q
    two = LOWRANK_FACTOR
    start = 0
    for factor, small, large in (
        (1.0, dlat_q, norm1_ref),
        (two, latent_q_ref[...], dq_ref),
        (two, latent_d_ref[...], sens_ref),
        (1.0, dlat_gu_ref[...], norm2_ref),
        (1.0, dlat_o_ref[...], attended_ref),
        (two, latent_o_ref[...], dbranch_ref),
    ):
        rows = small.shape[1]
        early_ref[start : start + rows, :] = (factor * mm_tn(small, large[...])).astype(BF16)
        start += rows


def early_gradients(*operands):
    count, width = operands[0].shape
    slots = operands[1].shape[0]
    return simple_call(
        early_gradients_kernel,
        "early_gradients",
        (
            jax.ShapeDtypeStruct((count, slots), BF16),
            jax.ShapeDtypeStruct((7 * slots, width), BF16),
        ),
        operands,
        2 * count * width * 8 * slots,
    )


def key_value_gradients_kernel(turn_ref, *refs):
    received, refs = refs[:-12], refs[-12:]
    early_ref, cos_ref, sin_ref, right_ref, seen_ref, latent_ref, norm_ref = refs[:7]
    dkv_ref, dlat_ref, even_ref, odd_ref, late_ref = refs[7:12]
    half = HEAD_DIM // 2
    total = received[0][...].astype(F32)
    for source in received[1:]:
        total = total + source[...].astype(F32)
    kv_width = total.shape[1] // 2
    pieces = []
    for start in range(0, kv_width, LANES):
        value = total[:, start : start + LANES]
        turned = value * sin_ref[...]
        first = lax.rem(lane_of(turned.shape), HEAD_DIM) < half
        turned = jnp.where(
            first, pltpu.roll(turned, LANES - half, 1), -pltpu.roll(turned, half, 1)
        )
        pieces.append((value * cos_ref[...] + turned).astype(BF16))
    dkv = jnp.concatenate([*pieces, total[:, kv_width:].astype(BF16)], axis=1)
    dkv_ref[...] = dkv
    dlat = (LOWRANK_FACTOR * mm_nt(dkv, right_ref[...]) * seen_ref[...]).astype(BF16)
    dlat_ref[...] = dlat
    late_ref[...] = mm_tn(dlat, norm_ref[...]).astype(BF16)
    thin = (LOWRANK_FACTOR * mm_tn(latent_ref[...], dkv)).astype(BF16)
    rows, head = late_ref.shape[0], early_ref.shape[0]
    thin = jnp.concatenate([thin[: rows // 2, :kv_width], thin[rows // 2 :, kv_width:]], axis=0)
    share = even_ref.shape[2]
    for place in range(2 * even_ref.shape[0]):
        pack_ref = (even_ref, odd_ref)[place % 2]
        columns = pl.ds(pl.multiple_of((place ^ turn_ref[0]) * share, share), share)
        pack_ref[place // 2, :head, :] = early_ref[:, columns]
        pack_ref[place // 2, head : head + rows, :] = late_ref[:, columns]
        for index, start in enumerate(range(0, kv_width, share)):
            first = head + (index + 1) * rows
            pack_ref[place // 2, first : first + rows, :] = thin[:, start : start + share]


def key_value_gradients(turn, received, early, cosines, sines, kv_right, seen_two, latent_kv, norm1):
    members = lax.axis_size("grp")
    count, kv_two = received[0].shape
    rows, width = kv_right.shape[0], norm1.shape[1]
    share = width // members
    packed = early.shape[0] + rows * (1 + kv_two // 2 // share)
    operands = (*received, early, cosines, sines, kv_right, seen_two, latent_kv, norm1)
    pack = jax.ShapeDtypeStruct((members // 2, packed, share), BF16)
    return pl.pallas_call(
        key_value_gradients_kernel,
        out_shape=(
            jax.ShapeDtypeStruct((count, kv_two), BF16),
            jax.ShapeDtypeStruct((count, rows), BF16),
            pack,
            pack,
        ),
        in_specs=[pl.BlockSpec(memory_space=pltpu.SMEM)]
        + [pl.BlockSpec(memory_space=pltpu.VMEM)] * len(operands),
        scratch_shapes=[pltpu.VMEM((rows, width), BF16)],
        compiler_params=pltpu.CompilerParams(vmem_limit_bytes=32 << 20),
        cost_estimate=pl.CostEstimate(
            flops=2 * count * rows * (width + 2 * kv_two),
            transcendentals=0,
            bytes_accessed=sum(array.size * array.dtype.itemsize for array in operands),
        ),
        name="key_value_gradients",
    )(turn, *operands)


def place_kernel(jobs, groups, slots, *refs):
    place_ref, refs = refs[0], refs[1:]
    outs = refs[len(refs) - len(jobs) :]
    for (source, index, is_right), out_ref in zip(jobs, outs):
        value = jnp.concatenate(
            [
                refs[source * groups + g][index * slots : (index + 1) * slots, :]
                for g in range(groups)
            ],
            axis=0,
        )
        if is_right:
            out_ref[...] = mm_tn(place_ref[...], value)
        else:
            out_ref[...] = mm_tn(value, place_ref[...])


def place_gradients(place, sources, slots, jobs):
    groups = len(sources[0])
    narrow = place.shape[1]
    shapes = []
    for source, _, is_right in jobs:
        size = sources[source][0].shape[1]
        shapes.append(
            jax.ShapeDtypeStruct((narrow, size) if is_right else (size, narrow), F32)
        )
    return pl.pallas_call(
        functools.partial(place_kernel, jobs, groups, slots),
        out_shape=tuple(shapes),
        compiler_params=pltpu.CompilerParams(vmem_limit_bytes=32 << 20),
        cost_estimate=pl.CostEstimate(
            flops=2 * sum(shape.size for shape in shapes) * place.shape[0],
            transcendentals=0,
            bytes_accessed=4 * sum(shape.size for shape in shapes),
        ),
        name="place_gradients",
    )(place, *[array for source in sources for array in source])


def round_groups(array):
    groups = lax.axis_size("rep")
    return [array] + [
        lax.ppermute(array, "rep", [(i, (i + shift) % groups) for i in range(groups)])
        for shift in range(1, groups)
    ]


def shards(
    tokens,
    response_sensitivity,
    seq_lengths,
    prefix_lengths,
    adapter_ids,
    attn_gain,
    mlp_gain,
    qkv_weight,
    out_weight,
    gate_up_weight,
    down_weight,
    query_in,
    asking_right_pieces,
    key_in,
    lookup_right_pieces,
    value_in,
    content_right_pieces,
    output_in,
    final_right_pieces,
    gate_in,
    switch_right_pieces,
    up_in,
    lift_right_pieces,
    down_in,
    lower_right_pieces,
):
    count, width = tokens.shape
    members = lax.axis_size("grp")
    groups = lax.axis_size("rep")
    kv_width = lookup_right_pieces.shape[1]
    narrow = query_in.shape[1]
    group = lax.axis_index("rep")
    member = lax.axis_index("grp")
    lengths = lax.dynamic_slice_in_dim(seq_lengths, 2 * group, 2)
    prefixes = lax.dynamic_slice_in_dim(prefix_lengths, 2 * group, 2)
    chosen_ids = lax.dynamic_slice_in_dim(adapter_ids, 2 * group, 2)
    key_count = count * members
    sens = response_sensitivity

    paired = members == 8 and groups % 2 == 0
    qkv_full = lax.all_gather(qkv_weight, "grp", axis=1, tiled=True)
    if paired:
        steps = gather_hidden_block(gate_up_weight, down_weight)
        transfers = next(steps)
    else:
        out_full = lax.all_gather(out_weight, "grp", axis=1, tiled=True)
        down_full = lax.all_gather(down_weight, "grp", axis=1, tiled=True)
        gate_up_full = lax.all_gather(gate_up_weight, "grp", axis=1, tiled=True)

    turn = member if paired else 0
    key_index = jnp.arange(key_count, dtype=jnp.int32)
    key_index = (key_index // count ^ turn) * count + key_index % count
    key_second = (key_index >= lengths[0]).astype(jnp.int32)
    key_position = key_index - key_second * lengths[0]
    own_index = member * count + jnp.arange(count, dtype=jnp.int32)
    own_second = (own_index >= lengths[0]).astype(jnp.int32)
    position = own_index - own_second * lengths[0]
    prefix = jnp.where(own_second == 0, prefixes[0], prefixes[1])
    allowed = (key_second[:, None] == own_second[None, :]) & (
        (key_position[:, None] <= position[None, :]) | (key_position[:, None] < prefix[None, :])
    )
    bias = jnp.where(allowed, 0.0, MASKED).astype(F32)
    first_key = own_second[0] * lengths[0]
    last_key = jnp.max(own_second * lengths[0] + jnp.maximum(position, prefix - 1))
    span = jnp.stack(
        [first_key // KEY_BLOCK, last_key // KEY_BLOCK + 1, turn * count // KEY_BLOCK]
    ).astype(jnp.int32)

    slots = 2 * RANK
    columns = jnp.arange(narrow, dtype=jnp.int32)
    slot = jnp.arange(slots, dtype=jnp.int32)
    slot_column = jnp.where(slot < RANK, chosen_ids[0], chosen_ids[1]) * RANK + slot % RANK
    pick = (columns[:, None] == slot_column[None, :]).astype(BF16)

    def seen_by(device):
        index = device * count + jnp.arange(count, dtype=jnp.int32)
        second = (index >= lengths[0]).astype(jnp.int32)
        return (second[:, None] == slot[None, :] // RANK).astype(F32)

    def pick_in(weight):
        return mm(weight, pick).astype(BF16)

    def pick_right(weight):
        return mm_tn(pick, weight).astype(BF16)

    seen = seen_by(member)
    seen_three = jnp.concatenate([seen, seen, seen], axis=1)
    qkv_in = jnp.concatenate([pick_in(query_in), pick_in(key_in), pick_in(value_in)], axis=1)
    asking = pick_right(asking_right_pieces)
    lookup = pick_right(lookup_right_pieces)
    content = pick_right(content_right_pieces)
    none = jnp.zeros_like(lookup)
    kv_right = jnp.concatenate(
        [jnp.concatenate([lookup, none], axis=1), jnp.concatenate([none, content], axis=1)], axis=0
    )
    out_in = pick_in(output_in)
    final = pick_right(final_right_pieces)
    lower = pick_right(lower_right_pieces)
    small = (
        jnp.concatenate([pick_in(gate_in), pick_in(up_in)], axis=1),
        pick_right(switch_right_pieces),
        pick_right(lift_right_pieces),
        lax.dot_general(
            pick, down_in, (((0,), (1,)), ((), ())), preferred_element_type=F32
        ).astype(BF16),
        lower,
    )

    cycle = jnp.arange(groups * slots, dtype=jnp.int32)
    source = (group - cycle // slots) % groups
    sequence = 2 * source + cycle % slots // RANK
    sequences = jnp.arange(adapter_ids.shape[0], dtype=jnp.int32)
    theirs = jnp.where(sequence[:, None] == sequences[None, :], adapter_ids[None, :], 0)
    all_column = jnp.sum(theirs, axis=1) * RANK + cycle % RANK
    place = (all_column[:, None] == columns[None, :]).astype(BF16)
    incoming = tokens.astype(F32)
    scale_one = inverse_rms(incoming)
    norm1 = (incoming * scale_one * attn_gain).astype(BF16)
    if paired:
        block = down_weight.shape[0] // ACROSS_Y
        start = member % ACROSS_Y * block
        pieces = [lax.dynamic_slice_in_dim(piece, start, block, 1) for piece in small[1:4]]
        others = (seen_by(member ^ mask) for mask in (CORE, ACROSS_X, ACROSS_X | CORE))
        ready = (*transfers, asking, kv_right, out_in, final, lower, place, small[0], *pieces)
        norm1, ready = tie(norm1, (*ready, *others))
        transfers = ready[: len(transfers)]
        asking, kv_right, out_in, final, lower, place, ffn_in, *ready = ready[len(transfers) :]
        small = (ffn_in, lower, *ready[:3])
        all_seen = (seen, *ready[3:])
        transfers = steps.send(transfers)
        out_full = lax.all_gather(out_weight, "grp", axis=1, tiled=True)
    latent_qkv = (mm(norm1, qkv_in) * seen_three).astype(BF16)
    latent_q, latent_kv = latent_qkv[:, :slots], latent_qkv[:, slots:]
    half = HEAD_DIM // 2
    freqs = 10000.0 ** (-2.0 * jnp.arange(half).astype(F32) / HEAD_DIM)
    freqs = jnp.tile(freqs, LANES // half)
    angles = position.astype(F32)[:, None] * freqs[None, :]
    cosines, sines = jnp.cos(angles), jnp.sin(angles)

    def widen(table, size):
        return jnp.tile(table, (1, size // LANES))

    qkv = mm(norm1, qkv_full)
    query = qkv[:, :width] + LOWRANK_FACTOR * mm(latent_q, asking)
    own_kv = qkv[:, width:] + LOWRANK_FACTOR * mm(latent_kv, kv_right)
    query = rotate(query, widen(cosines, width), widen(sines, width)).astype(BF16)
    query = query * jnp.asarray(HEAD_DIM**-0.5, BF16)
    key_own = rotate(own_kv[:, :kv_width], widen(cosines, kv_width), widen(sines, kv_width))
    key_value = jnp.concatenate([key_own, own_kv[:, kv_width:]], axis=1).astype(BF16)
    if paired:
        key_value, transfers = tie(key_value, transfers)
        key_value, (ready, *transfers) = tie(gather_key_values(key_value), (sens, *transfers))
        transfers = steps.send(transfers)
        sens_near, sens_across = flip(ready, CORE), flip(ready, ACROSS_X)
    else:
        key_value = lax.all_gather(key_value, "grp", axis=0, tiled=True)
    attended_low, lse = attention_forward(span, query, key_value, bias)
    if paired:
        attended_low, (sens_near, *transfers) = tie(attended_low, (sens_near, *transfers))
        transfers = (sens_across, *steps.send(transfers))

    latent_o = (mm(attended_low, out_in) * seen).astype(BF16)
    stream = incoming + (mm(attended_low, out_full) + LOWRANK_FACTOR * mm(latent_o, final))
    scale_two = inverse_rms(stream)
    norm2 = (stream * scale_two * mlp_gain).astype(BF16)
    if paired:
        norm2, (sens_across, *transfers) = tie(norm2, transfers)
        sens_pairs = [(sens, sens_near), (sens_across, flip(sens_across, CORE))]
        transfers = steps.send(transfers)
        try:
            steps.send(transfers)
        except StopIteration as stop:
            weights = stop.value
        (finish, shares), dnorm2, latent_d, dlat_gu, deep = feed_forward_shared(
            norm2, sens_pairs, weights, small, all_seen
        )
    else:
        (finish, shares), dnorm2, latent_d, dlat_gu, deep = feed_forward_alone(
            norm2, sens, gate_up_full, down_full, small, seen
        )
    dhidden = sens.astype(F32) + norm_backward(stream, scale_two, mlp_gain, dnorm2)
    dbranch = dhidden.astype(BF16)
    dlat_o = (LOWRANK_FACTOR * mm_nt(dbranch, final) * seen).astype(BF16)
    dattended = (mm_nt(dbranch, out_full) + mm_nt(dlat_o, out_in)).astype(BF16)

    dattended, (deep,) = tie(dattended, (deep,))
    deep_sum = lax.psum_scatter(deep, "grp", scatter_dimension=0, tiled=True)[0]

    dq, dkv_even, dkv_odd = attention_backward(
        span, query, dattended, attended_low, lse, key_value, bias, cosines, sines
    )
    dkv_odd, (deep_sum, *shares) = tie(dkv_odd, (deep_sum, *shares))
    received, dq = exchange(dkv_even, dkv_odd, paired, dq)
    dlat_q, early = early_gradients(
        dq,
        asking,
        seen,
        latent_q,
        norm1,
        latent_d,
        sens,
        dlat_gu,
        norm2,
        dlat_o,
        attended_low,
        latent_o,
        dbranch,
    )
    dnorm_q = mm_nt(dq, qkv_full[:, :width]) + mm_nt(dlat_q, qkv_in[:, :slots])
    turns = jnp.full((1,), turn, jnp.int32)
    dkv, dlat_kv, late_even, late_odd = key_value_gradients(
        turns, received, early, cosines, sines, kv_right, seen_three[:, : 2 * slots], latent_kv, norm1
    )
    deep_sum = round_groups(deep_sum)
    late_parts = [part.astype(F32) for part in exchange(late_even, late_odd, paired)[0]]
    late_sum = round_groups(sum(late_parts[1:], late_parts[0]).astype(BF16))
    level_response = (stream + finish(shares)).astype(BF16)
    dnorm1 = dnorm_q + mm_nt(dkv, qkv_full[:, width:]) + mm_nt(dlat_kv, qkv_in[:, slots:])
    input_grad = (dhidden + norm_backward(incoming, scale_one, attn_gain, dnorm1)).astype(BF16)

    share = width // members
    pieces = kv_width // share
    thin_start = 9 * slots
    thin_sum = [
        jnp.concatenate(
            [
                array[thin_start + 2 * slots * i : thin_start + 2 * slots * (i + 1)]
                for i in range(pieces)
            ],
            axis=1,
        )
        for array in late_sum
    ]
    jobs = (
        (0, 0, False),
        (0, 1, True),
        (0, 7, False),
        (2, 0, True),
        (0, 8, False),
        (2, 1, True),
        (0, 5, False),
        (0, 6, True),
        (0, 3, False),
        (1, 1, True),
        (0, 4, False),
        (1, 2, True),
        (1, 0, False),
        (0, 2, True),
    )
    grads = list(place_gradients(place, (late_sum, deep_sum, thin_sum), slots, jobs))
    own = kv_width // members
    for index in (3, 5):
        grads[index] = lax.dynamic_slice_in_dim(grads[index], member * own, own, 1)
    return (level_response, input_grad, *grads)


def solution(mesh):
    rows = P(("rep", "grp"), None)
    split = P(None, "grp")
    in_specs = (rows, rows, *[P()] * 5, *[split] * 4, *[P()] * 14)
    out_specs = (rows, rows, *[P("grp", None), P(None, "grp")] * 7)
    return jax.shard_map(shards, mesh=mesh, in_specs=in_specs, out_specs=out_specs, check_vma=False)
```
